32 devices in a mesh: grp: 2 (over x), ep: 16 (over z, y, core).
Axes of the slice: x: 2, y: 2, z: 4, core: 2. Of those that a mesh axis runs over, the one named last changes fastest.
Arguments:
- tokens: bfloat16 [2, 4096, 1280], P('grp', 'ep'), may hold values from -18 to 18
- doc_lengths: int32 [2, 4], P('grp'), may hold values from 1 to 2048, 4096 in all within a row
- expert_ids: int32 [2, 4096, 7], P('grp', 'ep'), may hold values from 0 to 15, all different within a row; in each aligned block of 256 rows (0 to 255, 256 to 511, ..., all dimensions but the last counted through in order) at most 192 rows name the same one
- out_grad: bfloat16 [2, 4096, 1280], P('grp', 'ep'), may hold values from -6 to 6
- mixer_gain: float32 [1280], replicated, may hold values from 0.5 to 1.5
- query_weight: bfloat16 [1280, 1280], replicated, may hold values from -0.4375 to 0.4375
- key_weight: bfloat16 [1280, 1280], replicated, may hold values from -0.15625 to 0.15625
- value_weight: bfloat16 [1280, 1280], replicated, may hold values from -0.15625 to 0.15625
- output_weight: bfloat16 [1280, 1280], replicated, may hold values from -2.5 to 2.5
- ffn_gain: float32 [1280], replicated, may hold values from 0.5 to 1.5
- router_weight: bfloat16 [1280, 16], replicated, may hold values from -0.078125 to 0.078125
- shared_gate: bfloat16 [1280, 896], replicated, may hold values from -0.15625 to 0.15625
- shared_up: bfloat16 [1280, 896], replicated, may hold values from -0.15625 to 0.15625
- shared_down: bfloat16 [896, 1280], replicated, may hold values from -0.375 to 0.375
- expert_gate: bfloat16 [16, 1280, 896], P('ep'), may hold values from -0.15625 to 0.15625
- expert_up: bfloat16 [16, 1280, 896], P('ep'), may hold values from -0.15625 to 0.15625
- expert_down: bfloat16 [16, 896, 1280], P('ep'), may hold values from -0.75 to 0.75
Outputs:
- layer_out: bfloat16 [2, 4096, 1280], P('grp', 'ep')
- tokens_grad: bfloat16 [2, 4096, 1280], P('grp', 'ep')
- mixer_gain_grad: float32 [1280], P(('grp', 'ep'))
- query_weight_grad: float32 [1280, 1280], P(('grp', 'ep'))
- key_weight_grad: float32 [1280, 1280], P(('grp', 'ep'))
- value_weight_grad: float32 [1280, 1280], P(('grp', 'ep'))
- output_weight_grad: float32 [1280, 1280], P(('grp', 'ep'))
- ffn_gain_grad: float32 [1280], P(('grp', 'ep'))
- router_weight_grad: float32 [1280, 16], P(('grp', 'ep'))
- shared_gate_grad: float32 [1280, 896], P(('grp', 'ep'))
- shared_up_grad: float32 [1280, 896], P(('grp', 'ep'))
- shared_down_grad: float32 [896, 1280], P(None, ('grp', 'ep'))
- expert_gate_grad: float32 [16, 1280, 896], P('ep', 'grp')
- expert_up_grad: float32 [16, 1280, 896], P('ep', 'grp')
- expert_down_grad: float32 [16, 896, 1280], P('ep', None, 'grp')
- stream_rms: float32 [3], replicated
The draws below stay inside these ranges and needn't reach their ends.
Inputs may be any that keep to these rules, and one draw needn't show every extreme that they name: Each row of doc_lengths sums to 4096, and its largest entry is 2048. `expert_ids`: a token names 7 different experts; the tokens of one device name one expert at most 192 times.
All inputs are finite; a program needn't handle non-finite values.
Results may differ from the reference program's by a relative error of at most 0.025.
Values may be sent and summed in bfloat16 or wider, within the bound.
A program may use at most 384 MiB of HBM per device.

```python
import math
import jax
import jax.numpy as jnp
import numpy as np
from jax import lax

D = 1280
HEADS = 10
HEAD = 128
FF = 896
TOP = 7
TOK_DEV = 256
DOCS = 4
SEQ = 4096
GROUPS = 2
TOKENS = 8192
EXPERTS = 16
CAP = 192


def draw_tokens(key, part):
    position = jnp.arange(GROUPS * SEQ, dtype=jnp.float32).reshape(GROUPS, SEQ, 1) / (GROUPS * SEQ)
    entries = jnp.clip(jax.random.normal(key, (GROUPS, SEQ, D), jnp.float32), -6.0, 6.0)
    rising = jnp.exp(jnp.log(3.0) * position)
    return (entries * rising).astype(jnp.bfloat16)


def block_levels(rng, shape, cuts, low, top_value):
    factor_of = 1.0
    for axis_at, parts in cuts:
        draws = jax.random.uniform(jax.random.fold_in(jax.random.fold_in(rng, 6), axis_at), (parts,), jnp.float32, low / len(cuts), top_value / len(cuts))
        factor_of = factor_of * jnp.repeat(jnp.exp(draws), shape[axis_at] // parts).reshape((-1,) + (1,) * (len(shape) - 1 - axis_at))
    return factor_of


def length_profile(number_of, total, most, skew):
    weights = [(1 << 20) // math.isqrt(standing ** skew) + 1 for standing in range(2, number_of + 1)]
    spare, given = total - most - (number_of - 1), [1] * (number_of - 1)
    while spare > 0:
        movable = [i for i in range(number_of - 1) if given[i] < most]
        pool, left = sum([weights[i] for i in movable]), spare
        for i in movable:
            extra = min(most - given[i], max(1, left * weights[i] // pool), spare)
            given[i] = given[i] + extra
            spare = spare - extra
    return np.array([most] + given)


def uneven_parts(key, count, total, limit, skew):
    if count == 2:
        one = jax.random.randint(key, (), max(1, total - limit), min(limit, total - 1) + 1)
        return jnp.stack([one, total - one])
    sizes = jnp.asarray(length_profile(count, total, limit, skew), jnp.int32)
    couples = (count - 1) // 2
    giver, receiver = sizes[1:1 + 2 * couples:2], sizes[2:2 + 2 * couples:2]
    slack = jnp.minimum(giver - 1, limit - receiver)
    passed = jax.random.randint(jax.random.fold_in(key, 1), (couples,), 0, 1 << 20) % (slack + 1)
    sizes = sizes.at[1:1 + 2 * couples:2].set(giver - passed).at[2:2 + 2 * couples:2].set(receiver + passed)
    return sizes[jax.random.permutation(jax.random.fold_in(key, 2), count)]


def assign_block(own_key, own, number, rows, amount, top, limit, slope):
    ranking = jax.random.permutation(own_key, amount)
    heavy_load, ordinary = portions_of(amount, rows * top, limit, slope, True), portions_of(amount, rows * top, limit, slope, False)
    places = jnp.arange(amount)

    def named(tallies, turn):
        used = int((tallies > 0).sum())
        fixed = max(1, used // 4)
        passed = fixed + (places - fixed + turn * (used - fixed)) % max(1, amount - fixed)
        return jnp.zeros((amount,), jnp.int32).at[ranking[jnp.where(places < fixed, places, passed)]].set(jnp.asarray(tallies, jnp.int32))

    tallies = jnp.where(number % 4 == 0, named(heavy_load, number // 4), named(ordinary, number - number // 4 - 1))
    mixed = jax.random.permutation(jax.random.fold_in(own, 3), amount)
    donor, taker = mixed[0:amount // 2 * 2:2], mixed[1:amount // 2 * 2:2]
    margin = jnp.minimum(tallies[donor] - 1, limit - tallies[taker]) // 2
    margin = jnp.where((donor == ranking[0]) | (taker == ranking[0]) | (tallies[taker] == 0), 0, jnp.maximum(margin, 0))
    passed = jax.random.randint(jax.random.fold_in(own, 4), (amount // 2,), 0, 1 << 20) % (margin + 1)
    tallies = tallies.at[donor].add(-passed).at[taker].add(passed)
    labels = jnp.searchsorted(jnp.cumsum(tallies), jnp.arange(rows * top), side="right").astype(jnp.int32)
    table = labels.reshape(top, rows).T
    table = table[jax.random.permutation(jax.random.fold_in(own, 1), rows)]
    turn = jax.random.randint(jax.random.fold_in(own, 2), (rows, 1), 0, top)
    return jnp.take_along_axis(table, (jnp.arange(top)[None, :] + turn) % top, axis=1)


def portions_of(amount, total, bound, skew, full):
    loads = [(1 << 20) // math.isqrt(standing ** skew) + 1 for standing in range(1, amount + 1)]
    largest = bound if full else min(bound, max(-(-total // amount), total * loads[0] // sum(loads)))
    least = 1 if total - largest >= amount - 1 else 0
    holding, spare = [largest] + [least] * (amount - 1), total - largest - least * (amount - 1)
    while spare > 0:
        movable = [i for i in range(1, amount) if holding[i] < largest] or [i for i in range(1, amount) if holding[i] < bound]
        pool, remaining = sum([loads[i] for i in movable]), spare
        for i in movable:
            extra = min(bound - holding[i], max(1, remaining * loads[i] // pool), spare)
            holding[i] = holding[i] + extra
            spare = spare - extra
    return np.array(holding)


def noise(stream_key, extent, spread, bound, shards=(), held_as=jnp.bfloat16):
    gain = block_levels(stream_key, extent, shards, -0.22, 0.18) if shards else 1.0
    drawn = jax.random.normal(stream_key, extent, jnp.float32) * spread * gain
    return jnp.minimum(jnp.maximum(drawn, -bound), bound).astype(held_as)


def setup_inputs(seed: int = 0) -> dict:
    key_of = jax.random.split(jax.random.key(seed), 18)
    tokens = draw_tokens(jax.random.fold_in(key_of[17], 71), 0)
    doc_lengths = jax.vmap(lambda own: uneven_parts(own, DOCS, SEQ, SEQ // 2, 2))(jax.random.split(key_of[1], GROUPS)).reshape((GROUPS, DOCS)).astype(jnp.int32)
    expert_ids_keys = jax.random.split(jax.random.fold_in(key_of[2], 1), GROUPS * SEQ // TOK_DEV)
    expert_ids_turns = jax.random.permutation(jax.random.fold_in(key_of[2], 3), GROUPS * SEQ // TOK_DEV)
    expert_ids = jax.vmap(lambda own, number: assign_block(jax.random.fold_in(key_of[2], 2), own, number, TOK_DEV, EXPERTS, TOP, CAP, 1))(expert_ids_keys, expert_ids_turns).reshape((GROUPS, SEQ, TOP))
    out_grad = noise(key_of[3], (GROUPS, SEQ, D), 1.0, 6.0, ((0, 2), (1, 16)))
    mixer_gain = jnp.clip(1.0 + 0.1 * jax.random.normal(key_of[4], (D,), jnp.float32), 0.5, 1.5)
    query_weight = noise(key_of[5], (D, HEADS * HEAD), (D // 6) ** -0.5, 0.4375)
    key_weight = noise(key_of[6], (D, HEADS * HEAD), D ** -0.5, 0.15625)
    value_weight = noise(key_of[7], (D, HEADS * HEAD), D ** -0.5, 0.15625)
    output_weight = noise(key_of[8], (HEADS * HEAD, D), (max(1, 20 * D // SEQ)) ** -0.5, 2.5)
    ffn_gain = jnp.clip(1.0 + 0.1 * jax.random.normal(key_of[9], (D,), jnp.float32), 0.5, 1.5)
    router_weight = noise(key_of[10], (D, EXPERTS), (4 * D) ** -0.5, 0.078125)
    shared_gate = noise(key_of[11], (D, FF), D ** -0.5, 0.15625)
    shared_up = noise(key_of[12], (D, FF), D ** -0.5, 0.15625)
    shared_down = noise(key_of[13], (FF, D), (max(1, FF // 4)) ** -0.5, 0.375)
    expert_gate = noise(key_of[14], (EXPERTS, D, FF), D ** -0.5, 0.15625, ((0, 16),))
    expert_up = noise(key_of[15], (EXPERTS, D, FF), D ** -0.5, 0.15625, ((0, 16),))
    expert_down = noise(key_of[16], (EXPERTS, FF, D), (max(1, FF // 16)) ** -0.5, 0.75, ((0, 16),))
    return dict(tokens=tokens, doc_lengths=doc_lengths, expert_ids=expert_ids, out_grad=out_grad, mixer_gain=mixer_gain, query_weight=query_weight, key_weight=key_weight, value_weight=value_weight, output_weight=output_weight, ffn_gain=ffn_gain, router_weight=router_weight, shared_gate=shared_gate, shared_up=shared_up, shared_down=shared_down, expert_gate=expert_gate, expert_up=expert_up, expert_down=expert_down)


epsilon = 1e-06
rope_base = 10000.0
masked_value = -1e+30

@jax.custom_vjp
def low(v):
    return lax.optimization_barrier(v.astype(jnp.bfloat16)).astype(jnp.float32)

@jax.custom_vjp
def low_back(v):
    return v

def low_keep(v):
    return (low(v), None)

def low_pass(kept, grad):
    return (grad,)

def back_keep(v):
    return (v, None)

def back_low(kept, grad):
    return (low(grad),)
low.defvjp(low_keep, low_pass)
low_back.defvjp(back_keep, back_low)

def product(left_op, right_op):
    return jnp.dot(left_op, right_op, precision=lax.Precision.HIGHEST)

def normed(values, gain_vec):
    return values * lax.rsqrt(lax.optimization_barrier(jnp.mean(values * values, axis=-1, keepdims=True)) + epsilon) * gain_vec

def rotary(values, positions):
    half_dim = values.shape[-1] // 2
    frequency = rope_base ** (-jnp.arange(half_dim, dtype=jnp.float32) / half_dim)
    angles = positions[:, None] * frequency[None, :]
    cosine = jnp.cos(angles)[:, None, :]
    sine_val = jnp.sin(angles)[:, None, :]
    lower_half = values[..., :half_dim]
    upper_half = values[..., half_dim:]
    return jnp.concatenate([lower_half * cosine - upper_half * sine_val, upper_half * cosine + lower_half * sine_val], axis=-1)

def group_layer(params, group_tokens, group_ids, group_lengths):
    mixer_gain, query_weight, key_weight, value_weight, output_weight, ffn_gain, router_weight, shared_gate, shared_up, shared_down, expert_gate, expert_up, expert_down = params
    token_pos = jnp.arange(SEQ, dtype=jnp.int32)
    position = token_pos.astype(jnp.float32)
    doc_ends = jnp.cumsum(group_lengths)
    doc_index = lax.optimization_barrier(jnp.sum((token_pos[:, None] >= doc_ends[None, :]).astype(jnp.int32), axis=1))
    hidden_low = low(normed(group_tokens, mixer_gain))
    query_lin = low_back(product(hidden_low, query_weight)).reshape(SEQ, HEADS, HEAD)
    key_lin = low_back(product(hidden_low, key_weight)).reshape(SEQ, HEADS, HEAD)
    values_low = low(low_back(product(hidden_low, value_weight))).reshape(SEQ, HEADS, HEAD)
    queries = low(rotary(query_lin, position) * HEAD ** (-0.5))
    keys_rot = low(rotary(key_lin, position))
    query_block = min(SEQ, 512)
    block_count = SEQ // query_block

    def attend(packed):
        query_part, first_row = packed
        query_pos = first_row + jnp.arange(query_block, dtype=jnp.int32)
        query_doc = lax.dynamic_slice_in_dim(doc_index, first_row, query_block)
        scores = low_back(jnp.einsum('qhd,khd->hqk', query_part, keys_rot, precision=lax.Precision.HIGHEST))
        visible = (query_doc[:, None] == doc_index[None, :]) & (token_pos[None, :] <= query_pos[:, None])
        scores = jnp.where(visible[None], scores, masked_value)
        weights = low(jax.nn.softmax(scores, axis=-1))
        return jnp.einsum('hqk,khd->qhd', weights, values_low, precision=lax.Precision.HIGHEST)
    firsts = jnp.arange(block_count, dtype=jnp.int32) * query_block
    mixed_heads = lax.map(jax.checkpoint(attend), (queries.reshape(block_count, query_block, HEADS, HEAD), firsts))
    mixed_low = low(low_back(mixed_heads.reshape(SEQ, HEADS * HEAD)))
    mixer_out = low_back(product(mixed_low, output_weight))
    residual = group_tokens + mixer_out
    ffn_low = low(normed(residual, ffn_gain))
    logits = low_back(product(ffn_low, router_weight))
    choose = (group_ids[:, :, None] == jnp.arange(EXPERTS, dtype=jnp.int32)[None, None, :]).astype(jnp.float32)
    chosen = jnp.einsum('tke,te->tk', choose, logits, precision=lax.Precision.HIGHEST)
    gate_probs = jax.nn.softmax(chosen, axis=-1)
    expert_share = jnp.einsum('tk,tke->et', gate_probs, choose, precision=lax.Precision.HIGHEST)
    shared_mid = low(jax.nn.silu(low_back(product(ffn_low, shared_gate))) * low_back(product(ffn_low, shared_up)))
    shared_out = product(shared_mid, shared_down)

    def expert(running, packed):
        gate_mat, up_mat, down_mat, share_row = packed
        expert_in = low_back(ffn_low)
        middle = low(jax.nn.silu(low_back(product(expert_in, gate_mat))) * low_back(product(expert_in, up_mat)))
        expert_out = low(low_back(product(middle, down_mat)))
        return (running + share_row[:, None] * expert_out, None)
    routed, unused = lax.scan(jax.checkpoint(expert), jnp.zeros((SEQ, D), jnp.float32), (expert_gate, expert_up, expert_down, expert_share))
    ffn_out = shared_out + routed
    layer_out = residual + ffn_out
    squares = jnp.stack([jnp.sum(residual * residual), jnp.sum(mixer_out * mixer_out), jnp.sum(layer_out * layer_out)])
    return (layer_out, squares)

def reference(tokens, doc_lengths, expert_ids, out_grad, mixer_gain, query_weight, key_weight, value_weight, output_weight, ffn_gain, router_weight, shared_gate, shared_up, shared_down, expert_gate, expert_up, expert_down):
    params = tuple((item.astype(jnp.float32) for item in (mixer_gain, query_weight, key_weight, value_weight, output_weight, ffn_gain, router_weight, shared_gate, shared_up, shared_down, expert_gate, expert_up, expert_down)))
    inputs = tokens.astype(jnp.float32)

    def forward(all_tokens, weights_all):

        def group_step(stat_sums, packed):
            group_tokens, group_ids, group_lengths = packed
            layer_out, squares = group_layer(weights_all, group_tokens, group_ids, group_lengths)
            return (stat_sums + squares, layer_out)
        stat_sums, outputs = lax.scan(group_step, jnp.zeros((3,), jnp.float32), (all_tokens, expert_ids, doc_lengths))
        return (outputs, stat_sums)
    (outputs, stat_sums), pull = jax.vjp(forward, inputs, params)
    tokens_grad, grads = pull((out_grad.astype(jnp.float32), jnp.zeros((3,), jnp.float32)))
    stream_rms = jnp.sqrt(stat_sums / (TOKENS * D))
    return (outputs.astype(jnp.bfloat16), tokens_grad.astype(jnp.bfloat16), grads[0], grads[1], grads[2], grads[3], grads[4], grads[5], grads[6], grads[7], grads[8], grads[9], grads[10], grads[11], grads[12], stream_rms)
```

```python
import functools

import jax
import jax.numpy as jnp
from jax import lax
from jax.experimental import pallas as pl
from jax.experimental.pallas import tpu as pltpu
from jax.sharding import PartitionSpec as P

HEADS = 10
HEAD = 128
TOP = 7

epsilon = 1e-06
rope_base = 10000.0
masked_value = -1e30


def normed(values, gain_vec):
    return (
        values * lax.rsqrt(jnp.mean(values * values, axis=-1, keepdims=True) + epsilon) * gain_vec
    )


def rotary(values, positions, direction):
    half_dim = values.shape[-1] // 2
    frequency = rope_base ** (-jnp.arange(half_dim, dtype=jnp.float32) / half_dim)
    angles = positions[:, None] * frequency[None, :]
    cosine = jnp.cos(angles)[:, None, :]
    sine_val = direction * jnp.sin(angles)[:, None, :]
    lower_half = values[..., :half_dim]
    upper_half = values[..., half_dim:]
    return jnp.concatenate(
        [lower_half * cosine - upper_half * sine_val, upper_half * cosine + lower_half * sine_val],
        axis=-1,
    )


def inner_left(left_op, right_op):
    return lax.dot_general(
        left_op, right_op, (((0,), (0,)), ((), ())), preferred_element_type=jnp.float32
    )


def inner_right(left_op, right_op):
    return lax.dot_general(
        left_op, right_op, (((1,), (1,)), ((), ())), preferred_element_type=jnp.float32
    )


def silu_parts(pre_act):
    sigmoid_val = jax.nn.sigmoid(pre_act)
    return (pre_act * sigmoid_val, sigmoid_val * (1.0 + pre_act * (1.0 - sigmoid_val)))


MESH = pl.DeviceIdType.MESH
VMEM_MOST = 64 * 1024 * 1024 - 65536


def when(cond):
    if cond is True:
        return lambda f: f()
    if cond is False:
        return lambda f: None
    return pl.when(cond)


def both(*conds):
    out = True
    for cond in conds:
        if cond is False:
            return False
        if cond is True:
            continue
        out = cond if out is True else jnp.logical_and(out, cond)
    return out


class Plan:
    def __init__(self, ep_count, window):
        self.long = 4
        self.wide = ep_count // 8
        self.window = window
        self.steps = (
            list(range(self.long // 2 + 1))
            if window
            else list(range(-(self.long - 1), self.long))
        )

    def place(self):
        me = lax.axis_index("ep")
        return me // (2 * self.wide), (me // 2) % self.wide, me % 2

    def slot(self, a, b, c):
        return (a * self.wide + b) * 2 + c

    def inside(self, a):
        return jnp.logical_and(a >= 0, a < self.long)

    def need(self, d, b, c, b0, c0):
        if not self.window or 0 < d < self.long // 2:
            return True
        if d == 0:
            return jnp.logical_or(b0 < b, jnp.logical_and(b0 == b, c0 <= c))
        return jnp.logical_or(b0 > b, jnp.logical_and(b0 == b, c0 >= c))

    def need_pair(self, d, b, b0):
        if not self.window or 0 < d < self.long // 2:
            return True
        return b0 < b if d == 0 else b0 > b

    def greet(self, a, b, c):
        barrier = pltpu.get_barrier_semaphore()

        def signal(cond, dev):
            @when(cond)
            def _():
                pl.semaphore_signal(barrier, inc=1, device_id={"ep": dev}, device_id_type=MESH)

        signal(a + 1 < self.long, self.slot(a + 1, b, c))
        signal(a > 0, self.slot(a - 1, b, c))
        for k in range(1, self.wide):
            signal(True, self.slot(a, (b + k) % self.wide, c))
        signal(True, self.slot(a, b, 1 - c))
        ends = (a == 0).astype(jnp.int32) + (a == self.long - 1).astype(jnp.int32)
        pl.semaphore_wait(barrier, self.wide + 2 - ends)


def gather_kernel(plan, pieces, x_ref, out_ref, ra, sa_up, sa_dn, rb, sb, rc, sc, own):
    a, b, c = plan.place()
    steps, wide = plan.steps, plan.wide
    at = {d: i for i, d in enumerate(steps)}
    rows = x_ref.shape[0] // pieces

    def part(q):
        return pl.ds(pl.multiple_of(q * rows, rows), rows)

    def copy(q, src, slot, ssem, rsem, dev):
        return pltpu.make_async_remote_copy(
            src_ref=src, dst_ref=out_ref.at[slot, part(q)], send_sem=ssem, recv_sem=rsem,
            device_id={"ep": dev}, device_id_type=MESH,
        )

    def hops(d, q):
        i = at[d]
        slot = plan.slot(a - d, b, c)
        src = x_ref.at[part(q)] if d == 0 else out_ref.at[slot, part(q)]
        real = plan.inside(a - d)
        out = []
        if d >= 0 and d + 1 in at:
            out.append((both(real, a + 1 < plan.long), lambda: copy(
                q, src, slot, sa_up.at[i, q], ra.at[at[d + 1], q], plan.slot(a + 1, b, c))))
        if d <= 0 and d - 1 in at:
            out.append((both(real, a > 0), lambda: copy(
                q, src, slot, sa_dn.at[i, q], ra.at[at[d - 1], q], plan.slot(a - 1, b, c))))
        for k in range(1, wide):
            to = (b + k) % wide
            out.append((both(real, plan.need_pair(d, to, b)), lambda k=k, to=to: copy(
                q, src, slot, sb.at[i, k, q], rb.at[i, k, q], plan.slot(a, to, c))))
        out.append((both(real, plan.need(d, b, 1 - c, b, c)), lambda: copy(
            q, src, slot, sc.at[i, 0, q], rc.at[i, 0, q], plan.slot(a, b, 1 - c))))
        return out

    def cross(d, k, q):
        i = at[d]
        b0 = (b + wide - k) % wide
        slot = plan.slot(a - d, b0, c)
        real = plan.inside(a - d)
        come = lambda: copy(q, x_ref.at[part(q)], slot, sb.at[i, k, q], rb.at[i, k, q], plan.slot(a, b, c))
        go = lambda: copy(q, out_ref.at[slot, part(q)], slot, sc.at[i, k, q], rc.at[i, k, q],
                          plan.slot(a, b, 1 - c))
        return (both(real, plan.need_pair(d, b, b0)), come,
                both(real, plan.need(d, b, 1 - c, b0, c)), go)

    plan.greet(a, b, c)
    keep = pltpu.make_async_copy(x_ref, out_ref.at[plan.slot(a, b, c)], own)

    @pl.loop(0, pieces)
    def _(q):
        for cond, go in hops(0, q):
            @when(cond)
            def _(go=go):
                go().start()

    keep.start()
    far = max(abs(d) for d in steps)
    for step in range(1, far + 3):
        @pl.loop(0, pieces)
        def _(q, step=step):
            for d in (step, -step):
                if d in at:
                    @when(plan.inside(a - d))
                    def _(d=d):
                        slot = plan.slot(a - d, b, c)
                        copy(q, x_ref.at[part(q)], slot, sa_up.at[0, q], ra.at[at[d], q],
                             plan.slot(a, b, c)).wait_recv()
                        for cond, go in hops(d, q):
                            @when(cond)
                            def _(go=go):
                                go().start()
            for d in sorted({step - 2, 2 - step}) if step > 1 else ():
                if d in at:
                    for k in range(1, wide):
                        came, come, goes, go = cross(d, k, q)
                        @when(came)
                        def _(come=come):
                            come().wait_recv()
                        @when(goes)
                        def _(go=go):
                            go().start()
    keep.wait()

    @pl.loop(0, pieces)
    def _(q):
        for d in steps:
            i = at[d]
            real = plan.inside(a - d)
            for k in range(wide):
                b0 = (b + wide - k) % wide
                slot = plan.slot(a - d, b0, 1 - c)
                @when(both(real, plan.need(d, b, c, b0, 1 - c)))
                def _(slot=slot, i=i, k=k):
                    copy(q, x_ref.at[part(q)], slot, sc.at[i, k, q], rc.at[i, k, q],
                         plan.slot(a, b, c)).wait_recv()
            for cond, go in hops(d, q):
                @when(cond)
                def _(go=go):
                    go().wait_send()
            for k in range(1, wide):
                came, come, goes, go = cross(d, k, q)
                @when(goes)
                def _(go=go):
                    go().wait_send()


def gather_rows(block, window, collective_id, pieces=4):
    ep_count = lax.axis_size("ep")
    plan = Plan(ep_count, window)
    n, wide = len(plan.steps), plan.wide
    sem = pltpu.SemaphoreType.DMA
    return pl.pallas_call(
        functools.partial(gather_kernel, plan, pieces),
        out_shape=jax.ShapeDtypeStruct((ep_count,) + block.shape, block.dtype),
        in_specs=[pl.BlockSpec(memory_space=pltpu.VMEM)],
        out_specs=pl.BlockSpec(memory_space=pl.ANY),
        scratch_shapes=[sem((n, pieces)), sem((n, pieces)), sem((n, pieces)), sem((n, wide, pieces)),
                        sem((n, wide, pieces)), sem((n, wide, pieces)), sem((n, wide, pieces)), sem],
        compiler_params=pltpu.CompilerParams(collective_id=collective_id, has_side_effects=True),
        name="gather_rows",
    )(block)


def add_rows(dst, others, out=None):
    rows = dst.shape[0]
    piece = next(p for p in (32, 16, 8, rows) if rows % p == 0)
    out = dst if out is None else out

    @pl.loop(0, rows // piece)
    def _(i):
        at = pl.ds(pl.multiple_of(i * piece, piece), piece)
        if len(others) == 1 and out.dtype == jnp.bfloat16:
            out[at, :] = dst[at, :] + others[0][at, :]
        else:
            total = dst[at, :].astype(jnp.float32)
            for other in others:
                total = total + other[at, :].astype(jnp.float32)
            out[at, :] = total.astype(out.dtype)


def scatter_kernel(plan, pieces, p_ref, out_ref, held, rcb, rbb, r_hi, r_lo, sc, rc, sb, rb, sa, rhi, rlo, ld):
    a, b, c = plan.place()
    steps, wide = plan.steps, plan.wide
    at = {d: i for i, d in enumerate(steps)}
    rows = p_ref.shape[1] // pieces

    def part(q):
        return pl.ds(pl.multiple_of(q * rows, rows), rows)

    def remote(src, dst, ssem, rsem, dev):
        return pltpu.make_async_remote_copy(
            src_ref=src, dst_ref=dst, send_sem=ssem, recv_sem=rsem,
            device_id={"ep": dev}, device_id_type=MESH,
        )

    order = sorted(steps, key=lambda d: -abs(d))
    ks = list(range(1, wide)) + [0]

    def load(d, k, q):
        i, b0 = at[d], (b + wide - k) % wide
        return (both(plan.inside(a - d), plan.need(d, b, c, b0, c)), lambda: pltpu.make_async_copy(
            p_ref.at[plan.slot(a - d, b0, c), part(q)], held.at[i, k, part(q)], ld.at[i, k, q]))

    def cross(d, k, q):
        i, b0 = at[d], (b + wide - k) % wide
        real = plan.inside(a - d)
        return (both(real, plan.need(d, b, c, b0, 1 - c)), lambda: remote(
            p_ref.at[plan.slot(a - d, b0, 1 - c), part(q)], rcb.at[i, k, part(q)], sc.at[i, k, q],
            rc.at[i, k, q], plan.slot(a, b, 1 - c)), both(real, plan.need(d, b, 1 - c, b0, c)))

    def over(d, k, q):
        i, b0 = at[d], (b + wide - k) % wide
        return (both(plan.inside(a - d), plan.need_pair(d, b, b0)), lambda: remote(
            held.at[i, k, part(q)], rbb.at[i, k - 1, part(q)], sb.at[i, k, q], rb.at[i, k, q],
            plan.slot(a, b0, c)))

    def along(d, q):
        i, up = at[d], d < 0
        j = at[d + 1 if up else d - 1]
        return plan.inside(a - d), lambda: remote(
            held.at[i, 0, part(q)], (r_lo if up else r_hi).at[j, part(q)], sa.at[i, q],
            (rlo if up else rhi).at[j, q], plan.slot(a + (1 if up else -1), b, c))

    plan.greet(a, b, c)
    for k in ks:
        @pl.loop(0, pieces)
        def _(q, k=k):
            for d in order:
                for cond, go in (cross(d, k, q)[:2], load(d, k, q)):
                    @when(cond)
                    def _(go=go):
                        go().start()

    def first(d, k, q):
        cond, go = load(d, k, q)
        @when(cond)
        def _():
            go().wait()
        _, cross_go, come = cross(d, k, q)
        @when(come)
        def _():
            cross_go().wait_recv()
            add_rows(held.at[at[d], k, part(q)], [rcb.at[at[d], k, part(q)]])

    for k in ks[:-1]:
        @pl.loop(0, pieces)
        def _(q, k=k):
            for d in order:
                first(d, k, q)
                cond, go = over(d, k, q)
                @when(cond)
                def _(go=go):
                    go().start()
    for d in order:
        @pl.loop(0, pieces)
        def _(q, d=d):
            i = at[d]
            real = plan.inside(a - d)
            first(d, 0, q)
            for k in range(1, wide):
                frm = (b + k) % wide
                @when(both(real, plan.need_pair(d, frm, b)))
                def _(k=k):
                    over(d, k, q)[1]().wait_recv()
                    add_rows(held.at[i, 0, part(q)], [rbb.at[i, k - 1, part(q)]])
            for inner, cond, buf, sem in ((d >= 0 and d + 1 in at, a + 1 < plan.long, r_hi, rhi),
                                          (d <= 0 and d - 1 in at, a > 0, r_lo, rlo)):
                if inner:
                    @when(both(real, cond))
                    def _(buf=buf, sem=sem):
                        remote(held.at[i, 0, part(q)], buf.at[i, part(q)], sa.at[i, q], sem.at[i, q],
                               plan.slot(a, b, c)).wait_recv()
                        add_rows(held.at[i, 0, part(q)], [buf.at[i, part(q)]])
            if d:
                cond, go = along(d, q)
                @when(cond)
                def _():
                    go().start()
    out_ref[...] = held[at[0], 0]

    @pl.loop(0, pieces)
    def _(q):
        for d in steps:
            sends = [cross(d, k, q)[:2] for k in range(wide)] + [over(d, k, q) for k in range(1, wide)]
            if d:
                sends.append(along(d, q))
            for cond, go in sends:
                @when(cond)
                def _(go=go):
                    go().wait_send()


def scatter_rows(parts, window, collective_id, pieces=4):
    ep_count, rows, width = parts.shape
    plan = Plan(ep_count, window)
    n, wide = len(plan.steps), plan.wide
    sem = lambda *lead: pltpu.SemaphoreType.DMA(lead + (pieces,))
    blocks = lambda *lead: pltpu.VMEM(lead + (rows, width), parts.dtype)
    return pl.pallas_call(
        functools.partial(scatter_kernel, plan, pieces),
        out_shape=jax.ShapeDtypeStruct((rows, width), parts.dtype),
        in_specs=[pl.BlockSpec(memory_space=pl.ANY)],
        out_specs=pl.BlockSpec(memory_space=pltpu.VMEM),
        scratch_shapes=[blocks(n, wide), blocks(n, wide), blocks(n, wide - 1), blocks(n), blocks(n),
                        sem(n, wide), sem(n, wide), sem(n, wide), sem(n, wide),
                        sem(n), sem(n), sem(n), sem(n, wide)],
        compiler_params=pltpu.CompilerParams(
            collective_id=collective_id, has_side_effects=True, vmem_limit_bytes=VMEM_MOST),
        name="scatter_rows",
    )(parts)


def whole_kernel(sizes, small, p_ref, s_ref, out_ref, so_ref, held, rcb, rxb, rbb, rab, sbuf, *sems):
    groups, long, wide = sizes
    g = lax.axis_index("grp")
    me = lax.axis_index("ep")
    a, b, c = me // (2 * wide), (me // 2) % wide, me % 2
    sc, rc, sx, rx, sb, rb, sa, ra, ld, ss, rs = sems

    def dev(gg, aa, bb, cc):
        return {"grp": gg, "ep": (aa * wide + bb) * 2 + cc}

    def slot(gg, aa, bb, cc):
        return ((gg * long + aa) * wide + bb) * 2 + cc

    def remote(src, dst, ssem, rsem, to):
        return pltpu.make_async_remote_copy(
            src_ref=src, dst_ref=dst, send_sem=ssem, recv_sem=rsem, device_id=to, device_id_type=MESH)

    peers = ([dev(g, a, b, 1 - c)] + [dev((g + k) % groups, a, b, c) for k in range(1, groups)]
             + [dev(g, a, (b + k) % wide, c) for k in range(1, wide)]
             + [dev(g, (a + k) % long, b, c) for k in range(1, long)])
    barrier = pltpu.get_barrier_semaphore()
    for to in peers:
        pl.semaphore_signal(barrier, inc=1, device_id=to, device_id_type=MESH)
    pl.semaphore_wait(barrier, len(peers))

    def spot(kx, ka, kb, cc):
        return slot((g + groups - kx) % groups, (a + long - ka) % long, (b + wide - kb) % wide, cc)

    keys = [(kx, ka, kb) for kx in list(range(1, groups)) + [0] for kb in list(range(1, wide)) + [0]
            for ka in list(range(1, long)) + [0]]
    cross = {}
    load = {}
    for kx, ka, kb in keys:
        key = (kx, ka, kb)
        cross[key] = remote(p_ref.at[spot(kx, ka, kb, 1 - c)], rcb.at[key], sc.at[key], rc.at[key],
                            dev(g, a, b, 1 - c))
        load[key] = pltpu.make_async_copy(p_ref.at[spot(kx, ka, kb, c)], held.at[key], ld.at[key])
        cross[key].start()
        load[key].start()

    def over_x(kx, ka, kb):
        return remote(held.at[kx, ka, kb], rxb.at[kx - 1, ka, kb], sx.at[kx - 1, ka, kb], rx.at[kx - 1, ka, kb],
                      dev((g + groups - kx) % groups, a, b, c))

    def over_b(ka, kb):
        return remote(held.at[0, ka, kb], rbb.at[ka, kb - 1], sb.at[ka, kb - 1], rb.at[ka, kb - 1],
                      dev(g, a, (b + wide - kb) % wide, c))

    def over_a(ka):
        return remote(held.at[0, ka, 0], rab.at[ka - 1], sa.at[ka - 1], ra.at[ka - 1],
                      dev(g, (a + long - ka) % long, b, c))

    for key in keys:
        load[key].wait()
        cross[key].wait_recv()
        add_rows(held.at[key], [rcb.at[key]])
        if key[0]:
            over_x(*key).start()

    if small:
        sbuf[0] = s_ref[...]
        spot_of = 1
        rounds = [[dev(g, a, b, 1 - c)],
                  [dev((g + k) % groups, a, b, c) for k in range(1, groups)],
                  [dev(g, a, (b + k) % wide, c) for k in range(1, wide)],
                  [dev(g, (a + k) % long, b, c) for k in range(1, long)]]
        copies = []
        for tos in rounds:
            mine = []
            for to in tos:
                mine.append(remote(so_ref if len(copies) else sbuf.at[0], sbuf.at[spot_of], ss.at[spot_of], rs.at[spot_of], to))
                spot_of += 1
            copies.append(mine)

    for kb in list(range(1, wide)) + [0]:
        for ka in list(range(1, long)) + [0]:
            for kx in range(1, groups):
                over_x(kx, ka, kb).wait_recv()
            add_rows(held.at[0, ka, kb], [rxb.at[kx - 1, ka, kb] for kx in range(1, groups)])
            if kb:
                over_b(ka, kb).start()
    for ka in list(range(1, long)) + [0]:
        for kb in range(1, wide):
            over_b(ka, kb).wait_recv()
        add_rows(held.at[0, ka, 0], [rbb.at[ka, kb - 1] for kb in range(1, wide)])
        if ka:
            over_a(ka).start()
    for ka in range(1, long):
        over_a(ka).wait_recv()
    add_rows(held.at[0, 0, 0], [rab.at[ka - 1] for ka in range(1, long)], out_ref)
    for key in keys:
        cross[key].wait_send()
        if key[0]:
            over_x(*key).wait_send()
    for ka in range(long):
        for kb in range(1, wide):
            over_b(ka, kb).wait_send()
        if ka:
            over_a(ka).wait_send()


def scatter_whole(parts, collective_id):
    count, rows, width = parts.shape
    groups, ep_count = lax.axis_size("grp"), lax.axis_size("ep")
    long, wide = 4, ep_count // 8
    sem = pltpu.SemaphoreType.DMA
    blocks = lambda *lead: pltpu.VMEM(lead + (rows, width), parts.dtype)
    full = (groups, long, wide)

    def kernel(p_ref, out_ref, *scratch):
        whole_kernel(full, False, p_ref, None, out_ref, None, *scratch[:5], None, *scratch[5:], None, None)

    return pl.pallas_call(
        kernel,
        out_shape=jax.ShapeDtypeStruct((rows, width), jnp.float32),
        in_specs=[pl.BlockSpec(memory_space=pl.ANY)],
        out_specs=pl.BlockSpec(memory_space=pltpu.VMEM),
        scratch_shapes=[blocks(*full), blocks(*full), blocks(groups - 1, long, wide), blocks(long, wide - 1),
                        blocks(long - 1),
                        sem(full), sem(full), sem((groups - 1, long, wide)), sem((groups - 1, long, wide)),
                        sem((long, wide - 1)), sem((long, wide - 1)), sem((long - 1,)), sem((long - 1,)), sem(full)],
        compiler_params=pltpu.CompilerParams(
            collective_id=collective_id, has_side_effects=True, vmem_limit_bytes=VMEM_MOST),
        name="scatter_whole",
    )(parts)


def visible_bias(shape, key_axis, first_key, start, first_query):
    key_pos = first_key + lax.broadcasted_iota(jnp.int32, shape, key_axis)
    query_pos = first_query + lax.broadcasted_iota(jnp.int32, shape, 1 - key_axis)
    seen = jnp.logical_and(key_pos >= start, key_pos <= query_pos)
    return jnp.where(seen, 0.0, masked_value)


def heads_at(h):
    return pl.ds(pl.multiple_of(h * HEAD, HEAD), HEAD)


def attend_kernel(info, q_ref, start_ref, kv_ref, mixed_ref, low_ref, total_ref, bias, top, norm, acc):
    step = pl.program_id(0)
    me, first_block = info[0], info[1]
    rows, width = q_ref.shape
    block = me - step

    @pl.when(step == 0)
    def _():
        top[...] = jnp.full_like(top, masked_value)
        norm[...] = jnp.zeros_like(norm)
        acc[...] = jnp.zeros_like(acc)

    @pl.when(block >= first_block)
    def _():
        bias[...] = visible_bias((rows, rows), 1, block * rows, start_ref[...], me * rows)

        @pl.loop(0, HEADS)
        def _(h):
            at = heads_at(h)
            values = kv_ref[0, :, pl.ds(pl.multiple_of(width + h * HEAD, HEAD), HEAD)]
            scores = inner_right(q_ref[:, at], kv_ref[0, :, at]) + bias[...]
            old = top[h]
            new = jnp.maximum(old, jnp.max(scores, axis=1, keepdims=True))
            weights = jnp.exp(scores - new)
            shrink = jnp.exp(old - new)
            top[h] = new
            norm[h] = norm[h] * shrink + jnp.sum(weights, axis=1, keepdims=True)
            acc[:, at] = acc[:, at] * shrink + jnp.dot(
                weights.astype(jnp.bfloat16), values, preferred_element_type=jnp.float32
            )

    @pl.when(step == pl.num_programs(0) - 1)
    def _():
        @pl.loop(0, HEADS)
        def _(h):
            at = heads_at(h)
            mixed = acc[:, at] / norm[h]
            mixed_ref[:, at] = mixed
            low_ref[:, at] = mixed.astype(jnp.bfloat16)
            total_ref[h] = top[h] + jnp.log(norm[h])


def attend(info, queries, start, pairs):
    rows, width = queries.shape
    steps = pairs.shape[0] // 2 + 1
    whole = lambda *shape: pl.BlockSpec(shape, lambda s, info: (0,) * len(shape))
    return pl.pallas_call(
        attend_kernel,
        out_shape=(
            jax.ShapeDtypeStruct((rows, width), jnp.float32),
            jax.ShapeDtypeStruct((rows, width), jnp.bfloat16),
            jax.ShapeDtypeStruct((HEADS, rows, 1), jnp.float32),
        ),
        grid_spec=pltpu.PrefetchScalarGridSpec(
            num_scalar_prefetch=1,
            grid=(steps,),
            in_specs=[
                whole(rows, width),
                whole(rows, 1),
                pl.BlockSpec((1, rows, 2 * width), lambda s, info: (jnp.maximum(info[0] - s, info[1]), 0, 0)),
            ],
            out_specs=(whole(rows, width), whole(rows, width), whole(HEADS, rows, 1)),
            scratch_shapes=[
                pltpu.VMEM((rows, rows), jnp.float32),
                pltpu.VMEM((HEADS, rows, 1), jnp.float32),
                pltpu.VMEM((HEADS, rows, 1), jnp.float32),
                pltpu.VMEM((rows, width), jnp.float32),
            ],
        ),
        cost_estimate=pl.CostEstimate(
            flops=4 * rows * rows * width * steps, bytes_accessed=4 * rows * width * steps, transcendentals=0
        ),
        name="attend",
    )(info, queries, start, pairs)


def attend_back_kernel(info, q_ref, g_ref, start_ref, total_ref, term_ref, kv_ref, dkv_ref, dq_ref, bias, acc):
    step = pl.program_id(0)
    me, first_block = info[0], info[1]
    rows, width = q_ref.shape
    block = me - step

    @pl.when(step == 0)
    def _():
        acc[...] = jnp.zeros_like(acc)

    @pl.when(block >= first_block)
    def _():
        bias[...] = visible_bias((rows, rows), 0, block * rows, start_ref[...], me * rows)

        @pl.loop(0, HEADS)
        def _(h):
            at = heads_at(h)
            late = pl.ds(pl.multiple_of(width + h * HEAD, HEAD), HEAD)
            keys, values = kv_ref[0, :, at], kv_ref[0, :, late]
            queries, grads = q_ref[:, at], g_ref[:, at]
            probs = jnp.exp(inner_right(keys, queries) + bias[...] - total_ref[h])
            prob_grad = inner_right(values, grads)
            score_grad = (probs * (prob_grad - term_ref[h])).astype(jnp.bfloat16)
            dkv_ref[0, :, late] = jnp.dot(
                probs.astype(jnp.bfloat16), grads, preferred_element_type=jnp.float32
            ).astype(jnp.bfloat16)
            dkv_ref[0, :, at] = jnp.dot(
                score_grad, queries, preferred_element_type=jnp.float32
            ).astype(jnp.bfloat16)
            acc[h] += inner_left(keys, score_grad)

    @pl.when(jnp.logical_and(block >= 0, block < first_block))
    def _():
        dkv_ref[...] = jnp.zeros_like(dkv_ref)

    @pl.when(step == pl.num_programs(0) - 1)
    def _():
        for h in range(HEADS):
            dq_ref[:, h * HEAD : (h + 1) * HEAD] = acc[h].T


def attend_back(info, queries, grads, start, total, term, pairs):
    rows, width = queries.shape
    count = pairs.shape[0]
    steps = count // 2 + 1
    whole = lambda *shape: pl.BlockSpec(shape, lambda s, info: (0,) * len(shape))
    return pl.pallas_call(
        attend_back_kernel,
        out_shape=(
            jax.ShapeDtypeStruct(pairs.shape, jnp.bfloat16),
            jax.ShapeDtypeStruct((rows, width), jnp.float32),
        ),
        grid_spec=pltpu.PrefetchScalarGridSpec(
            num_scalar_prefetch=1,
            grid=(steps,),
            in_specs=[
                whole(rows, width),
                whole(rows, width),
                whole(1, rows),
                whole(HEADS, 1, rows),
                whole(HEADS, 1, rows),
                pl.BlockSpec((1, rows, 2 * width), lambda s, info: (jnp.maximum(info[0] - s, info[1]), 0, 0)),
            ],
            out_specs=(
                pl.BlockSpec((1, rows, 2 * width), lambda s, info: (jnp.maximum(info[0] - s, 0), 0, 0)),
                whole(rows, width),
            ),
            scratch_shapes=[
                pltpu.VMEM((rows, rows), jnp.float32),
                pltpu.VMEM((HEADS, HEAD, rows), jnp.float32),
            ],
        ),
        cost_estimate=pl.CostEstimate(
            flops=10 * rows * rows * width * steps, bytes_accessed=8 * rows * width * steps, transcendentals=0
        ),
        name="attend_back",
    )(info, queries, grads, start, total, term, pairs)


def local(
    tokens,
    doc_lengths,
    expert_ids,
    out_grad,
    mixer_gain,
    query_weight,
    key_weight,
    value_weight,
    output_weight,
    ffn_gain,
    router_weight,
    shared_gate,
    shared_up,
    shared_down,
    expert_gate,
    expert_up,
    expert_down,
):
    rows, width = tokens.shape[1], tokens.shape[2]
    ep_count = lax.axis_size("ep")
    device_count = ep_count * lax.axis_size("grp")
    ep_index = lax.axis_index("ep")
    expert_count = router_weight.shape[1]
    capacity = min(rows, 12 * rows * TOP // (7 * expert_count))
    q_scale = HEAD ** (-0.5)
    low = lambda v: v.astype(jnp.bfloat16)
    wide = lambda v: v.astype(jnp.float32)
    dot = lambda left, right: jnp.dot(left, right, preferred_element_type=jnp.float32)

    grad_low = out_grad[0]
    grads_all = lax.all_gather(grad_low, "ep", axis=0, tiled=False)

    doc_ends = jnp.cumsum(doc_lengths[0])
    query_pos = ep_index * rows + jnp.arange(rows, dtype=jnp.int32)
    before = query_pos[:, None] >= doc_ends[None, :]
    start = jnp.max(jnp.where(before, doc_ends[None, :], 0), axis=1)
    info = jnp.stack([ep_index, start[0] // rows]).astype(jnp.int32)
    position = wide(query_pos)

    stream = wide(tokens[0])
    hidden_low = low(normed(stream, mixer_gain))
    heads = lambda v: v.reshape(rows, HEADS, HEAD)
    queries = low(rotary(heads(dot(hidden_low, query_weight)), position, 1.0) * q_scale).reshape(rows, width)
    keys = low(rotary(heads(dot(hidden_low, key_weight)), position, 1.0)).reshape(rows, width)
    values = low(dot(hidden_low, value_weight))
    pairs = gather_rows(jnp.concatenate([keys, values], axis=1), True, 1)
    mixed, mixed_low, log_total = attend(info, queries, start[:, None], pairs)
    mixer_out = dot(mixed_low, output_weight)
    residual = stream + mixer_out
    ffn_low = low(normed(residual, ffn_gain))

    logits = dot(ffn_low, router_weight)
    experts = jnp.arange(expert_count, dtype=jnp.int32)
    assigned = jnp.any(expert_ids[0][:, :, None] == experts[None, None, :], axis=1)
    shown = jnp.where(assigned, logits, masked_value)
    powers = jnp.where(assigned, jnp.exp(shown - jnp.max(shown, axis=1, keepdims=True)), 0.0)
    gate_probs = powers / jnp.sum(powers, axis=1, keepdims=True)
    probs_high = low(gate_probs)
    probs_rest = low(gate_probs - wide(probs_high))
    side = width + 2 * HEAD if 2 * expert_count > HEAD else width + HEAD
    pad = jnp.zeros((rows, side - width - 2 * expert_count), jnp.bfloat16)
    sent = jnp.concatenate([ffn_low, probs_high, probs_rest, pad], axis=1)
    arrived = gather_rows(sent, False, 2)

    own = experts[None, None, :] == ep_index
    high = arrived[:, :, width : width + expert_count]
    rest = arrived[:, :, width + expert_count : width + 2 * expert_count]
    share = jnp.sum(jnp.where(own, wide(high) + wide(rest), 0.0), axis=2)
    chosen = share > 0.0
    earlier = (jnp.arange(rows)[:, None] < jnp.arange(rows)[None, :]).astype(jnp.bfloat16)
    rank = dot(low(chosen), earlier).astype(jnp.int32)
    pick = (rank[:, None, :] == jnp.arange(capacity, dtype=jnp.int32)[None, :, None]) & chosen[:, None, :]
    pick_low = low(pick)
    take = lambda block: low(
        jnp.einsum("srt,std->srd", pick_low, block, preferred_element_type=jnp.float32)
    ).reshape(ep_count * capacity, -1)
    put = lambda flat: low(
        jnp.einsum(
            "srt,srd->std", pick_low, flat.reshape(ep_count, capacity, -1), preferred_element_type=jnp.float32
        )
    )
    flat_in = take(arrived[:, :, :width])
    flat_out_grad = take(grads_all)
    flat_share = jnp.sum(jnp.where(pick, share[:, None, :], 0.0), axis=2).reshape(-1, 1)
    gate_pre = dot(flat_in, expert_gate[0])
    up_pre = dot(flat_in, expert_up[0])
    expert_silu, expert_slope = silu_parts(gate_pre)
    middle = low(expert_silu * up_pre)
    result = low(dot(middle, expert_down[0]))
    gate_grad = jnp.sum(wide(result) * wide(flat_out_grad), axis=1, keepdims=True)
    result_grad = low(flat_share * wide(flat_out_grad))
    mid_grad = inner_right(result_grad, expert_down[0])
    pre_grad = low(mid_grad * up_pre * expert_slope)
    lift_grad = low(mid_grad * expert_silu)
    input_grad = low(inner_right(pre_grad, expert_gate[0]) + inner_right(lift_grad, expert_up[0]))
    gate_high = low(gate_grad)
    gate_rest = low(gate_grad - wide(gate_high))
    mine = low(experts[None, :] == ep_index)
    back = jnp.concatenate(
        [input_grad, gate_high * mine, gate_rest * mine,
         jnp.zeros((flat_in.shape[0], side - width - 2 * expert_count), jnp.bfloat16)], axis=1
    )
    back_sum = scatter_rows(put(back), False, 3)
    routed = wide(lax.psum_scatter(put(low(flat_share * wide(result))), "ep", scatter_dimension=0))
    half = lambda v: v.reshape(v.shape[0], lax.axis_size("grp"), -1)
    own_down_grad = low(jnp.einsum("rf,rgd->gfd", middle, half(result_grad), preferred_element_type=jnp.float32))
    own_gate_grad = low(inner_left(flat_in, pre_grad))
    own_up_grad = low(inner_left(flat_in, lift_grad))
    over_groups = lambda v: wide(lax.psum_scatter(v, "grp", scatter_dimension=0, tiled=True))
    gate_sum = over_groups(own_gate_grad)[None]
    up_sum = over_groups(own_up_grad)[None]
    down_sum = over_groups(own_down_grad)

    shared_pre = dot(ffn_low, shared_gate)
    shared_lift = dot(ffn_low, shared_up)
    shared_silu, shared_slope = silu_parts(shared_pre)
    shared_mid = low(shared_silu * shared_lift)
    shared_out = dot(shared_mid, shared_down)
    grad_out = wide(grad_low)
    shared_mid_grad = inner_right(grad_low, shared_down)
    shared_pre_grad = low(shared_mid_grad * shared_lift * shared_slope)
    shared_lift_grad = low(shared_mid_grad * shared_silu)
    ffn_grad = inner_right(shared_pre_grad, shared_gate) + inner_right(shared_lift_grad, shared_up)

    layer_out = residual + shared_out + routed
    gate_back = wide(back_sum[:, width : width + expert_count]) + wide(
        back_sum[:, width + expert_count : width + 2 * expert_count]
    )
    chosen_grad = gate_probs * (gate_back - jnp.sum(gate_probs * gate_back, axis=1, keepdims=True))
    logit_grad = low(chosen_grad)
    ffn_grad = ffn_grad + wide(back_sum[:, :width]) + inner_right(logit_grad, router_weight)
    _, ffn_pull = jax.vjp(normed, residual, ffn_gain)
    residual_part, ffn_gain_grad = ffn_pull(ffn_grad)
    residual_grad = grad_out + residual_part
    mixer_grad_low = low(residual_grad)
    mixed_grad = low(inner_right(mixer_grad_low, output_weight))
    row_term = jnp.sum(heads(wide(mixed_grad) * mixed), axis=2)
    pair_parts, query_sum = attend_back(
        info, queries, mixed_grad, start[None, :], log_total.reshape(HEADS, 1, rows),
        row_term.T.reshape(HEADS, 1, rows), pairs,
    )
    pair_grads = scatter_rows(pair_parts, True, 4)

    by_device = lambda v: low(v).reshape(device_count, width // device_count, -1)
    early = jnp.concatenate(
        [by_device(inner_left(ffn_low, shared_pre_grad)), by_device(inner_left(ffn_low, shared_lift_grad)),
         by_device(inner_left(grad_low, shared_mid)), by_device(inner_left(mixed_low, mixer_grad_low))], axis=2
    )
    early_sum = scatter_whole(early, 5)

    query_lin_grad = low(rotary(heads(query_sum * q_scale), position, -1.0)).reshape(rows, width)
    key_lin_grad = low(rotary(heads(wide(pair_grads[:, :width])), position, -1.0)).reshape(rows, width)
    value_lin_grad = pair_grads[:, width:]
    hidden_grad = (
        inner_right(query_lin_grad, query_weight)
        + inner_right(key_lin_grad, key_weight)
        + inner_right(value_lin_grad, value_weight)
    )
    _, mixer_pull = jax.vjp(normed, stream, mixer_gain)
    stream_part, mixer_gain_grad = mixer_pull(hidden_grad)
    tokens_grad = low(residual_grad + stream_part)

    squares = jnp.stack(
        [jnp.sum(residual * residual), jnp.sum(mixer_out * mixer_out), jnp.sum(layer_out * layer_out)]
    )
    extras = jnp.concatenate(
        [inner_left(ffn_low, logit_grad), mixer_gain_grad[:, None], ffn_gain_grad[:, None],
         jnp.broadcast_to(squares[None, :], (width, 3))], axis=1
    )
    extras = jnp.pad(extras, ((0, 0), (0, HEAD - extras.shape[1])))
    late = jnp.concatenate(
        [by_device(inner_left(hidden_low, query_lin_grad)), by_device(inner_left(hidden_low, key_lin_grad)),
         by_device(inner_left(hidden_low, value_lin_grad)), by_device(extras)], axis=2
    )
    late_sum = scatter_whole(late, 6)
    extra_sum = late_sum[:, 3 * width :]
    entry_count = rows * device_count * width
    stream_rms = jnp.sqrt(extra_sum[0, expert_count + 2 : expert_count + 5] / entry_count)
    ff = shared_gate.shape[1]
    return (
        low(layer_out)[None],
        tokens_grad[None],
        extra_sum[:, expert_count],
        late_sum[:, :width],
        late_sum[:, width : 2 * width],
        late_sum[:, 2 * width : 3 * width],
        early_sum[:, 3 * ff :],
        extra_sum[:, expert_count + 1],
        extra_sum[:, :expert_count],
        early_sum[:, :ff],
        early_sum[:, ff : 2 * ff],
        early_sum[:, 2 * ff : 3 * ff].T,
        gate_sum,
        up_sum,
        down_sum,
        stream_rms,
    )


def solution(mesh):
    return jax.shard_map(
        local,
        mesh=mesh,
        in_specs=(
            P("grp", "ep", None),
            P("grp", None),
            P("grp", "ep", None),
            P("grp", "ep", None),
            P(),
            P(),
            P(),
            P(),
            P(),
            P(),
            P(),
            P(),
            P(),
            P(),
            P("ep", None, None),
            P("ep", None, None),
            P("ep", None, None),
        ),
        out_specs=(
            P("grp", "ep", None),
            P("grp", "ep", None),
            P(("grp", "ep")),
            P(("grp", "ep"), None),
            P(("grp", "ep"), None),
            P(("grp", "ep"), None),
            P(("grp", "ep"), None),
            P(("grp", "ep")),
            P(("grp", "ep"), None),
            P(("grp", "ep"), None),
            P(("grp", "ep"), None),
            P(None, ("grp", "ep")),
            P("ep", "grp", None),
            P("ep", "grp", None),
            P("ep", None, "grp"),
            P(),
        ),
        check_vma=False,
    )
```

```python
import functools

import jax
import jax.numpy as jnp
from jax import lax
from jax.experimental import pallas as pl
from jax.experimental.pallas import tpu as pltpu
from jax.sharding import PartitionSpec as P

HEADS = 10
HEAD = 128
TOP = 7

epsilon = 1e-06
rope_base = 10000.0
masked_value = -1e30


def normed(values, gain_vec):
    return (
        values * lax.rsqrt(jnp.mean(values * values, axis=-1, keepdims=True) + epsilon) * gain_vec
    )


def inner_left(left_op, right_op):
    return lax.dot_general(
        left_op, right_op, (((0,), (0,)), ((), ())), preferred_element_type=jnp.float32
    )


def inner_right(left_op, right_op):
    return lax.dot_general(
        left_op, right_op, (((1,), (1,)), ((), ())), preferred_element_type=jnp.float32
    )


def silu_parts(pre_act):
    sigmoid_val = jax.nn.sigmoid(pre_act)
    return (pre_act * sigmoid_val, sigmoid_val * (1.0 + pre_act * (1.0 - sigmoid_val)))


MESH = pl.DeviceIdType.MESH
VMEM_MOST = 64 * 1024 * 1024 - 65536


def when(cond):
    if cond is True:
        return lambda f: f()
    if cond is False:
        return lambda f: None
    return pl.when(cond)


def both(*conds):
    out = True
    for cond in conds:
        if cond is False:
            return False
        if cond is True:
            continue
        out = cond if out is True else jnp.logical_and(out, cond)
    return out


class Plan:
    def __init__(self, ep_count, window):
        self.long = 4
        self.wide = ep_count // 8
        self.window = window
        self.steps = (
            list(range(self.long // 2 + 1))
            if window
            else list(range(-(self.long - 1), self.long))
        )

    def place(self):
        me = lax.axis_index("ep")
        return me // (2 * self.wide), (me // 2) % self.wide, me % 2

    def slot(self, a, b, c):
        return (a * self.wide + b) * 2 + c

    def inside(self, a):
        return jnp.logical_and(a >= 0, a < self.long)

    def need(self, d, b, c, b0, c0):
        if not self.window or 0 < d < self.long // 2:
            return True
        if d == 0:
            return jnp.logical_or(b0 < b, jnp.logical_and(b0 == b, c0 <= c))
        return jnp.logical_or(b0 > b, jnp.logical_and(b0 == b, c0 >= c))

    def need_pair(self, d, b, b0):
        if not self.window or 0 < d < self.long // 2:
            return True
        return b0 < b if d == 0 else b0 > b

    def greet(self, a, b, c):
        barrier = pltpu.get_barrier_semaphore()

        def signal(cond, dev):
            @when(cond)
            def _():
                pl.semaphore_signal(barrier, inc=1, device_id={"ep": dev}, device_id_type=MESH)

        signal(a + 1 < self.long, self.slot(a + 1, b, c))
        signal(a > 0, self.slot(a - 1, b, c))
        for k in range(1, self.wide):
            signal(True, self.slot(a, (b + k) % self.wide, c))
        signal(True, self.slot(a, b, 1 - c))
        ends = (a == 0).astype(jnp.int32) + (a == self.long - 1).astype(jnp.int32)
        pl.semaphore_wait(barrier, self.wide + 2 - ends)


def gather_kernel(plan, pieces, x_ref, out_ref, ra, sa_up, sa_dn, rb, sb, rc, sc, own):
    a, b, c = plan.place()
    steps, wide = plan.steps, plan.wide
    at = {d: i for i, d in enumerate(steps)}
    rows = x_ref.shape[0] // pieces

    def part(q):
        return pl.ds(pl.multiple_of(q * rows, rows), rows)

    def copy(q, src, slot, ssem, rsem, dev):
        return pltpu.make_async_remote_copy(
            src_ref=src, dst_ref=out_ref.at[slot, part(q)], send_sem=ssem, recv_sem=rsem,
            device_id={"ep": dev}, device_id_type=MESH,
        )

    def hops(d, q):
        i = at[d]
        slot = plan.slot(a - d, b, c)
        src = x_ref.at[part(q)] if d == 0 else out_ref.at[slot, part(q)]
        real = plan.inside(a - d)
        out = []
        if d >= 0 and d + 1 in at:
            out.append((both(real, a + 1 < plan.long), lambda: copy(
                q, src, slot, sa_up.at[i, q], ra.at[at[d + 1], q], plan.slot(a + 1, b, c))))
        if d <= 0 and d - 1 in at:
            out.append((both(real, a > 0), lambda: copy(
                q, src, slot, sa_dn.at[i, q], ra.at[at[d - 1], q], plan.slot(a - 1, b, c))))
        for k in range(1, wide):
            to = (b + k) % wide
            out.append((both(real, plan.need_pair(d, to, b)), lambda k=k, to=to: copy(
                q, src, slot, sb.at[i, k, q], rb.at[i, k, q], plan.slot(a, to, c))))
        out.append((both(real, plan.need(d, b, 1 - c, b, c)), lambda: copy(
            q, src, slot, sc.at[i, 0, q], rc.at[i, 0, q], plan.slot(a, b, 1 - c))))
        return out

    def cross(d, k, q):
        i = at[d]
        b0 = (b + wide - k) % wide
        slot = plan.slot(a - d, b0, c)
        real = plan.inside(a - d)
        come = lambda: copy(q, x_ref.at[part(q)], slot, sb.at[i, k, q], rb.at[i, k, q], plan.slot(a, b, c))
        go = lambda: copy(q, out_ref.at[slot, part(q)], slot, sc.at[i, k, q], rc.at[i, k, q],
                          plan.slot(a, b, 1 - c))
        return (both(real, plan.need_pair(d, b, b0)), come,
                both(real, plan.need(d, b, 1 - c, b0, c)), go)

    plan.greet(a, b, c)
    keep = pltpu.make_async_copy(x_ref, out_ref.at[plan.slot(a, b, c)], own)

    @pl.loop(0, pieces)
    def _(q):
        for cond, go in hops(0, q):
            @when(cond)
            def _(go=go):
                go().start()

    keep.start()
    far = max(abs(d) for d in steps)
    for step in range(1, far + 3):
        @pl.loop(0, pieces)
        def _(q, step=step):
            for d in (step, -step):
                if d in at:
                    @when(plan.inside(a - d))
                    def _(d=d):
                        slot = plan.slot(a - d, b, c)
                        copy(q, x_ref.at[part(q)], slot, sa_up.at[0, q], ra.at[at[d], q],
                             plan.slot(a, b, c)).wait_recv()
                        for cond, go in hops(d, q):
                            @when(cond)
                            def _(go=go):
                                go().start()
            for d in sorted({step - 2, 2 - step}) if step > 1 else ():
                if d in at:
                    for k in range(1, wide):
                        came, come, goes, go = cross(d, k, q)
                        @when(came)
                        def _(come=come):
                            come().wait_recv()
                        @when(goes)
                        def _(go=go):
                            go().start()
    keep.wait()

    @pl.loop(0, pieces)
    def _(q):
        for d in steps:
            i = at[d]
            real = plan.inside(a - d)
            for k in range(wide):
                b0 = (b + wide - k) % wide
                slot = plan.slot(a - d, b0, 1 - c)
                @when(both(real, plan.need(d, b, c, b0, 1 - c)))
                def _(slot=slot, i=i, k=k):
                    copy(q, x_ref.at[part(q)], slot, sc.at[i, k, q], rc.at[i, k, q],
                         plan.slot(a, b, c)).wait_recv()
            for cond, go in hops(d, q):
                @when(cond)
                def _(go=go):
                    go().wait_send()
            for k in range(1, wide):
                came, come, goes, go = cross(d, k, q)
                @when(goes)
                def _(go=go):
                    go().wait_send()


def gather_rows(block, window, collective_id, pieces=4):
    ep_count = lax.axis_size("ep")
    plan = Plan(ep_count, window)
    n, wide = len(plan.steps), plan.wide
    sem = pltpu.SemaphoreType.DMA
    return pl.pallas_call(
        functools.partial(gather_kernel, plan, pieces),
        out_shape=jax.ShapeDtypeStruct((ep_count,) + block.shape, block.dtype),
        in_specs=[pl.BlockSpec(memory_space=pltpu.VMEM)],
        out_specs=pl.BlockSpec(memory_space=pl.ANY),
        scratch_shapes=[sem((n, pieces)), sem((n, pieces)), sem((n, pieces)), sem((n, wide, pieces)),
                        sem((n, wide, pieces)), sem((n, wide, pieces)), sem((n, wide, pieces)), sem],
        compiler_params=pltpu.CompilerParams(collective_id=collective_id, has_side_effects=True),
        name="gather_rows",
    )(block)


def add_rows(dst, others, out=None):
    rows = dst.shape[0]
    piece = next(p for p in (32, 16, 8, rows) if rows % p == 0)
    out = dst if out is None else out

    @pl.loop(0, rows // piece)
    def _(i):
        at = pl.ds(pl.multiple_of(i * piece, piece), piece)
        if len(others) == 1 and out.dtype == jnp.bfloat16:
            out[at, :] = dst[at, :] + others[0][at, :]
        else:
            total = dst[at, :].astype(jnp.float32)
            for other in others:
                total = total + other[at, :].astype(jnp.float32)
            out[at, :] = total.astype(out.dtype)


def scatter_kernel(plan, pieces, p_ref, out_ref, held, rcb, rbb, r_hi, r_lo, sc, rc, sb, rb, sa, rhi, rlo, ld):
    a, b, c = plan.place()
    steps, wide = plan.steps, plan.wide
    at = {d: i for i, d in enumerate(steps)}
    rows = p_ref.shape[1] // pieces

    def part(q):
        return pl.ds(pl.multiple_of(q * rows, rows), rows)

    def remote(src, dst, ssem, rsem, dev):
        return pltpu.make_async_remote_copy(
            src_ref=src, dst_ref=dst, send_sem=ssem, recv_sem=rsem,
            device_id={"ep": dev}, device_id_type=MESH,
        )

    order = sorted(steps, key=lambda d: -abs(d))
    ks = list(range(1, wide)) + [0]

    def load(d, k, q):
        i, b0 = at[d], (b + wide - k) % wide
        return (both(plan.inside(a - d), plan.need(d, b, c, b0, c)), lambda: pltpu.make_async_copy(
            p_ref.at[plan.slot(a - d, b0, c), part(q)], held.at[i, k, part(q)], ld.at[i, k, q]))

    def cross(d, k, q):
        i, b0 = at[d], (b + wide - k) % wide
        real = plan.inside(a - d)
        return (both(real, plan.need(d, b, c, b0, 1 - c)), lambda: remote(
            p_ref.at[plan.slot(a - d, b0, 1 - c), part(q)], rcb.at[i, k, part(q)], sc.at[i, k, q],
            rc.at[i, k, q], plan.slot(a, b, 1 - c)), both(real, plan.need(d, b, 1 - c, b0, c)))

    def over(d, k, q):
        i, b0 = at[d], (b + wide - k) % wide
        return (both(plan.inside(a - d), plan.need_pair(d, b, b0)), lambda: remote(
            held.at[i, k, part(q)], rbb.at[i, k - 1, part(q)], sb.at[i, k, q], rb.at[i, k, q],
            plan.slot(a, b0, c)))

    def along(d, q):
        i, up = at[d], d < 0
        j = at[d + 1 if up else d - 1]
        return plan.inside(a - d), lambda: remote(
            held.at[i, 0, part(q)], (r_lo if up else r_hi).at[j, part(q)], sa.at[i, q],
            (rlo if up else rhi).at[j, q], plan.slot(a + (1 if up else -1), b, c))

    plan.greet(a, b, c)
    for k in ks:
        @pl.loop(0, pieces)
        def _(q, k=k):
            for d in order:
                for cond, go in (cross(d, k, q)[:2], load(d, k, q)):
                    @when(cond)
                    def _(go=go):
                        go().start()

    def first(d, k, q):
        cond, go = load(d, k, q)
        @when(cond)
        def _():
            go().wait()
        _, cross_go, come = cross(d, k, q)
        @when(come)
        def _():
            cross_go().wait_recv()
            add_rows(held.at[at[d], k, part(q)], [rcb.at[at[d], k, part(q)]])

    for k in ks[:-1]:
        @pl.loop(0, pieces)
        def _(q, k=k):
            for d in order:
                first(d, k, q)
                cond, go = over(d, k, q)
                @when(cond)
                def _(go=go):
                    go().start()
    for d in order:
        @pl.loop(0, pieces)
        def _(q, d=d):
            i = at[d]
            real = plan.inside(a - d)
            first(d, 0, q)
            for k in range(1, wide):
                frm = (b + k) % wide
                @when(both(real, plan.need_pair(d, frm, b)))
                def _(k=k):
                    over(d, k, q)[1]().wait_recv()
                    add_rows(held.at[i, 0, part(q)], [rbb.at[i, k - 1, part(q)]])
            for inner, cond, buf, sem in ((d >= 0 and d + 1 in at, a + 1 < plan.long, r_hi, rhi),
                                          (d <= 0 and d - 1 in at, a > 0, r_lo, rlo)):
                if inner:
                    @when(both(real, cond))
                    def _(buf=buf, sem=sem):
                        remote(held.at[i, 0, part(q)], buf.at[i, part(q)], sa.at[i, q], sem.at[i, q],
                               plan.slot(a, b, c)).wait_recv()
                        add_rows(held.at[i, 0, part(q)], [buf.at[i, part(q)]])
            if d:
                cond, go = along(d, q)
                @when(cond)
                def _():
                    go().start()
    out_ref[...] = held[at[0], 0]

    @pl.loop(0, pieces)
    def _(q):
        for d in steps:
            sends = [cross(d, k, q)[:2] for k in range(wide)] + [over(d, k, q) for k in range(1, wide)]
            if d:
                sends.append(along(d, q))
            for cond, go in sends:
                @when(cond)
                def _(go=go):
                    go().wait_send()


def scatter_rows(parts, window, collective_id, pieces=4):
    ep_count, rows, width = parts.shape
    plan = Plan(ep_count, window)
    n, wide = len(plan.steps), plan.wide
    sem = lambda *lead: pltpu.SemaphoreType.DMA(lead + (pieces,))
    blocks = lambda *lead: pltpu.VMEM(lead + (rows, width), parts.dtype)
    return pl.pallas_call(
        functools.partial(scatter_kernel, plan, pieces),
        out_shape=jax.ShapeDtypeStruct((rows, width), parts.dtype),
        in_specs=[pl.BlockSpec(memory_space=pl.ANY)],
        out_specs=pl.BlockSpec(memory_space=pltpu.VMEM),
        scratch_shapes=[blocks(n, wide), blocks(n, wide), blocks(n, wide - 1), blocks(n), blocks(n),
                        sem(n, wide), sem(n, wide), sem(n, wide), sem(n, wide),
                        sem(n), sem(n), sem(n), sem(n, wide)],
        compiler_params=pltpu.CompilerParams(
            collective_id=collective_id, has_side_effects=True, vmem_limit_bytes=VMEM_MOST),
        name="scatter_rows",
    )(parts)


def whole_kernel(sizes, p_ref, out_ref, held, rcb, rxb, rbb, rab, *sems):
    groups, long, wide = sizes
    g = lax.axis_index("grp")
    me = lax.axis_index("ep")
    a, b, c = me // (2 * wide), (me // 2) % wide, me % 2
    sc, rc, sx, rx, sb, rb, sa, ra, ld = sems

    def dev(gg, aa, bb, cc):
        return {"grp": gg, "ep": (aa * wide + bb) * 2 + cc}

    def slot(gg, aa, bb, cc):
        return ((gg * long + aa) * wide + bb) * 2 + cc

    def remote(src, dst, ssem, rsem, to):
        return pltpu.make_async_remote_copy(
            src_ref=src, dst_ref=dst, send_sem=ssem, recv_sem=rsem, device_id=to, device_id_type=MESH)

    peers = ([dev(g, a, b, 1 - c)] + [dev((g + k) % groups, a, b, c) for k in range(1, groups)]
             + [dev(g, a, (b + k) % wide, c) for k in range(1, wide)]
             + [dev(g, (a + k) % long, b, c) for k in range(1, long)])
    barrier = pltpu.get_barrier_semaphore()
    for to in peers:
        pl.semaphore_signal(barrier, inc=1, device_id=to, device_id_type=MESH)
    pl.semaphore_wait(barrier, len(peers))

    def spot(kx, ka, kb, cc):
        return slot((g + groups - kx) % groups, (a + long - ka) % long, (b + wide - kb) % wide, cc)

    keys = [(kx, ka, kb) for kx in list(range(1, groups)) + [0] for kb in list(range(1, wide)) + [0]
            for ka in list(range(1, long)) + [0]]
    cross = {}
    load = {}
    for kx, ka, kb in keys:
        key = (kx, ka, kb)
        cross[key] = remote(p_ref.at[spot(kx, ka, kb, 1 - c)], rcb.at[key], sc.at[key], rc.at[key],
                            dev(g, a, b, 1 - c))
        load[key] = pltpu.make_async_copy(p_ref.at[spot(kx, ka, kb, c)], held.at[key], ld.at[key])
        cross[key].start()
        load[key].start()

    def over_x(kx, ka, kb):
        return remote(held.at[kx, ka, kb], rxb.at[kx - 1, ka, kb], sx.at[kx - 1, ka, kb], rx.at[kx - 1, ka, kb],
                      dev((g + groups - kx) % groups, a, b, c))

    def over_b(ka, kb):
        return remote(held.at[0, ka, kb], rbb.at[ka, kb - 1], sb.at[ka, kb - 1], rb.at[ka, kb - 1],
                      dev(g, a, (b + wide - kb) % wide, c))

    def over_a(ka):
        return remote(held.at[0, ka, 0], rab.at[ka - 1], sa.at[ka - 1], ra.at[ka - 1],
                      dev(g, (a + long - ka) % long, b, c))

    for key in keys:
        load[key].wait()
        cross[key].wait_recv()
        add_rows(held.at[key], [rcb.at[key]])
        if key[0]:
            over_x(*key).start()

    for kb in list(range(1, wide)) + [0]:
        for ka in list(range(1, long)) + [0]:
            for kx in range(1, groups):
                over_x(kx, ka, kb).wait_recv()
            add_rows(held.at[0, ka, kb], [rxb.at[kx - 1, ka, kb] for kx in range(1, groups)])
            if kb:
                over_b(ka, kb).start()
    for ka in list(range(1, long)) + [0]:
        for kb in range(1, wide):
            over_b(ka, kb).wait_recv()
        add_rows(held.at[0, ka, 0], [rbb.at[ka, kb - 1] for kb in range(1, wide)])
        if ka:
            over_a(ka).start()
    for ka in range(1, long):
        over_a(ka).wait_recv()
    add_rows(held.at[0, 0, 0], [rab.at[ka - 1] for ka in range(1, long)], out_ref)
    for key in keys:
        cross[key].wait_send()
        if key[0]:
            over_x(*key).wait_send()
    for ka in range(long):
        for kb in range(1, wide):
            over_b(ka, kb).wait_send()
        if ka:
            over_a(ka).wait_send()


def scatter_whole(parts, collective_id):
    count, rows, width = parts.shape
    groups, ep_count = lax.axis_size("grp"), lax.axis_size("ep")
    long, wide = 4, ep_count // 8
    sem = pltpu.SemaphoreType.DMA
    blocks = lambda *lead: pltpu.VMEM(lead + (rows, width), parts.dtype)
    full = (groups, long, wide)

    def kernel(p_ref, out_ref, *scratch):
        whole_kernel(full, p_ref, out_ref, *scratch)

    return pl.pallas_call(
        kernel,
        out_shape=jax.ShapeDtypeStruct((rows, width), jnp.float32),
        in_specs=[pl.BlockSpec(memory_space=pl.ANY)],
        out_specs=pl.BlockSpec(memory_space=pltpu.VMEM),
        scratch_shapes=[blocks(*full), blocks(*full), blocks(groups - 1, long, wide), blocks(long, wide - 1),
                        blocks(long - 1),
                        sem(full), sem(full), sem((groups - 1, long, wide)), sem((groups - 1, long, wide)),
                        sem((long, wide - 1)), sem((long, wide - 1)), sem((long - 1,)), sem((long - 1,)), sem(full)],
        compiler_params=pltpu.CompilerParams(
            collective_id=collective_id, has_side_effects=True, vmem_limit_bytes=VMEM_MOST),
        name="scatter_whole",
    )(parts)


def visible_bias(shape, first_key, start, first_query):
    key_pos = first_key + lax.broadcasted_iota(jnp.int32, shape, 0)
    query_pos = first_query + lax.broadcasted_iota(jnp.int32, shape, 1)
    seen = jnp.logical_and(key_pos >= start, key_pos <= query_pos)
    return jnp.where(seen, 0.0, masked_value)


def lanes(first):
    return pl.ds(pl.multiple_of(first, HEAD), HEAD)


def turned(values, cosine, sine):
    return values * cosine + pltpu.roll(values, HEAD // 2, 1) * sine


def whole_spec(*shape):
    return pl.BlockSpec(shape, lambda *s: (0,) * len(shape))


def project_kernel(x_ref, gain_ref, cos_ref, sin_ref, wq_ref, wk_ref, wv_ref, hid_ref, q_ref, kv_ref, hidden):
    @pl.when(pl.program_id(0) == 0)
    def _():
        hidden[...] = normed(x_ref[...].astype(jnp.float32), gain_ref[...]).astype(jnp.bfloat16)
        hid_ref[...] = hidden[...]

    cosine, sine = cos_ref[...], sin_ref[...]
    q = jnp.dot(hidden[...], wq_ref[...], preferred_element_type=jnp.float32)
    k = jnp.dot(hidden[...], wk_ref[...], preferred_element_type=jnp.float32)
    v = jnp.dot(hidden[...], wv_ref[...], preferred_element_type=jnp.float32)
    for h in range(q.shape[1] // HEAD):
        at = slice(h * HEAD, (h + 1) * HEAD)
        q_ref[:, at] = (turned(q[:, at], cosine, sine) * HEAD ** (-0.5)).astype(jnp.bfloat16)
        kv_ref[:, 2 * h * HEAD : (2 * h + 1) * HEAD] = turned(k[:, at], cosine, sine).astype(jnp.bfloat16)
        kv_ref[:, (2 * h + 1) * HEAD : (2 * h + 2) * HEAD] = v[:, at].astype(jnp.bfloat16)


def project(tokens, gain, cosine, sine, wq, wk, wv):
    rows, width = tokens.shape
    tile = 2 * HEAD
    column = pl.BlockSpec((width, tile), lambda i: (0, i))
    return pl.pallas_call(
        project_kernel,
        out_shape=(
            jax.ShapeDtypeStruct((rows, width), jnp.bfloat16),
            jax.ShapeDtypeStruct((rows, width), jnp.bfloat16),
            jax.ShapeDtypeStruct((rows, 2 * width), jnp.bfloat16),
        ),
        grid=(width // tile,),
        in_specs=[whole_spec(rows, width), whole_spec(1, width), whole_spec(rows, HEAD), whole_spec(rows, HEAD),
                  column, column, column],
        out_specs=(whole_spec(rows, width), pl.BlockSpec((rows, tile), lambda i: (0, i)),
                   pl.BlockSpec((rows, 2 * tile), lambda i: (0, i))),
        scratch_shapes=[pltpu.VMEM((rows, width), jnp.bfloat16)],
        cost_estimate=pl.CostEstimate(flops=6 * rows * width * width, bytes_accessed=6 * width * width, transcendentals=0),
        name="project",
    )(tokens, gain[None, :], cosine, sine, wq, wk, wv)


def attend_kernel(info, q_ref, start_ref, kv_ref, mixed_ref, low_ref, total_ref, bias, top, norm):
    step = pl.program_id(0)
    me, first_block = info[0], info[1]
    rows = q_ref.shape[0]
    block = me - step

    @pl.when(step == 0)
    def _():
        top[...] = jnp.full_like(top, masked_value)
        norm[...] = jnp.zeros_like(norm)
        mixed_ref[...] = jnp.zeros_like(mixed_ref)

    @pl.when(block >= first_block)
    def _():
        bias[...] = visible_bias((rows, rows), block * rows, start_ref[...], me * rows)

        @pl.loop(0, HEADS, unroll=2)
        def _(h):
            keys, values = kv_ref[0, :, lanes(2 * h * HEAD)], kv_ref[0, :, lanes((2 * h + 1) * HEAD)]
            scores = inner_right(keys, q_ref[:, lanes(h * HEAD)]) + bias[...]
            old = top[h]
            new = jnp.maximum(old, jnp.max(scores, axis=0, keepdims=True))
            weights = jnp.exp(scores - new)
            shrink = jnp.exp(old - new)
            top[h] = new
            norm[h] = norm[h] * shrink + jnp.sum(weights, axis=0, keepdims=True)
            mixed_ref[h] = mixed_ref[h] * shrink + inner_left(values, weights.astype(jnp.bfloat16))

    @pl.when(step == pl.num_programs(0) - 1)
    def _():
        for h in range(HEADS):
            mixed = mixed_ref[h] / norm[h]
            mixed_ref[h] = mixed
            low_ref[:, h * HEAD : (h + 1) * HEAD] = mixed.T.astype(jnp.bfloat16)
            total_ref[h] = top[h] + jnp.log(norm[h])


def attend(info, queries, start, pairs):
    rows, width = queries.shape
    steps = pairs.shape[0] // 2 + 1
    return pl.pallas_call(
        attend_kernel,
        out_shape=(
            jax.ShapeDtypeStruct((HEADS, HEAD, rows), jnp.float32),
            jax.ShapeDtypeStruct((rows, width), jnp.bfloat16),
            jax.ShapeDtypeStruct((HEADS, 1, rows), jnp.float32),
        ),
        grid_spec=pltpu.PrefetchScalarGridSpec(
            num_scalar_prefetch=1,
            grid=(steps,),
            in_specs=[
                whole_spec(rows, width),
                whole_spec(1, rows),
                pl.BlockSpec((1, rows, 2 * width), lambda s, info: (jnp.maximum(info[0] - s, info[1]), 0, 0)),
            ],
            out_specs=(whole_spec(HEADS, HEAD, rows), whole_spec(rows, width), whole_spec(HEADS, 1, rows)),
            scratch_shapes=[
                pltpu.VMEM((rows, rows), jnp.float32),
                pltpu.VMEM((HEADS, 1, rows), jnp.float32),
                pltpu.VMEM((HEADS, 1, rows), jnp.float32),
            ],
        ),
        cost_estimate=pl.CostEstimate(
            flops=4 * rows * rows * width * steps, bytes_accessed=4 * rows * width * steps, transcendentals=0
        ),
        name="attend",
    )(info, queries, start, pairs)


def attend_back_kernel(
    info, q_ref, g_ref, mixed_ref, start_ref, total_ref, cos_ref, sin_ref, kv_ref, dkv_ref, dq_ref, bias, acc, term
):
    step = pl.program_id(0)
    me, first_block = info[0], info[1]
    rows = q_ref.shape[0]
    block = me - step

    @pl.when(step == 0)
    def _():
        acc[...] = jnp.zeros_like(acc)
        for h in range(HEADS):
            grads = g_ref[:, h * HEAD : (h + 1) * HEAD].astype(jnp.float32).T
            term[h] = jnp.sum(grads * mixed_ref[h], axis=0, keepdims=True)

    @pl.when(block >= first_block)
    def _():
        bias[...] = visible_bias((rows, rows), block * rows, start_ref[...], me * rows)

        @pl.loop(0, HEADS, unroll=2)
        def _(h):
            early, late, at = lanes(2 * h * HEAD), lanes((2 * h + 1) * HEAD), lanes(h * HEAD)
            keys, values = kv_ref[0, :, early], kv_ref[0, :, late]
            queries, grads = q_ref[:, at], g_ref[:, at]
            probs = jnp.exp(inner_right(keys, queries) + bias[...] - total_ref[h])
            prob_grad = inner_right(values, grads)
            score_grad = (probs * (prob_grad - term[h])).astype(jnp.bfloat16)
            dkv_ref[0, :, late] = jnp.dot(
                probs.astype(jnp.bfloat16), grads, preferred_element_type=jnp.float32
            ).astype(jnp.bfloat16)
            dkv_ref[0, :, early] = jnp.dot(
                score_grad, queries, preferred_element_type=jnp.float32
            ).astype(jnp.bfloat16)
            acc[h] += inner_left(keys, score_grad)

    @pl.when(jnp.logical_and(block >= 0, block < first_block))
    def _():
        dkv_ref[...] = jnp.zeros_like(dkv_ref)

    @pl.when(step == pl.num_programs(0) - 1)
    def _():
        for h in range(HEADS):
            back = turned(acc[h].T * HEAD ** (-0.5), cos_ref[...], -sin_ref[...])
            dq_ref[:, h * HEAD : (h + 1) * HEAD] = back.astype(jnp.bfloat16)


def attend_back(info, queries, grads, mixed, start, total, cosine, sine, pairs):
    rows, width = queries.shape
    count = pairs.shape[0]
    steps = count // 2 + 1
    return pl.pallas_call(
        attend_back_kernel,
        out_shape=(
            jax.ShapeDtypeStruct(pairs.shape, jnp.bfloat16),
            jax.ShapeDtypeStruct((rows, width), jnp.bfloat16),
        ),
        grid_spec=pltpu.PrefetchScalarGridSpec(
            num_scalar_prefetch=1,
            grid=(steps,),
            in_specs=[
                whole_spec(rows, width),
                whole_spec(rows, width),
                whole_spec(HEADS, HEAD, rows),
                whole_spec(1, rows),
                whole_spec(HEADS, 1, rows),
                whole_spec(rows, HEAD),
                whole_spec(rows, HEAD),
                pl.BlockSpec((1, rows, 2 * width), lambda s, info: (jnp.maximum(info[0] - s, info[1]), 0, 0)),
            ],
            out_specs=(
                pl.BlockSpec((1, rows, 2 * width), lambda s, info: (jnp.maximum(info[0] - s, 0), 0, 0)),
                whole_spec(rows, width),
            ),
            scratch_shapes=[
                pltpu.VMEM((rows, rows), jnp.float32),
                pltpu.VMEM((HEADS, HEAD, rows), jnp.float32),
                pltpu.VMEM((HEADS, 1, rows), jnp.float32),
            ],
        ),
        cost_estimate=pl.CostEstimate(
            flops=10 * rows * rows * width * steps, bytes_accessed=8 * rows * width * steps, transcendentals=0
        ),
        name="attend_back",
    )(info, queries, grads, mixed, start, total, cosine, sine, pairs)


def finish_kernel(
    x_ref, gain_ref, res_ref, hid_ref, q_ref, kv_ref, cos_ref, sin_ref, wq_ref, wk_ref, wv_ref,
    dw_ref, out_ref, gain_out, acc,
):
    step = pl.program_id(0)

    @pl.when(step == 0)
    def _():
        acc[...] = jnp.zeros_like(acc)

    cosine, sine = cos_ref[...], sin_ref[...]
    count = q_ref.shape[1] // HEAD
    keys = jnp.concatenate(
        [turned(kv_ref[:, 2 * h * HEAD : (2 * h + 1) * HEAD].astype(jnp.float32), cosine, -sine).astype(jnp.bfloat16)
         for h in range(count)], axis=1)
    values = jnp.concatenate([kv_ref[:, (2 * h + 1) * HEAD : (2 * h + 2) * HEAD] for h in range(count)], axis=1)
    grads = (q_ref[...], keys, values)
    acc[...] += (
        inner_right(grads[0], wq_ref[...]) + inner_right(grads[1], wk_ref[...]) + inner_right(grads[2], wv_ref[...])
    )
    hidden = hid_ref[...]
    for i in range(3):
        dw_ref[i] = inner_left(hidden, grads[i]).astype(jnp.bfloat16)

    @pl.when(step == pl.num_programs(0) - 1)
    def _():
        values, gain, grad = x_ref[...].astype(jnp.float32), gain_ref[...], acc[...]
        scale = lax.rsqrt(jnp.mean(values * values, axis=1, keepdims=True) + epsilon)
        inner = jnp.mean(gain * grad * values, axis=1, keepdims=True)
        part = scale * gain * grad - values * (scale * scale * scale) * inner
        out_ref[...] = (res_ref[...] + part).astype(jnp.bfloat16)
        gain_out[...] = jnp.sum(grad * values * scale, axis=0, keepdims=True)


def finish(tokens, gain, residual_grad, hidden, query_grad, pair_grads, cosine, sine, wq, wk, wv):
    rows, width = tokens.shape
    tile = 2 * HEAD
    column = pl.BlockSpec((width, tile), lambda i: (0, i))
    return pl.pallas_call(
        finish_kernel,
        out_shape=(
            jax.ShapeDtypeStruct((3, width, width), jnp.bfloat16),
            jax.ShapeDtypeStruct((rows, width), jnp.bfloat16),
            jax.ShapeDtypeStruct((1, width), jnp.float32),
        ),
        grid=(width // tile,),
        in_specs=[whole_spec(rows, width), whole_spec(1, width), whole_spec(rows, width), whole_spec(rows, width),
                  pl.BlockSpec((rows, tile), lambda i: (0, i)), pl.BlockSpec((rows, 2 * tile), lambda i: (0, i)),
                  whole_spec(rows, HEAD), whole_spec(rows, HEAD), column, column, column],
        out_specs=(pl.BlockSpec((3, width, tile), lambda i: (0, 0, i)), whole_spec(rows, width), whole_spec(1, width)),
        scratch_shapes=[pltpu.VMEM((rows, width), jnp.float32)],
        cost_estimate=pl.CostEstimate(flops=12 * rows * width * width, bytes_accessed=12 * width * width, transcendentals=0),
        name="finish",
    )(tokens, gain[None, :], residual_grad, hidden, query_grad, pair_grads, cosine, sine, wq, wk, wv)


def experts_kernel(
    where_ref, x_ref, g_ref, rank_row, rank_col, share_row, wg_ref, wu_ref, wd_ref,
    back_ref, routed_ref, in_ref, pre_ref, lift_ref, mid_ref, og_ref, grads,
):
    blocks, rows, side = x_ref.shape
    capacity = in_ref.shape[0] // blocks
    width = og_ref.shape[1]
    dot = lambda left, right: jnp.dot(left, right, preferred_element_type=jnp.float32)
    shares = []
    for i in range(blocks):
        at = slice(i * capacity, (i + 1) * capacity)
        hit = rank_row[i] == lax.broadcasted_iota(jnp.int32, (capacity, rows), 0)
        pick = jnp.where(hit, 1.0, 0.0)
        shares.append(jnp.sum(pick * share_row[i], axis=1, keepdims=True))
        pick = pick.astype(jnp.bfloat16)
        in_ref[at, :] = dot(pick, x_ref[i, :, :width]).astype(jnp.bfloat16)
        grads[at, :] = dot(pick, g_ref[i]).astype(jnp.bfloat16)
    share = jnp.concatenate(shares, axis=0)
    pre = dot(in_ref[...], wg_ref[0])
    lift = dot(in_ref[...], wu_ref[0])
    silu, slope = silu_parts(pre)
    mid_ref[...] = (silu * lift).astype(jnp.bfloat16)
    lift_slope = lift * slope
    result = dot(mid_ref[...], wd_ref[0]).astype(jnp.bfloat16).astype(jnp.float32)
    grad = grads[...].astype(jnp.float32)
    gate_grad = jnp.sum(result * grad, axis=1, keepdims=True)
    og_ref[...] = (share * grad).astype(jnp.bfloat16)
    given = (share * result).astype(jnp.bfloat16)
    mid_grad = inner_right(og_ref[...], wd_ref[0])
    pre_ref[...] = (mid_grad * lift_slope).astype(jnp.bfloat16)
    lift_ref[...] = (mid_grad * silu).astype(jnp.bfloat16)
    in_grad = (inner_right(pre_ref[...], wg_ref[0]) + inner_right(lift_ref[...], wu_ref[0])).astype(jnp.bfloat16)
    lane = lax.broadcasted_iota(jnp.int32, (blocks * capacity, side - width), 1)
    high = gate_grad.astype(jnp.bfloat16).astype(jnp.float32)
    extra = jnp.where(lane == where_ref[0], high, jnp.where(lane == where_ref[1], gate_grad - high, 0.0))
    extra = extra.astype(jnp.bfloat16)
    for i in range(blocks):
        at = slice(i * capacity, (i + 1) * capacity)
        hit = rank_col[i] == lax.broadcasted_iota(jnp.int32, (rows, capacity), 1)
        put = jnp.where(hit, 1.0, 0.0).astype(jnp.bfloat16)
        back_ref[i, :, :width] = dot(put, in_grad[at, :]).astype(jnp.bfloat16)
        back_ref[i, :, width:] = dot(put, extra[at, :]).astype(jnp.bfloat16)
        routed_ref[i] = dot(put, given[at, :]).astype(jnp.bfloat16)


def run_experts(places, arrived, grads, rank, share, gate, up, down, capacity):
    count, rows, side = arrived.shape
    width, ff = gate.shape[1], gate.shape[2]
    blocks = 384 // capacity
    flat = count * capacity
    once = lambda *shape: pl.BlockSpec(shape, lambda i, p: (0,) * len(shape), pipeline_mode=pl.Buffered(1))
    lead = lambda *shape: pl.BlockSpec((blocks,) + shape, lambda i, p: (i, 0, 0))
    tall = lambda wide: pl.BlockSpec((blocks * capacity, wide), lambda i, p: (i, 0))
    shape = lambda *dims: jax.ShapeDtypeStruct(dims, jnp.bfloat16)
    return pl.pallas_call(
        experts_kernel,
        out_shape=(shape(count, rows, side), shape(count, rows, width), shape(flat, width), shape(flat, ff),
                   shape(flat, ff), shape(flat, ff), shape(flat, width)),
        grid_spec=pltpu.PrefetchScalarGridSpec(
            num_scalar_prefetch=1,
            grid=(count // blocks,),
            in_specs=[lead(rows, side), lead(rows, width), lead(1, rows), lead(rows, 1), lead(1, rows),
                      once(1, width, ff), once(1, width, ff), once(1, ff, width)],
            out_specs=(lead(rows, side), lead(rows, width), tall(width), tall(ff), tall(ff), tall(ff), tall(width)),
            scratch_shapes=[pltpu.VMEM((blocks * capacity, width), jnp.bfloat16)],
        ),
        compiler_params=pltpu.CompilerParams(vmem_limit_bytes=VMEM_MOST),
        cost_estimate=pl.CostEstimate(flops=16 * flat * width * ff, bytes_accessed=16 * flat * width, transcendentals=0),
        name="run_experts",
    )(places, arrived, grads, rank[:, None, :], rank[:, :, None], share[:, None, :], gate, up, down)


def local(
    tokens,
    doc_lengths,
    expert_ids,
    out_grad,
    mixer_gain,
    query_weight,
    key_weight,
    value_weight,
    output_weight,
    ffn_gain,
    router_weight,
    shared_gate,
    shared_up,
    shared_down,
    expert_gate,
    expert_up,
    expert_down,
):
    rows, width = tokens.shape[1], tokens.shape[2]
    ep_count = lax.axis_size("ep")
    device_count = ep_count * lax.axis_size("grp")
    ep_index = lax.axis_index("ep")
    expert_count = router_weight.shape[1]
    capacity = min(rows, 12 * rows * TOP // (7 * expert_count))
    low = lambda v: v.astype(jnp.bfloat16)
    wide = lambda v: v.astype(jnp.float32)
    dot = lambda left, right: jnp.dot(left, right, preferred_element_type=jnp.float32)

    grad_low = out_grad[0]

    doc_ends = jnp.cumsum(doc_lengths[0])
    query_pos = ep_index * rows + jnp.arange(rows, dtype=jnp.int32)
    before = query_pos[:, None] >= doc_ends[None, :]
    start = jnp.max(jnp.where(before, doc_ends[None, :], 0), axis=1)
    info = jnp.stack([ep_index, start[0] // rows]).astype(jnp.int32)
    half_dim = HEAD // 2
    frequency = rope_base ** (-jnp.arange(half_dim, dtype=jnp.float32) / half_dim)
    angles = wide(query_pos)[:, None] * frequency[None, :]
    cosine, sine = jnp.cos(angles), jnp.sin(angles)
    cosine = jnp.concatenate([cosine, cosine], axis=1)
    sine = jnp.concatenate([-sine, sine], axis=1)

    stream = wide(tokens[0])
    hidden_low, queries, own_pairs = project(
        tokens[0], mixer_gain, cosine, sine, query_weight, key_weight, value_weight
    )
    pairs = gather_rows(own_pairs, True, 1, 8)
    grad_later, pairs = lax.optimization_barrier((grad_low, pairs))
    grads_all = lax.all_gather(grad_later, "ep", axis=0, tiled=False)
    mixed, mixed_low, log_total = attend(info, queries, start[None, :], pairs)
    mixer_out = dot(mixed_low, output_weight)
    residual = stream + mixer_out
    ffn_low = low(normed(residual, ffn_gain))

    logits = dot(ffn_low, router_weight)
    experts = jnp.arange(expert_count, dtype=jnp.int32)
    assigned = jnp.any(expert_ids[0][:, :, None] == experts[None, None, :], axis=1)
    shown = jnp.where(assigned, logits, masked_value)
    powers = jnp.where(assigned, jnp.exp(shown - jnp.max(shown, axis=1, keepdims=True)), 0.0)
    gate_probs = powers / jnp.sum(powers, axis=1, keepdims=True)
    probs_high = low(gate_probs)
    probs_rest = low(gate_probs - wide(probs_high))
    side = width + 2 * HEAD if 2 * expert_count > HEAD else width + HEAD
    pad = jnp.zeros((rows, side - width - 2 * expert_count), jnp.bfloat16)
    sent = jnp.concatenate([ffn_low, probs_high, probs_rest, pad], axis=1)
    arrived = gather_rows(sent, False, 2)

    own = experts[None, None, :] == ep_index
    high = arrived[:, :, width : width + expert_count]
    rest = arrived[:, :, width + expert_count : width + 2 * expert_count]
    share = jnp.sum(jnp.where(own, wide(high) + wide(rest), 0.0), axis=2)
    chosen = share > 0.0
    earlier = (jnp.arange(rows)[:, None] < jnp.arange(rows)[None, :]).astype(jnp.bfloat16)
    rank = dot(low(chosen), earlier).astype(jnp.int32)
    rank = jnp.where(chosen, rank, -1)
    places = jnp.stack([ep_index, expert_count + ep_index]).astype(jnp.int32)
    back, given, flat_in, pre_grad, lift_grad, middle, result_grad = run_experts(
        places, arrived, grads_all, rank, share, expert_gate, expert_up, expert_down, capacity
    )
    back_sum = scatter_rows(back, False, 3, 2)
    given, back_sum = lax.optimization_barrier((given, back_sum))
    routed = wide(lax.psum_scatter(given, "ep", scatter_dimension=0))
    group_count = lax.axis_size("grp")
    split = width // group_count
    own_down_grad = jnp.concatenate(
        [low(inner_left(middle, result_grad[:, i * split : (i + 1) * split])) for i in range(group_count)], axis=0
    )
    own_gate_grad = low(inner_left(flat_in, pre_grad))
    own_up_grad = low(inner_left(flat_in, lift_grad))
    over_groups = lambda v: wide(lax.psum_scatter(v, "grp", scatter_dimension=0, tiled=True))[None]
    gate_sum = over_groups(own_gate_grad)
    up_sum = over_groups(own_up_grad)
    down_sum = over_groups(own_down_grad)

    shared_pre = dot(ffn_low, shared_gate)
    shared_lift = dot(ffn_low, shared_up)
    shared_silu, shared_slope = silu_parts(shared_pre)
    shared_mid = low(shared_silu * shared_lift)
    shared_out = dot(shared_mid, shared_down)
    grad_out = wide(grad_low)
    shared_mid_grad = inner_right(grad_low, shared_down)
    shared_pre_grad = low(shared_mid_grad * shared_lift * shared_slope)
    shared_lift_grad = low(shared_mid_grad * shared_silu)
    ffn_grad = inner_right(shared_pre_grad, shared_gate) + inner_right(shared_lift_grad, shared_up)

    layer_out = residual + shared_out + routed
    gate_back = wide(back_sum[:, width : width + expert_count]) + wide(
        back_sum[:, width + expert_count : width + 2 * expert_count]
    )
    chosen_grad = gate_probs * (gate_back - jnp.sum(gate_probs * gate_back, axis=1, keepdims=True))
    logit_grad = low(chosen_grad)
    ffn_grad = ffn_grad + wide(back_sum[:, :width]) + inner_right(logit_grad, router_weight)
    _, ffn_pull = jax.vjp(normed, residual, ffn_gain)
    residual_part, ffn_gain_grad = ffn_pull(ffn_grad)
    residual_grad = grad_out + residual_part
    mixer_grad_low = low(residual_grad)
    mixed_grad = low(inner_right(mixer_grad_low, output_weight))
    pair_parts, query_lin_grad = attend_back(
        info, queries, mixed_grad, mixed, start[None, :], log_total, cosine, sine, pairs
    )
    pair_grads = scatter_rows(pair_parts, True, 4, 2)

    by_device = lambda v: low(v).reshape(device_count, width // device_count, -1)
    early = jnp.concatenate(
        [by_device(inner_left(ffn_low, shared_pre_grad)), by_device(inner_left(ffn_low, shared_lift_grad)),
         by_device(inner_left(grad_low, shared_mid)), by_device(inner_left(mixed_low, mixer_grad_low))], axis=2
    )
    early_sum = scatter_whole(early, 5)

    weight_grads, tokens_grad, mixer_gain_grad = finish(
        tokens[0], mixer_gain, residual_grad, hidden_low, query_lin_grad, pair_grads, cosine, sine,
        query_weight, key_weight, value_weight,
    )
    squares = jnp.stack(
        [jnp.sum(residual * residual), jnp.sum(mixer_out * mixer_out), jnp.sum(layer_out * layer_out)]
    )
    extras = jnp.concatenate(
        [inner_left(ffn_low, logit_grad), mixer_gain_grad.T, ffn_gain_grad[:, None],
         jnp.broadcast_to(squares[None, :], (width, 3))], axis=1
    )
    extras = jnp.pad(extras, ((0, 0), (0, HEAD - extras.shape[1])))
    late = jnp.concatenate(
        [by_device(weight_grads[0]), by_device(weight_grads[1]), by_device(weight_grads[2]), by_device(extras)], axis=2
    )
    late_sum = scatter_whole(late, 6)
    extra_sum = late_sum[:, 3 * width :]
    entry_count = rows * device_count * width
    stream_rms = jnp.sqrt(extra_sum[0, expert_count + 2 : expert_count + 5] / entry_count)
    ff = shared_gate.shape[1]
    return (
        low(layer_out)[None],
        tokens_grad[None],
        extra_sum[:, expert_count],
        late_sum[:, :width],
        late_sum[:, width : 2 * width],
        late_sum[:, 2 * width : 3 * width],
        early_sum[:, 3 * ff :],
        extra_sum[:, expert_count + 1],
        extra_sum[:, :expert_count],
        early_sum[:, :ff],
        early_sum[:, ff : 2 * ff],
        early_sum[:, 2 * ff : 3 * ff].T,
        gate_sum,
        up_sum,
        down_sum,
        stream_rms,
    )


def solution(mesh):
    return jax.shard_map(
        local,
        mesh=mesh,
        in_specs=(
            P("grp", "ep", None),
            P("grp", None),
            P("grp", "ep", None),
            P("grp", "ep", None),
            P(),
            P(),
            P(),
            P(),
            P(),
            P(),
            P(),
            P(),
            P(),
            P(),
            P("ep", None, None),
            P("ep", None, None),
            P("ep", None, None),
        ),
        out_specs=(
            P("grp", "ep", None),
            P("grp", "ep", None),
            P(("grp", "ep")),
            P(("grp", "ep"), None),
            P(("grp", "ep"), None),
            P(("grp", "ep"), None),
            P(("grp", "ep"), None),
            P(("grp", "ep")),
            P(("grp", "ep"), None),
            P(("grp", "ep"), None),
            P(("grp", "ep"), None),
            P(None, ("grp", "ep")),
            P("ep", "grp", None),
            P("ep", "grp", None),
            P("ep", None, "grp"),
            P(),
        ),
        check_vma=False,
    )
```

```python
import functools

import jax
import jax.numpy as jnp
from jax import lax
from jax.experimental import pallas as pl
from jax.experimental.pallas import tpu as pltpu
from jax.sharding import PartitionSpec as P

HEADS = 10
HEAD = 128
TOP = 7

epsilon = 1e-06
rope_base = 10000.0
masked_value = -1e30


def normed(values, gain_vec):
    return (
        values * lax.rsqrt(jnp.mean(values * values, axis=-1, keepdims=True) + epsilon) * gain_vec
    )


def inner_left(left_op, right_op):
    return lax.dot_general(
        left_op, right_op, (((0,), (0,)), ((), ())), preferred_element_type=jnp.float32
    )


def inner_right(left_op, right_op):
    return lax.dot_general(
        left_op, right_op, (((1,), (1,)), ((), ())), preferred_element_type=jnp.float32
    )


def silu_parts(pre_act):
    sigmoid_val = jax.nn.sigmoid(pre_act)
    return (pre_act * sigmoid_val, sigmoid_val * (1.0 + pre_act * (1.0 - sigmoid_val)))


MESH = pl.DeviceIdType.MESH
VMEM_MOST = 64 * 1024 * 1024 - 65536


def when(cond):
    if cond is True:
        return lambda f: f()
    if cond is False:
        return lambda f: None
    return pl.when(cond)


def both(*conds):
    out = True
    for cond in conds:
        if cond is False:
            return False
        if cond is True:
            continue
        out = cond if out is True else jnp.logical_and(out, cond)
    return out


class Plan:
    def __init__(self, ep_count, window):
        self.long = 4
        self.wide = ep_count // 8
        self.window = window
        self.steps = (
            list(range(self.long // 2 + 1))
            if window
            else list(range(-(self.long - 1), self.long))
        )

    def place(self):
        me = lax.axis_index("ep")
        return me // (2 * self.wide), (me // 2) % self.wide, me % 2

    def slot(self, a, b, c):
        return (a * self.wide + b) * 2 + c

    def plane(self, a, d):
        return d if self.window else jnp.clip(a - d, 0, self.long - 1)

    def planes(self):
        return len(self.steps) if self.window else self.long

    def inside(self, a):
        return jnp.logical_and(a >= 0, a < self.long)

    def need(self, d, b, c, b0, c0):
        if not self.window or 0 < d < self.long // 2:
            return True
        if d == 0:
            return jnp.logical_or(b0 < b, jnp.logical_and(b0 == b, c0 <= c))
        return jnp.logical_or(b0 > b, jnp.logical_and(b0 == b, c0 >= c))

    def need_pair(self, d, b, b0):
        if not self.window or 0 < d < self.long // 2:
            return True
        return b0 < b if d == 0 else b0 > b

    def greet(self, a, b, c):
        barrier = pltpu.get_barrier_semaphore()

        def signal(cond, dev):
            @when(cond)
            def _():
                pl.semaphore_signal(barrier, inc=1, device_id={"ep": dev}, device_id_type=MESH)

        signal(a + 1 < self.long, self.slot(a + 1, b, c))
        signal(a > 0, self.slot(a - 1, b, c))
        for k in range(1, self.wide):
            signal(True, self.slot(a, (b + k) % self.wide, c))
        signal(True, self.slot(a, b, 1 - c))
        ends = (a == 0).astype(jnp.int32) + (a == self.long - 1).astype(jnp.int32)
        pl.semaphore_wait(barrier, self.wide + 2 - ends)


def gather_kernel(plan, pieces, x_ref, out_ref, ra, sa_up, sa_dn, rb, sb, rc, sc, own):
    a, b, c = plan.place()
    steps, wide = plan.steps, plan.wide
    at = {d: i for i, d in enumerate(steps)}
    rows = x_ref.shape[0] // pieces

    def part(q):
        return pl.ds(pl.multiple_of(q * rows, rows), rows)

    def copy(q, src, slot, ssem, rsem, dev):
        return pltpu.make_async_remote_copy(
            src_ref=src, dst_ref=out_ref.at[slot, part(q)], send_sem=ssem, recv_sem=rsem,
            device_id={"ep": dev}, device_id_type=MESH,
        )

    def hops(d, q):
        i = at[d]
        slot = plan.slot(a - d, b, c)
        src = x_ref.at[part(q)] if d == 0 else out_ref.at[slot, part(q)]
        real = plan.inside(a - d)
        out = []
        if d >= 0 and d + 1 in at:
            out.append((both(real, a + 1 < plan.long), lambda: copy(
                q, src, slot, sa_up.at[i, q], ra.at[at[d + 1], q], plan.slot(a + 1, b, c))))
        if d <= 0 and d - 1 in at:
            out.append((both(real, a > 0), lambda: copy(
                q, src, slot, sa_dn.at[i, q], ra.at[at[d - 1], q], plan.slot(a - 1, b, c))))
        for k in range(1, wide):
            to = (b + k) % wide
            out.append((both(real, plan.need_pair(d, to, b)), lambda k=k, to=to: copy(
                q, src, slot, sb.at[i, k, q], rb.at[i, k, q], plan.slot(a, to, c))))
        out.append((both(real, plan.need(d, b, 1 - c, b, c)), lambda: copy(
            q, src, slot, sc.at[i, 0, q], rc.at[i, 0, q], plan.slot(a, b, 1 - c))))
        return out

    def cross(d, k, q):
        i = at[d]
        b0 = (b + wide - k) % wide
        slot = plan.slot(a - d, b0, c)
        real = plan.inside(a - d)
        come = lambda: copy(q, x_ref.at[part(q)], slot, sb.at[i, k, q], rb.at[i, k, q], plan.slot(a, b, c))
        go = lambda: copy(q, out_ref.at[slot, part(q)], slot, sc.at[i, k, q], rc.at[i, k, q],
                          plan.slot(a, b, 1 - c))
        return (both(real, plan.need_pair(d, b, b0)), come,
                both(real, plan.need(d, b, 1 - c, b0, c)), go)

    plan.greet(a, b, c)
    keep = pltpu.make_async_copy(x_ref, out_ref.at[plan.slot(a, b, c)], own)

    @pl.loop(0, pieces)
    def _(q):
        for cond, go in hops(0, q):
            @when(cond)
            def _(go=go):
                go().start()

    keep.start()
    far = max(abs(d) for d in steps)
    for step in range(1, far + 3):
        @pl.loop(0, pieces)
        def _(q, step=step):
            for d in (step, -step):
                if d in at:
                    @when(plan.inside(a - d))
                    def _(d=d):
                        slot = plan.slot(a - d, b, c)
                        copy(q, x_ref.at[part(q)], slot, sa_up.at[0, q], ra.at[at[d], q],
                             plan.slot(a, b, c)).wait_recv()
                        for cond, go in hops(d, q):
                            @when(cond)
                            def _(go=go):
                                go().start()
            for d in sorted({step - 2, 2 - step}) if step > 1 else ():
                if d in at:
                    for k in range(1, wide):
                        came, come, goes, go = cross(d, k, q)
                        @when(came)
                        def _(come=come):
                            come().wait_recv()
                        @when(goes)
                        def _(go=go):
                            go().start()
    keep.wait()

    @pl.loop(0, pieces)
    def _(q):
        for d in steps:
            i = at[d]
            real = plan.inside(a - d)
            for k in range(wide):
                b0 = (b + wide - k) % wide
                slot = plan.slot(a - d, b0, 1 - c)
                @when(both(real, plan.need(d, b, c, b0, 1 - c)))
                def _(slot=slot, i=i, k=k):
                    copy(q, x_ref.at[part(q)], slot, sc.at[i, k, q], rc.at[i, k, q],
                         plan.slot(a, b, c)).wait_recv()
            for cond, go in hops(d, q):
                @when(cond)
                def _(go=go):
                    go().wait_send()
            for k in range(1, wide):
                came, come, goes, go = cross(d, k, q)
                @when(goes)
                def _(go=go):
                    go().wait_send()


def gather_rows(block, window, collective_id, pieces=4):
    ep_count = lax.axis_size("ep")
    plan = Plan(ep_count, window)
    n, wide = len(plan.steps), plan.wide
    sem = pltpu.SemaphoreType.DMA
    return pl.pallas_call(
        functools.partial(gather_kernel, plan, pieces),
        out_shape=jax.ShapeDtypeStruct((ep_count,) + block.shape, block.dtype),
        in_specs=[pl.BlockSpec(memory_space=pltpu.VMEM)],
        out_specs=pl.BlockSpec(memory_space=pl.ANY),
        scratch_shapes=[sem((n, pieces)), sem((n, pieces)), sem((n, pieces)), sem((n, wide, pieces)),
                        sem((n, wide, pieces)), sem((n, wide, pieces)), sem((n, wide, pieces)), sem],
        compiler_params=pltpu.CompilerParams(collective_id=collective_id, has_side_effects=True),
        name="gather_rows",
    )(block)


def add_rows(dst, others, out=None):
    rows, width = dst.shape
    out = dst if out is None else out
    small = rows <= 64
    piece = 32 if rows % 32 == 0 else rows
    lanes = width if rows % 32 == 0 else 4 * HEAD
    whole = width // lanes * lanes

    def add(at):
        if len(others) == 1 and out.dtype == jnp.bfloat16:
            out[at] = dst[at] + others[0][at]
        else:
            total = dst[at].astype(jnp.float32)
            for other in others:
                total = total + other[at].astype(jnp.float32)
            out[at] = total.astype(out.dtype)

    if piece == rows:
        @pl.loop(0, whole // lanes)
        def _(i):
            add((slice(None), pl.ds(pl.multiple_of(i * lanes, lanes), lanes)))

        if whole < width:
            add((slice(None), pl.ds(whole, width - whole)))
    else:
        @pl.loop(0, rows // piece)
        def _(i):
            add((pl.ds(pl.multiple_of(i * piece, piece), piece), slice(None)))


def send(src, dst, ssem, rsem, to):
    return pltpu.make_async_remote_copy(
        src_ref=src, dst_ref=dst, send_sem=ssem, recv_sem=rsem, device_id=to, device_id_type=MESH
    )


def run_if(cond, go):
    @when(cond)
    def _():
        go()


class RowSum:
    @staticmethod
    def scratch(plan, rows, width, dtype, pieces):
        n, wide = plan.planes(), plan.wide
        blocks = lambda *lead: pltpu.VMEM(lead + (rows, width), dtype)
        sem = lambda *lead: pltpu.SemaphoreType.DMA(lead + (pieces,))
        return [blocks(n, wide), blocks(n, wide), blocks(n, wide - 1), blocks(n), blocks(n),
                sem(n, wide), sem(n, wide), sem(n, wide), sem(n, wide), sem(n), sem(n), sem(n), sem(n, wide)]

    def __init__(self, plan, pieces, p_ref, scratch):
        self.plan, self.pieces, self.p_ref = plan, pieces, p_ref
        (self.held, self.rcb, self.rbb, self.r_hi, self.r_lo,
         self.sc, self.rc, self.sb, self.rb, self.sa, self.rhi, self.rlo, self.ld) = scratch
        self.a, self.b, self.c = plan.place()
        self.rows = p_ref.shape[1] // pieces
        self.order = sorted(plan.steps, key=lambda d: -abs(d))

    def part(self, q):
        return pl.ds(pl.multiple_of(q * self.rows, self.rows), self.rows)

    def dev(self, a, b, c):
        return {"ep": self.plan.slot(a, b, c)}

    def source(self, k):
        return (self.b + self.plan.wide - k) % self.plan.wide

    def load(self, d, k, q):
        p, i, b0 = self.plan, self.plan.plane(self.a, d), self.source(k)
        return both(p.inside(self.a - d), p.need(d, self.b, self.c, b0, self.c)), lambda: pltpu.make_async_copy(
            self.p_ref.at[p.slot(self.a - d, b0, self.c), self.part(q)], self.held.at[i, k, self.part(q)],
            self.ld.at[i, k, q])

    def cross(self, d, k, q):
        p, i, b0, c = self.plan, self.plan.plane(self.a, d), self.source(k), self.c
        real = p.inside(self.a - d)
        return (both(real, p.need(d, self.b, c, b0, 1 - c)), lambda: send(
            self.p_ref.at[p.slot(self.a - d, b0, 1 - c), self.part(q)], self.rcb.at[i, k, self.part(q)],
            self.sc.at[i, k, q], self.rc.at[i, k, q], self.dev(self.a, self.b, 1 - c)),
            both(real, p.need(d, self.b, 1 - c, b0, c)))

    def over(self, d, k, q):
        p, i, b0 = self.plan, self.plan.plane(self.a, d), self.source(k)
        return both(p.inside(self.a - d), p.need_pair(d, self.b, b0)), lambda: send(
            self.held.at[i, k, self.part(q)], self.rbb.at[i, k - 1, self.part(q)], self.sb.at[i, k, q],
            self.rb.at[i, k, q], self.dev(self.a, b0, self.c))

    def along(self, d, q):
        p, i, up = self.plan, self.plan.plane(self.a, d), d < 0
        j = d - 1 if p.window else i
        return p.inside(self.a - d), lambda: send(
            self.held.at[i, 0, self.part(q)], (self.r_lo if up else self.r_hi).at[j, self.part(q)],
            self.sa.at[i, q], (self.rlo if up else self.rhi).at[j, q],
            self.dev(self.a + (1 if up else -1), self.b, self.c))

    def start(self, ks):
        for k in ks:
            @pl.loop(0, self.pieces)
            def _(q, k=k):
                for d in self.order:
                    for cond, go in (self.cross(d, k, q)[:2], self.load(d, k, q)):
                        run_if(cond, lambda go=go: go().start())

    def first(self, d, k, q):
        i = self.plan.plane(self.a, d)
        cond, go = self.load(d, k, q)
        run_if(cond, lambda: go().wait())
        _, come_go, come = self.cross(d, k, q)

        def take():
            come_go().wait_recv()
            add_rows(self.held.at[i, k, self.part(q)], [self.rcb.at[i, k, self.part(q)]])

        run_if(come, take)

    def stage_over(self, k):
        @pl.loop(0, self.pieces)
        def _(q):
            for d in self.order:
                self.first(d, k, q)
                cond, go = self.over(d, k, q)
                run_if(cond, lambda go=go: go().start())

    def stage_dests(self, low, high):
        @pl.loop(low, high)
        def _(q):
            for d in self.order:
                self.dest(d, q)

    def dest(self, d, q):
        p, a, b, steps = self.plan, self.a, self.b, self.plan.steps
        i = p.plane(a, d)
        real = p.inside(a - d)
        mine = self.held.at[i, 0, self.part(q)]
        self.first(d, 0, q)
        for k in range(1, p.wide):
            def take(k=k):
                self.over(d, k, q)[1]().wait_recv()
                add_rows(mine, [self.rbb.at[i, k - 1, self.part(q)]])

            run_if(both(real, p.need_pair(d, (b + k) % p.wide, b)), take)
        for inner, cond, buf, sem in ((d >= 0 and d + 1 in steps, a + 1 < p.long, self.r_hi, self.rhi),
                                      (d <= 0 and d - 1 in steps, a > 0, self.r_lo, self.rlo)):
            if inner:
                def take(buf=buf, sem=sem):
                    send(mine, buf.at[i, self.part(q)], self.sa.at[i, q], sem.at[i, q],
                         self.dev(a, b, self.c)).wait_recv()
                    add_rows(mine, [buf.at[i, self.part(q)]])

                run_if(both(real, cond), take)
        if d:
            cond, go = self.along(d, q)
            run_if(cond, lambda: go().start())

    def result(self):
        return self.held[self.plan.plane(self.a, 0), 0]

    def drain(self):
        @pl.loop(0, self.pieces)
        def _(q):
            for d in self.plan.steps:
                sends = [self.cross(d, k, q)[:2] for k in range(self.plan.wide)]
                sends += [self.over(d, k, q) for k in range(1, self.plan.wide)]
                if d:
                    sends.append(self.along(d, q))
                for cond, go in sends:
                    run_if(cond, lambda go=go: go().wait_send())


def scatter_rows(parts, window, collective_id, pieces=4):
    ep_count, rows, width = parts.shape
    plan = Plan(ep_count, window)

    def kernel(p_ref, out_ref, *scratch):
        total = RowSum(plan, pieces, p_ref, scratch)
        plan.greet(total.a, total.b, total.c)
        ks = list(range(1, plan.wide)) + [0]
        total.start(ks)
        for k in ks[:-1]:
            total.stage_over(k)
        total.stage_dests(0, pieces)
        out_ref[...] = total.result()
        total.drain()

    return pl.pallas_call(
        kernel,
        out_shape=jax.ShapeDtypeStruct((rows, width), parts.dtype),
        in_specs=[pl.BlockSpec(memory_space=pl.ANY)],
        out_specs=pl.BlockSpec(memory_space=pltpu.VMEM),
        scratch_shapes=RowSum.scratch(plan, rows, width, parts.dtype, pieces),
        compiler_params=pltpu.CompilerParams(
            collective_id=collective_id, has_side_effects=True, vmem_limit_bytes=VMEM_MOST),
        name="scatter_rows",
    )(parts)


class Place:
    def __init__(self, groups, ep_count):
        self.sizes = {"x": groups, "a": 4, "b": ep_count // 8}

    def locate(self):
        me, wide = lax.axis_index("ep"), self.sizes["b"]
        self.at = {"x": lax.axis_index("grp"), "a": me // (2 * wide), "b": (me // 2) % wide, "c": me % 2}

    def dev(self, **moved):
        at = {**self.at, **moved}
        return {"grp": at["x"], "ep": (at["a"] * self.sizes["b"] + at["b"]) * 2 + at["c"]}

    def slot(self, **moved):
        at = {**self.at, **moved}
        return ((at["x"] * self.sizes["a"] + at["a"]) * self.sizes["b"] + at["b"]) * 2 + at["c"]

    def back(self, axis, k):
        return (self.at[axis] + self.sizes[axis] - k) % self.sizes[axis]

    def greet(self):
        peers = [self.dev(c=1 - self.at["c"])] + [
            self.dev(**{axis: self.back(axis, k)}) for axis in "xba" for k in range(1, self.sizes[axis])]
        barrier = pltpu.get_barrier_semaphore()
        for to in peers:
            pl.semaphore_signal(barrier, inc=1, device_id=to, device_id_type=MESH)
        pl.semaphore_wait(barrier, len(peers))


def from_far(size):
    return list(range(1, size)) + [0]


class WholeSum:
    @staticmethod
    def scratch(sizes, axes, rows, width, dtype, sources):
        n1, n2, n3 = (sizes[axis] for axis in axes)
        blocks = lambda *lead: pltpu.VMEM(lead + (rows, width), dtype)
        sem = lambda *lead: pltpu.SemaphoreType.DMA(lead)
        full = (n1, n2, n3)
        one, two, three = (n1 - 1, n2, n3), (n2 - 1, n3), (n3 - 1,)
        return [blocks(*full), blocks(*full), blocks(*one), blocks(*two), blocks(*three),
                sem(*full, sources), sem(*full, sources), sem(*full, sources), sem(*one), sem(*one), sem(*two), sem(*two), sem(*three), sem(*three)]

    def __init__(self, place, axes, pieces, scratch):
        self.place, self.axes, self.pieces = place, axes, pieces
        (self.held, self.rcb, self.r1, self.r2, self.r3,
         self.ld, self.sc, self.rc, self.s1, self.q1, self.s2, self.q2, self.s3, self.q3) = scratch
        self.n1, self.n2, self.n3 = (place.sizes[axis] for axis in axes)
        self.groups = [[(k1, k2, k3) for k2 in from_far(self.n2) for k3 in from_far(self.n3)]
                       for k1 in from_far(self.n1)]

    def slot(self, key, c):
        return self.place.slot(c=c, **{axis: self.place.back(axis, k) for axis, k in zip(self.axes, key)})

    def loads(self, key):
        c = self.place.at["c"]
        for n, (ref, first, at, count) in enumerate(self.pieces):
            frm, to = pl.ds(first, count), pl.ds(at, count)
            yield pltpu.make_async_copy(
                ref.at[self.slot(key, c), :, frm], self.held.at[key + (slice(None), to)],
                self.ld.at[key + (n,)])

    def crossings(self, key):
        c = self.place.at["c"]
        for n, (ref, first, at, count) in enumerate(self.pieces):
            frm, to = pl.ds(first, count), pl.ds(at, count)
            yield send(ref.at[self.slot(key, 1 - c), :, frm], self.rcb.at[key + (slice(None), to)],
                       self.sc.at[key + (n,)], self.rc.at[key + (n,)], self.place.dev(c=1 - c))

    def hop(self, level, key):
        buf, ssem, rsem = ((self.r1, self.s1, self.q1), (self.r2, self.s2, self.q2), (self.r3, self.s3, self.q3))[level]
        axis, k = self.axes[level], key[level]
        far = (k - 1,) + key[level + 1 :]
        return send(self.held.at[key], buf.at[far], ssem.at[far], rsem.at[far],
                    self.place.dev(**{axis: self.place.back(axis, k)}))

    def start(self, i):
        for key in self.groups[i]:
            for go in self.crossings(key):
                go.start()
            for go in self.loads(key):
                go.start()

    def stage_core(self, i):
        for key in self.groups[i]:
            for go in self.loads(key):
                go.wait()
            for go in self.crossings(key):
                go.wait_recv()
            add_rows(self.held.at[key], [self.rcb.at[key]])
            if key[0]:
                self.hop(0, key).start()

    def stage_one(self, k2):
        for k3 in from_far(self.n3):
            for k1 in range(1, self.n1):
                self.hop(0, (k1, k2, k3)).wait_recv()
            add_rows(self.held.at[0, k2, k3], [self.r1.at[k1 - 1, k2, k3] for k1 in range(1, self.n1)])
            if k2:
                self.hop(1, (0, k2, k3)).start()

    def stage_two(self):
        for k3 in from_far(self.n3):
            for k2 in range(1, self.n2):
                self.hop(1, (0, k2, k3)).wait_recv()
            add_rows(self.held.at[0, 0, k3], [self.r2.at[k2 - 1, k3] for k2 in range(1, self.n2)])
            if k3:
                self.hop(2, (0, 0, k3)).start()

    def stage_three(self, out):
        for k3 in range(1, self.n3):
            self.hop(2, (0, 0, k3)).wait_recv()
        add_rows(self.held.at[0, 0, 0], [self.r3.at[k3 - 1] for k3 in range(1, self.n3)], out)

    def drain(self):
        for group in self.groups:
            for key in group:
                for go in self.crossings(key):
                    go.wait_send()
                if key[0]:
                    self.hop(0, key).wait_send()
                elif key[1]:
                    self.hop(1, key).wait_send()
                elif key[2]:
                    self.hop(2, key).wait_send()


def scatter_whole(parts, collective_id, pairs=None):
    rows = parts[0].shape[1]
    width = sum(part.shape[2] for part in parts)
    groups, ep_count = lax.axis_size("grp"), lax.axis_size("ep")
    place = Place(groups, ep_count)
    tiles = width // HEAD
    cuts = [0, tiles // 2 * HEAD, width]
    orders = ["xba", "xba" if pairs is not None else "bxa"]

    def kernel(*refs):
        sources, refs = refs[: len(parts)], refs[len(parts) :]
        if pairs is not None:
            pair_ref, refs = refs[0], refs[1:]
        out_ref, refs = refs[0], refs[1:]
        if pairs is not None:
            pair_out, refs = refs[0], refs[1:]
        place.locate()
        sums = []
        for n, axes in enumerate(orders):
            low, high, first, pieces = cuts[n], cuts[n + 1], 0, []
            for ref in sources:
                begin, end = max(low, first), min(high, first + ref.shape[2])
                if begin < end:
                    pieces.append((ref, begin - first, begin - low, end - begin))
                first += ref.shape[2]
            sums.append(WholeSum(place, axes, pieces, refs[:14]))
            refs = refs[14:]
        outs = [out_ref.at[:, pl.ds(cuts[n], cuts[n + 1] - cuts[n])] for n in range(len(orders))]
        place.greet()
        if pairs is None:
            couples = [sums[n : n + 2] for n in range(0, len(sums), 2)]
            for couple in couples:
                for i in range(max(s.n1 for s in couple)):
                    for s in couple:
                        if i < s.n1:
                            s.start(i)

            def core(couple):
                for i in range(max(s.n1 for s in couple)):
                    for s in couple:
                        if i < s.n1:
                            s.stage_core(i)

            def one(couple):
                for i in range(max(s.n2 for s in couple)):
                    for s in couple:
                        if i < s.n2:
                            s.stage_one(from_far(s.n2)[i])

            def two(couple):
                for s in couple:
                    s.stage_two()

            for stage in (core, one, two):
                for couple in couples:
                    stage(couple)
            for s, out in zip(sums, outs):
                s.stage_three(out)
        else:
            total = RowSum(plan, 4, pair_ref, refs)
            ks = from_far(plan.wide)
            for one in sums:
                for i in range(one.n1 - 1):
                    one.start(i)
            total.start(ks[:-1])
            for one in sums:
                one.start(one.n1 - 1)
            total.start(ks[-1:])
            for one in sums:
                for i in range(one.n1 - 1):
                    one.stage_core(i)
            for k in ks[:-1]:
                total.stage_over(k)
            for one in sums:
                one.stage_core(one.n1 - 1)
            total.stage_dests(0, 2)
            for k2 in from_far(sums[0].n2):
                sums[0].stage_one(k2)
            total.stage_dests(2, 3)
            sums[0].stage_two()
            for one in sums[1:]:
                for k2 in from_far(one.n2):
                    one.stage_one(k2)
            total.stage_dests(3, 4)
            for one in sums[1:]:
                one.stage_two()
            pair_out[...] = total.result()
            for one, out in zip(sums, outs):
                one.stage_three(out)
            total.drain()
        for s in sums:
            s.drain()

    operands, anywhere = list(parts), pl.BlockSpec(memory_space=pl.ANY)
    out_shape = [jax.ShapeDtypeStruct((rows, width), jnp.float32)]
    scratch = []
    for n, axes in enumerate(orders):
        scratch += WholeSum.scratch(place.sizes, axes, rows, cuts[n + 1] - cuts[n], parts[0].dtype, len(parts))
    if pairs is not None:
        plan = Plan(ep_count, True)
        operands.append(pairs)
        out_shape.append(jax.ShapeDtypeStruct(pairs.shape[1:], pairs.dtype))
        scratch += RowSum.scratch(plan, pairs.shape[1], pairs.shape[2], pairs.dtype, 4)
    got = pl.pallas_call(
        kernel,
        out_shape=tuple(out_shape),
        in_specs=[anywhere] * len(operands),
        out_specs=tuple(pl.BlockSpec(memory_space=pltpu.VMEM) for _ in out_shape),
        scratch_shapes=scratch,
        compiler_params=pltpu.CompilerParams(
            collective_id=collective_id, has_side_effects=True, vmem_limit_bytes=VMEM_MOST),
        name="scatter_whole" if pairs is None else "scatter_pairs",
    )(*operands)
    return got[0] if pairs is None else got


def visible_bias(shape, first_key, start, first_query):
    key_pos = first_key + lax.broadcasted_iota(jnp.int32, shape, 0)
    query_pos = first_query + lax.broadcasted_iota(jnp.int32, shape, 1)
    seen = jnp.logical_and(key_pos >= start, key_pos <= query_pos)
    return jnp.where(seen, 0.0, masked_value)


def lanes(first):
    return pl.ds(pl.multiple_of(first, HEAD), HEAD)


def turned(values, cosine, sine):
    return values * cosine + pltpu.roll(values, HEAD // 2, 1) * sine


def whole_spec(*shape):
    return pl.BlockSpec(shape, lambda *s: (0,) * len(shape))


def project_kernel(x_ref, gain_ref, cos_ref, sin_ref, wq_ref, wk_ref, wv_ref, hid_ref, q_ref, kv_ref, hidden):
    @pl.when(pl.program_id(0) == 0)
    def _():
        hidden[...] = normed(x_ref[...].astype(jnp.float32), gain_ref[...]).astype(jnp.bfloat16)
        hid_ref[...] = hidden[...]

    cosine, sine = cos_ref[...], sin_ref[...]
    q = jnp.dot(hidden[...], wq_ref[...], preferred_element_type=jnp.float32)
    k = jnp.dot(hidden[...], wk_ref[...], preferred_element_type=jnp.float32)
    v = jnp.dot(hidden[...], wv_ref[...], preferred_element_type=jnp.float32)
    for h in range(q.shape[1] // HEAD):
        at = slice(h * HEAD, (h + 1) * HEAD)
        q_ref[:, at] = (turned(q[:, at], cosine, sine) * HEAD ** (-0.5)).astype(jnp.bfloat16)
        kv_ref[:, 2 * h * HEAD : (2 * h + 1) * HEAD] = turned(k[:, at], cosine, sine).astype(jnp.bfloat16)
        kv_ref[:, (2 * h + 1) * HEAD : (2 * h + 2) * HEAD] = v[:, at].astype(jnp.bfloat16)


def project(tokens, gain, cosine, sine, wq, wk, wv):
    rows, width = tokens.shape
    tile = 2 * HEAD
    column = pl.BlockSpec((width, tile), lambda i: (0, i))
    return pl.pallas_call(
        project_kernel,
        out_shape=(
            jax.ShapeDtypeStruct((rows, width), jnp.bfloat16),
            jax.ShapeDtypeStruct((rows, width), jnp.bfloat16),
            jax.ShapeDtypeStruct((rows, 2 * width), jnp.bfloat16),
        ),
        grid=(width // tile,),
        in_specs=[whole_spec(rows, width), whole_spec(1, width), whole_spec(rows, HEAD), whole_spec(rows, HEAD),
                  column, column, column],
        out_specs=(whole_spec(rows, width), pl.BlockSpec((rows, tile), lambda i: (0, i)),
                   pl.BlockSpec((rows, 2 * tile), lambda i: (0, i))),
        scratch_shapes=[pltpu.VMEM((rows, width), jnp.bfloat16)],
        cost_estimate=pl.CostEstimate(flops=6 * rows * width * width, bytes_accessed=6 * width * width, transcendentals=0),
        name="project",
    )(tokens, gain[None, :], cosine, sine, wq, wk, wv)


def attend_kernel(info, q_ref, start_ref, kv_ref, mixed_ref, low_ref, total_ref, bias, top, norm):
    step = pl.program_id(0)
    me, first_block = info[0], info[1]
    rows = q_ref.shape[0]
    block = me - step

    @pl.when(step == 0)
    def _():
        top[...] = jnp.full_like(top, masked_value)
        norm[...] = jnp.zeros_like(norm)
        mixed_ref[...] = jnp.zeros_like(mixed_ref)

    @pl.when(block >= first_block)
    def _():
        bias[...] = visible_bias((rows, rows), block * rows, start_ref[...], me * rows)

        @pl.loop(0, HEADS, unroll=2)
        def _(h):
            keys, values = kv_ref[0, :, lanes(2 * h * HEAD)], kv_ref[0, :, lanes((2 * h + 1) * HEAD)]
            scores = inner_right(keys, q_ref[:, lanes(h * HEAD)]) + bias[...]
            old = top[h]
            new = jnp.maximum(old, jnp.max(scores, axis=0, keepdims=True))
            weights = jnp.exp(scores - new)
            shrink = jnp.exp(old - new)
            top[h] = new
            norm[h] = norm[h] * shrink + jnp.sum(weights, axis=0, keepdims=True)
            mixed_ref[h] = mixed_ref[h] * shrink + inner_left(values, weights.astype(jnp.bfloat16))

    @pl.when(step == pl.num_programs(0) - 1)
    def _():
        for h in range(HEADS):
            mixed = mixed_ref[h] / norm[h]
            mixed_ref[h] = mixed
            low_ref[:, h * HEAD : (h + 1) * HEAD] = mixed.T.astype(jnp.bfloat16)
            total_ref[h] = top[h] + jnp.log(norm[h])


def attend(info, queries, start, pairs):
    rows, width = queries.shape
    steps = pairs.shape[0] // 2 + 1
    return pl.pallas_call(
        attend_kernel,
        out_shape=(
            jax.ShapeDtypeStruct((HEADS, HEAD, rows), jnp.float32),
            jax.ShapeDtypeStruct((rows, width), jnp.bfloat16),
            jax.ShapeDtypeStruct((HEADS, 1, rows), jnp.float32),
        ),
        grid_spec=pltpu.PrefetchScalarGridSpec(
            num_scalar_prefetch=1,
            grid=(steps,),
            in_specs=[
                whole_spec(rows, width),
                whole_spec(1, rows),
                pl.BlockSpec((1, rows, 2 * width), lambda s, info: (jnp.maximum(info[0] - s, info[1]), 0, 0)),
            ],
            out_specs=(whole_spec(HEADS, HEAD, rows), whole_spec(rows, width), whole_spec(HEADS, 1, rows)),
            scratch_shapes=[
                pltpu.VMEM((rows, rows), jnp.float32),
                pltpu.VMEM((HEADS, 1, rows), jnp.float32),
                pltpu.VMEM((HEADS, 1, rows), jnp.float32),
            ],
        ),
        cost_estimate=pl.CostEstimate(
            flops=4 * rows * rows * width * steps, bytes_accessed=4 * rows * width * steps, transcendentals=0
        ),
        name="attend",
    )(info, queries, start, pairs)


def attend_back_kernel(
    info, q_ref, g_ref, mixed_ref, start_ref, total_ref, cos_ref, sin_ref, kv_ref, dkv_ref, dq_ref, bias, acc, term
):
    step = pl.program_id(0)
    me, first_block = info[0], info[1]
    rows = q_ref.shape[0]
    block = me - step

    @pl.when(step == 0)
    def _():
        acc[...] = jnp.zeros_like(acc)
        for h in range(HEADS):
            grads = g_ref[:, h * HEAD : (h + 1) * HEAD].astype(jnp.float32).T
            term[h] = jnp.sum(grads * mixed_ref[h], axis=0, keepdims=True)

    @pl.when(block >= first_block)
    def _():
        bias[...] = visible_bias((rows, rows), block * rows, start_ref[...], me * rows)

        @pl.loop(0, HEADS, unroll=2)
        def _(h):
            early, late, at = lanes(2 * h * HEAD), lanes((2 * h + 1) * HEAD), lanes(h * HEAD)
            keys, values = kv_ref[0, :, early], kv_ref[0, :, late]
            queries, grads = q_ref[:, at], g_ref[:, at]
            probs = jnp.exp(inner_right(keys, queries) + bias[...] - total_ref[h])
            prob_grad = inner_right(values, grads)
            score_grad = (probs * (prob_grad - term[h])).astype(jnp.bfloat16)
            dkv_ref[0, :, late] = jnp.dot(
                probs.astype(jnp.bfloat16), grads, preferred_element_type=jnp.float32
            ).astype(jnp.bfloat16)
            dkv_ref[0, :, early] = jnp.dot(
                score_grad, queries, preferred_element_type=jnp.float32
            ).astype(jnp.bfloat16)
            acc[h] += inner_left(keys, score_grad)

    @pl.when(jnp.logical_and(block >= 0, block < first_block))
    def _():
        dkv_ref[...] = jnp.zeros_like(dkv_ref)

    @pl.when(step == pl.num_programs(0) - 1)
    def _():
        for h in range(HEADS):
            back = turned(acc[h].T * HEAD ** (-0.5), cos_ref[...], -sin_ref[...])
            dq_ref[:, h * HEAD : (h + 1) * HEAD] = back.astype(jnp.bfloat16)


def attend_back(info, queries, grads, mixed, start, total, cosine, sine, pairs):
    rows, width = queries.shape
    count = pairs.shape[0]
    steps = count // 2 + 1
    return pl.pallas_call(
        attend_back_kernel,
        out_shape=(
            jax.ShapeDtypeStruct(pairs.shape, jnp.bfloat16),
            jax.ShapeDtypeStruct((rows, width), jnp.bfloat16),
        ),
        grid_spec=pltpu.PrefetchScalarGridSpec(
            num_scalar_prefetch=1,
            grid=(steps,),
            in_specs=[
                whole_spec(rows, width),
                whole_spec(rows, width),
                whole_spec(HEADS, HEAD, rows),
                whole_spec(1, rows),
                whole_spec(HEADS, 1, rows),
                whole_spec(rows, HEAD),
                whole_spec(rows, HEAD),
                pl.BlockSpec((1, rows, 2 * width), lambda s, info: (jnp.maximum(info[0] - s, info[1]), 0, 0)),
            ],
            out_specs=(
                pl.BlockSpec((1, rows, 2 * width), lambda s, info: (jnp.maximum(info[0] - s, 0), 0, 0)),
                whole_spec(rows, width),
            ),
            scratch_shapes=[
                pltpu.VMEM((rows, rows), jnp.float32),
                pltpu.VMEM((HEADS, HEAD, rows), jnp.float32),
                pltpu.VMEM((HEADS, 1, rows), jnp.float32),
            ],
        ),
        cost_estimate=pl.CostEstimate(
            flops=10 * rows * rows * width * steps, bytes_accessed=8 * rows * width * steps, transcendentals=0
        ),
        name="attend_back",
    )(info, queries, grads, mixed, start, total, cosine, sine, pairs)


def finish_kernel(
    x_ref, gain_ref, res_ref, hid_ref, q_ref, kv_ref, cos_ref, sin_ref, wq_ref, wk_ref, wv_ref,
    dq_ref, dk_ref, dv_ref, out_ref, gain_out, acc,
):
    step = pl.program_id(0)

    @pl.when(step == 0)
    def _():
        acc[...] = jnp.zeros_like(acc)

    cosine, sine = cos_ref[...], sin_ref[...]
    count = q_ref.shape[1] // HEAD
    keys = jnp.concatenate(
        [turned(kv_ref[:, 2 * h * HEAD : (2 * h + 1) * HEAD].astype(jnp.float32), cosine, -sine).astype(jnp.bfloat16)
         for h in range(count)], axis=1)
    values = jnp.concatenate([kv_ref[:, (2 * h + 1) * HEAD : (2 * h + 2) * HEAD] for h in range(count)], axis=1)
    grads = (q_ref[...], keys, values)
    acc[...] += (
        inner_right(grads[0], wq_ref[...]) + inner_right(grads[1], wk_ref[...]) + inner_right(grads[2], wv_ref[...])
    )
    hidden = hid_ref[...]
    for ref, grad in zip((dq_ref, dk_ref, dv_ref), grads):
        ref[...] = inner_left(hidden, grad).astype(jnp.bfloat16)

    @pl.when(step == pl.num_programs(0) - 1)
    def _():
        values, gain, grad = x_ref[...].astype(jnp.float32), gain_ref[...], acc[...]
        scale = lax.rsqrt(jnp.mean(values * values, axis=1, keepdims=True) + epsilon)
        inner = jnp.mean(gain * grad * values, axis=1, keepdims=True)
        part = scale * gain * grad - values * (scale * scale * scale) * inner
        out_ref[...] = (res_ref[...] + part).astype(jnp.bfloat16)
        gain_out[...] = jnp.sum(grad * values * scale, axis=0, keepdims=True)


def finish(tokens, gain, residual_grad, hidden, query_grad, pair_grads, cosine, sine, wq, wk, wv):
    rows, width = tokens.shape
    tile = 2 * HEAD
    column = pl.BlockSpec((width, tile), lambda i: (0, i))
    return pl.pallas_call(
        finish_kernel,
        out_shape=(
            jax.ShapeDtypeStruct((width, width), jnp.bfloat16),
            jax.ShapeDtypeStruct((width, width), jnp.bfloat16),
            jax.ShapeDtypeStruct((width, width), jnp.bfloat16),
            jax.ShapeDtypeStruct((rows, width), jnp.bfloat16),
            jax.ShapeDtypeStruct((1, width), jnp.float32),
        ),
        grid=(width // tile,),
        in_specs=[whole_spec(rows, width), whole_spec(1, width), whole_spec(rows, width), whole_spec(rows, width),
                  pl.BlockSpec((rows, tile), lambda i: (0, i)), pl.BlockSpec((rows, 2 * tile), lambda i: (0, i)),
                  whole_spec(rows, HEAD), whole_spec(rows, HEAD), column, column, column],
        out_specs=(column, column, column, whole_spec(rows, width), whole_spec(1, width)),
        scratch_shapes=[pltpu.VMEM((rows, width), jnp.float32)],
        cost_estimate=pl.CostEstimate(flops=12 * rows * width * width, bytes_accessed=12 * width * width, transcendentals=0),
        name="finish",
    )(tokens, gain[None, :], residual_grad, hidden, query_grad, pair_grads, cosine, sine, wq, wk, wv)


def experts_kernel(
    where_ref, x_ref, g_ref, rank_row, rank_col, share_row, wg_ref, wu_ref, wd_ref,
    back_ref, routed_ref, in_ref, pre_ref, lift_ref, mid_ref, og_ref, grads,
):
    blocks, rows, side = x_ref.shape
    capacity = in_ref.shape[0] // blocks
    width = og_ref.shape[1]
    dot = lambda left, right: jnp.dot(left, right, preferred_element_type=jnp.float32)
    shares = []
    for i in range(blocks):
        at = slice(i * capacity, (i + 1) * capacity)
        hit = rank_row[i] == lax.broadcasted_iota(jnp.int32, (capacity, rows), 0)
        pick = jnp.where(hit, 1.0, 0.0)
        shares.append(jnp.sum(pick * share_row[i], axis=1, keepdims=True))
        pick = pick.astype(jnp.bfloat16)
        in_ref[at, :] = dot(pick, x_ref[i, :, :width]).astype(jnp.bfloat16)
        grads[at, :] = dot(pick, g_ref[i]).astype(jnp.bfloat16)
    share = jnp.concatenate(shares, axis=0)
    pre = dot(in_ref[...], wg_ref[0])
    lift = dot(in_ref[...], wu_ref[0])
    silu, slope = silu_parts(pre)
    mid_ref[...] = (silu * lift).astype(jnp.bfloat16)
    lift_slope = lift * slope
    result = dot(mid_ref[...], wd_ref[0]).astype(jnp.bfloat16).astype(jnp.float32)
    grad = grads[...].astype(jnp.float32)
    gate_grad = jnp.sum(result * grad, axis=1, keepdims=True)
    og_ref[...] = (share * grad).astype(jnp.bfloat16)
    given = (share * result).astype(jnp.bfloat16)
    mid_grad = inner_right(og_ref[...], wd_ref[0])
    pre_ref[...] = (mid_grad * lift_slope).astype(jnp.bfloat16)
    lift_ref[...] = (mid_grad * silu).astype(jnp.bfloat16)
    in_grad = (inner_right(pre_ref[...], wg_ref[0]) + inner_right(lift_ref[...], wu_ref[0])).astype(jnp.bfloat16)
    lane = lax.broadcasted_iota(jnp.int32, (blocks * capacity, side - width), 1)
    high = gate_grad.astype(jnp.bfloat16).astype(jnp.float32)
    extra = jnp.where(lane == where_ref[0], high, jnp.where(lane == where_ref[1], gate_grad - high, 0.0))
    extra = extra.astype(jnp.bfloat16)
    for i in range(blocks):
        at = slice(i * capacity, (i + 1) * capacity)
        hit = rank_col[i] == lax.broadcasted_iota(jnp.int32, (rows, capacity), 1)
        put = jnp.where(hit, 1.0, 0.0).astype(jnp.bfloat16)
        back_ref[i, :, :width] = dot(put, in_grad[at, :]).astype(jnp.bfloat16)
        back_ref[i, :, width:] = dot(put, extra[at, :]).astype(jnp.bfloat16)
        routed_ref[i] = dot(put, given[at, :]).astype(jnp.bfloat16)


def run_experts(places, arrived, grads, rank, share, gate, up, down, capacity):
    count, rows, side = arrived.shape
    width, ff = gate.shape[1], gate.shape[2]
    blocks = 384 // capacity
    flat = count * capacity
    once = lambda *shape: pl.BlockSpec(shape, lambda i, p: (0,) * len(shape), pipeline_mode=pl.Buffered(1))
    lead = lambda *shape: pl.BlockSpec((blocks,) + shape, lambda i, p: (i, 0, 0))
    tall = lambda wide: pl.BlockSpec((blocks * capacity, wide), lambda i, p: (i, 0))
    shape = lambda *dims: jax.ShapeDtypeStruct(dims, jnp.bfloat16)
    return pl.pallas_call(
        experts_kernel,
        out_shape=(shape(count, rows, side), shape(count, rows, width), shape(flat, width), shape(flat, ff),
                   shape(flat, ff), shape(flat, ff), shape(flat, width)),
        grid_spec=pltpu.PrefetchScalarGridSpec(
            num_scalar_prefetch=1,
            grid=(count // blocks,),
            in_specs=[lead(rows, side), lead(rows, width), lead(1, rows), lead(rows, 1), lead(1, rows),
                      once(1, width, ff), once(1, width, ff), once(1, ff, width)],
            out_specs=(lead(rows, side), lead(rows, width), tall(width), tall(ff), tall(ff), tall(ff), tall(width)),
            scratch_shapes=[pltpu.VMEM((blocks * capacity, width), jnp.bfloat16)],
        ),
        compiler_params=pltpu.CompilerParams(vmem_limit_bytes=VMEM_MOST),
        cost_estimate=pl.CostEstimate(flops=16 * flat * width * ff, bytes_accessed=16 * flat * width, transcendentals=0),
        name="run_experts",
    )(places, arrived, grads, rank[:, None, :], rank[:, :, None], share[:, None, :], gate, up, down)


def local(
    tokens,
    doc_lengths,
    expert_ids,
    out_grad,
    mixer_gain,
    query_weight,
    key_weight,
    value_weight,
    output_weight,
    ffn_gain,
    router_weight,
    shared_gate,
    shared_up,
    shared_down,
    expert_gate,
    expert_up,
    expert_down,
):
    rows, width = tokens.shape[1], tokens.shape[2]
    ep_count = lax.axis_size("ep")
    device_count = ep_count * lax.axis_size("grp")
    ep_index = lax.axis_index("ep")
    expert_count = router_weight.shape[1]
    capacity = min(rows, 12 * rows * TOP // (7 * expert_count))
    low = lambda v: v.astype(jnp.bfloat16)
    wide = lambda v: v.astype(jnp.float32)
    dot = lambda left, right: jnp.dot(left, right, preferred_element_type=jnp.float32)

    grad_low = out_grad[0]

    doc_ends = jnp.cumsum(doc_lengths[0])
    query_pos = ep_index * rows + jnp.arange(rows, dtype=jnp.int32)
    before = query_pos[:, None] >= doc_ends[None, :]
    start = jnp.max(jnp.where(before, doc_ends[None, :], 0), axis=1)
    info = jnp.stack([ep_index, start[0] // rows]).astype(jnp.int32)
    half_dim = HEAD // 2
    frequency = rope_base ** (-jnp.arange(half_dim, dtype=jnp.float32) / half_dim)
    angles = wide(query_pos)[:, None] * frequency[None, :]
    cosine, sine = jnp.cos(angles), jnp.sin(angles)
    cosine = jnp.concatenate([cosine, cosine], axis=1)
    sine = jnp.concatenate([-sine, sine], axis=1)

    stream = wide(tokens[0])
    hidden_low, queries, own_pairs = project(
        tokens[0], mixer_gain, cosine, sine, query_weight, key_weight, value_weight
    )
    pairs = gather_rows(own_pairs, True, 1, 8)
    grad_later, pairs = lax.optimization_barrier((grad_low, pairs))
    grads_all = lax.all_gather(grad_later, "ep", axis=0, tiled=False)
    mixed, mixed_low, log_total = attend(info, queries, start[None, :], pairs)
    mixer_out = dot(mixed_low, output_weight)
    residual = stream + mixer_out
    ffn_low = low(normed(residual, ffn_gain))

    logits = dot(ffn_low, router_weight)
    experts = jnp.arange(expert_count, dtype=jnp.int32)
    assigned = jnp.any(expert_ids[0][:, :, None] == experts[None, None, :], axis=1)
    shown = jnp.where(assigned, logits, masked_value)
    powers = jnp.where(assigned, jnp.exp(shown - jnp.max(shown, axis=1, keepdims=True)), 0.0)
    gate_probs = powers / jnp.sum(powers, axis=1, keepdims=True)
    probs_high = low(gate_probs)
    probs_rest = low(gate_probs - wide(probs_high))
    side = width + 2 * HEAD if 2 * expert_count > HEAD else width + HEAD
    pad = jnp.zeros((rows, side - width - 2 * expert_count), jnp.bfloat16)
    sent = jnp.concatenate([ffn_low, probs_high, probs_rest, pad], axis=1)
    arrived = gather_rows(sent, False, 2)

    own = experts[None, None, :] == ep_index
    high = arrived[:, :, width : width + expert_count]
    rest = arrived[:, :, width + expert_count : width + 2 * expert_count]
    share = jnp.sum(jnp.where(own, wide(high) + wide(rest), 0.0), axis=2)
    chosen = share > 0.0
    earlier = (jnp.arange(rows)[:, None] < jnp.arange(rows)[None, :]).astype(jnp.bfloat16)
    rank = dot(low(chosen), earlier).astype(jnp.int32)
    rank = jnp.where(chosen, rank, -1)
    places = jnp.stack([ep_index, expert_count + ep_index]).astype(jnp.int32)
    back, given, flat_in, pre_grad, lift_grad, middle, result_grad = run_experts(
        places, arrived, grads_all, rank, share, expert_gate, expert_up, expert_down, capacity
    )
    back_sum = scatter_rows(back, False, 3)
    given, back_sum = lax.optimization_barrier((given, back_sum))
    routed = wide(lax.psum_scatter(given, "ep", scatter_dimension=0))
    group_count = lax.axis_size("grp")
    split = width // group_count
    own_down_grad = jnp.concatenate(
        [low(inner_left(middle, result_grad[:, i * split : (i + 1) * split])) for i in range(group_count)], axis=0
    )
    own_gate_grad = low(inner_left(flat_in, pre_grad))
    own_up_grad = low(inner_left(flat_in, lift_grad))
    over_groups = lambda v: wide(lax.psum_scatter(v, "grp", scatter_dimension=0, tiled=True))[None]
    gate_sum = over_groups(own_gate_grad)
    up_sum = over_groups(own_up_grad)
    down_sum = over_groups(own_down_grad)

    shared_pre = dot(ffn_low, shared_gate)
    shared_lift = dot(ffn_low, shared_up)
    shared_silu, shared_slope = silu_parts(shared_pre)
    shared_mid = low(shared_silu * shared_lift)
    shared_out = dot(shared_mid, shared_down)
    grad_out = wide(grad_low)
    shared_mid_grad = inner_right(grad_low, shared_down)
    shared_pre_grad = low(shared_mid_grad * shared_lift * shared_slope)
    shared_lift_grad = low(shared_mid_grad * shared_silu)
    ffn_grad = inner_right(shared_pre_grad, shared_gate) + inner_right(shared_lift_grad, shared_up)

    layer_out = residual + shared_out + routed
    gate_back = wide(back_sum[:, width : width + expert_count]) + wide(
        back_sum[:, width + expert_count : width + 2 * expert_count]
    )
    chosen_grad = gate_probs * (gate_back - jnp.sum(gate_probs * gate_back, axis=1, keepdims=True))
    logit_grad = low(chosen_grad)
    ffn_grad = ffn_grad + wide(back_sum[:, :width]) + inner_right(logit_grad, router_weight)
    _, ffn_pull = jax.vjp(normed, residual, ffn_gain)
    residual_part, ffn_gain_grad = ffn_pull(ffn_grad)
    residual_grad = grad_out + residual_part
    mixer_grad_low = low(residual_grad)
    mixed_grad = low(inner_right(mixer_grad_low, output_weight))
    pair_parts, query_lin_grad = attend_back(
        info, queries, mixed_grad, mixed, start[None, :], log_total, cosine, sine, pairs
    )
    by_device = lambda v: low(v).reshape(device_count, width // device_count, -1)
    early = [
        by_device(part)
        for part in (inner_left(ffn_low, shared_pre_grad), inner_left(ffn_low, shared_lift_grad),
                     inner_left(grad_low, shared_mid), inner_left(mixed_low, mixer_grad_low))
    ]
    if ep_count > 16:
        pair_grads = scatter_rows(pair_parts, True, 4)
        early_sum = scatter_whole(early, 5)
    else:
        early_sum, pair_grads = scatter_whole(early, 5, pair_parts)

    query_part, key_part, value_part, tokens_grad, mixer_gain_grad = finish(
        tokens[0], mixer_gain, residual_grad, hidden_low, query_lin_grad, pair_grads, cosine, sine,
        query_weight, key_weight, value_weight,
    )
    squares = jnp.stack(
        [jnp.sum(residual * residual), jnp.sum(mixer_out * mixer_out), jnp.sum(layer_out * layer_out)]
    )
    extras = jnp.concatenate(
        [inner_left(ffn_low, logit_grad), mixer_gain_grad.T, ffn_gain_grad[:, None],
         jnp.broadcast_to(squares[None, :], (width, 3))], axis=1
    )
    extras = jnp.pad(extras, ((0, 0), (0, HEAD - extras.shape[1])))
    late_sum = scatter_whole([by_device(v) for v in (query_part, key_part, value_part, extras)], 6)
    extra_sum = late_sum[:, 3 * width :]
    entry_count = rows * device_count * width
    stream_rms = jnp.sqrt(extra_sum[0, expert_count + 2 : expert_count + 5] / entry_count)
    ff = shared_gate.shape[1]
    return (
        low(layer_out)[None],
        tokens_grad[None],
        extra_sum[:, expert_count],
        late_sum[:, :width],
        late_sum[:, width : 2 * width],
        late_sum[:, 2 * width : 3 * width],
        early_sum[:, 3 * ff :],
        extra_sum[:, expert_count + 1],
        extra_sum[:, :expert_count],
        early_sum[:, :ff],
        early_sum[:, ff : 2 * ff],
        early_sum[:, 2 * ff : 3 * ff].T,
        gate_sum,
        up_sum,
        down_sum,
        stream_rms,
    )


def solution(mesh):
    return jax.shard_map(
        local,
        mesh=mesh,
        in_specs=(
            P("grp", "ep", None),
            P("grp", None),
            P("grp", "ep", None),
            P("grp", "ep", None),
            P(),
            P(),
            P(),
            P(),
            P(),
            P(),
            P(),
            P(),
            P(),
            P(),
            P("ep", None, None),
            P("ep", None, None),
            P("ep", None, None),
        ),
        out_specs=(
            P("grp", "ep", None),
            P("grp", "ep", None),
            P(("grp", "ep")),
            P(("grp", "ep"), None),
            P(("grp", "ep"), None),
            P(("grp", "ep"), None),
            P(("grp", "ep"), None),
            P(("grp", "ep")),
            P(("grp", "ep"), None),
            P(("grp", "ep"), None),
            P(("grp", "ep"), None),
            P(None, ("grp", "ep")),
            P("ep", "grp", None),
            P("ep", "grp", None),
            P("ep", None, "grp"),
            P(),
        ),
        check_vma=False,
    )
```

```python
import functools

import jax
import jax.numpy as jnp
from jax import lax
from jax.experimental import pallas as pl
from jax.experimental.pallas import tpu as pltpu
from jax.sharding import PartitionSpec as P

HEADS = 10
HEAD = 128
TOP = 7

epsilon = 1e-06
rope_base = 10000.0
masked_value = -1e30


def normed(values, gain_vec):
    return (
        values * lax.rsqrt(jnp.mean(values * values, axis=-1, keepdims=True) + epsilon) * gain_vec
    )


def inner_left(left_op, right_op):
    return lax.dot_general(
        left_op, right_op, (((0,), (0,)), ((), ())), preferred_element_type=jnp.float32
    )


def inner_right(left_op, right_op):
    return lax.dot_general(
        left_op, right_op, (((1,), (1,)), ((), ())), preferred_element_type=jnp.float32
    )


def silu_parts(pre_act):
    sigmoid_val = jax.nn.sigmoid(pre_act)
    return (pre_act * sigmoid_val, sigmoid_val * (1.0 + pre_act * (1.0 - sigmoid_val)))


MESH = pl.DeviceIdType.MESH
VMEM_MOST = 64 * 1024 * 1024 - 65536


def when(cond):
    if cond is True:
        return lambda f: f()
    if cond is False:
        return lambda f: None
    return pl.when(cond)


def both(*conds):
    out = True
    for cond in conds:
        if cond is False:
            return False
        if cond is True:
            continue
        out = cond if out is True else jnp.logical_and(out, cond)
    return out


class Plan:
    def __init__(self, ep_count, window):
        self.long = 4
        self.wide = ep_count // 8
        self.window = window
        self.steps = (
            list(range(self.long // 2 + 1))
            if window
            else list(range(-(self.long - 1), self.long))
        )

    def place(self):
        me = lax.axis_index("ep")
        return me // (2 * self.wide), (me // 2) % self.wide, me % 2

    def slot(self, a, b, c):
        return (a * self.wide + b) * 2 + c

    def plane(self, a, d):
        return d if self.window else jnp.clip(a - d, 0, self.long - 1)

    def planes(self):
        return len(self.steps) if self.window else self.long

    def inside(self, a):
        return jnp.logical_and(a >= 0, a < self.long)

    def need(self, d, b, c, b0, c0):
        if not self.window or 0 < d < self.long // 2:
            return True
        if d == 0:
            return jnp.logical_or(b0 < b, jnp.logical_and(b0 == b, c0 <= c))
        return jnp.logical_or(b0 > b, jnp.logical_and(b0 == b, c0 >= c))

    def need_pair(self, d, b, b0):
        if not self.window or 0 < d < self.long // 2:
            return True
        return b0 < b if d == 0 else b0 > b

    def greet(self, a, b, c):
        barrier = pltpu.get_barrier_semaphore()

        def signal(cond, dev):
            @when(cond)
            def _():
                pl.semaphore_signal(barrier, inc=1, device_id={"ep": dev}, device_id_type=MESH)

        signal(a + 1 < self.long, self.slot(a + 1, b, c))
        signal(a > 0, self.slot(a - 1, b, c))
        for k in range(1, self.wide):
            signal(True, self.slot(a, (b + k) % self.wide, c))
        signal(True, self.slot(a, b, 1 - c))
        ends = (a == 0).astype(jnp.int32) + (a == self.long - 1).astype(jnp.int32)
        pl.semaphore_wait(barrier, self.wide + 2 - ends)


def gather_kernel(plan, pieces, x_ref, out_ref, ra, sa_up, sa_dn, rb, sb, rc, sc, own):
    a, b, c = plan.place()
    steps, wide = plan.steps, plan.wide
    at = {d: i for i, d in enumerate(steps)}
    rows = x_ref.shape[0] // pieces

    def part(q):
        return pl.ds(pl.multiple_of(q * rows, rows), rows)

    def copy(q, src, slot, ssem, rsem, dev):
        return pltpu.make_async_remote_copy(
            src_ref=src, dst_ref=out_ref.at[slot, part(q)], send_sem=ssem, recv_sem=rsem,
            device_id={"ep": dev}, device_id_type=MESH,
        )

    def hops(d, q):
        i = at[d]
        slot = plan.slot(a - d, b, c)
        src = x_ref.at[part(q)] if d == 0 else out_ref.at[slot, part(q)]
        real = plan.inside(a - d)
        out = []
        if d >= 0 and d + 1 in at:
            out.append((both(real, a + 1 < plan.long), lambda: copy(
                q, src, slot, sa_up.at[i, q], ra.at[at[d + 1], q], plan.slot(a + 1, b, c))))
        if d <= 0 and d - 1 in at:
            out.append((both(real, a > 0), lambda: copy(
                q, src, slot, sa_dn.at[i, q], ra.at[at[d - 1], q], plan.slot(a - 1, b, c))))
        for k in range(1, wide):
            to = (b + k) % wide
            out.append((both(real, plan.need_pair(d, to, b)), lambda k=k, to=to: copy(
                q, src, slot, sb.at[i, k, q], rb.at[i, k, q], plan.slot(a, to, c))))
        out.append((both(real, plan.need(d, b, 1 - c, b, c)), lambda: copy(
            q, src, slot, sc.at[i, 0, q], rc.at[i, 0, q], plan.slot(a, b, 1 - c))))
        return out

    def cross(d, k, q):
        i = at[d]
        b0 = (b + wide - k) % wide
        slot = plan.slot(a - d, b0, c)
        real = plan.inside(a - d)
        come = lambda: copy(q, x_ref.at[part(q)], slot, sb.at[i, k, q], rb.at[i, k, q], plan.slot(a, b, c))
        go = lambda: copy(q, out_ref.at[slot, part(q)], slot, sc.at[i, k, q], rc.at[i, k, q],
                          plan.slot(a, b, 1 - c))
        return (both(real, plan.need_pair(d, b, b0)), come,
                both(real, plan.need(d, b, 1 - c, b0, c)), go)

    plan.greet(a, b, c)
    keep = pltpu.make_async_copy(x_ref, out_ref.at[plan.slot(a, b, c)], own)

    @pl.loop(0, pieces)
    def _(q):
        for cond, go in hops(0, q):
            @when(cond)
            def _(go=go):
                go().start()

    keep.start()
    far = max(abs(d) for d in steps)
    for step in range(1, far + 3):
        @pl.loop(0, pieces)
        def _(q, step=step):
            for d in (step, -step):
                if d in at:
                    @when(plan.inside(a - d))
                    def _(d=d):
                        slot = plan.slot(a - d, b, c)
                        copy(q, x_ref.at[part(q)], slot, sa_up.at[0, q], ra.at[at[d], q],
                             plan.slot(a, b, c)).wait_recv()
                        for cond, go in hops(d, q):
                            @when(cond)
                            def _(go=go):
                                go().start()
            for d in sorted({step - 2, 2 - step}) if step > 1 else ():
                if d in at:
                    for k in range(1, wide):
                        came, come, goes, go = cross(d, k, q)
                        @when(came)
                        def _(come=come):
                            come().wait_recv()
                        @when(goes)
                        def _(go=go):
                            go().start()
    keep.wait()

    @pl.loop(0, pieces)
    def _(q):
        for d in steps:
            i = at[d]
            real = plan.inside(a - d)
            for k in range(wide):
                b0 = (b + wide - k) % wide
                slot = plan.slot(a - d, b0, 1 - c)
                @when(both(real, plan.need(d, b, c, b0, 1 - c)))
                def _(slot=slot, i=i, k=k):
                    copy(q, x_ref.at[part(q)], slot, sc.at[i, k, q], rc.at[i, k, q],
                         plan.slot(a, b, c)).wait_recv()
            for cond, go in hops(d, q):
                @when(cond)
                def _(go=go):
                    go().wait_send()
            for k in range(1, wide):
                came, come, goes, go = cross(d, k, q)
                @when(goes)
                def _(go=go):
                    go().wait_send()


def gather_rows(block, window, collective_id, pieces=4):
    ep_count = lax.axis_size("ep")
    plan = Plan(ep_count, window)
    n, wide = len(plan.steps), plan.wide
    sem = pltpu.SemaphoreType.DMA
    return pl.pallas_call(
        functools.partial(gather_kernel, plan, pieces),
        out_shape=jax.ShapeDtypeStruct((ep_count,) + block.shape, block.dtype),
        in_specs=[pl.BlockSpec(memory_space=pltpu.VMEM)],
        out_specs=pl.BlockSpec(memory_space=pl.ANY),
        scratch_shapes=[sem((n, pieces)), sem((n, pieces)), sem((n, pieces)), sem((n, wide, pieces)),
                        sem((n, wide, pieces)), sem((n, wide, pieces)), sem((n, wide, pieces)), sem],
        compiler_params=pltpu.CompilerParams(collective_id=collective_id, has_side_effects=True),
        name="gather_rows",
    )(block)


def add_rows(dst, others, out=None):
    rows, width = dst.shape
    out = dst if out is None else out
    small = rows <= 64
    piece = 32 if rows % 32 == 0 else rows
    lanes = width if rows % 32 == 0 else 4 * HEAD
    whole = width // lanes * lanes

    def add(at):
        if len(others) == 1 and out.dtype == jnp.bfloat16:
            out[at] = dst[at] + others[0][at]
        else:
            total = dst[at].astype(jnp.float32)
            for other in others:
                total = total + other[at].astype(jnp.float32)
            out[at] = total.astype(out.dtype)

    if piece == rows:
        @pl.loop(0, whole // lanes)
        def _(i):
            add((slice(None), pl.ds(pl.multiple_of(i * lanes, lanes), lanes)))

        if whole < width:
            add((slice(None), pl.ds(whole, width - whole)))
    else:
        @pl.loop(0, rows // piece)
        def _(i):
            add((pl.ds(pl.multiple_of(i * piece, piece), piece), slice(None)))


def send(src, dst, ssem, rsem, to):
    return pltpu.make_async_remote_copy(
        src_ref=src, dst_ref=dst, send_sem=ssem, recv_sem=rsem, device_id=to, device_id_type=MESH
    )


def run_if(cond, go):
    @when(cond)
    def _():
        go()


class RowSum:
    @staticmethod
    def scratch(plan, rows, width, dtype, pieces):
        n, wide = plan.planes(), plan.wide
        blocks = lambda *lead: pltpu.VMEM(lead + (rows, width), dtype)
        sem = lambda *lead: pltpu.SemaphoreType.DMA(lead + (pieces,))
        return [blocks(n, wide), blocks(n, wide), blocks(n, wide - 1), blocks(n), blocks(n),
                sem(n, wide), sem(n, wide), sem(n, wide), sem(n, wide), sem(n), sem(n), sem(n), sem(n, wide)]

    def __init__(self, plan, pieces, p_ref, scratch):
        self.plan, self.pieces, self.p_ref = plan, pieces, p_ref
        (self.held, self.rcb, self.rbb, self.r_hi, self.r_lo,
         self.sc, self.rc, self.sb, self.rb, self.sa, self.rhi, self.rlo, self.ld) = scratch
        self.a, self.b, self.c = plan.place()
        self.rows = p_ref.shape[1] // pieces
        self.order = sorted(plan.steps, key=lambda d: -abs(d))

    def part(self, q):
        return pl.ds(pl.multiple_of(q * self.rows, self.rows), self.rows)

    def dev(self, a, b, c):
        return {"ep": self.plan.slot(a, b, c)}

    def source(self, k):
        return (self.b + self.plan.wide - k) % self.plan.wide

    def load(self, d, k, q):
        p, i, b0 = self.plan, self.plan.plane(self.a, d), self.source(k)
        return both(p.inside(self.a - d), p.need(d, self.b, self.c, b0, self.c)), lambda: pltpu.make_async_copy(
            self.p_ref.at[p.slot(self.a - d, b0, self.c), self.part(q)], self.held.at[i, k, self.part(q)],
            self.ld.at[i, k, q])

    def cross(self, d, k, q):
        p, i, b0, c = self.plan, self.plan.plane(self.a, d), self.source(k), self.c
        real = p.inside(self.a - d)
        return (both(real, p.need(d, self.b, c, b0, 1 - c)), lambda: send(
            self.p_ref.at[p.slot(self.a - d, b0, 1 - c), self.part(q)], self.rcb.at[i, k, self.part(q)],
            self.sc.at[i, k, q], self.rc.at[i, k, q], self.dev(self.a, self.b, 1 - c)),
            both(real, p.need(d, self.b, 1 - c, b0, c)))

    def over(self, d, k, q):
        p, i, b0 = self.plan, self.plan.plane(self.a, d), self.source(k)
        return both(p.inside(self.a - d), p.need_pair(d, self.b, b0)), lambda: send(
            self.held.at[i, k, self.part(q)], self.rbb.at[i, k - 1, self.part(q)], self.sb.at[i, k, q],
            self.rb.at[i, k, q], self.dev(self.a, b0, self.c))

    def along(self, d, q):
        p, i, up = self.plan, self.plan.plane(self.a, d), d < 0
        j = d - 1 if p.window else i
        return p.inside(self.a - d), lambda: send(
            self.held.at[i, 0, self.part(q)], (self.r_lo if up else self.r_hi).at[j, self.part(q)],
            self.sa.at[i, q], (self.rlo if up else self.rhi).at[j, q],
            self.dev(self.a + (1 if up else -1), self.b, self.c))

    def start(self, ks):
        for k in ks:
            @pl.loop(0, self.pieces)
            def _(q, k=k):
                for d in self.order:
                    for cond, go in (self.cross(d, k, q)[:2], self.load(d, k, q)):
                        run_if(cond, lambda go=go: go().start())

    def first(self, d, k, q):
        i = self.plan.plane(self.a, d)
        cond, go = self.load(d, k, q)
        run_if(cond, lambda: go().wait())
        _, come_go, come = self.cross(d, k, q)

        def take():
            come_go().wait_recv()
            add_rows(self.held.at[i, k, self.part(q)], [self.rcb.at[i, k, self.part(q)]])

        run_if(come, take)

    def stage_over(self, k):
        @pl.loop(0, self.pieces)
        def _(q):
            for d in self.order:
                self.first(d, k, q)
                cond, go = self.over(d, k, q)
                run_if(cond, lambda go=go: go().start())

    def stage_dests(self, low, high):
        @pl.loop(low, high)
        def _(q):
            for d in self.order:
                self.dest(d, q)

    def dest(self, d, q):
        p, a, b, steps = self.plan, self.a, self.b, self.plan.steps
        i = p.plane(a, d)
        real = p.inside(a - d)
        mine = self.held.at[i, 0, self.part(q)]
        self.first(d, 0, q)
        for k in range(1, p.wide):
            def take(k=k):
                self.over(d, k, q)[1]().wait_recv()
                add_rows(mine, [self.rbb.at[i, k - 1, self.part(q)]])

            run_if(both(real, p.need_pair(d, (b + k) % p.wide, b)), take)
        for inner, cond, buf, sem in ((d >= 0 and d + 1 in steps, a + 1 < p.long, self.r_hi, self.rhi),
                                      (d <= 0 and d - 1 in steps, a > 0, self.r_lo, self.rlo)):
            if inner:
                def take(buf=buf, sem=sem):
                    send(mine, buf.at[i, self.part(q)], self.sa.at[i, q], sem.at[i, q],
                         self.dev(a, b, self.c)).wait_recv()
                    add_rows(mine, [buf.at[i, self.part(q)]])

                run_if(both(real, cond), take)
        if d:
            cond, go = self.along(d, q)
            run_if(cond, lambda: go().start())

    def result(self):
        return self.held[self.plan.plane(self.a, 0), 0]

    def drain(self):
        @pl.loop(0, self.pieces)
        def _(q):
            for d in self.plan.steps:
                sends = [self.cross(d, k, q)[:2] for k in range(self.plan.wide)]
                sends += [self.over(d, k, q) for k in range(1, self.plan.wide)]
                if d:
                    sends.append(self.along(d, q))
                for cond, go in sends:
                    run_if(cond, lambda go=go: go().wait_send())


def scatter_rows(parts, window, collective_id, pieces=4):
    ep_count, rows, width = parts.shape
    plan = Plan(ep_count, window)

    def kernel(p_ref, out_ref, *scratch):
        total = RowSum(plan, pieces, p_ref, scratch)
        plan.greet(total.a, total.b, total.c)
        ks = list(range(1, plan.wide)) + [0]
        total.start(ks)
        for k in ks[:-1]:
            total.stage_over(k)
        total.stage_dests(0, pieces)
        out_ref[...] = total.result()
        total.drain()

    return pl.pallas_call(
        kernel,
        out_shape=jax.ShapeDtypeStruct((rows, width), parts.dtype),
        in_specs=[pl.BlockSpec(memory_space=pl.ANY)],
        out_specs=pl.BlockSpec(memory_space=pltpu.VMEM),
        scratch_shapes=RowSum.scratch(plan, rows, width, parts.dtype, pieces),
        compiler_params=pltpu.CompilerParams(
            collective_id=collective_id, has_side_effects=True, vmem_limit_bytes=VMEM_MOST),
        name="scatter_rows",
    )(parts)


class Place:
    def __init__(self, groups, ep_count):
        self.sizes = {"x": groups, "a": 4, "b": ep_count // 8}

    def locate(self):
        me, wide = lax.axis_index("ep"), self.sizes["b"]
        self.at = {"x": lax.axis_index("grp"), "a": me // (2 * wide), "b": (me // 2) % wide, "c": me % 2}

    def dev(self, **moved):
        at = {**self.at, **moved}
        return {"grp": at["x"], "ep": (at["a"] * self.sizes["b"] + at["b"]) * 2 + at["c"]}

    def slot(self, **moved):
        at = {**self.at, **moved}
        return ((at["x"] * self.sizes["a"] + at["a"]) * self.sizes["b"] + at["b"]) * 2 + at["c"]

    def back(self, axis, k):
        return (self.at[axis] + self.sizes[axis] - k) % self.sizes[axis]

    def greet(self):
        peers = [self.dev(c=1 - self.at["c"])] + [
            self.dev(**{axis: self.back(axis, k)}) for axis in "xba" for k in range(1, self.sizes[axis])]
        barrier = pltpu.get_barrier_semaphore()
        for to in peers:
            pl.semaphore_signal(barrier, inc=1, device_id=to, device_id_type=MESH)
        pl.semaphore_wait(barrier, len(peers))


def from_far(size):
    return list(range(1, size)) + [0]


class WholeSum:
    @staticmethod
    def scratch(sizes, axes, rows, width, dtype, sources):
        n1, n2, n3 = (sizes[axis] for axis in axes)
        blocks = lambda *lead: pltpu.VMEM(lead + (rows, width), dtype)
        sem = lambda *lead: pltpu.SemaphoreType.DMA(lead)
        full = (n1, n2, n3)
        one, two, three = (n1 - 1, n2, n3), (n2 - 1, n3), (n3 - 1,)
        return [blocks(*full), blocks(*full), blocks(*one), blocks(*two), blocks(*three),
                sem(*full, sources), sem(*full, sources), sem(*full, sources), sem(*one), sem(*one), sem(*two), sem(*two), sem(*three), sem(*three)]

    def __init__(self, place, axes, pieces, scratch):
        self.place, self.axes, self.pieces = place, axes, pieces
        (self.held, self.rcb, self.r1, self.r2, self.r3,
         self.ld, self.sc, self.rc, self.s1, self.q1, self.s2, self.q2, self.s3, self.q3) = scratch
        self.n1, self.n2, self.n3 = (place.sizes[axis] for axis in axes)
        self.groups = [[(k1, k2, k3) for k2 in from_far(self.n2) for k3 in from_far(self.n3)]
                       for k1 in from_far(self.n1)]

    def slot(self, key, c):
        return self.place.slot(c=c, **{axis: self.place.back(axis, k) for axis, k in zip(self.axes, key)})

    def loads(self, key):
        c = self.place.at["c"]
        for n, (ref, first, at, count) in enumerate(self.pieces):
            frm, to = pl.ds(first, count), pl.ds(at, count)
            yield pltpu.make_async_copy(
                ref.at[self.slot(key, c), :, frm], self.held.at[key + (slice(None), to)],
                self.ld.at[key + (n,)])

    def crossings(self, key):
        c = self.place.at["c"]
        for n, (ref, first, at, count) in enumerate(self.pieces):
            frm, to = pl.ds(first, count), pl.ds(at, count)
            yield send(ref.at[self.slot(key, 1 - c), :, frm], self.rcb.at[key + (slice(None), to)],
                       self.sc.at[key + (n,)], self.rc.at[key + (n,)], self.place.dev(c=1 - c))

    def hop(self, level, key):
        buf, ssem, rsem = ((self.r1, self.s1, self.q1), (self.r2, self.s2, self.q2), (self.r3, self.s3, self.q3))[level]
        axis, k = self.axes[level], key[level]
        far = (k - 1,) + key[level + 1 :]
        return send(self.held.at[key], buf.at[far], ssem.at[far], rsem.at[far],
                    self.place.dev(**{axis: self.place.back(axis, k)}))

    def start(self, i):
        for key in self.groups[i]:
            for go in self.crossings(key):
                go.start()
            for go in self.loads(key):
                go.start()

    def stage_core(self, i):
        for key in self.groups[i]:
            for go in self.loads(key):
                go.wait()
            for go in self.crossings(key):
                go.wait_recv()
            add_rows(self.held.at[key], [self.rcb.at[key]])
            if key[0]:
                self.hop(0, key).start()

    def stage_one(self, k2):
        for k3 in from_far(self.n3):
            for k1 in range(1, self.n1):
                self.hop(0, (k1, k2, k3)).wait_recv()
            add_rows(self.held.at[0, k2, k3], [self.r1.at[k1 - 1, k2, k3] for k1 in range(1, self.n1)])
            if k2:
                self.hop(1, (0, k2, k3)).start()

    def stage_two(self):
        for k3 in from_far(self.n3):
            for k2 in range(1, self.n2):
                self.hop(1, (0, k2, k3)).wait_recv()
            add_rows(self.held.at[0, 0, k3], [self.r2.at[k2 - 1, k3] for k2 in range(1, self.n2)])
            if k3:
                self.hop(2, (0, 0, k3)).start()

    def stage_three(self, out):
        for k3 in range(1, self.n3):
            self.hop(2, (0, 0, k3)).wait_recv()
        add_rows(self.held.at[0, 0, 0], [self.r3.at[k3 - 1] for k3 in range(1, self.n3)], out)

    def drain(self):
        for group in self.groups:
            for key in group:
                for go in self.crossings(key):
                    go.wait_send()
                if key[0]:
                    self.hop(0, key).wait_send()
                elif key[1]:
                    self.hop(1, key).wait_send()
                elif key[2]:
                    self.hop(2, key).wait_send()


def scatter_whole(parts, collective_id, pairs=None):
    rows = parts[0].shape[1]
    width = sum(part.shape[2] for part in parts)
    groups, ep_count = lax.axis_size("grp"), lax.axis_size("ep")
    place = Place(groups, ep_count)
    tiles = width // HEAD
    cuts = [0, tiles // 2 * HEAD, width]
    orders = ["xba", "xba" if pairs is not None else "bxa"]

    def kernel(*refs):
        sources, refs = refs[: len(parts)], refs[len(parts) :]
        if pairs is not None:
            pair_ref, refs = refs[0], refs[1:]
        out_ref, refs = refs[0], refs[1:]
        if pairs is not None:
            pair_out, refs = refs[0], refs[1:]
        place.locate()
        sums = []
        for n, axes in enumerate(orders):
            low, high, first, pieces = cuts[n], cuts[n + 1], 0, []
            for ref in sources:
                begin, end = max(low, first), min(high, first + ref.shape[2])
                if begin < end:
                    pieces.append((ref, begin - first, begin - low, end - begin))
                first += ref.shape[2]
            sums.append(WholeSum(place, axes, pieces, refs[:14]))
            refs = refs[14:]
        outs = [out_ref.at[:, pl.ds(cuts[n], cuts[n + 1] - cuts[n])] for n in range(len(orders))]
        place.greet()
        if pairs is None:
            couples = [sums[n : n + 2] for n in range(0, len(sums), 2)]
            for couple in couples:
                for i in range(max(s.n1 for s in couple)):
                    for s in couple:
                        if i < s.n1:
                            s.start(i)

            def core(couple):
                for i in range(max(s.n1 for s in couple)):
                    for s in couple:
                        if i < s.n1:
                            s.stage_core(i)

            def one(couple):
                for i in range(max(s.n2 for s in couple)):
                    for s in couple:
                        if i < s.n2:
                            s.stage_one(from_far(s.n2)[i])

            def two(couple):
                for s in couple:
                    s.stage_two()

            for stage in (core, one, two):
                for couple in couples:
                    stage(couple)
            for s, out in zip(sums, outs):
                s.stage_three(out)
        else:
            total = RowSum(plan, 4, pair_ref, refs)
            ks = from_far(plan.wide)
            for one in sums:
                for i in range(one.n1 - 1):
                    one.start(i)
            total.start(ks[:-1])
            for one in sums:
                one.start(one.n1 - 1)
            total.start(ks[-1:])
            for one in sums:
                for i in range(one.n1 - 1):
                    one.stage_core(i)
            for k in ks[:-1]:
                total.stage_over(k)
            for one in sums:
                one.stage_core(one.n1 - 1)
            total.stage_dests(0, 2)
            for k2 in from_far(sums[0].n2):
                sums[0].stage_one(k2)
            total.stage_dests(2, 3)
            sums[0].stage_two()
            for one in sums[1:]:
                for k2 in from_far(one.n2):
                    one.stage_one(k2)
            total.stage_dests(3, 4)
            for one in sums[1:]:
                one.stage_two()
            pair_out[...] = total.result()
            for one, out in zip(sums, outs):
                one.stage_three(out)
            total.drain()
        for s in sums:
            s.drain()

    operands, anywhere = list(parts), pl.BlockSpec(memory_space=pl.ANY)
    out_shape = [jax.ShapeDtypeStruct((rows, width), jnp.float32)]
    scratch = []
    for n, axes in enumerate(orders):
        scratch += WholeSum.scratch(place.sizes, axes, rows, cuts[n + 1] - cuts[n], parts[0].dtype, len(parts))
    if pairs is not None:
        plan = Plan(ep_count, True)
        operands.append(pairs)
        out_shape.append(jax.ShapeDtypeStruct(pairs.shape[1:], pairs.dtype))
        scratch += RowSum.scratch(plan, pairs.shape[1], pairs.shape[2], pairs.dtype, 4)
    got = pl.pallas_call(
        kernel,
        out_shape=tuple(out_shape),
        in_specs=[anywhere] * len(operands),
        out_specs=tuple(pl.BlockSpec(memory_space=pltpu.VMEM) for _ in out_shape),
        scratch_shapes=scratch,
        compiler_params=pltpu.CompilerParams(
            collective_id=collective_id, has_side_effects=True, vmem_limit_bytes=VMEM_MOST),
        name="scatter_whole" if pairs is None else "scatter_pairs",
    )(*operands)
    return got[0] if pairs is None else got


def scatter_experts(parts, lefts, rights, collective_id):
    ep_count, rows, width = parts.shape
    flat, tall = lefts[0].shape
    ff = rights[0].shape[1]
    half, depth = tall // 2, flat // 3
    plan, pieces = Plan(ep_count, False), 4
    place = Place(lax.axis_size("grp"), ep_count)
    left_of = [0, 0, 1]
    hooks = (4, 5, 6, 7, 10, 11, 12, 13, 16, 17)
    kinds, units = len(rights), 2 * len(rights)
    steps = units * 3

    def kernel(p_ref, in_ref, og_ref, pre_ref, lift_ref, mid_ref, out_ref, w0, w1, w2, acc, left, right, gone, came,
               ls, rs, gs, cs, *scratch):
        left_refs, right_refs, outs = (in_ref, og_ref), (pre_ref, lift_ref, mid_ref), (w0, w1, w2)
        place.locate()
        total = RowSum(plan, pieces, p_ref, scratch)
        g = place.at["x"]
        place.greet()

        def fetch(kind, step):
            chunk, slot = step % 3, step % 2
            mine = (step >= 3 * kinds).astype(jnp.int32)
            first = pl.multiple_of(jnp.where(mine == 1, g, 1 - g) * half, HEAD)
            at = pl.ds(pl.multiple_of(chunk * depth, depth), depth)
            return (pltpu.make_async_copy(left_refs[left_of[kind]].at[at, pl.ds(first, half)], left.at[slot], ls.at[slot]),
                    pltpu.make_async_copy(right_refs[kind].at[at, :], right.at[slot], rs.at[slot]))

        def per_kind(step, go):
            for kind in range(kinds):
                run_if((step // 3) % kinds == kind, lambda kind=kind: go(kind))

        def begin(step):
            def go(kind):
                for copy in fetch(kind, step):
                    copy.start()
            per_kind(step, go)

        def away(kind):
            return send(gone.at[kind], came.at[kind], gs.at[kind], cs.at[kind], place.dev(x=place.back("x", 1)))

        def meet(n):
            q, distance = n // plan.long, plan.long - 1 - n % plan.long
            for d in sorted({-distance, distance}):
                total.dest(d, q)

        ks = from_far(plan.wide)
        total.start(ks)
        begin(jnp.int32(0))
        for k in ks[:-1]:
            total.stage_over(k)

        @pl.loop(0, steps)
        def _(step):
            run_if(step + 1 < steps, lambda: begin(step + 1))

            def ready(kind):
                for copy in fetch(kind, step):
                    copy.wait()
            per_kind(step, ready)
            slot = step % 2
            product = inner_left(left[slot], right[slot])
            fresh = step % 3 == 0

            @pl.when(fresh)
            def _():
                acc[...] = product

            @pl.when(jnp.logical_not(fresh))
            def _():
                acc[...] += product

            def done(kind):
                @pl.when(step < 3 * kinds)
                def _():
                    gone[kind] = acc[...].astype(jnp.bfloat16)
                    away(kind).start()

                @pl.when(step >= 3 * kinds)
                def _():
                    outs[kind][...] = acc[...]

            run_if(step % 3 == 2, lambda: per_kind(step, done))
            for n, at in enumerate(hooks):
                run_if(step == at, lambda n=n: meet(n))

        for n in range(len(hooks), pieces * plan.long):
            meet(n)
        out_ref[...] = total.result()
        for kind in range(kinds):
            away(kind).wait_recv()
            piece = 32

            @pl.loop(0, half // piece)
            def _(i, kind=kind):
                at = pl.ds(pl.multiple_of(i * piece, piece), piece)
                outs[kind][at, :] = outs[kind][at, :] + came[kind, at, :].astype(jnp.float32)

        for kind in range(kinds):
            away(kind).wait_send()
        total.drain()

    anywhere = pl.BlockSpec(memory_space=pl.ANY)
    sem = lambda n: pltpu.SemaphoreType.DMA((n,))
    outs = [jax.ShapeDtypeStruct((rows, width), parts.dtype)] + [jax.ShapeDtypeStruct((half, ff), jnp.float32)] * kinds
    return pl.pallas_call(
        kernel,
        out_shape=tuple(outs),
        in_specs=[anywhere] * 6,
        out_specs=tuple(pl.BlockSpec(memory_space=pltpu.VMEM) for _ in outs),
        scratch_shapes=[
            pltpu.VMEM((half, ff), jnp.float32),
            pltpu.VMEM((2, depth, half), jnp.bfloat16),
            pltpu.VMEM((2, depth, ff), jnp.bfloat16),
            pltpu.VMEM((kinds, half, ff), jnp.bfloat16),
            pltpu.VMEM((kinds, half, ff), jnp.bfloat16),
            sem(2), sem(2), sem(kinds), sem(kinds),
        ] + RowSum.scratch(plan, rows, width, parts.dtype, pieces),
        compiler_params=pltpu.CompilerParams(
            collective_id=collective_id, has_side_effects=True, vmem_limit_bytes=VMEM_MOST),
        name="scatter_experts",
    )(parts, *lefts, *rights)


def visible_bias(shape, first_key, start, first_query):
    key_pos = first_key + lax.broadcasted_iota(jnp.int32, shape, 0)
    query_pos = first_query + lax.broadcasted_iota(jnp.int32, shape, 1)
    seen = jnp.logical_and(key_pos >= start, key_pos <= query_pos)
    return jnp.where(seen, 0.0, masked_value)


def lanes(first):
    return pl.ds(pl.multiple_of(first, HEAD), HEAD)


def turned(values, cosine, sine):
    return values * cosine + pltpu.roll(values, HEAD // 2, 1) * sine


def whole_spec(*shape):
    return pl.BlockSpec(shape, lambda *s: (0,) * len(shape))


def project_kernel(x_ref, gain_ref, cos_ref, sin_ref, wq_ref, wk_ref, wv_ref, hid_ref, q_ref, kv_ref, hidden):
    @pl.when(pl.program_id(0) == 0)
    def _():
        hidden[...] = normed(x_ref[...].astype(jnp.float32), gain_ref[...]).astype(jnp.bfloat16)
        hid_ref[...] = hidden[...]

    cosine, sine = cos_ref[...], sin_ref[...]
    q = jnp.dot(hidden[...], wq_ref[...], preferred_element_type=jnp.float32)
    k = jnp.dot(hidden[...], wk_ref[...], preferred_element_type=jnp.float32)
    v = jnp.dot(hidden[...], wv_ref[...], preferred_element_type=jnp.float32)
    for h in range(q.shape[1] // HEAD):
        at = slice(h * HEAD, (h + 1) * HEAD)
        q_ref[:, at] = (turned(q[:, at], cosine, sine) * HEAD ** (-0.5)).astype(jnp.bfloat16)
        kv_ref[:, 2 * h * HEAD : (2 * h + 1) * HEAD] = turned(k[:, at], cosine, sine).astype(jnp.bfloat16)
        kv_ref[:, (2 * h + 1) * HEAD : (2 * h + 2) * HEAD] = v[:, at].astype(jnp.bfloat16)


def project(tokens, gain, cosine, sine, wq, wk, wv):
    rows, width = tokens.shape
    tile = 2 * HEAD
    column = pl.BlockSpec((width, tile), lambda i: (0, i))
    return pl.pallas_call(
        project_kernel,
        out_shape=(
            jax.ShapeDtypeStruct((rows, width), jnp.bfloat16),
            jax.ShapeDtypeStruct((rows, width), jnp.bfloat16),
            jax.ShapeDtypeStruct((rows, 2 * width), jnp.bfloat16),
        ),
        grid=(width // tile,),
        in_specs=[whole_spec(rows, width), whole_spec(1, width), whole_spec(rows, HEAD), whole_spec(rows, HEAD),
                  column, column, column],
        out_specs=(whole_spec(rows, width), pl.BlockSpec((rows, tile), lambda i: (0, i)),
                   pl.BlockSpec((rows, 2 * tile), lambda i: (0, i))),
        scratch_shapes=[pltpu.VMEM((rows, width), jnp.bfloat16)],
        cost_estimate=pl.CostEstimate(flops=6 * rows * width * width, bytes_accessed=6 * width * width, transcendentals=0),
        name="project",
    )(tokens, gain[None, :], cosine, sine, wq, wk, wv)


def attend_kernel(info, q_ref, start_ref, kv_ref, mixed_ref, low_ref, total_ref, bias, top, norm):
    step = pl.program_id(0)
    me, first_block = info[0], info[1]
    rows = q_ref.shape[0]
    block = me - step

    @pl.when(step == 0)
    def _():
        top[...] = jnp.full_like(top, masked_value)
        norm[...] = jnp.zeros_like(norm)
        mixed_ref[...] = jnp.zeros_like(mixed_ref)

    @pl.when(block >= first_block)
    def _():
        bias[...] = visible_bias((rows, rows), block * rows, start_ref[...], me * rows)

        @pl.loop(0, HEADS, unroll=2)
        def _(h):
            keys, values = kv_ref[0, :, lanes(2 * h * HEAD)], kv_ref[0, :, lanes((2 * h + 1) * HEAD)]
            scores = inner_right(keys, q_ref[:, lanes(h * HEAD)]) + bias[...]
            old = top[h]
            new = jnp.maximum(old, jnp.max(scores, axis=0, keepdims=True))
            weights = jnp.exp(scores - new)
            shrink = jnp.exp(old - new)
            top[h] = new
            norm[h] = norm[h] * shrink + jnp.sum(weights, axis=0, keepdims=True)
            mixed_ref[h] = mixed_ref[h] * shrink + inner_left(values, weights.astype(jnp.bfloat16))

    @pl.when(step == pl.num_programs(0) - 1)
    def _():
        for h in range(HEADS):
            mixed = mixed_ref[h] / norm[h]
            mixed_ref[h] = mixed
            low_ref[:, h * HEAD : (h + 1) * HEAD] = mixed.T.astype(jnp.bfloat16)
            total_ref[h] = top[h] + jnp.log(norm[h])


def attend(info, queries, start, pairs):
    rows, width = queries.shape
    steps = pairs.shape[0] // 2 + 1
    return pl.pallas_call(
        attend_kernel,
        out_shape=(
            jax.ShapeDtypeStruct((HEADS, HEAD, rows), jnp.float32),
            jax.ShapeDtypeStruct((rows, width), jnp.bfloat16),
            jax.ShapeDtypeStruct((HEADS, 1, rows), jnp.float32),
        ),
        grid_spec=pltpu.PrefetchScalarGridSpec(
            num_scalar_prefetch=1,
            grid=(steps,),
            in_specs=[
                whole_spec(rows, width),
                whole_spec(1, rows),
                pl.BlockSpec((1, rows, 2 * width), lambda s, info: (jnp.maximum(info[0] - s, info[1]), 0, 0)),
            ],
            out_specs=(whole_spec(HEADS, HEAD, rows), whole_spec(rows, width), whole_spec(HEADS, 1, rows)),
            scratch_shapes=[
                pltpu.VMEM((rows, rows), jnp.float32),
                pltpu.VMEM((HEADS, 1, rows), jnp.float32),
                pltpu.VMEM((HEADS, 1, rows), jnp.float32),
            ],
        ),
        cost_estimate=pl.CostEstimate(
            flops=4 * rows * rows * width * steps, bytes_accessed=4 * rows * width * steps, transcendentals=0
        ),
        name="attend",
    )(info, queries, start, pairs)


def attend_back_kernel(
    info, q_ref, g_ref, mixed_ref, start_ref, total_ref, cos_ref, sin_ref, kv_ref, dkv_ref, dq_ref, bias, acc, term
):
    step = pl.program_id(0)
    me, first_block = info[0], info[1]
    rows = q_ref.shape[0]
    block = me - step

    @pl.when(step == 0)
    def _():
        acc[...] = jnp.zeros_like(acc)
        for h in range(HEADS):
            grads = g_ref[:, h * HEAD : (h + 1) * HEAD].astype(jnp.float32).T
            term[h] = jnp.sum(grads * mixed_ref[h], axis=0, keepdims=True)

    @pl.when(block >= first_block)
    def _():
        bias[...] = visible_bias((rows, rows), block * rows, start_ref[...], me * rows)

        @pl.loop(0, HEADS, unroll=2)
        def _(h):
            early, late, at = lanes(2 * h * HEAD), lanes((2 * h + 1) * HEAD), lanes(h * HEAD)
            keys, values = kv_ref[0, :, early], kv_ref[0, :, late]
            queries, grads = q_ref[:, at], g_ref[:, at]
            probs = jnp.exp(inner_right(keys, queries) + bias[...] - total_ref[h])
            prob_grad = inner_right(values, grads)
            score_grad = (probs * (prob_grad - term[h])).astype(jnp.bfloat16)
            dkv_ref[0, :, late] = jnp.dot(
                probs.astype(jnp.bfloat16), grads, preferred_element_type=jnp.float32
            ).astype(jnp.bfloat16)
            dkv_ref[0, :, early] = jnp.dot(
                score_grad, queries, preferred_element_type=jnp.float32
            ).astype(jnp.bfloat16)
            acc[h] += inner_left(keys, score_grad)

    @pl.when(jnp.logical_and(block >= 0, block < first_block))
    def _():
        dkv_ref[...] = jnp.zeros_like(dkv_ref)

    @pl.when(step == pl.num_programs(0) - 1)
    def _():
        for h in range(HEADS):
            back = turned(acc[h].T * HEAD ** (-0.5), cos_ref[...], -sin_ref[...])
            dq_ref[:, h * HEAD : (h + 1) * HEAD] = back.astype(jnp.bfloat16)


def attend_back(info, queries, grads, mixed, start, total, cosine, sine, pairs):
    rows, width = queries.shape
    count = pairs.shape[0]
    steps = count // 2 + 1
    return pl.pallas_call(
        attend_back_kernel,
        out_shape=(
            jax.ShapeDtypeStruct(pairs.shape, jnp.bfloat16),
            jax.ShapeDtypeStruct((rows, width), jnp.bfloat16),
        ),
        grid_spec=pltpu.PrefetchScalarGridSpec(
            num_scalar_prefetch=1,
            grid=(steps,),
            in_specs=[
                whole_spec(rows, width),
                whole_spec(rows, width),
                whole_spec(HEADS, HEAD, rows),
                whole_spec(1, rows),
                whole_spec(HEADS, 1, rows),
                whole_spec(rows, HEAD),
                whole_spec(rows, HEAD),
                pl.BlockSpec((1, rows, 2 * width), lambda s, info: (jnp.maximum(info[0] - s, info[1]), 0, 0)),
            ],
            out_specs=(
                pl.BlockSpec((1, rows, 2 * width), lambda s, info: (jnp.maximum(info[0] - s, 0), 0, 0)),
                whole_spec(rows, width),
            ),
            scratch_shapes=[
                pltpu.VMEM((rows, rows), jnp.float32),
                pltpu.VMEM((HEADS, HEAD, rows), jnp.float32),
                pltpu.VMEM((HEADS, 1, rows), jnp.float32),
            ],
        ),
        cost_estimate=pl.CostEstimate(
            flops=10 * rows * rows * width * steps, bytes_accessed=8 * rows * width * steps, transcendentals=0
        ),
        name="attend_back",
    )(info, queries, grads, mixed, start, total, cosine, sine, pairs)


def finish_kernel(
    x_ref, gain_ref, res_ref, hid_ref, q_ref, kv_ref, cos_ref, sin_ref, wq_ref, wk_ref, wv_ref,
    dq_ref, dk_ref, dv_ref, out_ref, gain_out, acc,
):
    step = pl.program_id(0)

    @pl.when(step == 0)
    def _():
        acc[...] = jnp.zeros_like(acc)

    cosine, sine = cos_ref[...], sin_ref[...]
    count = q_ref.shape[1] // HEAD
    keys = jnp.concatenate(
        [turned(kv_ref[:, 2 * h * HEAD : (2 * h + 1) * HEAD].astype(jnp.float32), cosine, -sine).astype(jnp.bfloat16)
         for h in range(count)], axis=1)
    values = jnp.concatenate([kv_ref[:, (2 * h + 1) * HEAD : (2 * h + 2) * HEAD] for h in range(count)], axis=1)
    grads = (q_ref[...], keys, values)
    acc[...] += (
        inner_right(grads[0], wq_ref[...]) + inner_right(grads[1], wk_ref[...]) + inner_right(grads[2], wv_ref[...])
    )
    hidden = hid_ref[...]
    for ref, grad in zip((dq_ref, dk_ref, dv_ref), grads):
        ref[...] = inner_left(hidden, grad).astype(jnp.bfloat16)

    @pl.when(step == pl.num_programs(0) - 1)
    def _():
        values, gain, grad = x_ref[...].astype(jnp.float32), gain_ref[...], acc[...]
        scale = lax.rsqrt(jnp.mean(values * values, axis=1, keepdims=True) + epsilon)
        inner = jnp.mean(gain * grad * values, axis=1, keepdims=True)
        part = scale * gain * grad - values * (scale * scale * scale) * inner
        out_ref[...] = (res_ref[...] + part).astype(jnp.bfloat16)
        gain_out[...] = jnp.sum(grad * values * scale, axis=0, keepdims=True)


def finish(tokens, gain, residual_grad, hidden, query_grad, pair_grads, cosine, sine, wq, wk, wv):
    rows, width = tokens.shape
    tile = 2 * HEAD
    column = pl.BlockSpec((width, tile), lambda i: (0, i))
    return pl.pallas_call(
        finish_kernel,
        out_shape=(
            jax.ShapeDtypeStruct((width, width), jnp.bfloat16),
            jax.ShapeDtypeStruct((width, width), jnp.bfloat16),
            jax.ShapeDtypeStruct((width, width), jnp.bfloat16),
            jax.ShapeDtypeStruct((rows, width), jnp.bfloat16),
            jax.ShapeDtypeStruct((1, width), jnp.float32),
        ),
        grid=(width // tile,),
        in_specs=[whole_spec(rows, width), whole_spec(1, width), whole_spec(rows, width), whole_spec(rows, width),
                  pl.BlockSpec((rows, tile), lambda i: (0, i)), pl.BlockSpec((rows, 2 * tile), lambda i: (0, i)),
                  whole_spec(rows, HEAD), whole_spec(rows, HEAD), column, column, column],
        out_specs=(column, column, column, whole_spec(rows, width), whole_spec(1, width)),
        scratch_shapes=[pltpu.VMEM((rows, width), jnp.float32)],
        cost_estimate=pl.CostEstimate(flops=12 * rows * width * width, bytes_accessed=12 * width * width, transcendentals=0),
        name="finish",
    )(tokens, gain[None, :], residual_grad, hidden, query_grad, pair_grads, cosine, sine, wq, wk, wv)


def experts_kernel(
    where_ref, x_ref, g_ref, rank_row, rank_col, share_row, wg_ref, wu_ref, wd_ref,
    back_ref, routed_ref, in_ref, pre_ref, lift_ref, mid_ref, og_ref, grads,
):
    blocks, rows, side = x_ref.shape
    capacity = in_ref.shape[0] // blocks
    width = og_ref.shape[1]
    dot = lambda left, right: jnp.dot(left, right, preferred_element_type=jnp.float32)
    shares = []
    for i in range(blocks):
        at = slice(i * capacity, (i + 1) * capacity)
        hit = rank_row[i] == lax.broadcasted_iota(jnp.int32, (capacity, rows), 0)
        pick = jnp.where(hit, 1.0, 0.0)
        shares.append(jnp.sum(pick * share_row[i], axis=1, keepdims=True))
        pick = pick.astype(jnp.bfloat16)
        in_ref[at, :] = dot(pick, x_ref[i, :, :width]).astype(jnp.bfloat16)
        grads[at, :] = dot(pick, g_ref[i]).astype(jnp.bfloat16)
    share = jnp.concatenate(shares, axis=0)
    pre = dot(in_ref[...], wg_ref[0])
    lift = dot(in_ref[...], wu_ref[0])
    silu, slope = silu_parts(pre)
    mid_ref[...] = (silu * lift).astype(jnp.bfloat16)
    lift_slope = lift * slope
    result = dot(mid_ref[...], wd_ref[0]).astype(jnp.bfloat16).astype(jnp.float32)
    grad = grads[...].astype(jnp.float32)
    gate_grad = jnp.sum(result * grad, axis=1, keepdims=True)
    og_ref[...] = (share * grad).astype(jnp.bfloat16)
    given = (share * result).astype(jnp.bfloat16)
    mid_grad = inner_right(og_ref[...], wd_ref[0])
    pre_ref[...] = (mid_grad * lift_slope).astype(jnp.bfloat16)
    lift_ref[...] = (mid_grad * silu).astype(jnp.bfloat16)
    in_grad = (inner_right(pre_ref[...], wg_ref[0]) + inner_right(lift_ref[...], wu_ref[0])).astype(jnp.bfloat16)
    lane = lax.broadcasted_iota(jnp.int32, (blocks * capacity, side - width), 1)
    high = gate_grad.astype(jnp.bfloat16).astype(jnp.float32)
    extra = jnp.where(lane == where_ref[0], high, jnp.where(lane == where_ref[1], gate_grad - high, 0.0))
    extra = extra.astype(jnp.bfloat16)
    for i in range(blocks):
        at = slice(i * capacity, (i + 1) * capacity)
        hit = rank_col[i] == lax.broadcasted_iota(jnp.int32, (rows, capacity), 1)
        put = jnp.where(hit, 1.0, 0.0).astype(jnp.bfloat16)
        back_ref[i, :, :width] = dot(put, in_grad[at, :]).astype(jnp.bfloat16)
        back_ref[i, :, width:] = dot(put, extra[at, :]).astype(jnp.bfloat16)
        routed_ref[i] = dot(put, given[at, :]).astype(jnp.bfloat16)


def run_experts(places, arrived, grads, rank, share, gate, up, down, capacity):
    count, rows, side = arrived.shape
    width, ff = gate.shape[1], gate.shape[2]
    blocks = 384 // capacity
    flat = count * capacity
    once = lambda *shape: pl.BlockSpec(shape, lambda i, p: (0,) * len(shape), pipeline_mode=pl.Buffered(1))
    lead = lambda *shape: pl.BlockSpec((blocks,) + shape, lambda i, p: (i, 0, 0))
    tall = lambda wide: pl.BlockSpec((blocks * capacity, wide), lambda i, p: (i, 0))
    shape = lambda *dims: jax.ShapeDtypeStruct(dims, jnp.bfloat16)
    return pl.pallas_call(
        experts_kernel,
        out_shape=(shape(count, rows, side), shape(count, rows, width), shape(flat, width), shape(flat, ff),
                   shape(flat, ff), shape(flat, ff), shape(flat, width)),
        grid_spec=pltpu.PrefetchScalarGridSpec(
            num_scalar_prefetch=1,
            grid=(count // blocks,),
            in_specs=[lead(rows, side), lead(rows, width), lead(1, rows), lead(rows, 1), lead(1, rows),
                      once(1, width, ff), once(1, width, ff), once(1, ff, width)],
            out_specs=(lead(rows, side), lead(rows, width), tall(width), tall(ff), tall(ff), tall(ff), tall(width)),
            scratch_shapes=[pltpu.VMEM((blocks * capacity, width), jnp.bfloat16)],
        ),
        compiler_params=pltpu.CompilerParams(vmem_limit_bytes=VMEM_MOST),
        cost_estimate=pl.CostEstimate(flops=16 * flat * width * ff, bytes_accessed=16 * flat * width, transcendentals=0),
        name="run_experts",
    )(places, arrived, grads, rank[:, None, :], rank[:, :, None], share[:, None, :], gate, up, down)


def local(
    tokens,
    doc_lengths,
    expert_ids,
    out_grad,
    mixer_gain,
    query_weight,
    key_weight,
    value_weight,
    output_weight,
    ffn_gain,
    router_weight,
    shared_gate,
    shared_up,
    shared_down,
    expert_gate,
    expert_up,
    expert_down,
):
    rows, width = tokens.shape[1], tokens.shape[2]
    ep_count = lax.axis_size("ep")
    device_count = ep_count * lax.axis_size("grp")
    ep_index = lax.axis_index("ep")
    expert_count = router_weight.shape[1]
    capacity = min(rows, 12 * rows * TOP // (7 * expert_count))
    low = lambda v: v.astype(jnp.bfloat16)
    wide = lambda v: v.astype(jnp.float32)
    dot = lambda left, right: jnp.dot(left, right, preferred_element_type=jnp.float32)

    grad_low = out_grad[0]

    doc_ends = jnp.cumsum(doc_lengths[0])
    query_pos = ep_index * rows + jnp.arange(rows, dtype=jnp.int32)
    before = query_pos[:, None] >= doc_ends[None, :]
    start = jnp.max(jnp.where(before, doc_ends[None, :], 0), axis=1)
    info = jnp.stack([ep_index, start[0] // rows]).astype(jnp.int32)
    half_dim = HEAD // 2
    frequency = rope_base ** (-jnp.arange(half_dim, dtype=jnp.float32) / half_dim)
    angles = wide(query_pos)[:, None] * frequency[None, :]
    cosine, sine = jnp.cos(angles), jnp.sin(angles)
    cosine = jnp.concatenate([cosine, cosine], axis=1)
    sine = jnp.concatenate([-sine, sine], axis=1)

    stream = wide(tokens[0])
    hidden_low, queries, own_pairs = project(
        tokens[0], mixer_gain, cosine, sine, query_weight, key_weight, value_weight
    )
    pairs = gather_rows(own_pairs, True, 1, 8)
    grad_later, pairs = lax.optimization_barrier((grad_low, pairs))
    grads_all = lax.all_gather(grad_later, "ep", axis=0, tiled=False)
    mixed, mixed_low, log_total = attend(info, queries, start[None, :], pairs)
    mixer_out = dot(mixed_low, output_weight)
    residual = stream + mixer_out
    ffn_low = low(normed(residual, ffn_gain))

    logits = dot(ffn_low, router_weight)
    experts = jnp.arange(expert_count, dtype=jnp.int32)
    assigned = jnp.any(expert_ids[0][:, :, None] == experts[None, None, :], axis=1)
    shown = jnp.where(assigned, logits, masked_value)
    powers = jnp.where(assigned, jnp.exp(shown - jnp.max(shown, axis=1, keepdims=True)), 0.0)
    gate_probs = powers / jnp.sum(powers, axis=1, keepdims=True)
    probs_high = low(gate_probs)
    probs_rest = low(gate_probs - wide(probs_high))
    side = width + 2 * HEAD if 2 * expert_count > HEAD else width + HEAD
    pad = jnp.zeros((rows, side - width - 2 * expert_count), jnp.bfloat16)
    sent = jnp.concatenate([ffn_low, probs_high, probs_rest, pad], axis=1)
    arrived = gather_rows(sent, False, 2)

    own = experts[None, None, :] == ep_index
    high = arrived[:, :, width : width + expert_count]
    rest = arrived[:, :, width + expert_count : width + 2 * expert_count]
    share = jnp.sum(jnp.where(own, wide(high) + wide(rest), 0.0), axis=2)
    chosen = share > 0.0
    earlier = (jnp.arange(rows)[:, None] < jnp.arange(rows)[None, :]).astype(jnp.bfloat16)
    rank = dot(low(chosen), earlier).astype(jnp.int32)
    rank = jnp.where(chosen, rank, -1)
    places = jnp.stack([ep_index, expert_count + ep_index]).astype(jnp.int32)
    back, given, flat_in, pre_grad, lift_grad, middle, result_grad = run_experts(
        places, arrived, grads_all, rank, share, expert_gate, expert_up, expert_down, capacity
    )
    routed = wide(lax.psum_scatter(given, "ep", scatter_dimension=0))
    group_count = lax.axis_size("grp")
    if group_count == 2:
        back_sum, gate_sum, up_sum, down_sum = scatter_experts(
            back, (flat_in, result_grad), (pre_grad, lift_grad, middle), 3
        )
        gate_sum, up_sum, down_sum = gate_sum[None], up_sum[None], down_sum.T[None]
    else:
        back_sum = scatter_rows(back, False, 3)
        split = width // group_count
        own_down_grad = jnp.concatenate(
            [low(inner_left(middle, result_grad[:, i * split : (i + 1) * split])) for i in range(group_count)], axis=0
        )
        over_groups = lambda v: wide(lax.psum_scatter(v, "grp", scatter_dimension=0, tiled=True))[None]
        gate_sum = over_groups(low(inner_left(flat_in, pre_grad)))
        up_sum = over_groups(low(inner_left(flat_in, lift_grad)))
        down_sum = over_groups(own_down_grad)

    shared_pre = dot(ffn_low, shared_gate)
    shared_lift = dot(ffn_low, shared_up)
    shared_silu, shared_slope = silu_parts(shared_pre)
    shared_mid = low(shared_silu * shared_lift)
    shared_out = dot(shared_mid, shared_down)
    grad_out = wide(grad_low)
    shared_mid_grad = inner_right(grad_low, shared_down)
    shared_pre_grad = low(shared_mid_grad * shared_lift * shared_slope)
    shared_lift_grad = low(shared_mid_grad * shared_silu)
    ffn_grad = inner_right(shared_pre_grad, shared_gate) + inner_right(shared_lift_grad, shared_up)

    layer_out = residual + shared_out + routed
    gate_back = wide(back_sum[:, width : width + expert_count]) + wide(
        back_sum[:, width + expert_count : width + 2 * expert_count]
    )
    chosen_grad = gate_probs * (gate_back - jnp.sum(gate_probs * gate_back, axis=1, keepdims=True))
    logit_grad = low(chosen_grad)
    ffn_grad = ffn_grad + wide(back_sum[:, :width]) + inner_right(logit_grad, router_weight)
    _, ffn_pull = jax.vjp(normed, residual, ffn_gain)
    residual_part, ffn_gain_grad = ffn_pull(ffn_grad)
    residual_grad = grad_out + residual_part
    mixer_grad_low = low(residual_grad)
    mixed_grad = low(inner_right(mixer_grad_low, output_weight))
    pair_parts, query_lin_grad = attend_back(
        info, queries, mixed_grad, mixed, start[None, :], log_total, cosine, sine, pairs
    )
    by_device = lambda v: low(v).reshape(device_count, width // device_count, -1)
    early = [
        by_device(part)
        for part in (inner_left(ffn_low, shared_pre_grad), inner_left(ffn_low, shared_lift_grad),
                     inner_left(grad_low, shared_mid), inner_left(mixed_low, mixer_grad_low))
    ]
    if ep_count > 16:
        pair_grads = scatter_rows(pair_parts, True, 4)
        early_sum = scatter_whole(early, 5)
    else:
        early_sum, pair_grads = scatter_whole(early, 5, pair_parts)

    query_part, key_part, value_part, tokens_grad, mixer_gain_grad = finish(
        tokens[0], mixer_gain, residual_grad, hidden_low, query_lin_grad, pair_grads, cosine, sine,
        query_weight, key_weight, value_weight,
    )
    squares = jnp.stack(
        [jnp.sum(residual * residual), jnp.sum(mixer_out * mixer_out), jnp.sum(layer_out * layer_out)]
    )
    extras = jnp.concatenate(
        [inner_left(ffn_low, logit_grad), mixer_gain_grad.T, ffn_gain_grad[:, None],
         jnp.broadcast_to(squares[None, :], (width, 3))], axis=1
    )
    extras = jnp.pad(extras, ((0, 0), (0, HEAD - extras.shape[1])))
    late_sum = scatter_whole([by_device(v) for v in (query_part, key_part, value_part, extras)], 6)
    extra_sum = late_sum[:, 3 * width :]
    entry_count = rows * device_count * width
    stream_rms = jnp.sqrt(extra_sum[0, expert_count + 2 : expert_count + 5] / entry_count)
    ff = shared_gate.shape[1]
    return (
        low(layer_out)[None],
        tokens_grad[None],
        extra_sum[:, expert_count],
        late_sum[:, :width],
        late_sum[:, width : 2 * width],
        late_sum[:, 2 * width : 3 * width],
        early_sum[:, 3 * ff :],
        extra_sum[:, expert_count + 1],
        extra_sum[:, :expert_count],
        early_sum[:, :ff],
        early_sum[:, ff : 2 * ff],
        early_sum[:, 2 * ff : 3 * ff].T,
        gate_sum,
        up_sum,
        down_sum,
        stream_rms,
    )


def solution(mesh):
    return jax.shard_map(
        local,
        mesh=mesh,
        in_specs=(
            P("grp", "ep", None),
            P("grp", None),
            P("grp", "ep", None),
            P("grp", "ep", None),
            P(),
            P(),
            P(),
            P(),
            P(),
            P(),
            P(),
            P(),
            P(),
            P(),
            P("ep", None, None),
            P("ep", None, None),
            P("ep", None, None),
        ),
        out_specs=(
            P("grp", "ep", None),
            P("grp", "ep", None),
            P(("grp", "ep")),
            P(("grp", "ep"), None),
            P(("grp", "ep"), None),
            P(("grp", "ep"), None),
            P(("grp", "ep"), None),
            P(("grp", "ep")),
            P(("grp", "ep"), None),
            P(("grp", "ep"), None),
            P(("grp", "ep"), None),
            P(None, ("grp", "ep")),
            P("ep", "grp", None),
            P("ep", "grp", None),
            P("ep", None, "grp"),
            P(),
        ),
        check_vma=False,
    )
```

```python
import functools

import jax
import jax.numpy as jnp
from jax import lax
from jax.experimental import pallas as pl
from jax.experimental.pallas import tpu as pltpu
from jax.sharding import PartitionSpec as P

HEADS = 10
HEAD = 128
TOP = 7

epsilon = 1e-06
rope_base = 10000.0
masked_value = -1e30


def normed(values, gain_vec):
    return (
        values * lax.rsqrt(jnp.mean(values * values, axis=-1, keepdims=True) + epsilon) * gain_vec
    )


def inner_left(left_op, right_op):
    return lax.dot_general(
        left_op, right_op, (((0,), (0,)), ((), ())), preferred_element_type=jnp.float32
    )


def inner_right(left_op, right_op):
    return lax.dot_general(
        left_op, right_op, (((1,), (1,)), ((), ())), preferred_element_type=jnp.float32
    )


def silu_parts(pre_act):
    sigmoid_val = jax.nn.sigmoid(pre_act)
    return (pre_act * sigmoid_val, sigmoid_val * (1.0 + pre_act * (1.0 - sigmoid_val)))


MESH = pl.DeviceIdType.MESH
VMEM_MOST = 64 * 1024 * 1024 - 65536


def when(cond):
    if cond is True:
        return lambda f: f()
    if cond is False:
        return lambda f: None
    return pl.when(cond)


def both(*conds):
    out = True
    for cond in conds:
        if cond is False:
            return False
        if cond is True:
            continue
        out = cond if out is True else jnp.logical_and(out, cond)
    return out


class Plan:
    def __init__(self, ep_count, window):
        self.long = 4
        self.wide = ep_count // 8
        self.window = window
        self.steps = (
            list(range(self.long // 2 + 1))
            if window
            else list(range(-(self.long - 1), self.long))
        )

    def place(self):
        me = lax.axis_index("ep")
        return me // (2 * self.wide), (me // 2) % self.wide, me % 2

    def slot(self, a, b, c):
        return (a * self.wide + b) * 2 + c

    def plane(self, a, d):
        return d if self.window else jnp.clip(a - d, 0, self.long - 1)

    def planes(self):
        return len(self.steps) if self.window else self.long

    def inside(self, a):
        return jnp.logical_and(a >= 0, a < self.long)

    def need(self, d, b, c, b0, c0):
        if not self.window or 0 < d < self.long // 2:
            return True
        if d == 0:
            return jnp.logical_or(b0 < b, jnp.logical_and(b0 == b, c0 <= c))
        return jnp.logical_or(b0 > b, jnp.logical_and(b0 == b, c0 >= c))

    def need_pair(self, d, b, b0):
        if not self.window or 0 < d < self.long // 2:
            return True
        return b0 < b if d == 0 else b0 > b

    def greet(self, a, b, c):
        barrier = pltpu.get_barrier_semaphore()

        def signal(cond, dev):
            @when(cond)
            def _():
                pl.semaphore_signal(barrier, inc=1, device_id={"ep": dev}, device_id_type=MESH)

        signal(a + 1 < self.long, self.slot(a + 1, b, c))
        signal(a > 0, self.slot(a - 1, b, c))
        for k in range(1, self.wide):
            signal(True, self.slot(a, (b + k) % self.wide, c))
        signal(True, self.slot(a, b, 1 - c))
        ends = (a == 0).astype(jnp.int32) + (a == self.long - 1).astype(jnp.int32)
        pl.semaphore_wait(barrier, self.wide + 2 - ends)


def gather_kernel(plan, pieces, x_ref, out_ref, ra, sa_up, sa_dn, rb, sb, rc, sc, own):
    a, b, c = plan.place()
    steps, wide = plan.steps, plan.wide
    at = {d: i for i, d in enumerate(steps)}
    rows = x_ref.shape[0] // pieces

    def part(q):
        return pl.ds(pl.multiple_of(q * rows, rows), rows)

    def copy(q, src, slot, ssem, rsem, dev):
        return pltpu.make_async_remote_copy(
            src_ref=src, dst_ref=out_ref.at[slot, part(q)], send_sem=ssem, recv_sem=rsem,
            device_id={"ep": dev}, device_id_type=MESH,
        )

    def hops(d, q):
        i = at[d]
        slot = plan.slot(a - d, b, c)
        src = x_ref.at[part(q)] if d == 0 else out_ref.at[slot, part(q)]
        real = plan.inside(a - d)
        out = []
        if d >= 0 and d + 1 in at:
            out.append((both(real, a + 1 < plan.long), lambda: copy(
                q, src, slot, sa_up.at[i, q], ra.at[at[d + 1], q], plan.slot(a + 1, b, c))))
        if d <= 0 and d - 1 in at:
            out.append((both(real, a > 0), lambda: copy(
                q, src, slot, sa_dn.at[i, q], ra.at[at[d - 1], q], plan.slot(a - 1, b, c))))
        for k in range(1, wide):
            to = (b + k) % wide
            out.append((both(real, plan.need_pair(d, to, b)), lambda k=k, to=to: copy(
                q, src, slot, sb.at[i, k, q], rb.at[i, k, q], plan.slot(a, to, c))))
        out.append((both(real, plan.need(d, b, 1 - c, b, c)), lambda: copy(
            q, src, slot, sc.at[i, 0, q], rc.at[i, 0, q], plan.slot(a, b, 1 - c))))
        return out

    def cross(d, k, q):
        i = at[d]
        b0 = (b + wide - k) % wide
        slot = plan.slot(a - d, b0, c)
        real = plan.inside(a - d)
        come = lambda: copy(q, x_ref.at[part(q)], slot, sb.at[i, k, q], rb.at[i, k, q], plan.slot(a, b, c))
        go = lambda: copy(q, out_ref.at[slot, part(q)], slot, sc.at[i, k, q], rc.at[i, k, q],
                          plan.slot(a, b, 1 - c))
        return (both(real, plan.need_pair(d, b, b0)), come,
                both(real, plan.need(d, b, 1 - c, b0, c)), go)

    plan.greet(a, b, c)
    keep = pltpu.make_async_copy(x_ref, out_ref.at[plan.slot(a, b, c)], own)

    @pl.loop(0, pieces)
    def _(q):
        for cond, go in hops(0, q):
            @when(cond)
            def _(go=go):
                go().start()

    keep.start()
    far = max(abs(d) for d in steps)
    for step in range(1, far + 3):
        @pl.loop(0, pieces)
        def _(q, step=step):
            for d in (step, -step):
                if d in at:
                    @when(plan.inside(a - d))
                    def _(d=d):
                        slot = plan.slot(a - d, b, c)
                        copy(q, x_ref.at[part(q)], slot, sa_up.at[0, q], ra.at[at[d], q],
                             plan.slot(a, b, c)).wait_recv()
                        for cond, go in hops(d, q):
                            @when(cond)
                            def _(go=go):
                                go().start()
            for d in sorted({step - 2, 2 - step}) if step > 1 else ():
                if d in at:
                    for k in range(1, wide):
                        came, come, goes, go = cross(d, k, q)
                        @when(came)
                        def _(come=come):
                            come().wait_recv()
                        @when(goes)
                        def _(go=go):
                            go().start()
    keep.wait()

    @pl.loop(0, pieces)
    def _(q):
        for d in steps:
            i = at[d]
            real = plan.inside(a - d)
            for k in range(wide):
                b0 = (b + wide - k) % wide
                slot = plan.slot(a - d, b0, 1 - c)
                @when(both(real, plan.need(d, b, c, b0, 1 - c)))
                def _(slot=slot, i=i, k=k):
                    copy(q, x_ref.at[part(q)], slot, sc.at[i, k, q], rc.at[i, k, q],
                         plan.slot(a, b, c)).wait_recv()
            for cond, go in hops(d, q):
                @when(cond)
                def _(go=go):
                    go().wait_send()
            for k in range(1, wide):
                came, come, goes, go = cross(d, k, q)
                @when(goes)
                def _(go=go):
                    go().wait_send()


def gather_rows(block, window, collective_id, pieces=4):
    ep_count = lax.axis_size("ep")
    plan = Plan(ep_count, window)
    n, wide = len(plan.steps), plan.wide
    sem = pltpu.SemaphoreType.DMA
    return pl.pallas_call(
        functools.partial(gather_kernel, plan, pieces),
        out_shape=jax.ShapeDtypeStruct((ep_count,) + block.shape, block.dtype),
        in_specs=[pl.BlockSpec(memory_space=pltpu.VMEM)],
        out_specs=pl.BlockSpec(memory_space=pl.ANY),
        scratch_shapes=[sem((n, pieces)), sem((n, pieces)), sem((n, pieces)), sem((n, wide, pieces)),
                        sem((n, wide, pieces)), sem((n, wide, pieces)), sem((n, wide, pieces)), sem],
        compiler_params=pltpu.CompilerParams(collective_id=collective_id, has_side_effects=True),
        name="gather_rows",
    )(block)


def add_rows(dst, others, out=None):
    rows, width = dst.shape
    out = dst if out is None else out
    small = rows <= 64
    piece = 32 if rows % 32 == 0 else rows
    lanes = width if rows % 32 == 0 else 4 * HEAD
    whole = width // lanes * lanes

    def add(at):
        if len(others) == 1 and out.dtype == jnp.bfloat16:
            out[at] = dst[at] + others[0][at]
        else:
            total = dst[at].astype(jnp.float32)
            for other in others:
                total = total + other[at].astype(jnp.float32)
            out[at] = total.astype(out.dtype)

    if piece == rows:
        @pl.loop(0, whole // lanes)
        def _(i):
            add((slice(None), pl.ds(pl.multiple_of(i * lanes, lanes), lanes)))

        if whole < width:
            add((slice(None), pl.ds(whole, width - whole)))
    else:
        @pl.loop(0, rows // piece)
        def _(i):
            add((pl.ds(pl.multiple_of(i * piece, piece), piece), slice(None)))


def send(src, dst, ssem, rsem, to):
    return pltpu.make_async_remote_copy(
        src_ref=src, dst_ref=dst, send_sem=ssem, recv_sem=rsem, device_id=to, device_id_type=MESH
    )


def run_if(cond, go):
    @when(cond)
    def _():
        go()


class RowSum:
    @staticmethod
    def scratch(plan, rows, width, dtype, pieces):
        n, wide = plan.planes(), plan.wide
        blocks = lambda *lead: pltpu.VMEM(lead + (rows, width), dtype)
        sem = lambda *lead: pltpu.SemaphoreType.DMA(lead + (pieces,))
        return [blocks(n, wide), blocks(n, wide), blocks(n, wide - 1), blocks(n), blocks(1 if plan.window else n),
                sem(n, wide), sem(n, wide), sem(n, wide), sem(n, wide), sem(n), sem(n), sem(n), sem(n, wide)]

    def __init__(self, plan, pieces, p_ref, scratch):
        self.plan, self.pieces, self.p_ref = plan, pieces, p_ref
        (self.held, self.rcb, self.rbb, self.r_hi, self.r_lo,
         self.sc, self.rc, self.sb, self.rb, self.sa, self.rhi, self.rlo, self.ld) = scratch
        self.a, self.b, self.c = plan.place()
        self.ready = len(p_ref.shape) == 4
        self.rows = p_ref.shape[-2] // pieces
        self.order = sorted(plan.steps, key=lambda d: -abs(d))

    def part(self, q):
        return pl.ds(pl.multiple_of(q * self.rows, self.rows), self.rows)

    def dev(self, a, b, c):
        return {"ep": self.plan.slot(a, b, c)}

    def source(self, k):
        return (self.b + self.plan.wide - k) % self.plan.wide

    def load(self, d, k, q):
        p, i, b0 = self.plan, self.plan.plane(self.a, d), self.source(k)
        return both(p.inside(self.a - d), p.need(d, self.b, self.c, b0, self.c)), lambda: pltpu.make_async_copy(
            self.p_ref.at[p.slot(self.a - d, b0, self.c), self.part(q)], self.held.at[i, k, self.part(q)],
            self.ld.at[i, k, q])

    def cross(self, d, k, q):
        p, i, b0, c = self.plan, self.plan.plane(self.a, d), self.source(k), self.c
        real = p.inside(self.a - d)
        at = (i, k) if self.ready else (p.slot(self.a - d, b0, 1 - c),)
        return (both(real, p.need(d, self.b, c, b0, 1 - c)), lambda: send(
            self.p_ref.at[at + (self.part(q),)], self.rcb.at[i, k, self.part(q)],
            self.sc.at[i, k, q], self.rc.at[i, k, q], self.dev(self.a, self.b, 1 - c)),
            both(real, p.need(d, self.b, 1 - c, b0, c)))

    def over(self, d, k, q):
        p, i, b0 = self.plan, self.plan.plane(self.a, d), self.source(k)
        return both(p.inside(self.a - d), p.need_pair(d, self.b, b0)), lambda: send(
            self.held.at[i, k, self.part(q)], self.rbb.at[i, k - 1, self.part(q)], self.sb.at[i, k, q],
            self.rb.at[i, k, q], self.dev(self.a, b0, self.c))

    def along(self, d, q):
        p, i, up = self.plan, self.plan.plane(self.a, d), d < 0
        j = d - 1 if p.window else i
        return p.inside(self.a - d), lambda: send(
            self.held.at[i, 0, self.part(q)], (self.r_lo if up else self.r_hi).at[j, self.part(q)],
            self.sa.at[i, q], (self.rlo if up else self.rhi).at[j, q],
            self.dev(self.a + (1 if up else -1), self.b, self.c))

    def start(self, ks):
        for k in ks:
            @pl.loop(0, self.pieces)
            def _(q, k=k):
                for d in self.order:
                    for cond, go in (self.cross(d, k, q)[:2], self.load(d, k, q)):
                        run_if(cond, lambda go=go: go().start())

    def first(self, d, k, q):
        i = self.plan.plane(self.a, d)
        if not self.ready:
            cond, go = self.load(d, k, q)
            run_if(cond, lambda: go().wait())
        _, come_go, come = self.cross(d, k, q)

        def take():
            come_go().wait_recv()
            add_rows(self.held.at[i, k, self.part(q)], [self.rcb.at[i, k, self.part(q)]])

        run_if(come, take)

    def stage_over(self, k):
        @pl.loop(0, self.pieces)
        def _(q):
            for d in self.order:
                self.first(d, k, q)
                cond, go = self.over(d, k, q)
                run_if(cond, lambda go=go: go().start())

    def stage_dests(self, low, high):
        @pl.loop(low, high)
        def _(q):
            for d in self.order:
                self.dest(d, q)

    def dest(self, d, q):
        p, a, b, steps = self.plan, self.a, self.b, self.plan.steps
        i = p.plane(a, d)
        real = p.inside(a - d)
        mine = self.held.at[i, 0, self.part(q)]
        self.first(d, 0, q)
        for k in range(1, p.wide):
            def take(k=k):
                self.over(d, k, q)[1]().wait_recv()
                add_rows(mine, [self.rbb.at[i, k - 1, self.part(q)]])

            run_if(both(real, p.need_pair(d, (b + k) % p.wide, b)), take)
        for inner, cond, buf, sem in ((d >= 0 and d + 1 in steps, a + 1 < p.long, self.r_hi, self.rhi),
                                      (d <= 0 and d - 1 in steps, a > 0, self.r_lo, self.rlo)):
            if inner:
                def take(buf=buf, sem=sem):
                    send(mine, buf.at[i, self.part(q)], self.sa.at[i, q], sem.at[i, q],
                         self.dev(a, b, self.c)).wait_recv()
                    add_rows(mine, [buf.at[i, self.part(q)]])

                run_if(both(real, cond), take)
        if d:
            cond, go = self.along(d, q)
            run_if(cond, lambda: go().start())

    def result(self):
        return self.held[self.plan.plane(self.a, 0), 0]

    def drain(self):
        @pl.loop(0, self.pieces)
        def _(q):
            for d in self.plan.steps:
                sends = [self.cross(d, k, q)[:2] for k in range(self.plan.wide)]
                sends += [self.over(d, k, q) for k in range(1, self.plan.wide)]
                if d:
                    sends.append(self.along(d, q))
                for cond, go in sends:
                    run_if(cond, lambda go=go: go().wait_send())


def scatter_rows(parts, window, collective_id, pieces=4):
    ep_count, rows, width = parts.shape
    plan = Plan(ep_count, window)

    def kernel(p_ref, out_ref, *scratch):
        total = RowSum(plan, pieces, p_ref, scratch)
        plan.greet(total.a, total.b, total.c)
        ks = list(range(1, plan.wide)) + [0]
        total.start(ks)
        for k in ks[:-1]:
            total.stage_over(k)
        total.stage_dests(0, pieces)
        out_ref[...] = total.result()
        total.drain()

    return pl.pallas_call(
        kernel,
        out_shape=jax.ShapeDtypeStruct((rows, width), parts.dtype),
        in_specs=[pl.BlockSpec(memory_space=pl.ANY)],
        out_specs=pl.BlockSpec(memory_space=pltpu.VMEM),
        scratch_shapes=RowSum.scratch(plan, rows, width, parts.dtype, pieces),
        compiler_params=pltpu.CompilerParams(
            collective_id=collective_id, has_side_effects=True, vmem_limit_bytes=VMEM_MOST),
        name="scatter_rows",
    )(parts)


class Place:
    def __init__(self, groups, ep_count):
        self.sizes = {"x": groups, "a": 4, "b": ep_count // 8}

    def locate(self):
        me, wide = lax.axis_index("ep"), self.sizes["b"]
        self.at = {"x": lax.axis_index("grp"), "a": me // (2 * wide), "b": (me // 2) % wide, "c": me % 2}

    def dev(self, **moved):
        at = {**self.at, **moved}
        return {"grp": at["x"], "ep": (at["a"] * self.sizes["b"] + at["b"]) * 2 + at["c"]}

    def slot(self, **moved):
        at = {**self.at, **moved}
        return ((at["x"] * self.sizes["a"] + at["a"]) * self.sizes["b"] + at["b"]) * 2 + at["c"]

    def back(self, axis, k):
        return (self.at[axis] + self.sizes[axis] - k) % self.sizes[axis]

    def greet(self):
        peers = [self.dev(c=1 - self.at["c"])] + [
            self.dev(**{axis: self.back(axis, k)}) for axis in "xba" for k in range(1, self.sizes[axis])]
        barrier = pltpu.get_barrier_semaphore()
        for to in peers:
            pl.semaphore_signal(barrier, inc=1, device_id=to, device_id_type=MESH)
        pl.semaphore_wait(barrier, len(peers))


def from_far(size):
    return list(range(1, size)) + [0]


class WholeSum:
    @staticmethod
    def scratch(sizes, axes, rows, width, dtype, sources):
        n1, n2, n3 = (sizes[axis] for axis in axes)
        blocks = lambda *lead: pltpu.VMEM(lead + (rows, width), dtype)
        sem = lambda *lead: pltpu.SemaphoreType.DMA(lead)
        full = (n1, n2, n3)
        one, two, three = (n1 - 1, n2, n3), (n2 - 1, n3), (n3 - 1,)
        return [blocks(*full), blocks(*full), blocks(*one), blocks(*two), blocks(*three),
                sem(*full, sources), sem(*full, sources), sem(*full, sources), sem(*one), sem(*one), sem(*two), sem(*two), sem(*three), sem(*three)]

    def __init__(self, place, axes, pieces, scratch):
        self.place, self.axes, self.pieces = place, axes, pieces
        (self.held, self.rcb, self.r1, self.r2, self.r3,
         self.ld, self.sc, self.rc, self.s1, self.q1, self.s2, self.q2, self.s3, self.q3) = scratch
        self.n1, self.n2, self.n3 = (place.sizes[axis] for axis in axes)
        self.groups = [[(k1, k2, k3) for k2 in from_far(self.n2) for k3 in from_far(self.n3)]
                       for k1 in from_far(self.n1)]

    def slot(self, key, c):
        return self.place.slot(c=c, **{axis: self.place.back(axis, k) for axis, k in zip(self.axes, key)})

    def loads(self, key):
        c = self.place.at["c"]
        for n, (ref, first, at, count) in enumerate(self.pieces):
            frm, to = pl.ds(first, count), pl.ds(at, count)
            yield pltpu.make_async_copy(
                ref.at[self.slot(key, c), :, frm], self.held.at[key + (slice(None), to)],
                self.ld.at[key + (n,)])

    def crossings(self, key):
        c = self.place.at["c"]
        for n, (ref, first, at, count) in enumerate(self.pieces):
            frm, to = pl.ds(first, count), pl.ds(at, count)
            yield send(ref.at[self.slot(key, 1 - c), :, frm], self.rcb.at[key + (slice(None), to)],
                       self.sc.at[key + (n,)], self.rc.at[key + (n,)], self.place.dev(c=1 - c))

    def hop(self, level, key):
        buf, ssem, rsem = ((self.r1, self.s1, self.q1), (self.r2, self.s2, self.q2), (self.r3, self.s3, self.q3))[level]
        axis, k = self.axes[level], key[level]
        far = (k - 1,) + key[level + 1 :]
        return send(self.held.at[key], buf.at[far], ssem.at[far], rsem.at[far],
                    self.place.dev(**{axis: self.place.back(axis, k)}))

    def start(self, i):
        for key in self.groups[i]:
            for go in self.crossings(key):
                go.start()
            for go in self.loads(key):
                go.start()

    def stage_core(self, i):
        for key in self.groups[i]:
            for go in self.loads(key):
                go.wait()
            for go in self.crossings(key):
                go.wait_recv()
            add_rows(self.held.at[key], [self.rcb.at[key]])
            if key[0]:
                self.hop(0, key).start()

    def stage_one(self, k2):
        for k3 in from_far(self.n3):
            for k1 in range(1, self.n1):
                self.hop(0, (k1, k2, k3)).wait_recv()
            add_rows(self.held.at[0, k2, k3], [self.r1.at[k1 - 1, k2, k3] for k1 in range(1, self.n1)])
            if k2:
                self.hop(1, (0, k2, k3)).start()

    def stage_two(self):
        for k3 in from_far(self.n3):
            for k2 in range(1, self.n2):
                self.hop(1, (0, k2, k3)).wait_recv()
            add_rows(self.held.at[0, 0, k3], [self.r2.at[k2 - 1, k3] for k2 in range(1, self.n2)])
            if k3:
                self.hop(2, (0, 0, k3)).start()

    def stage_three(self, out):
        for k3 in range(1, self.n3):
            self.hop(2, (0, 0, k3)).wait_recv()
        add_rows(self.held.at[0, 0, 0], [self.r3.at[k3 - 1] for k3 in range(1, self.n3)], out)

    def drain(self):
        for group in self.groups:
            for key in group:
                for go in self.crossings(key):
                    go.wait_send()
                if key[0]:
                    self.hop(0, key).wait_send()
                elif key[1]:
                    self.hop(1, key).wait_send()
                elif key[2]:
                    self.hop(2, key).wait_send()


def pieces_of(sources, low, high):
    pieces, first = [], 0
    for ref in sources:
        begin, end = max(low, first), min(high, first + ref.shape[2])
        if begin < end:
            pieces.append((ref, begin - first, begin - low, end - begin))
        first += ref.shape[2]
    return pieces


def scatter_whole(parts, collective_id):
    rows = parts[0].shape[1]
    width = sum(part.shape[2] for part in parts)
    groups, ep_count = lax.axis_size("grp"), lax.axis_size("ep")
    place = Place(groups, ep_count)
    tiles = width // HEAD
    cuts = [0, tiles // 2 * HEAD, width]
    orders = ["xba", "bxa"]

    def kernel(*refs):
        sources, refs = refs[: len(parts)], refs[len(parts) :]
        out_ref, refs = refs[0], refs[1:]
        place.locate()
        sums = []
        for n, axes in enumerate(orders):
            pieces = pieces_of(sources, cuts[n], cuts[n + 1])
            sums.append(WholeSum(place, axes, pieces, refs[:14]))
            refs = refs[14:]
        outs = [out_ref.at[:, pl.ds(cuts[n], cuts[n + 1] - cuts[n])] for n in range(len(orders))]
        place.greet()
        couples = [sums[n : n + 2] for n in range(0, len(sums), 2)]
        for couple in couples:
            for i in range(max(s.n1 for s in couple)):
                for s in couple:
                    if i < s.n1:
                        s.start(i)

        def core(couple):
            for i in range(max(s.n1 for s in couple)):
                for s in couple:
                    if i < s.n1:
                        s.stage_core(i)

        def one(couple):
            for i in range(max(s.n2 for s in couple)):
                for s in couple:
                    if i < s.n2:
                        s.stage_one(from_far(s.n2)[i])

        def two(couple):
            for s in couple:
                s.stage_two()

        for stage in (core, one, two):
            for couple in couples:
                stage(couple)
        for s, out in zip(sums, outs):
            s.stage_three(out)
        for s in sums:
            s.drain()

    operands, anywhere = list(parts), pl.BlockSpec(memory_space=pl.ANY)
    out_shape = [jax.ShapeDtypeStruct((rows, width), jnp.float32)]
    scratch = []
    for n, axes in enumerate(orders):
        scratch += WholeSum.scratch(place.sizes, axes, rows, cuts[n + 1] - cuts[n], parts[0].dtype, len(parts))
    got = pl.pallas_call(
        kernel,
        out_shape=tuple(out_shape),
        in_specs=[anywhere] * len(operands),
        out_specs=tuple(pl.BlockSpec(memory_space=pltpu.VMEM) for _ in out_shape),
        scratch_shapes=scratch,
        compiler_params=pltpu.CompilerParams(
            collective_id=collective_id, has_side_effects=True, vmem_limit_bytes=VMEM_MOST),
        name="scatter_whole",
    )(*operands)
    return got[0]


def scatter_experts(parts, lefts, rights, collective_id):
    ep_count, rows, width = parts.shape
    flat, tall = lefts[0].shape
    ff = rights[0].shape[1]
    half, depth = tall // 2, flat // 3
    plan, pieces = Plan(ep_count, False), 4
    place = Place(lax.axis_size("grp"), ep_count)
    left_of = [0, 0, 1]
    hooks = (4, 5, 6, 7, 10, 11, 12, 13, 16, 17)
    kinds, units = len(rights), 2 * len(rights)
    steps = units * 3

    def kernel(p_ref, in_ref, og_ref, pre_ref, lift_ref, mid_ref, out_ref, w0, w1, w2, acc, left, right, gone, came,
               ls, rs, gs, cs, *scratch):
        left_refs, right_refs, outs = (in_ref, og_ref), (pre_ref, lift_ref, mid_ref), (w0, w1, w2)
        place.locate()
        total = RowSum(plan, pieces, p_ref, scratch)
        g = place.at["x"]
        place.greet()

        def fetch(kind, step):
            chunk, slot = step % 3, step % 2
            mine = (step >= 3 * kinds).astype(jnp.int32)
            first = pl.multiple_of(jnp.where(mine == 1, g, 1 - g) * half, HEAD)
            at = pl.ds(pl.multiple_of(chunk * depth, depth), depth)
            return (pltpu.make_async_copy(left_refs[left_of[kind]].at[at, pl.ds(first, half)], left.at[slot], ls.at[slot]),
                    pltpu.make_async_copy(right_refs[kind].at[at, :], right.at[slot], rs.at[slot]))

        def per_kind(step, go):
            for kind in range(kinds):
                run_if((step // 3) % kinds == kind, lambda kind=kind: go(kind))

        def begin(step):
            def go(kind):
                for copy in fetch(kind, step):
                    copy.start()
            per_kind(step, go)

        def away(kind):
            return send(gone.at[kind], came.at[kind], gs.at[kind], cs.at[kind], place.dev(x=place.back("x", 1)))

        def meet(n):
            q, distance = n // plan.long, plan.long - 1 - n % plan.long
            for d in sorted({-distance, distance}):
                total.dest(d, q)

        ks = from_far(plan.wide)
        total.start(ks)
        begin(jnp.int32(0))
        for k in ks[:-1]:
            total.stage_over(k)

        @pl.loop(0, steps)
        def _(step):
            run_if(step + 1 < steps, lambda: begin(step + 1))

            def ready(kind):
                for copy in fetch(kind, step):
                    copy.wait()
            per_kind(step, ready)
            slot = step % 2
            product = inner_left(left[slot], right[slot])
            fresh = step % 3 == 0

            @pl.when(fresh)
            def _():
                acc[...] = product

            @pl.when(jnp.logical_not(fresh))
            def _():
                acc[...] += product

            def done(kind):
                @pl.when(step < 3 * kinds)
                def _():
                    gone[kind] = acc[...].astype(jnp.bfloat16)
                    away(kind).start()

                @pl.when(step >= 3 * kinds)
                def _():
                    outs[kind][...] = acc[...]

            run_if(step % 3 == 2, lambda: per_kind(step, done))
            for n, at in enumerate(hooks):
                run_if(step == at, lambda n=n: meet(n))

        for n in range(len(hooks), pieces * plan.long):
            meet(n)
        out_ref[...] = total.result()
        for kind in range(kinds):
            away(kind).wait_recv()
            piece = 32

            @pl.loop(0, half // piece)
            def _(i, kind=kind):
                at = pl.ds(pl.multiple_of(i * piece, piece), piece)
                outs[kind][at, :] = outs[kind][at, :] + came[kind, at, :].astype(jnp.float32)

        for kind in range(kinds):
            away(kind).wait_send()
        total.drain()

    anywhere = pl.BlockSpec(memory_space=pl.ANY)
    sem = lambda n: pltpu.SemaphoreType.DMA((n,))
    outs = [jax.ShapeDtypeStruct((rows, width), parts.dtype)] + [jax.ShapeDtypeStruct((half, ff), jnp.float32)] * kinds
    return pl.pallas_call(
        kernel,
        out_shape=tuple(outs),
        in_specs=[anywhere] * 6,
        out_specs=tuple(pl.BlockSpec(memory_space=pltpu.VMEM) for _ in outs),
        scratch_shapes=[
            pltpu.VMEM((half, ff), jnp.float32),
            pltpu.VMEM((2, depth, half), jnp.bfloat16),
            pltpu.VMEM((2, depth, ff), jnp.bfloat16),
            pltpu.VMEM((kinds, half, ff), jnp.bfloat16),
            pltpu.VMEM((kinds, half, ff), jnp.bfloat16),
            sem(2), sem(2), sem(kinds), sem(kinds),
        ] + RowSum.scratch(plan, rows, width, parts.dtype, pieces),
        compiler_params=pltpu.CompilerParams(
            collective_id=collective_id, has_side_effects=True, vmem_limit_bytes=VMEM_MOST),
        name="scatter_experts",
    )(parts, *lefts, *rights)


def visible_bias(shape, first_key, start, first_query):
    key_pos = first_key + lax.broadcasted_iota(jnp.int32, shape, 0)
    query_pos = first_query + lax.broadcasted_iota(jnp.int32, shape, 1)
    seen = jnp.logical_and(key_pos >= start, key_pos <= query_pos)
    return jnp.where(seen, 0.0, masked_value)


def lanes(first):
    return pl.ds(pl.multiple_of(first, HEAD), HEAD)


def turned(values, cosine, sine):
    return values * cosine + pltpu.roll(values, HEAD // 2, 1) * sine


def whole_spec(*shape):
    return pl.BlockSpec(shape, lambda *s: (0,) * len(shape))


def project_kernel(x_ref, gain_ref, cos_ref, sin_ref, wq_ref, wk_ref, wv_ref, hid_ref, q_ref, kv_ref, hidden):
    @pl.when(pl.program_id(0) == 0)
    def _():
        hidden[...] = normed(x_ref[...].astype(jnp.float32), gain_ref[...]).astype(jnp.bfloat16)
        hid_ref[...] = hidden[...]

    cosine, sine = cos_ref[...], sin_ref[...]
    q = jnp.dot(hidden[...], wq_ref[...], preferred_element_type=jnp.float32)
    k = jnp.dot(hidden[...], wk_ref[...], preferred_element_type=jnp.float32)
    v = jnp.dot(hidden[...], wv_ref[...], preferred_element_type=jnp.float32)
    for h in range(q.shape[1] // HEAD):
        at = slice(h * HEAD, (h + 1) * HEAD)
        q_ref[:, at] = (turned(q[:, at], cosine, sine) * HEAD ** (-0.5)).astype(jnp.bfloat16)
        kv_ref[:, 2 * h * HEAD : (2 * h + 1) * HEAD] = turned(k[:, at], cosine, sine).astype(jnp.bfloat16)
        kv_ref[:, (2 * h + 1) * HEAD : (2 * h + 2) * HEAD] = v[:, at].astype(jnp.bfloat16)


def project(tokens, gain, cosine, sine, wq, wk, wv):
    rows, width = tokens.shape
    tile = 2 * HEAD
    column = pl.BlockSpec((width, tile), lambda i: (0, i))
    return pl.pallas_call(
        project_kernel,
        out_shape=(
            jax.ShapeDtypeStruct((rows, width), jnp.bfloat16),
            jax.ShapeDtypeStruct((rows, width), jnp.bfloat16),
            jax.ShapeDtypeStruct((rows, 2 * width), jnp.bfloat16),
        ),
        grid=(width // tile,),
        in_specs=[whole_spec(rows, width), whole_spec(1, width), whole_spec(rows, HEAD), whole_spec(rows, HEAD),
                  column, column, column],
        out_specs=(whole_spec(rows, width), pl.BlockSpec((rows, tile), lambda i: (0, i)),
                   pl.BlockSpec((rows, 2 * tile), lambda i: (0, i))),
        scratch_shapes=[pltpu.VMEM((rows, width), jnp.bfloat16)],
        cost_estimate=pl.CostEstimate(flops=6 * rows * width * width, bytes_accessed=6 * width * width, transcendentals=0),
        name="project",
    )(tokens, gain[None, :], cosine, sine, wq, wk, wv)


def attend_kernel(info, q_ref, start_ref, kv_ref, mixed_ref, low_ref, total_ref, bias, top, norm):
    step = pl.program_id(0)
    me, first_block = info[0], info[1]
    rows = q_ref.shape[0]
    block = me - step

    @pl.when(step == 0)
    def _():
        top[...] = jnp.full_like(top, masked_value)
        norm[...] = jnp.zeros_like(norm)
        mixed_ref[...] = jnp.zeros_like(mixed_ref)

    @pl.when(block >= first_block)
    def _():
        bias[...] = visible_bias((rows, rows), block * rows, start_ref[...], me * rows)

        @pl.loop(0, HEADS, unroll=2)
        def _(h):
            keys, values = kv_ref[0, :, lanes(2 * h * HEAD)], kv_ref[0, :, lanes((2 * h + 1) * HEAD)]
            scores = inner_right(keys, q_ref[:, lanes(h * HEAD)]) + bias[...]
            old = top[h]
            new = jnp.maximum(old, jnp.max(scores, axis=0, keepdims=True))
            weights = jnp.exp(scores - new)
            shrink = jnp.exp(old - new)
            top[h] = new
            norm[h] = norm[h] * shrink + jnp.sum(weights, axis=0, keepdims=True)
            mixed_ref[h] = mixed_ref[h] * shrink + inner_left(values, weights.astype(jnp.bfloat16))

    @pl.when(step == pl.num_programs(0) - 1)
    def _():
        for h in range(HEADS):
            mixed = mixed_ref[h] / norm[h]
            mixed_ref[h] = mixed
            low_ref[:, h * HEAD : (h + 1) * HEAD] = mixed.T.astype(jnp.bfloat16)
            total_ref[h] = top[h] + jnp.log(norm[h])


def attend(info, queries, start, pairs):
    rows, width = queries.shape
    steps = pairs.shape[0] // 2 + 1
    return pl.pallas_call(
        attend_kernel,
        out_shape=(
            jax.ShapeDtypeStruct((HEADS, HEAD, rows), jnp.float32),
            jax.ShapeDtypeStruct((rows, width), jnp.bfloat16),
            jax.ShapeDtypeStruct((HEADS, 1, rows), jnp.float32),
        ),
        grid_spec=pltpu.PrefetchScalarGridSpec(
            num_scalar_prefetch=1,
            grid=(steps,),
            in_specs=[
                whole_spec(rows, width),
                whole_spec(1, rows),
                pl.BlockSpec((1, rows, 2 * width), lambda s, info: (jnp.maximum(info[0] - s, info[1]), 0, 0)),
            ],
            out_specs=(whole_spec(HEADS, HEAD, rows), whole_spec(rows, width), whole_spec(HEADS, 1, rows)),
            scratch_shapes=[
                pltpu.VMEM((rows, rows), jnp.float32),
                pltpu.VMEM((HEADS, 1, rows), jnp.float32),
                pltpu.VMEM((HEADS, 1, rows), jnp.float32),
            ],
        ),
        cost_estimate=pl.CostEstimate(
            flops=4 * rows * rows * width * steps, bytes_accessed=4 * rows * width * steps, transcendentals=0
        ),
        name="attend",
    )(info, queries, start, pairs)


def attend_back_kernel(
    info, q_ref, g_ref, mixed_ref, start_ref, total_ref, cos_ref, sin_ref, kv_ref, dkv_ref, dq_ref, bias, acc, term
):
    step = pl.program_id(0)
    me, first_block = info[0], info[1]
    rows = q_ref.shape[0]
    block = me - step

    @pl.when(step == 0)
    def _():
        acc[...] = jnp.zeros_like(acc)
        for h in range(HEADS):
            grads = g_ref[:, h * HEAD : (h + 1) * HEAD].astype(jnp.float32).T
            term[h] = jnp.sum(grads * mixed_ref[h], axis=0, keepdims=True)

    @pl.when(block >= first_block)
    def _():
        bias[...] = visible_bias((rows, rows), block * rows, start_ref[...], me * rows)

        @pl.loop(0, HEADS, unroll=2)
        def _(h):
            early, late, at = lanes(2 * h * HEAD), lanes((2 * h + 1) * HEAD), lanes(h * HEAD)
            keys, values = kv_ref[0, :, early], kv_ref[0, :, late]
            queries, grads = q_ref[:, at], g_ref[:, at]
            probs = jnp.exp(inner_right(keys, queries) + bias[...] - total_ref[h])
            prob_grad = inner_right(values, grads)
            score_grad = (probs * (prob_grad - term[h])).astype(jnp.bfloat16)
            dkv_ref[0, :, late] = jnp.dot(
                probs.astype(jnp.bfloat16), grads, preferred_element_type=jnp.float32
            ).astype(jnp.bfloat16)
            dkv_ref[0, :, early] = jnp.dot(
                score_grad, queries, preferred_element_type=jnp.float32
            ).astype(jnp.bfloat16)
            acc[h] += inner_left(keys, score_grad)

    @pl.when(jnp.logical_and(block >= 0, block < first_block))
    def _():
        dkv_ref[...] = jnp.zeros_like(dkv_ref)

    @pl.when(step == pl.num_programs(0) - 1)
    def _():
        for h in range(HEADS):
            back = turned(acc[h].T * HEAD ** (-0.5), cos_ref[...], -sin_ref[...])
            dq_ref[:, h * HEAD : (h + 1) * HEAD] = back.astype(jnp.bfloat16)


def attend_back(info, queries, grads, mixed, start, total, cosine, sine, pairs):
    rows, width = queries.shape
    count = pairs.shape[0]
    steps = count // 2 + 1
    return pl.pallas_call(
        attend_back_kernel,
        out_shape=(
            jax.ShapeDtypeStruct(pairs.shape, jnp.bfloat16),
            jax.ShapeDtypeStruct((rows, width), jnp.bfloat16),
        ),
        grid_spec=pltpu.PrefetchScalarGridSpec(
            num_scalar_prefetch=1,
            grid=(steps,),
            in_specs=[
                whole_spec(rows, width),
                whole_spec(rows, width),
                whole_spec(HEADS, HEAD, rows),
                whole_spec(1, rows),
                whole_spec(HEADS, 1, rows),
                whole_spec(rows, HEAD),
                whole_spec(rows, HEAD),
                pl.BlockSpec((1, rows, 2 * width), lambda s, info: (jnp.maximum(info[0] - s, info[1]), 0, 0)),
            ],
            out_specs=(
                pl.BlockSpec((1, rows, 2 * width), lambda s, info: (jnp.maximum(info[0] - s, 0), 0, 0)),
                whole_spec(rows, width),
            ),
            scratch_shapes=[
                pltpu.VMEM((rows, rows), jnp.float32),
                pltpu.VMEM((HEADS, HEAD, rows), jnp.float32),
                pltpu.VMEM((HEADS, 1, rows), jnp.float32),
            ],
        ),
        cost_estimate=pl.CostEstimate(
            flops=10 * rows * rows * width * steps, bytes_accessed=8 * rows * width * steps, transcendentals=0
        ),
        name="attend_back",
    )(info, queries, grads, mixed, start, total, cosine, sine, pairs)


def finish_kernel(
    x_ref, gain_ref, res_ref, hid_ref, q_ref, kv_ref, cos_ref, sin_ref, wq_ref, wk_ref, wv_ref,
    dq_ref, dk_ref, dv_ref, out_ref, gain_out, acc,
):
    step = pl.program_id(0)

    @pl.when(step == 0)
    def _():
        acc[...] = jnp.zeros_like(acc)

    cosine, sine = cos_ref[...], sin_ref[...]
    count = q_ref.shape[1] // HEAD
    keys = jnp.concatenate(
        [turned(kv_ref[:, 2 * h * HEAD : (2 * h + 1) * HEAD].astype(jnp.float32), cosine, -sine).astype(jnp.bfloat16)
         for h in range(count)], axis=1)
    values = jnp.concatenate([kv_ref[:, (2 * h + 1) * HEAD : (2 * h + 2) * HEAD] for h in range(count)], axis=1)
    grads = (q_ref[...], keys, values)
    acc[...] += (
        inner_right(grads[0], wq_ref[...]) + inner_right(grads[1], wk_ref[...]) + inner_right(grads[2], wv_ref[...])
    )
    hidden = hid_ref[...]
    for ref, grad in zip((dq_ref, dk_ref, dv_ref), grads):
        ref[...] = inner_left(hidden, grad).astype(jnp.bfloat16)

    @pl.when(step == pl.num_programs(0) - 1)
    def _():
        values, gain, grad = x_ref[...].astype(jnp.float32), gain_ref[...], acc[...]
        scale = lax.rsqrt(jnp.mean(values * values, axis=1, keepdims=True) + epsilon)
        inner = jnp.mean(gain * grad * values, axis=1, keepdims=True)
        part = scale * gain * grad - values * (scale * scale * scale) * inner
        out_ref[...] = (res_ref[...] + part).astype(jnp.bfloat16)
        gain_out[...] = jnp.sum(grad * values * scale, axis=0, keepdims=True)


def finish(tokens, gain, residual_grad, hidden, query_grad, pair_grads, cosine, sine, wq, wk, wv):
    rows, width = tokens.shape
    tile = 2 * HEAD
    column = pl.BlockSpec((width, tile), lambda i: (0, i))
    return pl.pallas_call(
        finish_kernel,
        out_shape=(
            jax.ShapeDtypeStruct((width, width), jnp.bfloat16),
            jax.ShapeDtypeStruct((width, width), jnp.bfloat16),
            jax.ShapeDtypeStruct((width, width), jnp.bfloat16),
            jax.ShapeDtypeStruct((rows, width), jnp.bfloat16),
            jax.ShapeDtypeStruct((1, width), jnp.float32),
        ),
        grid=(width // tile,),
        in_specs=[whole_spec(rows, width), whole_spec(1, width), whole_spec(rows, width), whole_spec(rows, width),
                  pl.BlockSpec((rows, tile), lambda i: (0, i)), pl.BlockSpec((rows, 2 * tile), lambda i: (0, i)),
                  whole_spec(rows, HEAD), whole_spec(rows, HEAD), column, column, column],
        out_specs=(column, column, column, whole_spec(rows, width), whole_spec(1, width)),
        scratch_shapes=[pltpu.VMEM((rows, width), jnp.float32)],
        cost_estimate=pl.CostEstimate(flops=12 * rows * width * width, bytes_accessed=12 * width * width, transcendentals=0),
        name="finish",
    )(tokens, gain[None, :], residual_grad, hidden, query_grad, pair_grads, cosine, sine, wq, wk, wv)


def experts_kernel(
    where_ref, x_ref, g_ref, rank_row, rank_col, share_row, wg_ref, wu_ref, wd_ref,
    back_ref, routed_ref, in_ref, pre_ref, lift_ref, mid_ref, og_ref, grads,
):
    blocks, rows, side = x_ref.shape
    capacity = in_ref.shape[0] // blocks
    width = og_ref.shape[1]
    dot = lambda left, right: jnp.dot(left, right, preferred_element_type=jnp.float32)
    shares = []
    for i in range(blocks):
        at = slice(i * capacity, (i + 1) * capacity)
        hit = rank_row[i] == lax.broadcasted_iota(jnp.int32, (capacity, rows), 0)
        pick = jnp.where(hit, 1.0, 0.0)
        shares.append(jnp.sum(pick * share_row[i], axis=1, keepdims=True))
        pick = pick.astype(jnp.bfloat16)
        in_ref[at, :] = dot(pick, x_ref[i, :, :width]).astype(jnp.bfloat16)
        grads[at, :] = dot(pick, g_ref[i]).astype(jnp.bfloat16)
    share = jnp.concatenate(shares, axis=0)
    pre = dot(in_ref[...], wg_ref[0])
    lift = dot(in_ref[...], wu_ref[0])
    silu, slope = silu_parts(pre)
    mid_ref[...] = (silu * lift).astype(jnp.bfloat16)
    lift_slope = lift * slope
    result = dot(mid_ref[...], wd_ref[0]).astype(jnp.bfloat16).astype(jnp.float32)
    grad = grads[...].astype(jnp.float32)
    gate_grad = jnp.sum(result * grad, axis=1, keepdims=True)
    og_ref[...] = (share * grad).astype(jnp.bfloat16)
    given = (share * result).astype(jnp.bfloat16)
    mid_grad = inner_right(og_ref[...], wd_ref[0])
    pre_ref[...] = (mid_grad * lift_slope).astype(jnp.bfloat16)
    lift_ref[...] = (mid_grad * silu).astype(jnp.bfloat16)
    in_grad = (inner_right(pre_ref[...], wg_ref[0]) + inner_right(lift_ref[...], wu_ref[0])).astype(jnp.bfloat16)
    lane = lax.broadcasted_iota(jnp.int32, (blocks * capacity, side - width), 1)
    high = gate_grad.astype(jnp.bfloat16).astype(jnp.float32)
    extra = jnp.where(lane == where_ref[0], high, jnp.where(lane == where_ref[1], gate_grad - high, 0.0))
    extra = extra.astype(jnp.bfloat16)
    for i in range(blocks):
        at = slice(i * capacity, (i + 1) * capacity)
        hit = rank_col[i] == lax.broadcasted_iota(jnp.int32, (rows, capacity), 1)
        put = jnp.where(hit, 1.0, 0.0).astype(jnp.bfloat16)
        back_ref[i, :, :width] = dot(put, in_grad[at, :]).astype(jnp.bfloat16)
        back_ref[i, :, width:] = dot(put, extra[at, :]).astype(jnp.bfloat16)
        routed_ref[i] = dot(put, given[at, :]).astype(jnp.bfloat16)


def run_experts(places, arrived, grads, rank, share, gate, up, down, capacity):
    count, rows, side = arrived.shape
    width, ff = gate.shape[1], gate.shape[2]
    blocks = 384 // capacity
    flat = count * capacity
    once = lambda *shape: pl.BlockSpec(shape, lambda i, p: (0,) * len(shape), pipeline_mode=pl.Buffered(1))
    lead = lambda *shape: pl.BlockSpec((blocks,) + shape, lambda i, p: (i, 0, 0))
    tall = lambda wide: pl.BlockSpec((blocks * capacity, wide), lambda i, p: (i, 0))
    shape = lambda *dims: jax.ShapeDtypeStruct(dims, jnp.bfloat16)
    return pl.pallas_call(
        experts_kernel,
        out_shape=(shape(count, rows, side), shape(count, rows, width), shape(flat, width), shape(flat, ff),
                   shape(flat, ff), shape(flat, ff), shape(flat, width)),
        grid_spec=pltpu.PrefetchScalarGridSpec(
            num_scalar_prefetch=1,
            grid=(count // blocks,),
            in_specs=[lead(rows, side), lead(rows, width), lead(1, rows), lead(rows, 1), lead(1, rows),
                      once(1, width, ff), once(1, width, ff), once(1, ff, width)],
            out_specs=(lead(rows, side), lead(rows, width), tall(width), tall(ff), tall(ff), tall(ff), tall(width)),
            scratch_shapes=[pltpu.VMEM((blocks * capacity, width), jnp.bfloat16)],
        ),
        compiler_params=pltpu.CompilerParams(vmem_limit_bytes=VMEM_MOST),
        cost_estimate=pl.CostEstimate(flops=16 * flat * width * ff, bytes_accessed=16 * flat * width, transcendentals=0),
        name="run_experts",
    )(places, arrived, grads, rank[:, None, :], rank[:, :, None], share[:, None, :], gate, up, down)


def attend_back_sum(queries, grads, mixed, start, total, cosine, sine, pairs, parts, collective_id):
    rows, width = queries.shape
    ep_count = pairs.shape[0]
    part_rows, part_width = parts[0].shape[1], sum(part.shape[2] for part in parts)
    plan, pieces = Plan(ep_count, True), 4
    place = Place(lax.axis_size("grp"), ep_count)
    n, wide = plan.planes(), plan.wide
    cuts = [0, part_width // HEAD // 2 * HEAD, part_width]

    def kernel(q_ref, g_ref, mixed_ref, start_ref, total_ref, cos_ref, sin_ref, pair_ref, *refs):
        sources, refs = refs[: len(parts)], refs[len(parts) :]
        out_ref, pair_out, dq_ref, bias, acc, term, kv, staged, kv_sem = refs[:9]
        refs = refs[9:]
        place.locate()
        sums = []
        for i in range(2):
            sums.append(WholeSum(place, "xba", pieces_of(sources, cuts[i], cuts[i + 1]), refs[:14]))
            refs = refs[14:]
        sum_rows = RowSum(plan, pieces, staged, refs)
        a, b, c = sum_rows.a, sum_rows.b, sum_rows.c
        me = plan.slot(a, b, c)
        order, ks = sum_rows.order, from_far(wide)
        turns = [(k, d) for k in ks for d in order]

        def block(turn, other):
            k, d = turns[turn]
            b0, c0 = sum_rows.source(k), jnp.where(other, 1 - c, c)
            there = both(plan.inside(a - d), plan.need(d, b, c, b0, c0))
            return there, plan.slot(a - d, b0, c0)

        def fetch(turn, other):
            there, slot = block(turn, other)
            held = jnp.where(other, 0, 1)
            return there, lambda: pltpu.make_async_copy(pair_ref.at[slot], kv.at[held], kv_sem.at[held])

        def begin(turn, other):
            there, go = fetch(turn, other)
            run_if(there, lambda: go().start())

        def compute(turn, other, target):
            there, slot = block(turn, other)
            held = 0 if other else 1

            def work():
                fetch(turn, other)[1]().wait()
                bias[...] = visible_bias((rows, rows), slot * rows, start_ref[...], me * rows)

                @pl.loop(0, HEADS, unroll=2)
                def _(h):
                    early, late, at = lanes(2 * h * HEAD), lanes((2 * h + 1) * HEAD), lanes(h * HEAD)
                    keys, values = kv[held, :, early], kv[held, :, late]
                    own, grad = q_ref[:, at], g_ref[:, at]
                    probs = jnp.exp(inner_right(keys, own) + bias[...] - total_ref[h])
                    score_grad = (probs * (inner_right(values, grad) - term[h])).astype(jnp.bfloat16)
                    target[:, late] = jnp.dot(
                        probs.astype(jnp.bfloat16), grad, preferred_element_type=jnp.float32
                    ).astype(jnp.bfloat16)
                    target[:, early] = jnp.dot(
                        score_grad, own, preferred_element_type=jnp.float32
                    ).astype(jnp.bfloat16)
                    acc[h] += inner_left(keys, score_grad)

            run_if(there, work)

        def turn_of(turn):
            k, d = turns[turn]
            i = plan.plane(a, d)
            compute(turn, True, staged.at[i, k])
            if turn + 1 < len(turns):
                begin(turn + 1, True)
            cond = sum_rows.cross(d, k, 0)[0]
            for q in range(pieces):
                run_if(cond, lambda q=q: sum_rows.cross(d, k, q)[1]().start())
            compute(turn, False, sum_rows.held.at[i, k])
            if turn + 1 < len(turns):
                begin(turn + 1, False)

        def pass_on(turn):
            k, d = turns[turn]

            @pl.loop(0, pieces)
            def _(q):
                sum_rows.first(d, k, q)
                cond, go = sum_rows.over(d, k, q)
                run_if(cond, lambda: go().start())

        begin(0, True)
        begin(0, False)
        acc[...] = jnp.zeros_like(acc)
        for h in range(HEADS):
            grad = g_ref[:, h * HEAD : (h + 1) * HEAD].astype(jnp.float32).T
            term[h] = jnp.sum(grad * mixed_ref[h], axis=0, keepdims=True)
        place.greet()
        far = (wide - 1) * len(order)
        for one in sums:
            for i in range(one.n1 - 1):
                one.start(i)
        turn_of(0)
        for one in sums:
            for i in range(one.n1 - 1):
                one.stage_core(i)
        for one in sums:
            one.start(one.n1 - 1)
        for turn in range(1, len(turns)):
            turn_of(turn)
            if turn <= far:
                pass_on(turn - 1)
            if turn == far:
                for one in sums:
                    one.stage_core(one.n1 - 1)
        for h in range(HEADS):
            back = turned(acc[h].T * HEAD ** (-0.5), cos_ref[...], -sin_ref[...])
            dq_ref[:, h * HEAD : (h + 1) * HEAD] = back.astype(jnp.bfloat16)
        sum_rows.stage_dests(0, 2)
        for k2 in from_far(sums[0].n2):
            sums[0].stage_one(k2)
        sum_rows.stage_dests(2, 3)
        sums[0].stage_two()
        for k2 in from_far(sums[1].n2):
            sums[1].stage_one(k2)
        sum_rows.stage_dests(3, 4)
        sums[1].stage_two()
        pair_out[...] = sum_rows.result()
        for i, one in enumerate(sums):
            one.stage_three(out_ref.at[:, pl.ds(cuts[i], cuts[i + 1] - cuts[i])])
        sum_rows.drain()
        for one in sums:
            one.drain()

    anywhere, near = pl.BlockSpec(memory_space=pl.ANY), pl.BlockSpec(memory_space=pltpu.VMEM)
    scratch = [
        pltpu.VMEM((rows, rows), jnp.float32),
        pltpu.VMEM((HEADS, HEAD, rows), jnp.float32),
        pltpu.VMEM((HEADS, 1, rows), jnp.float32),
        pltpu.VMEM((2, rows, 2 * width), jnp.bfloat16),
        pltpu.VMEM((n, wide, rows, 2 * width), jnp.bfloat16),
        pltpu.SemaphoreType.DMA((2,)),
    ]
    for i in range(2):
        scratch += WholeSum.scratch(place.sizes, "xba", part_rows, cuts[i + 1] - cuts[i], parts[0].dtype, len(parts))
    scratch += RowSum.scratch(plan, rows, 2 * width, pairs.dtype, pieces)
    return pl.pallas_call(
        kernel,
        out_shape=(jax.ShapeDtypeStruct((part_rows, part_width), jnp.float32),
                   jax.ShapeDtypeStruct((rows, 2 * width), pairs.dtype),
                   jax.ShapeDtypeStruct((rows, width), jnp.bfloat16)),
        in_specs=[near] * 7 + [anywhere] * (1 + len(parts)),
        out_specs=(near, near, near),
        scratch_shapes=scratch,
        compiler_params=pltpu.CompilerParams(
            collective_id=collective_id, has_side_effects=True, vmem_limit_bytes=VMEM_MOST),
        name="attend_back_sum",
    )(queries, grads, mixed, start, total, cosine, sine, pairs, *parts)


def local(
    tokens,
    doc_lengths,
    expert_ids,
    out_grad,
    mixer_gain,
    query_weight,
    key_weight,
    value_weight,
    output_weight,
    ffn_gain,
    router_weight,
    shared_gate,
    shared_up,
    shared_down,
    expert_gate,
    expert_up,
    expert_down,
):
    rows, width = tokens.shape[1], tokens.shape[2]
    ep_count = lax.axis_size("ep")
    device_count = ep_count * lax.axis_size("grp")
    ep_index = lax.axis_index("ep")
    expert_count = router_weight.shape[1]
    capacity = min(rows, 12 * rows * TOP // (7 * expert_count))
    low = lambda v: v.astype(jnp.bfloat16)
    wide = lambda v: v.astype(jnp.float32)
    dot = lambda left, right: jnp.dot(left, right, preferred_element_type=jnp.float32)

    grad_low = out_grad[0]

    doc_ends = jnp.cumsum(doc_lengths[0])
    query_pos = ep_index * rows + jnp.arange(rows, dtype=jnp.int32)
    before = query_pos[:, None] >= doc_ends[None, :]
    start = jnp.max(jnp.where(before, doc_ends[None, :], 0), axis=1)
    info = jnp.stack([ep_index, start[0] // rows]).astype(jnp.int32)
    half_dim = HEAD // 2
    frequency = rope_base ** (-jnp.arange(half_dim, dtype=jnp.float32) / half_dim)
    angles = wide(query_pos)[:, None] * frequency[None, :]
    cosine, sine = jnp.cos(angles), jnp.sin(angles)
    cosine = jnp.concatenate([cosine, cosine], axis=1)
    sine = jnp.concatenate([-sine, sine], axis=1)

    stream = wide(tokens[0])
    hidden_low, queries, own_pairs = project(
        tokens[0], mixer_gain, cosine, sine, query_weight, key_weight, value_weight
    )
    pairs = gather_rows(own_pairs, True, 1, 8)
    grad_later, pairs = lax.optimization_barrier((grad_low, pairs))
    grads_all = lax.all_gather(grad_later, "ep", axis=0, tiled=False)
    mixed, mixed_low, log_total = attend(info, queries, start[None, :], pairs)
    mixer_out = dot(mixed_low, output_weight)
    residual = stream + mixer_out
    ffn_low = low(normed(residual, ffn_gain))

    logits = dot(ffn_low, router_weight)
    experts = jnp.arange(expert_count, dtype=jnp.int32)
    assigned = jnp.any(expert_ids[0][:, :, None] == experts[None, None, :], axis=1)
    shown = jnp.where(assigned, logits, masked_value)
    powers = jnp.where(assigned, jnp.exp(shown - jnp.max(shown, axis=1, keepdims=True)), 0.0)
    gate_probs = powers / jnp.sum(powers, axis=1, keepdims=True)
    probs_high = low(gate_probs)
    probs_rest = low(gate_probs - wide(probs_high))
    side = width + 2 * HEAD if 2 * expert_count > HEAD else width + HEAD
    pad = jnp.zeros((rows, side - width - 2 * expert_count), jnp.bfloat16)
    sent = jnp.concatenate([ffn_low, probs_high, probs_rest, pad], axis=1)
    arrived = gather_rows(sent, False, 2)

    own = experts[None, None, :] == ep_index
    high = arrived[:, :, width : width + expert_count]
    rest = arrived[:, :, width + expert_count : width + 2 * expert_count]
    share = jnp.sum(jnp.where(own, wide(high) + wide(rest), 0.0), axis=2)
    chosen = share > 0.0
    earlier = (jnp.arange(rows)[:, None] < jnp.arange(rows)[None, :]).astype(jnp.bfloat16)
    rank = dot(low(chosen), earlier).astype(jnp.int32)
    rank = jnp.where(chosen, rank, -1)
    places = jnp.stack([ep_index, expert_count + ep_index]).astype(jnp.int32)
    back, given, flat_in, pre_grad, lift_grad, middle, result_grad = run_experts(
        places, arrived, grads_all, rank, share, expert_gate, expert_up, expert_down, capacity
    )
    routed = wide(lax.psum_scatter(given, "ep", scatter_dimension=0))
    group_count = lax.axis_size("grp")
    if group_count == 2:
        back_sum, gate_sum, up_sum, down_sum = scatter_experts(
            back, (flat_in, result_grad), (pre_grad, lift_grad, middle), 3
        )
        gate_sum, up_sum, down_sum = gate_sum[None], up_sum[None], down_sum.T[None]
    else:
        back_sum = scatter_rows(back, False, 3)
        split = width // group_count
        own_down_grad = jnp.concatenate(
            [low(inner_left(middle, result_grad[:, i * split : (i + 1) * split])) for i in range(group_count)], axis=0
        )
        over_groups = lambda v: wide(lax.psum_scatter(v, "grp", scatter_dimension=0, tiled=True))[None]
        gate_sum = over_groups(low(inner_left(flat_in, pre_grad)))
        up_sum = over_groups(low(inner_left(flat_in, lift_grad)))
        down_sum = over_groups(own_down_grad)

    shared_pre = dot(ffn_low, shared_gate)
    shared_lift = dot(ffn_low, shared_up)
    shared_silu, shared_slope = silu_parts(shared_pre)
    shared_mid = low(shared_silu * shared_lift)
    shared_out = dot(shared_mid, shared_down)
    grad_out = wide(grad_low)
    shared_mid_grad = inner_right(grad_low, shared_down)
    shared_pre_grad = low(shared_mid_grad * shared_lift * shared_slope)
    shared_lift_grad = low(shared_mid_grad * shared_silu)
    ffn_grad = inner_right(shared_pre_grad, shared_gate) + inner_right(shared_lift_grad, shared_up)

    layer_out = residual + shared_out + routed
    gate_back = wide(back_sum[:, width : width + expert_count]) + wide(
        back_sum[:, width + expert_count : width + 2 * expert_count]
    )
    chosen_grad = gate_probs * (gate_back - jnp.sum(gate_probs * gate_back, axis=1, keepdims=True))
    logit_grad = low(chosen_grad)
    ffn_grad = ffn_grad + wide(back_sum[:, :width]) + inner_right(logit_grad, router_weight)
    _, ffn_pull = jax.vjp(normed, residual, ffn_gain)
    residual_part, ffn_gain_grad = ffn_pull(ffn_grad)
    residual_grad = grad_out + residual_part
    mixer_grad_low = low(residual_grad)
    mixed_grad = low(inner_right(mixer_grad_low, output_weight))
    by_device = lambda v: low(v).reshape(device_count, width // device_count, -1)
    early = [
        by_device(part)
        for part in (inner_left(ffn_low, shared_pre_grad), inner_left(ffn_low, shared_lift_grad),
                     inner_left(grad_low, shared_mid), inner_left(mixed_low, mixer_grad_low))
    ]
    if ep_count > 16:
        pair_parts, query_lin_grad = attend_back(
            info, queries, mixed_grad, mixed, start[None, :], log_total, cosine, sine, pairs
        )
        pair_grads = scatter_rows(pair_parts, True, 4)
        early_sum = scatter_whole(early, 5)
    else:
        early_sum, pair_grads, query_lin_grad = attend_back_sum(
            queries, mixed_grad, mixed, start[None, :], log_total, cosine, sine, pairs, early, 5
        )

    query_part, key_part, value_part, tokens_grad, mixer_gain_grad = finish(
        tokens[0], mixer_gain, residual_grad, hidden_low, query_lin_grad, pair_grads, cosine, sine,
        query_weight, key_weight, value_weight,
    )
    squares = jnp.stack(
        [jnp.sum(residual * residual), jnp.sum(mixer_out * mixer_out), jnp.sum(layer_out * layer_out)]
    )
    extras = jnp.concatenate(
        [inner_left(ffn_low, logit_grad), mixer_gain_grad.T, ffn_gain_grad[:, None],
         jnp.broadcast_to(squares[None, :], (width, 3))], axis=1
    )
    extras = jnp.pad(extras, ((0, 0), (0, HEAD - extras.shape[1])))
    late_sum = scatter_whole([by_device(v) for v in (query_part, key_part, value_part, extras)], 6)
    extra_sum = late_sum[:, 3 * width :]
    entry_count = rows * device_count * width
    stream_rms = jnp.sqrt(extra_sum[0, expert_count + 2 : expert_count + 5] / entry_count)
    ff = shared_gate.shape[1]
    return (
        low(layer_out)[None],
        tokens_grad[None],
        extra_sum[:, expert_count],
        late_sum[:, :width],
        late_sum[:, width : 2 * width],
        late_sum[:, 2 * width : 3 * width],
        early_sum[:, 3 * ff :],
        extra_sum[:, expert_count + 1],
        extra_sum[:, :expert_count],
        early_sum[:, :ff],
        early_sum[:, ff : 2 * ff],
        early_sum[:, 2 * ff : 3 * ff].T,
        gate_sum,
        up_sum,
        down_sum,
        stream_rms,
    )


def solution(mesh):
    return jax.shard_map(
        local,
        mesh=mesh,
        in_specs=(
            P("grp", "ep", None),
            P("grp", None),
            P("grp", "ep", None),
            P("grp", "ep", None),
            P(),
            P(),
            P(),
            P(),
            P(),
            P(),
            P(),
            P(),
            P(),
            P(),
            P("ep", None, None),
            P("ep", None, None),
            P("ep", None, None),
        ),
        out_specs=(
            P("grp", "ep", None),
            P("grp", "ep", None),
            P(("grp", "ep")),
            P(("grp", "ep"), None),
            P(("grp", "ep"), None),
            P(("grp", "ep"), None),
            P(("grp", "ep"), None),
            P(("grp", "ep")),
            P(("grp", "ep"), None),
            P(("grp", "ep"), None),
            P(("grp", "ep"), None),
            P(None, ("grp", "ep")),
            P("ep", "grp", None),
            P("ep", "grp", None),
            P("ep", None, "grp"),
            P(),
        ),
        check_vma=False,
    )
```

```python
import functools

import jax
import jax.numpy as jnp
from jax import lax
from jax.experimental import pallas as pl
from jax.experimental.pallas import tpu as pltpu
from jax.sharding import PartitionSpec as P

HEADS = 10
HEAD = 128
TOP = 7

epsilon = 1e-06
rope_base = 10000.0
masked_value = -1e30


def normed(values, gain_vec):
    return (
        values * lax.rsqrt(jnp.mean(values * values, axis=-1, keepdims=True) + epsilon) * gain_vec
    )


def inner_left(left_op, right_op):
    return lax.dot_general(
        left_op, right_op, (((0,), (0,)), ((), ())), preferred_element_type=jnp.float32
    )


def inner_right(left_op, right_op):
    return lax.dot_general(
        left_op, right_op, (((1,), (1,)), ((), ())), preferred_element_type=jnp.float32
    )


def silu_parts(pre_act):
    sigmoid_val = jax.nn.sigmoid(pre_act)
    return (pre_act * sigmoid_val, sigmoid_val * (1.0 + pre_act * (1.0 - sigmoid_val)))


MESH = pl.DeviceIdType.MESH
COUPLES = 2
VMEM_MOST = 64 * 1024 * 1024 - 65536


def when(cond):
    if cond is True:
        return lambda f: f()
    if cond is False:
        return lambda f: None
    return pl.when(cond)


def both(*conds):
    out = True
    for cond in conds:
        if cond is False:
            return False
        if cond is True:
            continue
        out = cond if out is True else jnp.logical_and(out, cond)
    return out


class Plan:
    def __init__(self, ep_count, window):
        self.long = 4
        self.wide = ep_count // 8
        self.window = window
        self.steps = (
            list(range(self.long // 2 + 1))
            if window
            else list(range(-(self.long - 1), self.long))
        )

    def place(self):
        me = lax.axis_index("ep")
        return me // (2 * self.wide), (me // 2) % self.wide, me % 2

    def slot(self, a, b, c):
        return (a * self.wide + b) * 2 + c

    def plane(self, a, d):
        return d if self.window else jnp.clip(a - d, 0, self.long - 1)

    def planes(self):
        return len(self.steps) if self.window else self.long

    def inside(self, a):
        return jnp.logical_and(a >= 0, a < self.long)

    def need(self, d, b, c, b0, c0):
        if not self.window or 0 < d < self.long // 2:
            return True
        if d == 0:
            return jnp.logical_or(b0 < b, jnp.logical_and(b0 == b, c0 <= c))
        return jnp.logical_or(b0 > b, jnp.logical_and(b0 == b, c0 >= c))

    def need_pair(self, d, b, b0):
        if not self.window or 0 < d < self.long // 2:
            return True
        return b0 < b if d == 0 else b0 > b

    def greet(self, a, b, c):
        barrier = pltpu.get_barrier_semaphore()

        def signal(cond, dev):
            @when(cond)
            def _():
                pl.semaphore_signal(barrier, inc=1, device_id={"ep": dev}, device_id_type=MESH)

        signal(a + 1 < self.long, self.slot(a + 1, b, c))
        signal(a > 0, self.slot(a - 1, b, c))
        for k in range(1, self.wide):
            signal(True, self.slot(a, (b + k) % self.wide, c))
        signal(True, self.slot(a, b, 1 - c))
        ends = (a == 0).astype(jnp.int32) + (a == self.long - 1).astype(jnp.int32)
        pl.semaphore_wait(barrier, self.wide + 2 - ends)


def gather_kernel(plan, pieces, beside, x_ref, out_ref, ra, sa_up, sa_dn, rb, sb, rc, sc, own):
    a, b, c = plan.place()
    steps, wide = plan.steps, plan.wide
    at = {d: i for i, d in enumerate(steps)}
    rows = x_ref.shape[0] // pieces

    def part(q):
        return pl.ds(pl.multiple_of(q * rows, rows), rows)

    def copy(q, src, slot, ssem, rsem, dev):
        return pltpu.make_async_remote_copy(
            src_ref=src, dst_ref=out_ref.at[slot, part(q)], send_sem=ssem, recv_sem=rsem,
            device_id={"ep": dev}, device_id_type=MESH,
        )

    def hops(d, q):
        i = at[d]
        slot = plan.slot(a - d, b, c)
        src = x_ref.at[part(q)] if d == 0 else out_ref.at[slot, part(q)]
        real = plan.inside(a - d)
        out = []
        if d >= 0 and d + 1 in at:
            out.append((both(real, a + 1 < plan.long), lambda: copy(
                q, src, slot, sa_up.at[i, q], ra.at[at[d + 1], q], plan.slot(a + 1, b, c))))
        if d <= 0 and d - 1 in at:
            out.append((both(real, a > 0), lambda: copy(
                q, src, slot, sa_dn.at[i, q], ra.at[at[d - 1], q], plan.slot(a - 1, b, c))))
        for k in range(1, wide):
            to = (b + k) % wide
            out.append((both(real, plan.need_pair(d, to, b)), lambda k=k, to=to: copy(
                q, src, slot, sb.at[i, k, q], rb.at[i, k, q], plan.slot(a, to, c))))
        out.append((both(real, plan.need(d, b, 1 - c, b, c)), lambda: copy(
            q, src, slot, sc.at[i, 0, q], rc.at[i, 0, q], plan.slot(a, b, 1 - c))))
        return out

    def cross(d, k, q):
        i = at[d]
        b0 = (b + wide - k) % wide
        slot = plan.slot(a - d, b0, c)
        real = plan.inside(a - d)
        come = lambda: copy(q, x_ref.at[part(q)], slot, sb.at[i, k, q], rb.at[i, k, q], plan.slot(a, b, c))
        go = lambda: copy(q, out_ref.at[slot, part(q)], slot, sc.at[i, k, q], rc.at[i, k, q],
                          plan.slot(a, b, 1 - c))
        return (both(real, plan.need_pair(d, b, b0)), come,
                both(real, plan.need(d, b, 1 - c, b0, c)), go)

    plan.greet(a, b, c)
    keep = pltpu.make_async_copy(x_ref, out_ref.at[plan.slot(a, b, c)], own)

    @pl.loop(0, pieces)
    def _(q):
        for cond, go in hops(0, q):
            @when(cond)
            def _(go=go):
                go().start()

    keep.start()
    far = max(abs(d) for d in steps)
    for step in range(1, far + 3):
        beside(step - 1)

        @pl.loop(0, pieces)
        def _(q, step=step):
            for d in (step, -step):
                if d in at:
                    @when(plan.inside(a - d))
                    def _(d=d):
                        slot = plan.slot(a - d, b, c)
                        copy(q, x_ref.at[part(q)], slot, sa_up.at[0, q], ra.at[at[d], q],
                             plan.slot(a, b, c)).wait_recv()
                        for cond, go in hops(d, q):
                            @when(cond)
                            def _(go=go):
                                go().start()
            for d in sorted({step - 2, 2 - step}) if step > 1 else ():
                if d in at:
                    for k in range(1, wide):
                        came, come, goes, go = cross(d, k, q)
                        @when(came)
                        def _(come=come):
                            come().wait_recv()
                        @when(goes)
                        def _(go=go):
                            go().start()
    keep.wait()

    @pl.loop(0, pieces)
    def _(q):
        for d in steps:
            i = at[d]
            real = plan.inside(a - d)
            for k in range(wide):
                b0 = (b + wide - k) % wide
                slot = plan.slot(a - d, b0, 1 - c)
                @when(both(real, plan.need(d, b, c, b0, 1 - c)))
                def _(slot=slot, i=i, k=k):
                    copy(q, x_ref.at[part(q)], slot, sc.at[i, k, q], rc.at[i, k, q],
                         plan.slot(a, b, c)).wait_recv()
            for cond, go in hops(d, q):
                @when(cond)
                def _(go=go):
                    go().wait_send()
            for k in range(1, wide):
                came, come, goes, go = cross(d, k, q)
                @when(goes)
                def _(go=go):
                    go().wait_send()


def gather_rows(block, window, collective_id, pieces=4):
    ep_count = lax.axis_size("ep")
    plan = Plan(ep_count, window)
    n, wide = len(plan.steps), plan.wide
    sem = pltpu.SemaphoreType.DMA
    return pl.pallas_call(
        functools.partial(gather_kernel, plan, pieces, lambda n: None),
        out_shape=jax.ShapeDtypeStruct((ep_count,) + block.shape, block.dtype),
        in_specs=[pl.BlockSpec(memory_space=pltpu.VMEM)],
        out_specs=pl.BlockSpec(memory_space=pl.ANY),
        scratch_shapes=[sem((n, pieces)), sem((n, pieces)), sem((n, pieces)), sem((n, wide, pieces)),
                        sem((n, wide, pieces)), sem((n, wide, pieces)), sem((n, wide, pieces)), sem],
        compiler_params=pltpu.CompilerParams(collective_id=collective_id, has_side_effects=True),
        name="gather_rows",
    )(block)


def gather_shared(block, grads, gate, up, down, collective_id, pieces=4):
    ep_count = lax.axis_size("ep")
    plan = Plan(ep_count, False)
    n, wide = len(plan.steps), plan.wide
    rows, width = grads.shape
    ff = gate.shape[1]
    sem = pltpu.SemaphoreType.DMA
    stages = max(plan.steps) + 2
    tiles = ff // HEAD

    def kernel(x_ref, g_ref, wg_ref, wu_ref, wd_ref, out_ref, shared_ref, back_ref, dg_ref, du_ref, dd_ref, *sems):
        dot = lambda left, right: jnp.dot(left, right, preferred_element_type=jnp.float32)

        def tile(i):
            at = pl.ds(pl.multiple_of(i * HEAD, HEAD), HEAD)
            x, g = x_ref[:, :width], g_ref[...]
            w_gate, w_up, w_down = wg_ref[:, at], wu_ref[:, at], wd_ref[at, :]
            silu, slope = silu_parts(dot(x, w_gate))
            lift = dot(x, w_up)
            mid = (silu * lift).astype(jnp.bfloat16)
            mid_grad = inner_right(g, w_down)
            pre_grad = (mid_grad * lift * slope).astype(jnp.bfloat16)
            lift_grad = (mid_grad * silu).astype(jnp.bfloat16)
            out = dot(mid, w_down)
            back = inner_right(pre_grad, w_gate) + inner_right(lift_grad, w_up)

            @pl.when(i == 0)
            def _():
                shared_ref[...] = out
                back_ref[...] = back

            @pl.when(i > 0)
            def _():
                shared_ref[...] += out
                back_ref[...] += back

            dg_ref[:, at] = inner_left(x, pre_grad).astype(jnp.bfloat16)
            du_ref[:, at] = inner_left(x, lift_grad).astype(jnp.bfloat16)
            dd_ref[:, at] = inner_left(g, mid).astype(jnp.bfloat16)

        def beside(stage):
            pl.loop(tiles * stage // stages, tiles * (stage + 1) // stages)(tile)

        gather_kernel(plan, pieces, beside, x_ref, out_ref, *sems)

    near = pl.BlockSpec(memory_space=pltpu.VMEM)
    return pl.pallas_call(
        kernel,
        out_shape=(
            jax.ShapeDtypeStruct((ep_count,) + block.shape, block.dtype),
            jax.ShapeDtypeStruct((rows, width), jnp.float32),
            jax.ShapeDtypeStruct((rows, width), jnp.float32),
        ) + (jax.ShapeDtypeStruct((width, ff), jnp.bfloat16),) * 3,
        in_specs=[near] * 5,
        out_specs=(pl.BlockSpec(memory_space=pl.ANY),) + (near,) * 5,
        scratch_shapes=[sem((n, pieces)), sem((n, pieces)), sem((n, pieces)), sem((n, wide, pieces)),
                        sem((n, wide, pieces)), sem((n, wide, pieces)), sem((n, wide, pieces)), sem],
        compiler_params=pltpu.CompilerParams(
            collective_id=collective_id, has_side_effects=True, vmem_limit_bytes=VMEM_MOST),
        name="gather_shared",
    )(block, grads, gate, up, down)


def add_rows(dst, others, out=None):
    rows, width = dst.shape
    out = dst if out is None else out
    small = rows <= 64
    piece = 32 if rows % 32 == 0 else rows
    lanes = width if rows % 32 == 0 else 4 * HEAD
    whole = width // lanes * lanes

    def add(at):
        if len(others) == 1 and out.dtype == jnp.bfloat16:
            out[at] = dst[at] + others[0][at]
        else:
            total = dst[at].astype(jnp.float32)
            for other in others:
                total = total + other[at].astype(jnp.float32)
            out[at] = total.astype(out.dtype)

    if piece == rows:
        @pl.loop(0, whole // lanes)
        def _(i):
            add((slice(None), pl.ds(pl.multiple_of(i * lanes, lanes), lanes)))

        if whole < width:
            add((slice(None), pl.ds(whole, width - whole)))
    else:
        @pl.loop(0, rows // piece)
        def _(i):
            add((pl.ds(pl.multiple_of(i * piece, piece), piece), slice(None)))


def send(src, dst, ssem, rsem, to):
    return pltpu.make_async_remote_copy(
        src_ref=src, dst_ref=dst, send_sem=ssem, recv_sem=rsem, device_id=to, device_id_type=MESH
    )


def run_if(cond, go):
    @when(cond)
    def _():
        go()


class RowSum:
    @staticmethod
    def scratch(plan, rows, width, dtype, pieces):
        n, wide = plan.planes(), plan.wide
        blocks = lambda *lead: pltpu.VMEM(lead + (rows, width), dtype)
        sem = lambda *lead: pltpu.SemaphoreType.DMA(lead + (pieces,))
        return [blocks(n, wide), blocks(n, wide), blocks(n, wide - 1), blocks(n), blocks(1 if plan.window else n),
                sem(n, wide), sem(n, wide), sem(n, wide), sem(n, wide), sem(n), sem(n), sem(n), sem(n, wide)]

    def __init__(self, plan, pieces, p_ref, scratch):
        self.plan, self.pieces, self.p_ref = plan, pieces, p_ref
        (self.held, self.rcb, self.rbb, self.r_hi, self.r_lo,
         self.sc, self.rc, self.sb, self.rb, self.sa, self.rhi, self.rlo, self.ld) = scratch
        self.a, self.b, self.c = plan.place()
        self.ready = len(p_ref.shape) == 4
        self.rows = p_ref.shape[-2] // pieces
        self.order = sorted(plan.steps, key=lambda d: -abs(d))

    def part(self, q):
        return pl.ds(pl.multiple_of(q * self.rows, self.rows), self.rows)

    def dev(self, a, b, c):
        return {"ep": self.plan.slot(a, b, c)}

    def source(self, k):
        return (self.b + self.plan.wide - k) % self.plan.wide

    def load(self, d, k, q):
        p, i, b0 = self.plan, self.plan.plane(self.a, d), self.source(k)
        return both(p.inside(self.a - d), p.need(d, self.b, self.c, b0, self.c)), lambda: pltpu.make_async_copy(
            self.p_ref.at[p.slot(self.a - d, b0, self.c), self.part(q)], self.held.at[i, k, self.part(q)],
            self.ld.at[i, k, q])

    def cross(self, d, k, q):
        p, i, b0, c = self.plan, self.plan.plane(self.a, d), self.source(k), self.c
        real = p.inside(self.a - d)
        at = (i, k) if self.ready else (p.slot(self.a - d, b0, 1 - c),)
        return (both(real, p.need(d, self.b, c, b0, 1 - c)), lambda: send(
            self.p_ref.at[at + (self.part(q),)], self.rcb.at[i, k, self.part(q)],
            self.sc.at[i, k, q], self.rc.at[i, k, q], self.dev(self.a, self.b, 1 - c)),
            both(real, p.need(d, self.b, 1 - c, b0, c)))

    def over(self, d, k, q):
        p, i, b0 = self.plan, self.plan.plane(self.a, d), self.source(k)
        return both(p.inside(self.a - d), p.need_pair(d, self.b, b0)), lambda: send(
            self.held.at[i, k, self.part(q)], self.rbb.at[i, k - 1, self.part(q)], self.sb.at[i, k, q],
            self.rb.at[i, k, q], self.dev(self.a, b0, self.c))

    def along(self, d, q):
        p, i, up = self.plan, self.plan.plane(self.a, d), d < 0
        j = d - 1 if p.window else i
        return p.inside(self.a - d), lambda: send(
            self.held.at[i, 0, self.part(q)], (self.r_lo if up else self.r_hi).at[j, self.part(q)],
            self.sa.at[i, q], (self.rlo if up else self.rhi).at[j, q],
            self.dev(self.a + (1 if up else -1), self.b, self.c))

    def start(self, ks):
        for k in ks:
            @pl.loop(0, self.pieces)
            def _(q, k=k):
                for d in self.order:
                    for cond, go in (self.cross(d, k, q)[:2], self.load(d, k, q)):
                        run_if(cond, lambda go=go: go().start())

    def first(self, d, k, q):
        i = self.plan.plane(self.a, d)
        if not self.ready:
            cond, go = self.load(d, k, q)
            run_if(cond, lambda: go().wait())
        _, come_go, come = self.cross(d, k, q)

        def take():
            come_go().wait_recv()
            add_rows(self.held.at[i, k, self.part(q)], [self.rcb.at[i, k, self.part(q)]])

        run_if(come, take)

    def stage_over(self, k):
        @pl.loop(0, self.pieces)
        def _(q):
            for d in self.order:
                self.first(d, k, q)
                cond, go = self.over(d, k, q)
                run_if(cond, lambda go=go: go().start())

    def stage_dests(self, low, high):
        @pl.loop(low, high)
        def _(q):
            for d in self.order:
                self.dest(d, q)

    def dest(self, d, q):
        p, a, b, steps = self.plan, self.a, self.b, self.plan.steps
        i = p.plane(a, d)
        real = p.inside(a - d)
        mine = self.held.at[i, 0, self.part(q)]
        self.first(d, 0, q)
        for k in range(1, p.wide):
            def take(k=k):
                self.over(d, k, q)[1]().wait_recv()
                add_rows(mine, [self.rbb.at[i, k - 1, self.part(q)]])

            run_if(both(real, p.need_pair(d, (b + k) % p.wide, b)), take)
        for inner, cond, buf, sem in ((d >= 0 and d + 1 in steps, a + 1 < p.long, self.r_hi, self.rhi),
                                      (d <= 0 and d - 1 in steps, a > 0, self.r_lo, self.rlo)):
            if inner:
                def take(buf=buf, sem=sem):
                    send(mine, buf.at[i, self.part(q)], self.sa.at[i, q], sem.at[i, q],
                         self.dev(a, b, self.c)).wait_recv()
                    add_rows(mine, [buf.at[i, self.part(q)]])

                run_if(both(real, cond), take)
        if d:
            cond, go = self.along(d, q)
            run_if(cond, lambda: go().start())

    def result(self):
        return self.held[self.plan.plane(self.a, 0), 0]

    def drain(self):
        @pl.loop(0, self.pieces)
        def _(q):
            for d in self.plan.steps:
                sends = [self.cross(d, k, q)[:2] for k in range(self.plan.wide)]
                sends += [self.over(d, k, q) for k in range(1, self.plan.wide)]
                if d:
                    sends.append(self.along(d, q))
                for cond, go in sends:
                    run_if(cond, lambda go=go: go().wait_send())


def scatter_rows(parts, window, collective_id, pieces=4):
    ep_count, rows, width = parts.shape
    plan = Plan(ep_count, window)

    def kernel(p_ref, out_ref, *scratch):
        total = RowSum(plan, pieces, p_ref, scratch)
        plan.greet(total.a, total.b, total.c)
        ks = list(range(1, plan.wide)) + [0]
        total.start(ks)
        for k in ks[:-1]:
            total.stage_over(k)
        total.stage_dests(0, pieces)
        out_ref[...] = total.result()
        total.drain()

    return pl.pallas_call(
        kernel,
        out_shape=jax.ShapeDtypeStruct((rows, width), parts.dtype),
        in_specs=[pl.BlockSpec(memory_space=pl.ANY)],
        out_specs=pl.BlockSpec(memory_space=pltpu.VMEM),
        scratch_shapes=RowSum.scratch(plan, rows, width, parts.dtype, pieces),
        compiler_params=pltpu.CompilerParams(
            collective_id=collective_id, has_side_effects=True, vmem_limit_bytes=VMEM_MOST),
        name="scatter_rows",
    )(parts)


class Place:
    def __init__(self, groups, ep_count):
        self.sizes = {"x": groups, "a": 4, "b": ep_count // 8}

    def locate(self):
        me, wide = lax.axis_index("ep"), self.sizes["b"]
        self.at = {"x": lax.axis_index("grp"), "a": me // (2 * wide), "b": (me // 2) % wide, "c": me % 2}

    def dev(self, **moved):
        at = {**self.at, **moved}
        return {"grp": at["x"], "ep": (at["a"] * self.sizes["b"] + at["b"]) * 2 + at["c"]}

    def slot(self, **moved):
        at = {**self.at, **moved}
        return ((at["x"] * self.sizes["a"] + at["a"]) * self.sizes["b"] + at["b"]) * 2 + at["c"]

    def back(self, axis, k):
        return (self.at[axis] + self.sizes[axis] - k) % self.sizes[axis]

    def greet(self):
        peers = [self.dev(c=1 - self.at["c"])] + [
            self.dev(**{axis: self.back(axis, k)}) for axis in "xba" for k in range(1, self.sizes[axis])]
        barrier = pltpu.get_barrier_semaphore()
        for to in peers:
            pl.semaphore_signal(barrier, inc=1, device_id=to, device_id_type=MESH)
        pl.semaphore_wait(barrier, len(peers))


def from_far(size):
    return list(range(1, size)) + [0]


class WholeSum:
    @staticmethod
    def scratch(sizes, axes, rows, width, dtype, sources):
        n1, n2, n3 = (sizes[axis] for axis in axes)
        blocks = lambda *lead: pltpu.VMEM(lead + (rows, width), dtype)
        sem = lambda *lead: pltpu.SemaphoreType.DMA(lead)
        full = (n1, n2, n3)
        one, two, three = (n1 - 1, n2, n3), (n2 - 1, n3), (n3 - 1,)
        return [blocks(*full), blocks(*full), blocks(*one), blocks(*two), blocks(*three),
                sem(*full, sources), sem(*full, sources), sem(*full, sources), sem(*one), sem(*one), sem(*two), sem(*two), sem(*three), sem(*three)]

    def __init__(self, place, axes, pieces, scratch):
        self.place, self.axes, self.pieces = place, axes, pieces
        (self.held, self.rcb, self.r1, self.r2, self.r3,
         self.ld, self.sc, self.rc, self.s1, self.q1, self.s2, self.q2, self.s3, self.q3) = scratch
        self.n1, self.n2, self.n3 = (place.sizes[axis] for axis in axes)
        self.groups = [[(k1, k2, k3) for k2 in from_far(self.n2) for k3 in from_far(self.n3)]
                       for k1 in from_far(self.n1)]

    def slot(self, key, c):
        return self.place.slot(c=c, **{axis: self.place.back(axis, k) for axis, k in zip(self.axes, key)})

    def loads(self, key):
        c = self.place.at["c"]
        for n, (ref, first, at, count) in enumerate(self.pieces):
            frm, to = pl.ds(first, count), pl.ds(at, count)
            yield pltpu.make_async_copy(
                ref.at[self.slot(key, c), :, frm], self.held.at[key + (slice(None), to)],
                self.ld.at[key + (n,)])

    def crossings(self, key):
        c = self.place.at["c"]
        for n, (ref, first, at, count) in enumerate(self.pieces):
            frm, to = pl.ds(first, count), pl.ds(at, count)
            yield send(ref.at[self.slot(key, 1 - c), :, frm], self.rcb.at[key + (slice(None), to)],
                       self.sc.at[key + (n,)], self.rc.at[key + (n,)], self.place.dev(c=1 - c))

    def hop(self, level, key):
        buf, ssem, rsem = ((self.r1, self.s1, self.q1), (self.r2, self.s2, self.q2), (self.r3, self.s3, self.q3))[level]
        axis, k = self.axes[level], key[level]
        far = (k - 1,) + key[level + 1 :]
        return send(self.held.at[key], buf.at[far], ssem.at[far], rsem.at[far],
                    self.place.dev(**{axis: self.place.back(axis, k)}))

    def start(self, i):
        for key in self.groups[i]:
            for go in self.crossings(key):
                go.start()
            for go in self.loads(key):
                go.start()

    def stage_core(self, i):
        for key in self.groups[i]:
            for go in self.loads(key):
                go.wait()
            for go in self.crossings(key):
                go.wait_recv()
            add_rows(self.held.at[key], [self.rcb.at[key]])
            if key[0]:
                self.hop(0, key).start()

    def stage_one(self, k2):
        for k3 in from_far(self.n3):
            for k1 in range(1, self.n1):
                self.hop(0, (k1, k2, k3)).wait_recv()
            add_rows(self.held.at[0, k2, k3], [self.r1.at[k1 - 1, k2, k3] for k1 in range(1, self.n1)])
            if k2:
                self.hop(1, (0, k2, k3)).start()

    def stage_two(self):
        for k3 in from_far(self.n3):
            for k2 in range(1, self.n2):
                self.hop(1, (0, k2, k3)).wait_recv()
            add_rows(self.held.at[0, 0, k3], [self.r2.at[k2 - 1, k3] for k2 in range(1, self.n2)])
            if k3:
                self.hop(2, (0, 0, k3)).start()

    def stage_three(self, out):
        for k3 in range(1, self.n3):
            self.hop(2, (0, 0, k3)).wait_recv()
        add_rows(self.held.at[0, 0, 0], [self.r3.at[k3 - 1] for k3 in range(1, self.n3)], out)

    def drain(self):
        for group in self.groups:
            for key in group:
                for go in self.crossings(key):
                    go.wait_send()
                if key[0]:
                    self.hop(0, key).wait_send()
                elif key[1]:
                    self.hop(1, key).wait_send()
                elif key[2]:
                    self.hop(2, key).wait_send()


def pieces_of(sources, low, high):
    pieces, first = [], 0
    for ref in sources:
        begin, end = max(low, first), min(high, first + ref.shape[2])
        if begin < end:
            pieces.append((ref, begin - first, begin - low, end - begin))
        first += ref.shape[2]
    return pieces


def scatter_whole(parts, collective_id):
    rows = parts[0].shape[1]
    width = sum(part.shape[2] for part in parts)
    groups, ep_count = lax.axis_size("grp"), lax.axis_size("ep")
    place = Place(groups, ep_count)
    tiles = width // HEAD
    count = 2 * COUPLES
    cuts = [tiles * n // count * HEAD for n in range(count + 1)]
    orders = ["xba", "bxa"] * COUPLES

    def kernel(*refs):
        sources, refs = refs[: len(parts)], refs[len(parts) :]
        out_ref, refs = refs[0], refs[1:]
        place.locate()
        sums = []
        for n, axes in enumerate(orders):
            pieces = pieces_of(sources, cuts[n], cuts[n + 1])
            sums.append(WholeSum(place, axes, pieces, refs[:14]))
            refs = refs[14:]
        outs = [out_ref.at[:, pl.ds(cuts[n], cuts[n + 1] - cuts[n])] for n in range(len(orders))]
        place.greet()
        couples = [sums[n : n + 2] for n in range(0, len(sums), 2)]
        for couple in couples:
            for i in range(max(s.n1 for s in couple)):
                for s in couple:
                    if i < s.n1:
                        s.start(i)

        def core(couple):
            for i in range(max(s.n1 for s in couple)):
                for s in couple:
                    if i < s.n1:
                        s.stage_core(i)

        def one(couple):
            for i in range(max(s.n2 for s in couple)):
                for s in couple:
                    if i < s.n2:
                        s.stage_one(from_far(s.n2)[i])

        def two(couple):
            for s in couple:
                s.stage_two()

        core(couples[0])
        for n, couple in enumerate(couples):
            one(couple)
            if n + 1 < len(couples):
                core(couples[n + 1])
            two(couple)
        for s, out in zip(sums, outs):
            s.stage_three(out)
        for s in sums:
            s.drain()

    operands, anywhere = list(parts), pl.BlockSpec(memory_space=pl.ANY)
    out_shape = [jax.ShapeDtypeStruct((rows, width), jnp.float32)]
    scratch = []
    for n, axes in enumerate(orders):
        scratch += WholeSum.scratch(place.sizes, axes, rows, cuts[n + 1] - cuts[n], parts[0].dtype, len(parts))
    got = pl.pallas_call(
        kernel,
        out_shape=tuple(out_shape),
        in_specs=[anywhere] * len(operands),
        out_specs=tuple(pl.BlockSpec(memory_space=pltpu.VMEM) for _ in out_shape),
        scratch_shapes=scratch,
        compiler_params=pltpu.CompilerParams(
            collective_id=collective_id, has_side_effects=True, vmem_limit_bytes=VMEM_MOST),
        name="scatter_whole",
    )(*operands)
    return got[0]


def scatter_experts(parts, lefts, rights, collective_id):
    ep_count, rows, width = parts.shape
    flat, tall = lefts[0].shape
    ff = rights[0].shape[1]
    half, depth = tall // 2, flat // 3
    plan, pieces = Plan(ep_count, False), 4
    place = Place(lax.axis_size("grp"), ep_count)
    left_of = [0, 0, 1]
    hooks = (4, 5, 6, 7, 10, 11, 12, 13, 16, 17)
    kinds, units = len(rights), 2 * len(rights)
    steps = units * 3

    def kernel(p_ref, in_ref, og_ref, pre_ref, lift_ref, mid_ref, out_ref, w0, w1, w2, acc, left, right, gone, came,
               ls, rs, gs, cs, *scratch):
        left_refs, right_refs, outs = (in_ref, og_ref), (pre_ref, lift_ref, mid_ref), (w0, w1, w2)
        place.locate()
        total = RowSum(plan, pieces, p_ref, scratch)
        g = place.at["x"]
        place.greet()

        def fetch(kind, step):
            chunk, slot = step % 3, step % 2
            mine = (step >= 3 * kinds).astype(jnp.int32)
            first = pl.multiple_of(jnp.where(mine == 1, g, 1 - g) * half, HEAD)
            at = pl.ds(pl.multiple_of(chunk * depth, depth), depth)
            return (pltpu.make_async_copy(left_refs[left_of[kind]].at[at, pl.ds(first, half)], left.at[slot], ls.at[slot]),
                    pltpu.make_async_copy(right_refs[kind].at[at, :], right.at[slot], rs.at[slot]))

        def per_kind(step, go):
            for kind in range(kinds):
                run_if((step // 3) % kinds == kind, lambda kind=kind: go(kind))

        def begin(step):
            def go(kind):
                for copy in fetch(kind, step):
                    copy.start()
            per_kind(step, go)

        def away(kind):
            return send(gone.at[kind], came.at[kind], gs.at[kind], cs.at[kind], place.dev(x=place.back("x", 1)))

        def meet(n):
            q, distance = n // plan.long, plan.long - 1 - n % plan.long
            for d in sorted({-distance, distance}):
                total.dest(d, q)

        ks = from_far(plan.wide)
        total.start(ks)
        begin(jnp.int32(0))
        for k in ks[:-1]:
            total.stage_over(k)

        @pl.loop(0, steps)
        def _(step):
            run_if(step + 1 < steps, lambda: begin(step + 1))

            def ready(kind):
                for copy in fetch(kind, step):
                    copy.wait()
            per_kind(step, ready)
            slot = step % 2
            product = inner_left(left[slot], right[slot])
            fresh = step % 3 == 0

            @pl.when(fresh)
            def _():
                acc[...] = product

            @pl.when(jnp.logical_not(fresh))
            def _():
                acc[...] += product

            def done(kind):
                @pl.when(step < 3 * kinds)
                def _():
                    gone[kind] = acc[...].astype(jnp.bfloat16)
                    away(kind).start()

                @pl.when(step >= 3 * kinds)
                def _():
                    outs[kind][...] = acc[...]

            run_if(step % 3 == 2, lambda: per_kind(step, done))
            for n, at in enumerate(hooks):
                run_if(step == at, lambda n=n: meet(n))

        for n in range(len(hooks), pieces * plan.long):
            meet(n)
        out_ref[...] = total.result()
        for kind in range(kinds):
            away(kind).wait_recv()
            piece = 32

            @pl.loop(0, half // piece)
            def _(i, kind=kind):
                at = pl.ds(pl.multiple_of(i * piece, piece), piece)
                outs[kind][at, :] = outs[kind][at, :] + came[kind, at, :].astype(jnp.float32)

        for kind in range(kinds):
            away(kind).wait_send()
        total.drain()

    anywhere = pl.BlockSpec(memory_space=pl.ANY)
    sem = lambda n: pltpu.SemaphoreType.DMA((n,))
    outs = [jax.ShapeDtypeStruct((rows, width), parts.dtype)] + [jax.ShapeDtypeStruct((half, ff), jnp.float32)] * kinds
    return pl.pallas_call(
        kernel,
        out_shape=tuple(outs),
        in_specs=[anywhere] * 6,
        out_specs=tuple(pl.BlockSpec(memory_space=pltpu.VMEM) for _ in outs),
        scratch_shapes=[
            pltpu.VMEM((half, ff), jnp.float32),
            pltpu.VMEM((2, depth, half), jnp.bfloat16),
            pltpu.VMEM((2, depth, ff), jnp.bfloat16),
            pltpu.VMEM((kinds, half, ff), jnp.bfloat16),
            pltpu.VMEM((kinds, half, ff), jnp.bfloat16),
            sem(2), sem(2), sem(kinds), sem(kinds),
        ] + RowSum.scratch(plan, rows, width, parts.dtype, pieces),
        compiler_params=pltpu.CompilerParams(
            collective_id=collective_id, has_side_effects=True, vmem_limit_bytes=VMEM_MOST),
        name="scatter_experts",
    )(parts, *lefts, *rights)


def visible_bias(shape, first_key, start, first_query):
    key_pos = first_key + lax.broadcasted_iota(jnp.int32, shape, 0)
    query_pos = first_query + lax.broadcasted_iota(jnp.int32, shape, 1)
    seen = jnp.logical_and(key_pos >= start, key_pos <= query_pos)
    return jnp.where(seen, 0.0, masked_value)


def lanes(first):
    return pl.ds(pl.multiple_of(first, HEAD), HEAD)


def turned(values, cosine, sine):
    return values * cosine + pltpu.roll(values, HEAD // 2, 1) * sine


def whole_spec(*shape):
    return pl.BlockSpec(shape, lambda *s: (0,) * len(shape))


def project_kernel(x_ref, gain_ref, cos_ref, sin_ref, wq_ref, wk_ref, wv_ref, hid_ref, q_ref, kv_ref, hidden):
    @pl.when(pl.program_id(0) == 0)
    def _():
        hidden[...] = normed(x_ref[...].astype(jnp.float32), gain_ref[...]).astype(jnp.bfloat16)
        hid_ref[...] = hidden[...]

    cosine, sine = cos_ref[...], sin_ref[...]
    q = jnp.dot(hidden[...], wq_ref[...], preferred_element_type=jnp.float32)
    k = jnp.dot(hidden[...], wk_ref[...], preferred_element_type=jnp.float32)
    v = jnp.dot(hidden[...], wv_ref[...], preferred_element_type=jnp.float32)
    for h in range(q.shape[1] // HEAD):
        at = slice(h * HEAD, (h + 1) * HEAD)
        q_ref[:, at] = (turned(q[:, at], cosine, sine) * HEAD ** (-0.5)).astype(jnp.bfloat16)
        kv_ref[:, 2 * h * HEAD : (2 * h + 1) * HEAD] = turned(k[:, at], cosine, sine).astype(jnp.bfloat16)
        kv_ref[:, (2 * h + 1) * HEAD : (2 * h + 2) * HEAD] = v[:, at].astype(jnp.bfloat16)


def project(tokens, gain, cosine, sine, wq, wk, wv):
    rows, width = tokens.shape
    tile = 2 * HEAD
    column = pl.BlockSpec((width, tile), lambda i: (0, i))
    return pl.pallas_call(
        project_kernel,
        out_shape=(
            jax.ShapeDtypeStruct((rows, width), jnp.bfloat16),
            jax.ShapeDtypeStruct((rows, width), jnp.bfloat16),
            jax.ShapeDtypeStruct((rows, 2 * width), jnp.bfloat16),
        ),
        grid=(width // tile,),
        in_specs=[whole_spec(rows, width), whole_spec(1, width), whole_spec(rows, HEAD), whole_spec(rows, HEAD),
                  column, column, column],
        out_specs=(whole_spec(rows, width), pl.BlockSpec((rows, tile), lambda i: (0, i)),
                   pl.BlockSpec((rows, 2 * tile), lambda i: (0, i))),
        scratch_shapes=[pltpu.VMEM((rows, width), jnp.bfloat16)],
        cost_estimate=pl.CostEstimate(flops=6 * rows * width * width, bytes_accessed=6 * width * width, transcendentals=0),
        name="project",
    )(tokens, gain[None, :], cosine, sine, wq, wk, wv)


def attend_kernel(info, q_ref, start_ref, kv_ref, mixed_ref, low_ref, total_ref, bias, top, norm):
    step = pl.program_id(0)
    me, first_block = info[0], info[1]
    rows = q_ref.shape[0]
    block = me - step

    @pl.when(step == 0)
    def _():
        top[...] = jnp.full_like(top, masked_value)
        norm[...] = jnp.zeros_like(norm)
        mixed_ref[...] = jnp.zeros_like(mixed_ref)

    @pl.when(block >= first_block)
    def _():
        bias[...] = visible_bias((rows, rows), block * rows, start_ref[...], me * rows)

        @pl.loop(0, HEADS, unroll=2)
        def _(h):
            keys, values = kv_ref[0, :, lanes(2 * h * HEAD)], kv_ref[0, :, lanes((2 * h + 1) * HEAD)]
            scores = inner_right(keys, q_ref[:, lanes(h * HEAD)]) + bias[...]
            old = top[h]
            new = jnp.maximum(old, jnp.max(scores, axis=0, keepdims=True))
            weights = jnp.exp(scores - new)
            shrink = jnp.exp(old - new)
            top[h] = new
            norm[h] = norm[h] * shrink + jnp.sum(weights, axis=0, keepdims=True)
            mixed_ref[h] = mixed_ref[h] * shrink + inner_left(values, weights.astype(jnp.bfloat16))

    @pl.when(step == pl.num_programs(0) - 1)
    def _():
        for h in range(HEADS):
            mixed = mixed_ref[h] / norm[h]
            mixed_ref[h] = mixed
            low_ref[:, h * HEAD : (h + 1) * HEAD] = mixed.T.astype(jnp.bfloat16)
            total_ref[h] = top[h] + jnp.log(norm[h])


def attend(info, queries, start, pairs):
    rows, width = queries.shape
    steps = pairs.shape[0] // 2 + 1
    return pl.pallas_call(
        attend_kernel,
        out_shape=(
            jax.ShapeDtypeStruct((HEADS, HEAD, rows), jnp.float32),
            jax.ShapeDtypeStruct((rows, width), jnp.bfloat16),
            jax.ShapeDtypeStruct((HEADS, 1, rows), jnp.float32),
        ),
        grid_spec=pltpu.PrefetchScalarGridSpec(
            num_scalar_prefetch=1,
            grid=(steps,),
            in_specs=[
                whole_spec(rows, width),
                whole_spec(1, rows),
                pl.BlockSpec((1, rows, 2 * width), lambda s, info: (jnp.maximum(info[0] - s, info[1]), 0, 0)),
            ],
            out_specs=(whole_spec(HEADS, HEAD, rows), whole_spec(rows, width), whole_spec(HEADS, 1, rows)),
            scratch_shapes=[
                pltpu.VMEM((rows, rows), jnp.float32),
                pltpu.VMEM((HEADS, 1, rows), jnp.float32),
                pltpu.VMEM((HEADS, 1, rows), jnp.float32),
            ],
        ),
        cost_estimate=pl.CostEstimate(
            flops=4 * rows * rows * width * steps, bytes_accessed=4 * rows * width * steps, transcendentals=0
        ),
        name="attend",
    )(info, queries, start, pairs)


def attend_back_kernel(
    info, q_ref, g_ref, mixed_ref, start_ref, total_ref, cos_ref, sin_ref, kv_ref, dkv_ref, dq_ref, bias, acc, term
):
    step = pl.program_id(0)
    me, first_block = info[0], info[1]
    rows = q_ref.shape[0]
    block = me - step

    @pl.when(step == 0)
    def _():
        acc[...] = jnp.zeros_like(acc)
        for h in range(HEADS):
            grads = g_ref[:, h * HEAD : (h + 1) * HEAD].astype(jnp.float32).T
            term[h] = jnp.sum(grads * mixed_ref[h], axis=0, keepdims=True)

    @pl.when(block >= first_block)
    def _():
        bias[...] = visible_bias((rows, rows), block * rows, start_ref[...], me * rows)

        @pl.loop(0, HEADS, unroll=2)
        def _(h):
            early, late, at = lanes(2 * h * HEAD), lanes((2 * h + 1) * HEAD), lanes(h * HEAD)
            keys, values = kv_ref[0, :, early], kv_ref[0, :, late]
            queries, grads = q_ref[:, at], g_ref[:, at]
            probs = jnp.exp(inner_right(keys, queries) + bias[...] - total_ref[h])
            prob_grad = inner_right(values, grads)
            score_grad = (probs * (prob_grad - term[h])).astype(jnp.bfloat16)
            dkv_ref[0, :, late] = jnp.dot(
                probs.astype(jnp.bfloat16), grads, preferred_element_type=jnp.float32
            ).astype(jnp.bfloat16)
            dkv_ref[0, :, early] = jnp.dot(
                score_grad, queries, preferred_element_type=jnp.float32
            ).astype(jnp.bfloat16)
            acc[h] += inner_left(keys, score_grad)

    @pl.when(jnp.logical_and(block >= 0, block < first_block))
    def _():
        dkv_ref[...] = jnp.zeros_like(dkv_ref)

    @pl.when(step == pl.num_programs(0) - 1)
    def _():
        for h in range(HEADS):
            back = turned(acc[h].T * HEAD ** (-0.5), cos_ref[...], -sin_ref[...])
            dq_ref[:, h * HEAD : (h + 1) * HEAD] = back.astype(jnp.bfloat16)


def attend_back(info, queries, grads, mixed, start, total, cosine, sine, pairs):
    rows, width = queries.shape
    count = pairs.shape[0]
    steps = count // 2 + 1
    return pl.pallas_call(
        attend_back_kernel,
        out_shape=(
            jax.ShapeDtypeStruct(pairs.shape, jnp.bfloat16),
            jax.ShapeDtypeStruct((rows, width), jnp.bfloat16),
        ),
        grid_spec=pltpu.PrefetchScalarGridSpec(
            num_scalar_prefetch=1,
            grid=(steps,),
            in_specs=[
                whole_spec(rows, width),
                whole_spec(rows, width),
                whole_spec(HEADS, HEAD, rows),
                whole_spec(1, rows),
                whole_spec(HEADS, 1, rows),
                whole_spec(rows, HEAD),
                whole_spec(rows, HEAD),
                pl.BlockSpec((1, rows, 2 * width), lambda s, info: (jnp.maximum(info[0] - s, info[1]), 0, 0)),
            ],
            out_specs=(
                pl.BlockSpec((1, rows, 2 * width), lambda s, info: (jnp.maximum(info[0] - s, 0), 0, 0)),
                whole_spec(rows, width),
            ),
            scratch_shapes=[
                pltpu.VMEM((rows, rows), jnp.float32),
                pltpu.VMEM((HEADS, HEAD, rows), jnp.float32),
                pltpu.VMEM((HEADS, 1, rows), jnp.float32),
            ],
        ),
        cost_estimate=pl.CostEstimate(
            flops=10 * rows * rows * width * steps, bytes_accessed=8 * rows * width * steps, transcendentals=0
        ),
        name="attend_back",
    )(info, queries, grads, mixed, start, total, cosine, sine, pairs)


def finish_kernel(
    x_ref, gain_ref, res_ref, hid_ref, q_ref, kv_ref, cos_ref, sin_ref, wq_ref, wk_ref, wv_ref,
    dq_ref, dk_ref, dv_ref, out_ref, gain_out, acc,
):
    step = pl.program_id(0)

    @pl.when(step == 0)
    def _():
        acc[...] = jnp.zeros_like(acc)

    cosine, sine = cos_ref[...], sin_ref[...]
    count = q_ref.shape[1] // HEAD
    keys = jnp.concatenate(
        [turned(kv_ref[:, 2 * h * HEAD : (2 * h + 1) * HEAD].astype(jnp.float32), cosine, -sine).astype(jnp.bfloat16)
         for h in range(count)], axis=1)
    values = jnp.concatenate([kv_ref[:, (2 * h + 1) * HEAD : (2 * h + 2) * HEAD] for h in range(count)], axis=1)
    grads = (q_ref[...], keys, values)
    acc[...] += (
        inner_right(grads[0], wq_ref[...]) + inner_right(grads[1], wk_ref[...]) + inner_right(grads[2], wv_ref[...])
    )
    hidden = hid_ref[...]
    for ref, grad in zip((dq_ref, dk_ref, dv_ref), grads):
        ref[...] = inner_left(hidden, grad).astype(jnp.bfloat16)

    @pl.when(step == pl.num_programs(0) - 1)
    def _():
        values, gain, grad = x_ref[...].astype(jnp.float32), gain_ref[...], acc[...]
        scale = lax.rsqrt(jnp.mean(values * values, axis=1, keepdims=True) + epsilon)
        inner = jnp.mean(gain * grad * values, axis=1, keepdims=True)
        part = scale * gain * grad - values * (scale * scale * scale) * inner
        out_ref[...] = (res_ref[...] + part).astype(jnp.bfloat16)
        gain_out[...] = jnp.sum(grad * values * scale, axis=0, keepdims=True)


def finish(tokens, gain, residual_grad, hidden, query_grad, pair_grads, cosine, sine, wq, wk, wv):
    rows, width = tokens.shape
    tile = 2 * HEAD
    column = pl.BlockSpec((width, tile), lambda i: (0, i))
    return pl.pallas_call(
        finish_kernel,
        out_shape=(
            jax.ShapeDtypeStruct((width, width), jnp.bfloat16),
            jax.ShapeDtypeStruct((width, width), jnp.bfloat16),
            jax.ShapeDtypeStruct((width, width), jnp.bfloat16),
            jax.ShapeDtypeStruct((rows, width), jnp.bfloat16),
            jax.ShapeDtypeStruct((1, width), jnp.float32),
        ),
        grid=(width // tile,),
        in_specs=[whole_spec(rows, width), whole_spec(1, width), whole_spec(rows, width), whole_spec(rows, width),
                  pl.BlockSpec((rows, tile), lambda i: (0, i)), pl.BlockSpec((rows, 2 * tile), lambda i: (0, i)),
                  whole_spec(rows, HEAD), whole_spec(rows, HEAD), column, column, column],
        out_specs=(column, column, column, whole_spec(rows, width), whole_spec(1, width)),
        scratch_shapes=[pltpu.VMEM((rows, width), jnp.float32)],
        cost_estimate=pl.CostEstimate(flops=12 * rows * width * width, bytes_accessed=12 * width * width, transcendentals=0),
        name="finish",
    )(tokens, gain[None, :], residual_grad, hidden, query_grad, pair_grads, cosine, sine, wq, wk, wv)


def experts_kernel(
    where_ref, x_ref, g_ref, rank_row, rank_col, share_row, wg_ref, wu_ref, wd_ref,
    back_ref, routed_ref, in_ref, pre_ref, lift_ref, mid_ref, og_ref, grads,
):
    blocks, rows, side = x_ref.shape
    capacity = in_ref.shape[0] // blocks
    width = og_ref.shape[1]
    dot = lambda left, right: jnp.dot(left, right, preferred_element_type=jnp.float32)
    shares = []
    for i in range(blocks):
        at = slice(i * capacity, (i + 1) * capacity)
        hit = rank_row[i] == lax.broadcasted_iota(jnp.int32, (capacity, rows), 0)
        pick = jnp.where(hit, 1.0, 0.0)
        shares.append(jnp.sum(pick * share_row[i], axis=1, keepdims=True))
        pick = pick.astype(jnp.bfloat16)
        in_ref[at, :] = dot(pick, x_ref[i, :, :width]).astype(jnp.bfloat16)
        grads[at, :] = dot(pick, g_ref[i]).astype(jnp.bfloat16)
    share = jnp.concatenate(shares, axis=0)
    pre = dot(in_ref[...], wg_ref[0])
    lift = dot(in_ref[...], wu_ref[0])
    silu, slope = silu_parts(pre)
    mid_ref[...] = (silu * lift).astype(jnp.bfloat16)
    lift_slope = lift * slope
    result = dot(mid_ref[...], wd_ref[0]).astype(jnp.bfloat16).astype(jnp.float32)
    grad = grads[...].astype(jnp.float32)
    gate_grad = jnp.sum(result * grad, axis=1, keepdims=True)
    og_ref[...] = (share * grad).astype(jnp.bfloat16)
    given = (share * result).astype(jnp.bfloat16)
    mid_grad = inner_right(og_ref[...], wd_ref[0])
    pre_ref[...] = (mid_grad * lift_slope).astype(jnp.bfloat16)
    lift_ref[...] = (mid_grad * silu).astype(jnp.bfloat16)
    in_grad = (inner_right(pre_ref[...], wg_ref[0]) + inner_right(lift_ref[...], wu_ref[0])).astype(jnp.bfloat16)
    lane = lax.broadcasted_iota(jnp.int32, (blocks * capacity, side - width), 1)
    high = gate_grad.astype(jnp.bfloat16).astype(jnp.float32)
    extra = jnp.where(lane == where_ref[0], high, jnp.where(lane == where_ref[1], gate_grad - high, 0.0))
    extra = extra.astype(jnp.bfloat16)
    for i in range(blocks):
        at = slice(i * capacity, (i + 1) * capacity)
        hit = rank_col[i] == lax.broadcasted_iota(jnp.int32, (rows, capacity), 1)
        put = jnp.where(hit, 1.0, 0.0).astype(jnp.bfloat16)
        back_ref[i, :, :width] = dot(put, in_grad[at, :]).astype(jnp.bfloat16)
        back_ref[i, :, width:] = dot(put, extra[at, :]).astype(jnp.bfloat16)
        routed_ref[i] = dot(put, given[at, :]).astype(jnp.bfloat16)


def run_experts(places, arrived, grads, rank, share, gate, up, down, capacity):
    count, rows, side = arrived.shape
    width, ff = gate.shape[1], gate.shape[2]
    blocks = 384 // capacity
    flat = count * capacity
    once = lambda *shape: pl.BlockSpec(shape, lambda i, p: (0,) * len(shape), pipeline_mode=pl.Buffered(1))
    lead = lambda *shape: pl.BlockSpec((blocks,) + shape, lambda i, p: (i, 0, 0))
    tall = lambda wide: pl.BlockSpec((blocks * capacity, wide), lambda i, p: (i, 0))
    shape = lambda *dims: jax.ShapeDtypeStruct(dims, jnp.bfloat16)
    return pl.pallas_call(
        experts_kernel,
        out_shape=(shape(count, rows, side), shape(count, rows, width), shape(flat, width), shape(flat, ff),
                   shape(flat, ff), shape(flat, ff), shape(flat, width)),
        grid_spec=pltpu.PrefetchScalarGridSpec(
            num_scalar_prefetch=1,
            grid=(count // blocks,),
            in_specs=[lead(rows, side), lead(rows, width), lead(1, rows), lead(rows, 1), lead(1, rows),
                      once(1, width, ff), once(1, width, ff), once(1, ff, width)],
            out_specs=(lead(rows, side), lead(rows, width), tall(width), tall(ff), tall(ff), tall(ff), tall(width)),
            scratch_shapes=[pltpu.VMEM((blocks * capacity, width), jnp.bfloat16)],
        ),
        compiler_params=pltpu.CompilerParams(vmem_limit_bytes=VMEM_MOST),
        cost_estimate=pl.CostEstimate(flops=16 * flat * width * ff, bytes_accessed=16 * flat * width, transcendentals=0),
        name="run_experts",
    )(places, arrived, grads, rank[:, None, :], rank[:, :, None], share[:, None, :], gate, up, down)


def attend_back_sum(queries, grads, mixed, start, total, cosine, sine, pairs, parts, collective_id):
    rows, width = queries.shape
    ep_count = pairs.shape[0]
    part_rows, part_width = parts[0].shape[1], sum(part.shape[2] for part in parts)
    plan, pieces = Plan(ep_count, True), 4
    place = Place(lax.axis_size("grp"), ep_count)
    n, wide = plan.planes(), plan.wide
    cuts = [0, part_width // HEAD * 3 // 4 * HEAD, part_width]
    orders = ("xba", "bxa")

    def kernel(q_ref, g_ref, mixed_ref, start_ref, total_ref, cos_ref, sin_ref, pair_ref, *refs):
        sources, refs = refs[: len(parts)], refs[len(parts) :]
        out_ref, pair_out, dq_ref, bias, acc, term, kv, staged, kv_sem = refs[:9]
        refs = refs[9:]
        place.locate()
        sums = []
        for i in range(2):
            sums.append(WholeSum(place, orders[i], pieces_of(sources, cuts[i], cuts[i + 1]), refs[:14]))
            refs = refs[14:]
        sum_rows = RowSum(plan, pieces, staged, refs)
        a, b, c = sum_rows.a, sum_rows.b, sum_rows.c
        me = plan.slot(a, b, c)
        order, ks = sum_rows.order, from_far(wide)
        turns = [(k, d) for k in ks for d in order]

        def block(turn, other):
            k, d = turns[turn]
            b0, c0 = sum_rows.source(k), jnp.where(other, 1 - c, c)
            there = both(plan.inside(a - d), plan.need(d, b, c, b0, c0))
            return there, plan.slot(a - d, b0, c0)

        def fetch(turn, other):
            there, slot = block(turn, other)
            held = jnp.where(other, 0, 1)
            return there, lambda: pltpu.make_async_copy(pair_ref.at[slot], kv.at[held], kv_sem.at[held])

        def begin(turn, other):
            there, go = fetch(turn, other)
            run_if(there, lambda: go().start())

        def compute(turn, other, target):
            there, slot = block(turn, other)
            held = 0 if other else 1

            def work():
                fetch(turn, other)[1]().wait()
                bias[...] = visible_bias((rows, rows), slot * rows, start_ref[...], me * rows)

                @pl.loop(0, HEADS, unroll=2)
                def _(h):
                    early, late, at = lanes(2 * h * HEAD), lanes((2 * h + 1) * HEAD), lanes(h * HEAD)
                    keys, values = kv[held, :, early], kv[held, :, late]
                    own, grad = q_ref[:, at], g_ref[:, at]
                    probs = jnp.exp(inner_right(keys, own) + bias[...] - total_ref[h])
                    score_grad = (probs * (inner_right(values, grad) - term[h])).astype(jnp.bfloat16)
                    target[:, late] = jnp.dot(
                        probs.astype(jnp.bfloat16), grad, preferred_element_type=jnp.float32
                    ).astype(jnp.bfloat16)
                    target[:, early] = jnp.dot(
                        score_grad, own, preferred_element_type=jnp.float32
                    ).astype(jnp.bfloat16)
                    acc[h] += inner_left(keys, score_grad)

            run_if(there, work)

        def turn_of(turn):
            k, d = turns[turn]
            i = plan.plane(a, d)
            compute(turn, True, staged.at[i, k])
            if turn + 1 < len(turns):
                begin(turn + 1, True)
            cond = sum_rows.cross(d, k, 0)[0]
            for q in range(pieces):
                run_if(cond, lambda q=q: sum_rows.cross(d, k, q)[1]().start())
            compute(turn, False, sum_rows.held.at[i, k])
            if turn + 1 < len(turns):
                begin(turn + 1, False)

        def pass_on(turn):
            k, d = turns[turn]

            @pl.loop(0, pieces)
            def _(q):
                sum_rows.first(d, k, q)
                cond, go = sum_rows.over(d, k, q)
                run_if(cond, lambda: go().start())

        begin(0, True)
        begin(0, False)
        place.greet()
        for i in range(max(one.n1 for one in sums)):
            for one in sums:
                if i < one.n1:
                    one.start(i)
        acc[...] = jnp.zeros_like(acc)
        for h in range(HEADS):
            grad = g_ref[:, h * HEAD : (h + 1) * HEAD].astype(jnp.float32).T
            term[h] = jnp.sum(grad * mixed_ref[h], axis=0, keepdims=True)
        far = (wide - 1) * len(order)
        for one in sums:
            for i in range(one.n1 - 1):
                one.stage_core(i)
        first, second = sums
        ones = {far - 1: (second, 1), far: (first, 1), far + 1: (second, 0), far + 2: (first, 0)}
        for turn in range(len(turns)):
            turn_of(turn)
            if turn == 0:
                for one in sums:
                    one.stage_core(one.n1 - 1)
            elif turn <= far:
                pass_on(turn - 1)
            if turn in ones:
                one, part = ones[turn]
                for k2 in from_far(one.n2)[:-1] if part else [0]:
                    one.stage_one(k2)
        for h in range(HEADS):
            back = turned(acc[h].T * HEAD ** (-0.5), cos_ref[...], -sin_ref[...])
            dq_ref[:, h * HEAD : (h + 1) * HEAD] = back.astype(jnp.bfloat16)
        second.stage_two()
        sum_rows.stage_dests(0, pieces)
        pair_out[...] = sum_rows.result()
        first.stage_two()
        for i, one in enumerate(sums):
            one.stage_three(out_ref.at[:, pl.ds(cuts[i], cuts[i + 1] - cuts[i])])
        sum_rows.drain()
        for one in sums:
            one.drain()

    anywhere, near = pl.BlockSpec(memory_space=pl.ANY), pl.BlockSpec(memory_space=pltpu.VMEM)
    scratch = [
        pltpu.VMEM((rows, rows), jnp.float32),
        pltpu.VMEM((HEADS, HEAD, rows), jnp.float32),
        pltpu.VMEM((HEADS, 1, rows), jnp.float32),
        pltpu.VMEM((2, rows, 2 * width), jnp.bfloat16),
        pltpu.VMEM((n, wide, rows, 2 * width), jnp.bfloat16),
        pltpu.SemaphoreType.DMA((2,)),
    ]
    for i in range(2):
        scratch += WholeSum.scratch(place.sizes, orders[i], part_rows, cuts[i + 1] - cuts[i], parts[0].dtype, len(parts))
    scratch += RowSum.scratch(plan, rows, 2 * width, pairs.dtype, pieces)
    return pl.pallas_call(
        kernel,
        out_shape=(jax.ShapeDtypeStruct((part_rows, part_width), jnp.float32),
                   jax.ShapeDtypeStruct((rows, 2 * width), pairs.dtype),
                   jax.ShapeDtypeStruct((rows, width), jnp.bfloat16)),
        in_specs=[near] * 7 + [anywhere] * (1 + len(parts)),
        out_specs=(near, near, near),
        scratch_shapes=scratch,
        compiler_params=pltpu.CompilerParams(
            collective_id=collective_id, has_side_effects=True, vmem_limit_bytes=VMEM_MOST),
        name="attend_back_sum",
    )(queries, grads, mixed, start, total, cosine, sine, pairs, *parts)


def local(
    tokens,
    doc_lengths,
    expert_ids,
    out_grad,
    mixer_gain,
    query_weight,
    key_weight,
    value_weight,
    output_weight,
    ffn_gain,
    router_weight,
    shared_gate,
    shared_up,
    shared_down,
    expert_gate,
    expert_up,
    expert_down,
):
    rows, width = tokens.shape[1], tokens.shape[2]
    ep_count = lax.axis_size("ep")
    device_count = ep_count * lax.axis_size("grp")
    ep_index = lax.axis_index("ep")
    expert_count = router_weight.shape[1]
    capacity = min(rows, 12 * rows * TOP // (7 * expert_count))
    low = lambda v: v.astype(jnp.bfloat16)
    wide = lambda v: v.astype(jnp.float32)
    dot = lambda left, right: jnp.dot(left, right, preferred_element_type=jnp.float32)

    grad_low = out_grad[0]

    doc_ends = jnp.cumsum(doc_lengths[0])
    query_pos = ep_index * rows + jnp.arange(rows, dtype=jnp.int32)
    before = query_pos[:, None] >= doc_ends[None, :]
    start = jnp.max(jnp.where(before, doc_ends[None, :], 0), axis=1)
    info = jnp.stack([ep_index, start[0] // rows]).astype(jnp.int32)
    half_dim = HEAD // 2
    frequency = rope_base ** (-jnp.arange(half_dim, dtype=jnp.float32) / half_dim)
    angles = wide(query_pos)[:, None] * frequency[None, :]
    cosine, sine = jnp.cos(angles), jnp.sin(angles)
    cosine = jnp.concatenate([cosine, cosine], axis=1)
    sine = jnp.concatenate([-sine, sine], axis=1)

    stream = wide(tokens[0])
    hidden_low, queries, own_pairs = project(
        tokens[0], mixer_gain, cosine, sine, query_weight, key_weight, value_weight
    )
    pairs = gather_rows(own_pairs, True, 1, 8)
    grad_later, pairs = lax.optimization_barrier((grad_low, pairs))
    grads_all = lax.all_gather(grad_later, "ep", axis=0, tiled=False)
    mixed, mixed_low, log_total = attend(info, queries, start[None, :], pairs)
    mixer_out = dot(mixed_low, output_weight)
    residual = stream + mixer_out
    ffn_low = low(normed(residual, ffn_gain))

    logits = dot(ffn_low, router_weight)
    experts = jnp.arange(expert_count, dtype=jnp.int32)
    assigned = jnp.any(expert_ids[0][:, :, None] == experts[None, None, :], axis=1)
    shown = jnp.where(assigned, logits, masked_value)
    powers = jnp.where(assigned, jnp.exp(shown - jnp.max(shown, axis=1, keepdims=True)), 0.0)
    gate_probs = powers / jnp.sum(powers, axis=1, keepdims=True)
    probs_high = low(gate_probs)
    probs_rest = low(gate_probs - wide(probs_high))
    side = width + 2 * HEAD if 2 * expert_count > HEAD else width + HEAD
    pad = jnp.zeros((rows, side - width - 2 * expert_count), jnp.bfloat16)
    sent = jnp.concatenate([ffn_low, probs_high, probs_rest, pad], axis=1)
    arrived, shared_out, ffn_grad, shared_gate_part, shared_up_part, shared_down_part = gather_shared(
        sent, grad_low, shared_gate, shared_up, shared_down, 2
    )

    own = experts[None, None, :] == ep_index
    high = arrived[:, :, width : width + expert_count]
    rest = arrived[:, :, width + expert_count : width + 2 * expert_count]
    share = jnp.sum(jnp.where(own, wide(high) + wide(rest), 0.0), axis=2)
    chosen = share > 0.0
    earlier = (jnp.arange(rows)[:, None] < jnp.arange(rows)[None, :]).astype(jnp.bfloat16)
    rank = dot(low(chosen), earlier).astype(jnp.int32)
    rank = jnp.where(chosen, rank, -1)
    places = jnp.stack([ep_index, expert_count + ep_index]).astype(jnp.int32)
    back, given, flat_in, pre_grad, lift_grad, middle, result_grad = run_experts(
        places, arrived, grads_all, rank, share, expert_gate, expert_up, expert_down, capacity
    )
    routed = wide(lax.psum_scatter(given, "ep", scatter_dimension=0))
    group_count = lax.axis_size("grp")
    if group_count == 2:
        back_sum, gate_sum, up_sum, down_sum = scatter_experts(
            back, (flat_in, result_grad), (pre_grad, lift_grad, middle), 3
        )
        gate_sum, up_sum, down_sum = gate_sum[None], up_sum[None], down_sum.T[None]
    else:
        back_sum = scatter_rows(back, False, 3)
        split = width // group_count
        own_down_grad = jnp.concatenate(
            [low(inner_left(middle, result_grad[:, i * split : (i + 1) * split])) for i in range(group_count)], axis=0
        )
        over_groups = lambda v: wide(lax.psum_scatter(v, "grp", scatter_dimension=0, tiled=True))[None]
        gate_sum = over_groups(low(inner_left(flat_in, pre_grad)))
        up_sum = over_groups(low(inner_left(flat_in, lift_grad)))
        down_sum = over_groups(own_down_grad)

    grad_out = wide(grad_low)
    layer_out = residual + shared_out + routed
    gate_back = wide(back_sum[:, width : width + expert_count]) + wide(
        back_sum[:, width + expert_count : width + 2 * expert_count]
    )
    chosen_grad = gate_probs * (gate_back - jnp.sum(gate_probs * gate_back, axis=1, keepdims=True))
    logit_grad = low(chosen_grad)
    ffn_grad = ffn_grad + wide(back_sum[:, :width]) + inner_right(logit_grad, router_weight)
    _, ffn_pull = jax.vjp(normed, residual, ffn_gain)
    residual_part, ffn_gain_grad = ffn_pull(ffn_grad)
    residual_grad = grad_out + residual_part
    mixer_grad_low = low(residual_grad)
    mixed_grad = low(inner_right(mixer_grad_low, output_weight))
    by_device = lambda v: low(v).reshape(device_count, width // device_count, -1)
    early = [
        by_device(part)
        for part in (shared_gate_part, shared_up_part, shared_down_part, inner_left(mixed_low, mixer_grad_low))
    ]
    if ep_count > 16:
        pair_parts, query_lin_grad = attend_back(
            info, queries, mixed_grad, mixed, start[None, :], log_total, cosine, sine, pairs
        )
        pair_grads = scatter_rows(pair_parts, True, 4)
        early_sum = scatter_whole(early, 5)
    else:
        early_sum, pair_grads, query_lin_grad = attend_back_sum(
            queries, mixed_grad, mixed, start[None, :], log_total, cosine, sine, pairs, early, 5
        )

    query_part, key_part, value_part, tokens_grad, mixer_gain_grad = finish(
        tokens[0], mixer_gain, residual_grad, hidden_low, query_lin_grad, pair_grads, cosine, sine,
        query_weight, key_weight, value_weight,
    )
    squares = jnp.stack(
        [jnp.sum(residual * residual), jnp.sum(mixer_out * mixer_out), jnp.sum(layer_out * layer_out)]
    )
    extras = jnp.concatenate(
        [inner_left(ffn_low, logit_grad), mixer_gain_grad.T, ffn_gain_grad[:, None],
         jnp.broadcast_to(squares[None, :], (width, 3))], axis=1
    )
    extras = jnp.pad(extras, ((0, 0), (0, HEAD - extras.shape[1])))
    late_sum = scatter_whole([by_device(v) for v in (query_part, key_part, value_part, extras)], 6)
    extra_sum = late_sum[:, 3 * width :]
    entry_count = rows * device_count * width
    stream_rms = jnp.sqrt(extra_sum[0, expert_count + 2 : expert_count + 5] / entry_count)
    ff = shared_gate.shape[1]
    return (
        low(layer_out)[None],
        tokens_grad[None],
        extra_sum[:, expert_count],
        late_sum[:, :width],
        late_sum[:, width : 2 * width],
        late_sum[:, 2 * width : 3 * width],
        early_sum[:, 3 * ff :],
        extra_sum[:, expert_count + 1],
        extra_sum[:, :expert_count],
        early_sum[:, :ff],
        early_sum[:, ff : 2 * ff],
        early_sum[:, 2 * ff : 3 * ff].T,
        gate_sum,
        up_sum,
        down_sum,
        stream_rms,
    )


def solution(mesh):
    return jax.shard_map(
        local,
        mesh=mesh,
        in_specs=(
            P("grp", "ep", None),
            P("grp", None),
            P("grp", "ep", None),
            P("grp", "ep", None),
            P(),
            P(),
            P(),
            P(),
            P(),
            P(),
            P(),
            P(),
            P(),
            P(),
            P("ep", None, None),
            P("ep", None, None),
            P("ep", None, None),
        ),
        out_specs=(
            P("grp", "ep", None),
            P("grp", "ep", None),
            P(("grp", "ep")),
            P(("grp", "ep"), None),
            P(("grp", "ep"), None),
            P(("grp", "ep"), None),
            P(("grp", "ep"), None),
            P(("grp", "ep")),
            P(("grp", "ep"), None),
            P(("grp", "ep"), None),
            P(("grp", "ep"), None),
            P(None, ("grp", "ep")),
            P("ep", "grp", None),
            P("ep", "grp", None),
            P("ep", None, "grp"),
            P(),
        ),
        check_vma=False,
    )
```

```python
import functools

import jax
import jax.numpy as jnp
from jax import lax
from jax.experimental import pallas as pl
from jax.experimental.pallas import tpu as pltpu
from jax.sharding import PartitionSpec as P

HEADS = 10
HEAD = 128
TOP = 7

epsilon = 1e-06
rope_base = 10000.0
masked_value = -1e30


def normed(values, gain_vec):
    return (
        values * lax.rsqrt(jnp.mean(values * values, axis=-1, keepdims=True) + epsilon) * gain_vec
    )


def inner_left(left_op, right_op):
    return lax.dot_general(
        left_op, right_op, (((0,), (0,)), ((), ())), preferred_element_type=jnp.float32
    )


def inner_right(left_op, right_op):
    return lax.dot_general(
        left_op, right_op, (((1,), (1,)), ((), ())), preferred_element_type=jnp.float32
    )


def silu_parts(pre_act):
    sigmoid_val = jax.nn.sigmoid(pre_act)
    return (pre_act * sigmoid_val, sigmoid_val * (1.0 + pre_act * (1.0 - sigmoid_val)))


MESH = pl.DeviceIdType.MESH
COUPLES = 2
VMEM_MOST = 64 * 1024 * 1024 - 65536


def when(cond):
    if cond is True:
        return lambda f: f()
    if cond is False:
        return lambda f: None
    return pl.when(cond)


def both(*conds):
    out = True
    for cond in conds:
        if cond is False:
            return False
        if cond is True:
            continue
        out = cond if out is True else jnp.logical_and(out, cond)
    return out


class Plan:
    def __init__(self, ep_count, window):
        self.long = 4
        self.wide = ep_count // 8
        self.window = window
        self.steps = (
            list(range(self.long // 2 + 1))
            if window
            else list(range(-(self.long - 1), self.long))
        )

    def place(self):
        me = lax.axis_index("ep")
        return me // (2 * self.wide), (me // 2) % self.wide, me % 2

    def slot(self, a, b, c):
        return (a * self.wide + b) * 2 + c

    def plane(self, a, d):
        return d if self.window else jnp.clip(a - d, 0, self.long - 1)

    def planes(self):
        return len(self.steps) if self.window else self.long

    def inside(self, a):
        return jnp.logical_and(a >= 0, a < self.long)

    def need(self, d, b, c, b0, c0):
        if not self.window or 0 < d < self.long // 2:
            return True
        if d == 0:
            return jnp.logical_or(b0 < b, jnp.logical_and(b0 == b, c0 <= c))
        return jnp.logical_or(b0 > b, jnp.logical_and(b0 == b, c0 >= c))

    def need_pair(self, d, b, b0):
        if not self.window or 0 < d < self.long // 2:
            return True
        return b0 < b if d == 0 else b0 > b

    def greet(self, a, b, c):
        barrier = pltpu.get_barrier_semaphore()

        def signal(cond, dev):
            @when(cond)
            def _():
                pl.semaphore_signal(barrier, inc=1, device_id={"ep": dev}, device_id_type=MESH)

        signal(a + 1 < self.long, self.slot(a + 1, b, c))
        signal(a > 0, self.slot(a - 1, b, c))
        for k in range(1, self.wide):
            signal(True, self.slot(a, (b + k) % self.wide, c))
        signal(True, self.slot(a, b, 1 - c))
        ends = (a == 0).astype(jnp.int32) + (a == self.long - 1).astype(jnp.int32)
        pl.semaphore_wait(barrier, self.wide + 2 - ends)


def gather_kernel(plan, pieces, beside, x_ref, out_ref, ra, sa_up, sa_dn, rb, sb, rc, sc, own):
    a, b, c = plan.place()
    steps, wide = plan.steps, plan.wide
    at = {d: i for i, d in enumerate(steps)}
    rows = x_ref.shape[0] // pieces

    def part(q):
        return pl.ds(pl.multiple_of(q * rows, rows), rows)

    def copy(q, src, slot, ssem, rsem, dev):
        return pltpu.make_async_remote_copy(
            src_ref=src, dst_ref=out_ref.at[slot, part(q)], send_sem=ssem, recv_sem=rsem,
            device_id={"ep": dev}, device_id_type=MESH,
        )

    def hops(d, q):
        i = at[d]
        slot = plan.slot(a - d, b, c)
        src = x_ref.at[part(q)] if d == 0 else out_ref.at[slot, part(q)]
        real = plan.inside(a - d)
        out = []
        if d >= 0 and d + 1 in at:
            out.append((both(real, a + 1 < plan.long), lambda: copy(
                q, src, slot, sa_up.at[i, q], ra.at[at[d + 1], q], plan.slot(a + 1, b, c))))
        if d <= 0 and d - 1 in at:
            out.append((both(real, a > 0), lambda: copy(
                q, src, slot, sa_dn.at[i, q], ra.at[at[d - 1], q], plan.slot(a - 1, b, c))))
        for k in range(1, wide):
            to = (b + k) % wide
            out.append((both(real, plan.need_pair(d, to, b)), lambda k=k, to=to: copy(
                q, src, slot, sb.at[i, k, q], rb.at[i, k, q], plan.slot(a, to, c))))
        out.append((both(real, plan.need(d, b, 1 - c, b, c)), lambda: copy(
            q, src, slot, sc.at[i, 0, q], rc.at[i, 0, q], plan.slot(a, b, 1 - c))))
        return out

    def cross(d, k, q):
        i = at[d]
        b0 = (b + wide - k) % wide
        slot = plan.slot(a - d, b0, c)
        real = plan.inside(a - d)
        come = lambda: copy(q, x_ref.at[part(q)], slot, sb.at[i, k, q], rb.at[i, k, q], plan.slot(a, b, c))
        go = lambda: copy(q, out_ref.at[slot, part(q)], slot, sc.at[i, k, q], rc.at[i, k, q],
                          plan.slot(a, b, 1 - c))
        return (both(real, plan.need_pair(d, b, b0)), come,
                both(real, plan.need(d, b, 1 - c, b0, c)), go)

    plan.greet(a, b, c)
    keep = pltpu.make_async_copy(x_ref, out_ref.at[plan.slot(a, b, c)], own)

    @pl.loop(0, pieces)
    def _(q):
        for cond, go in hops(0, q):
            @when(cond)
            def _(go=go):
                go().start()

    keep.start()
    far = max(abs(d) for d in steps)
    for step in range(1, far + 3):
        beside(step - 1)

        @pl.loop(0, pieces)
        def _(q, step=step):
            for d in (step, -step):
                if d in at:
                    @when(plan.inside(a - d))
                    def _(d=d):
                        slot = plan.slot(a - d, b, c)
                        copy(q, x_ref.at[part(q)], slot, sa_up.at[0, q], ra.at[at[d], q],
                             plan.slot(a, b, c)).wait_recv()
                        for cond, go in hops(d, q):
                            @when(cond)
                            def _(go=go):
                                go().start()
            for d in sorted({step - 2, 2 - step}) if step > 1 else ():
                if d in at:
                    for k in range(1, wide):
                        came, come, goes, go = cross(d, k, q)
                        @when(came)
                        def _(come=come):
                            come().wait_recv()
                        @when(goes)
                        def _(go=go):
                            go().start()
    keep.wait()

    @pl.loop(0, pieces)
    def _(q):
        for d in steps:
            i = at[d]
            real = plan.inside(a - d)
            for k in range(wide):
                b0 = (b + wide - k) % wide
                slot = plan.slot(a - d, b0, 1 - c)
                @when(both(real, plan.need(d, b, c, b0, 1 - c)))
                def _(slot=slot, i=i, k=k):
                    copy(q, x_ref.at[part(q)], slot, sc.at[i, k, q], rc.at[i, k, q],
                         plan.slot(a, b, c)).wait_recv()
            for cond, go in hops(d, q):
                @when(cond)
                def _(go=go):
                    go().wait_send()
            for k in range(1, wide):
                came, come, goes, go = cross(d, k, q)
                @when(goes)
                def _(go=go):
                    go().wait_send()


def gather_rows(block, window, collective_id, pieces=4):
    ep_count = lax.axis_size("ep")
    plan = Plan(ep_count, window)
    n, wide = len(plan.steps), plan.wide
    sem = pltpu.SemaphoreType.DMA
    return pl.pallas_call(
        functools.partial(gather_kernel, plan, pieces, lambda n: None),
        out_shape=jax.ShapeDtypeStruct((ep_count,) + block.shape, block.dtype),
        in_specs=[pl.BlockSpec(memory_space=pltpu.VMEM)],
        out_specs=pl.BlockSpec(memory_space=pl.ANY),
        scratch_shapes=[sem((n, pieces)), sem((n, pieces)), sem((n, pieces)), sem((n, wide, pieces)),
                        sem((n, wide, pieces)), sem((n, wide, pieces)), sem((n, wide, pieces)), sem],
        compiler_params=pltpu.CompilerParams(collective_id=collective_id, has_side_effects=True),
        name="gather_rows",
    )(block)


def gather_shared(block, grads, gate, up, down, collective_id, pieces=4):
    ep_count = lax.axis_size("ep")
    plan = Plan(ep_count, False)
    n, wide = len(plan.steps), plan.wide
    rows, width = grads.shape
    ff = gate.shape[1]
    sem = pltpu.SemaphoreType.DMA
    stages = max(plan.steps) + 2
    tiles = ff // HEAD

    def kernel(x_ref, g_ref, wg_ref, wu_ref, wd_ref, out_ref, shared_ref, back_ref, dg_ref, du_ref, dd_ref, *sems):
        dot = lambda left, right: jnp.dot(left, right, preferred_element_type=jnp.float32)

        def tile(i):
            at = pl.ds(pl.multiple_of(i * HEAD, HEAD), HEAD)
            x, g = x_ref[:, :width], g_ref[...]
            w_gate, w_up, w_down = wg_ref[:, at], wu_ref[:, at], wd_ref[at, :]
            silu, slope = silu_parts(dot(x, w_gate))
            lift = dot(x, w_up)
            mid = (silu * lift).astype(jnp.bfloat16)
            mid_grad = inner_right(g, w_down)
            pre_grad = (mid_grad * lift * slope).astype(jnp.bfloat16)
            lift_grad = (mid_grad * silu).astype(jnp.bfloat16)
            out = dot(mid, w_down)
            back = inner_right(pre_grad, w_gate) + inner_right(lift_grad, w_up)

            @pl.when(i == 0)
            def _():
                shared_ref[...] = out
                back_ref[...] = back

            @pl.when(i > 0)
            def _():
                shared_ref[...] += out
                back_ref[...] += back

            dg_ref[:, at] = inner_left(x, pre_grad).astype(jnp.bfloat16)
            du_ref[:, at] = inner_left(x, lift_grad).astype(jnp.bfloat16)
            dd_ref[:, at] = inner_left(g, mid).astype(jnp.bfloat16)

        def beside(stage):
            pl.loop(tiles * stage // stages, tiles * (stage + 1) // stages)(tile)

        gather_kernel(plan, pieces, beside, x_ref, out_ref, *sems)

    near = pl.BlockSpec(memory_space=pltpu.VMEM)
    return pl.pallas_call(
        kernel,
        out_shape=(
            jax.ShapeDtypeStruct((ep_count,) + block.shape, block.dtype),
            jax.ShapeDtypeStruct((rows, width), jnp.float32),
            jax.ShapeDtypeStruct((rows, width), jnp.float32),
        ) + (jax.ShapeDtypeStruct((width, ff), jnp.bfloat16),) * 3,
        in_specs=[near] * 5,
        out_specs=(pl.BlockSpec(memory_space=pl.ANY),) + (near,) * 5,
        scratch_shapes=[sem((n, pieces)), sem((n, pieces)), sem((n, pieces)), sem((n, wide, pieces)),
                        sem((n, wide, pieces)), sem((n, wide, pieces)), sem((n, wide, pieces)), sem],
        compiler_params=pltpu.CompilerParams(
            collective_id=collective_id, has_side_effects=True, vmem_limit_bytes=VMEM_MOST),
        name="gather_shared",
    )(block, grads, gate, up, down)


def add_rows(dst, others, out=None):
    rows, width = dst.shape
    out = dst if out is None else out
    small = rows <= 64
    piece = 32 if rows % 32 == 0 else rows
    lanes = width if rows % 32 == 0 else 4 * HEAD
    whole = width // lanes * lanes

    def add(at):
        if len(others) == 1 and out.dtype == jnp.bfloat16:
            out[at] = dst[at] + others[0][at]
        else:
            total = dst[at].astype(jnp.float32)
            for other in others:
                total = total + other[at].astype(jnp.float32)
            out[at] = total.astype(out.dtype)

    if piece == rows:
        @pl.loop(0, whole // lanes)
        def _(i):
            add((slice(None), pl.ds(pl.multiple_of(i * lanes, lanes), lanes)))

        if whole < width:
            add((slice(None), pl.ds(whole, width - whole)))
    else:
        @pl.loop(0, rows // piece)
        def _(i):
            add((pl.ds(pl.multiple_of(i * piece, piece), piece), slice(None)))


def send(src, dst, ssem, rsem, to):
    return pltpu.make_async_remote_copy(
        src_ref=src, dst_ref=dst, send_sem=ssem, recv_sem=rsem, device_id=to, device_id_type=MESH
    )


def run_if(cond, go):
    @when(cond)
    def _():
        go()


class RowSum:
    @staticmethod
    def scratch(plan, rows, width, dtype, pieces):
        n, wide = plan.planes(), plan.wide
        blocks = lambda *lead: pltpu.VMEM(lead + (rows, width), dtype)
        sem = lambda *lead: pltpu.SemaphoreType.DMA(lead + (pieces,))
        return [blocks(n, wide), blocks(n, wide), blocks(n, wide - 1), blocks(n), blocks(1 if plan.window else n),
                sem(n, wide), sem(n, wide), sem(n, wide), sem(n, wide), sem(n), sem(n), sem(n), sem(n, wide)]

    def __init__(self, plan, pieces, p_ref, scratch):
        self.plan, self.pieces, self.p_ref = plan, pieces, p_ref
        (self.held, self.rcb, self.rbb, self.r_hi, self.r_lo,
         self.sc, self.rc, self.sb, self.rb, self.sa, self.rhi, self.rlo, self.ld) = scratch
        self.a, self.b, self.c = plan.place()
        self.ready = len(p_ref.shape) == 4
        self.rows = p_ref.shape[-2] // pieces
        self.order = sorted(plan.steps, key=lambda d: -abs(d))

    def part(self, q):
        return pl.ds(pl.multiple_of(q * self.rows, self.rows), self.rows)

    def dev(self, a, b, c):
        return {"ep": self.plan.slot(a, b, c)}

    def source(self, k):
        return (self.b + self.plan.wide - k) % self.plan.wide

    def load(self, d, k, q):
        p, i, b0 = self.plan, self.plan.plane(self.a, d), self.source(k)
        return both(p.inside(self.a - d), p.need(d, self.b, self.c, b0, self.c)), lambda: pltpu.make_async_copy(
            self.p_ref.at[p.slot(self.a - d, b0, self.c), self.part(q)], self.held.at[i, k, self.part(q)],
            self.ld.at[i, k, q])

    def cross(self, d, k, q):
        p, i, b0, c = self.plan, self.plan.plane(self.a, d), self.source(k), self.c
        real = p.inside(self.a - d)
        at = (i, k) if self.ready else (p.slot(self.a - d, b0, 1 - c),)
        return (both(real, p.need(d, self.b, c, b0, 1 - c)), lambda: send(
            self.p_ref.at[at + (self.part(q),)], self.rcb.at[i, k, self.part(q)],
            self.sc.at[i, k, q], self.rc.at[i, k, q], self.dev(self.a, self.b, 1 - c)),
            both(real, p.need(d, self.b, 1 - c, b0, c)))

    def over(self, d, k, q):
        p, i, b0 = self.plan, self.plan.plane(self.a, d), self.source(k)
        return both(p.inside(self.a - d), p.need_pair(d, self.b, b0)), lambda: send(
            self.held.at[i, k, self.part(q)], self.rbb.at[i, k - 1, self.part(q)], self.sb.at[i, k, q],
            self.rb.at[i, k, q], self.dev(self.a, b0, self.c))

    def along(self, d, q):
        p, i, up = self.plan, self.plan.plane(self.a, d), d < 0
        j = d - 1 if p.window else i
        return p.inside(self.a - d), lambda: send(
            self.held.at[i, 0, self.part(q)], (self.r_lo if up else self.r_hi).at[j, self.part(q)],
            self.sa.at[i, q], (self.rlo if up else self.rhi).at[j, q],
            self.dev(self.a + (1 if up else -1), self.b, self.c))

    def start(self, ks):
        for k in ks:
            @pl.loop(0, self.pieces)
            def _(q, k=k):
                for d in self.order:
                    for cond, go in (self.cross(d, k, q)[:2], self.load(d, k, q)):
                        run_if(cond, lambda go=go: go().start())

    def first(self, d, k, q):
        i = self.plan.plane(self.a, d)
        if not self.ready:
            cond, go = self.load(d, k, q)
            run_if(cond, lambda: go().wait())
        _, come_go, come = self.cross(d, k, q)

        def take():
            come_go().wait_recv()
            add_rows(self.held.at[i, k, self.part(q)], [self.rcb.at[i, k, self.part(q)]])

        run_if(come, take)

    def stage_over(self, k):
        @pl.loop(0, self.pieces)
        def _(q):
            for d in self.order:
                self.first(d, k, q)
                cond, go = self.over(d, k, q)
                run_if(cond, lambda go=go: go().start())

    def stage_dests(self, low, high):
        @pl.loop(low, high)
        def _(q):
            for d in self.order:
                self.dest(d, q)

    def stage_dest(self, d, low, high):
        @pl.loop(low, high)
        def _(q):
            self.dest(d, q)

    def dest(self, d, q):
        p, a, b, steps = self.plan, self.a, self.b, self.plan.steps
        i = p.plane(a, d)
        real = p.inside(a - d)
        mine = self.held.at[i, 0, self.part(q)]
        self.first(d, 0, q)
        for k in range(1, p.wide):
            def take(k=k):
                self.over(d, k, q)[1]().wait_recv()
                add_rows(mine, [self.rbb.at[i, k - 1, self.part(q)]])

            run_if(both(real, p.need_pair(d, (b + k) % p.wide, b)), take)
        for inner, cond, buf, sem in ((d >= 0 and d + 1 in steps, a + 1 < p.long, self.r_hi, self.rhi),
                                      (d <= 0 and d - 1 in steps, a > 0, self.r_lo, self.rlo)):
            if inner:
                def take(buf=buf, sem=sem):
                    send(mine, buf.at[i, self.part(q)], self.sa.at[i, q], sem.at[i, q],
                         self.dev(a, b, self.c)).wait_recv()
                    add_rows(mine, [buf.at[i, self.part(q)]])

                run_if(both(real, cond), take)
        if d:
            cond, go = self.along(d, q)
            run_if(cond, lambda: go().start())

    def result(self):
        return self.held[self.plan.plane(self.a, 0), 0]

    def drain(self):
        @pl.loop(0, self.pieces)
        def _(q):
            for d in self.plan.steps:
                sends = [self.cross(d, k, q)[:2] for k in range(self.plan.wide)]
                sends += [self.over(d, k, q) for k in range(1, self.plan.wide)]
                if d:
                    sends.append(self.along(d, q))
                for cond, go in sends:
                    run_if(cond, lambda go=go: go().wait_send())


def scatter_rows(parts, window, collective_id, pieces=4):
    ep_count, rows, width = parts.shape
    plan = Plan(ep_count, window)

    def kernel(p_ref, out_ref, *scratch):
        total = RowSum(plan, pieces, p_ref, scratch)
        plan.greet(total.a, total.b, total.c)
        ks = list(range(1, plan.wide)) + [0]
        total.start(ks)
        for k in ks[:-1]:
            total.stage_over(k)
        total.stage_dests(0, pieces)
        out_ref[...] = total.result()
        total.drain()

    return pl.pallas_call(
        kernel,
        out_shape=jax.ShapeDtypeStruct((rows, width), parts.dtype),
        in_specs=[pl.BlockSpec(memory_space=pl.ANY)],
        out_specs=pl.BlockSpec(memory_space=pltpu.VMEM),
        scratch_shapes=RowSum.scratch(plan, rows, width, parts.dtype, pieces),
        compiler_params=pltpu.CompilerParams(
            collective_id=collective_id, has_side_effects=True, vmem_limit_bytes=VMEM_MOST),
        name="scatter_rows",
    )(parts)


class Place:
    def __init__(self, groups, ep_count):
        self.sizes = {"x": groups, "a": 4, "b": ep_count // 8}

    def locate(self):
        me, wide = lax.axis_index("ep"), self.sizes["b"]
        self.at = {"x": lax.axis_index("grp"), "a": me // (2 * wide), "b": (me // 2) % wide, "c": me % 2}

    def dev(self, **moved):
        at = {**self.at, **moved}
        return {"grp": at["x"], "ep": (at["a"] * self.sizes["b"] + at["b"]) * 2 + at["c"]}

    def slot(self, **moved):
        at = {**self.at, **moved}
        return ((at["x"] * self.sizes["a"] + at["a"]) * self.sizes["b"] + at["b"]) * 2 + at["c"]

    def back(self, axis, k):
        return (self.at[axis] + self.sizes[axis] - k) % self.sizes[axis]

    def greet(self):
        peers = [self.dev(c=1 - self.at["c"])] + [
            self.dev(**{axis: self.back(axis, k)}) for axis in "xba" for k in range(1, self.sizes[axis])]
        barrier = pltpu.get_barrier_semaphore()
        for to in peers:
            pl.semaphore_signal(barrier, inc=1, device_id=to, device_id_type=MESH)
        pl.semaphore_wait(barrier, len(peers))


def from_far(size):
    return list(range(1, size)) + [0]


class WholeSum:
    @staticmethod
    def scratch(sizes, axes, rows, width, dtype, sources):
        n1, n2, n3 = (sizes[axis] for axis in axes)
        blocks = lambda *lead: pltpu.VMEM(lead + (rows, width), dtype)
        sem = lambda *lead: pltpu.SemaphoreType.DMA(lead)
        full = (n1, n2, n3)
        one, two, three = (n1 - 1, n2, n3), (n2 - 1, n3), (n3 - 1,)
        return [blocks(*full), blocks(*full), blocks(*one), blocks(*two), blocks(*three),
                sem(*full, sources), sem(*full, sources), sem(*full, sources), sem(*one), sem(*one), sem(*two), sem(*two), sem(*three), sem(*three)]

    def __init__(self, place, axes, pieces, scratch):
        self.place, self.axes, self.pieces = place, axes, pieces
        (self.held, self.rcb, self.r1, self.r2, self.r3,
         self.ld, self.sc, self.rc, self.s1, self.q1, self.s2, self.q2, self.s3, self.q3) = scratch
        self.n1, self.n2, self.n3 = (place.sizes[axis] for axis in axes)
        self.groups = [[(k1, k2, k3) for k2 in from_far(self.n2) for k3 in from_far(self.n3)]
                       for k1 in from_far(self.n1)]

    def slot(self, key, c):
        return self.place.slot(c=c, **{axis: self.place.back(axis, k) for axis, k in zip(self.axes, key)})

    def loads(self, key):
        c = self.place.at["c"]
        for n, (ref, first, at, count) in enumerate(self.pieces):
            frm, to = pl.ds(first, count), pl.ds(at, count)
            yield pltpu.make_async_copy(
                ref.at[self.slot(key, c), :, frm], self.held.at[key + (slice(None), to)],
                self.ld.at[key + (n,)])

    def crossings(self, key):
        c = self.place.at["c"]
        for n, (ref, first, at, count) in enumerate(self.pieces):
            frm, to = pl.ds(first, count), pl.ds(at, count)
            yield send(ref.at[self.slot(key, 1 - c), :, frm], self.rcb.at[key + (slice(None), to)],
                       self.sc.at[key + (n,)], self.rc.at[key + (n,)], self.place.dev(c=1 - c))

    def hop(self, level, key):
        buf, ssem, rsem = ((self.r1, self.s1, self.q1), (self.r2, self.s2, self.q2), (self.r3, self.s3, self.q3))[level]
        axis, k = self.axes[level], key[level]
        far = (k - 1,) + key[level + 1 :]
        return send(self.held.at[key], buf.at[far], ssem.at[far], rsem.at[far],
                    self.place.dev(**{axis: self.place.back(axis, k)}))

    def start(self, i):
        for key in self.groups[i]:
            for go in self.crossings(key):
                go.start()
            for go in self.loads(key):
                go.start()

    def stage_core(self, i):
        for key in self.groups[i]:
            for go in self.loads(key):
                go.wait()
            for go in self.crossings(key):
                go.wait_recv()
            add_rows(self.held.at[key], [self.rcb.at[key]])
            if key[0]:
                self.hop(0, key).start()

    def stage_one(self, k2):
        for k3 in from_far(self.n3):
            for k1 in range(1, self.n1):
                self.hop(0, (k1, k2, k3)).wait_recv()
            add_rows(self.held.at[0, k2, k3], [self.r1.at[k1 - 1, k2, k3] for k1 in range(1, self.n1)])
            if k2:
                self.hop(1, (0, k2, k3)).start()

    def stage_two(self):
        for k3 in from_far(self.n3):
            for k2 in range(1, self.n2):
                self.hop(1, (0, k2, k3)).wait_recv()
            add_rows(self.held.at[0, 0, k3], [self.r2.at[k2 - 1, k3] for k2 in range(1, self.n2)])
            if k3:
                self.hop(2, (0, 0, k3)).start()

    def stage_three(self, out):
        for k3 in range(1, self.n3):
            self.hop(2, (0, 0, k3)).wait_recv()
        add_rows(self.held.at[0, 0, 0], [self.r3.at[k3 - 1] for k3 in range(1, self.n3)], out)

    def drain(self):
        for group in self.groups:
            for key in group:
                for go in self.crossings(key):
                    go.wait_send()
                if key[0]:
                    self.hop(0, key).wait_send()
                elif key[1]:
                    self.hop(1, key).wait_send()
                elif key[2]:
                    self.hop(2, key).wait_send()


def pieces_of(sources, low, high):
    pieces, first = [], 0
    for ref in sources:
        begin, end = max(low, first), min(high, first + ref.shape[2])
        if begin < end:
            pieces.append((ref, begin - first, begin - low, end - begin))
        first += ref.shape[2]
    return pieces


def scatter_whole(parts, collective_id):
    rows = parts[0].shape[1]
    width = sum(part.shape[2] for part in parts)
    groups, ep_count = lax.axis_size("grp"), lax.axis_size("ep")
    place = Place(groups, ep_count)
    tiles = width // HEAD
    count = 2 * COUPLES
    cuts = [tiles * n // count * HEAD for n in range(count + 1)]
    orders = ["xba", "bxa"] * COUPLES

    def kernel(*refs):
        sources, refs = refs[: len(parts)], refs[len(parts) :]
        out_ref, refs = refs[0], refs[1:]
        place.locate()
        sums = []
        for n, axes in enumerate(orders):
            pieces = pieces_of(sources, cuts[n], cuts[n + 1])
            sums.append(WholeSum(place, axes, pieces, refs[:14]))
            refs = refs[14:]
        outs = [out_ref.at[:, pl.ds(cuts[n], cuts[n + 1] - cuts[n])] for n in range(len(orders))]
        place.greet()
        couples = [sums[n : n + 2] for n in range(0, len(sums), 2)]
        for couple in couples:
            for i in range(max(s.n1 for s in couple)):
                for s in couple:
                    if i < s.n1:
                        s.start(i)

        def core(couple):
            for i in range(max(s.n1 for s in couple)):
                for s in couple:
                    if i < s.n1:
                        s.stage_core(i)

        def one(couple):
            for i in range(max(s.n2 for s in couple)):
                for s in couple:
                    if i < s.n2:
                        s.stage_one(from_far(s.n2)[i])

        def two(couple):
            for s in couple:
                s.stage_two()

        core(couples[0])
        for n, couple in enumerate(couples):
            one(couple)
            if n + 1 < len(couples):
                core(couples[n + 1])
            two(couple)
        for s, out in zip(sums, outs):
            s.stage_three(out)
        for s in sums:
            s.drain()

    operands, anywhere = list(parts), pl.BlockSpec(memory_space=pl.ANY)
    out_shape = [jax.ShapeDtypeStruct((rows, width), jnp.float32)]
    scratch = []
    for n, axes in enumerate(orders):
        scratch += WholeSum.scratch(place.sizes, axes, rows, cuts[n + 1] - cuts[n], parts[0].dtype, len(parts))
    got = pl.pallas_call(
        kernel,
        out_shape=tuple(out_shape),
        in_specs=[anywhere] * len(operands),
        out_specs=tuple(pl.BlockSpec(memory_space=pltpu.VMEM) for _ in out_shape),
        scratch_shapes=scratch,
        compiler_params=pltpu.CompilerParams(
            collective_id=collective_id, has_side_effects=True, vmem_limit_bytes=VMEM_MOST),
        name="scatter_whole",
    )(*operands)
    return got[0]


def scatter_experts(parts, lefts, rights, collective_id):
    ep_count, rows, width = parts.shape
    flat, tall = lefts[0].shape
    ff = rights[0].shape[1]
    half, depth = tall // 2, flat // 3
    plan, pieces = Plan(ep_count, False), 4
    place = Place(lax.axis_size("grp"), ep_count)
    left_of = [0, 0, 1]
    hooks = (4, 5, 6, 7, 10, 11, 12, 13, 16, 17)
    kinds, units = len(rights), 2 * len(rights)
    steps = units * 3

    def kernel(p_ref, in_ref, og_ref, pre_ref, lift_ref, mid_ref, out_ref, w0, w1, w2, acc, left, right, gone, came,
               ls, rs, gs, cs, *scratch):
        left_refs, right_refs, outs = (in_ref, og_ref), (pre_ref, lift_ref, mid_ref), (w0, w1, w2)
        place.locate()
        total = RowSum(plan, pieces, p_ref, scratch)
        g = place.at["x"]
        place.greet()

        def fetch(kind, step):
            chunk, slot = step % 3, step % 2
            mine = (step >= 3 * kinds).astype(jnp.int32)
            first = pl.multiple_of(jnp.where(mine == 1, g, 1 - g) * half, HEAD)
            at = pl.ds(pl.multiple_of(chunk * depth, depth), depth)
            return (pltpu.make_async_copy(left_refs[left_of[kind]].at[at, pl.ds(first, half)], left.at[slot], ls.at[slot]),
                    pltpu.make_async_copy(right_refs[kind].at[at, :], right.at[slot], rs.at[slot]))

        def per_kind(step, go):
            for kind in range(kinds):
                run_if((step // 3) % kinds == kind, lambda kind=kind: go(kind))

        def begin(step):
            def go(kind):
                for copy in fetch(kind, step):
                    copy.start()
            per_kind(step, go)

        def away(kind):
            return send(gone.at[kind], came.at[kind], gs.at[kind], cs.at[kind], place.dev(x=place.back("x", 1)))

        def meet(n):
            q, distance = n // plan.long, plan.long - 1 - n % plan.long
            for d in sorted({-distance, distance}):
                total.dest(d, q)

        ks = from_far(plan.wide)
        total.start(ks)
        begin(jnp.int32(0))
        for k in ks[:-1]:
            total.stage_over(k)

        @pl.loop(0, steps)
        def _(step):
            run_if(step + 1 < steps, lambda: begin(step + 1))

            def ready(kind):
                for copy in fetch(kind, step):
                    copy.wait()
            per_kind(step, ready)
            slot = step % 2
            product = inner_left(left[slot], right[slot])
            fresh = step % 3 == 0

            @pl.when(fresh)
            def _():
                acc[...] = product

            @pl.when(jnp.logical_not(fresh))
            def _():
                acc[...] += product

            def done(kind):
                @pl.when(step < 3 * kinds)
                def _():
                    gone[kind] = acc[...].astype(jnp.bfloat16)
                    away(kind).start()

                @pl.when(step >= 3 * kinds)
                def _():
                    outs[kind][...] = acc[...]

            run_if(step % 3 == 2, lambda: per_kind(step, done))
            for n, at in enumerate(hooks):
                run_if(step == at, lambda n=n: meet(n))

        for n in range(len(hooks), pieces * plan.long):
            meet(n)
        out_ref[...] = total.result()
        for kind in range(kinds):
            away(kind).wait_recv()
            piece = 32

            @pl.loop(0, half // piece)
            def _(i, kind=kind):
                at = pl.ds(pl.multiple_of(i * piece, piece), piece)
                outs[kind][at, :] = outs[kind][at, :] + came[kind, at, :].astype(jnp.float32)

        for kind in range(kinds):
            away(kind).wait_send()
        total.drain()

    anywhere = pl.BlockSpec(memory_space=pl.ANY)
    sem = lambda n: pltpu.SemaphoreType.DMA((n,))
    outs = [jax.ShapeDtypeStruct((rows, width), parts.dtype)] + [jax.ShapeDtypeStruct((half, ff), jnp.float32)] * kinds
    return pl.pallas_call(
        kernel,
        out_shape=tuple(outs),
        in_specs=[anywhere] * 6,
        out_specs=tuple(pl.BlockSpec(memory_space=pltpu.VMEM) for _ in outs),
        scratch_shapes=[
            pltpu.VMEM((half, ff), jnp.float32),
            pltpu.VMEM((2, depth, half), jnp.bfloat16),
            pltpu.VMEM((2, depth, ff), jnp.bfloat16),
            pltpu.VMEM((kinds, half, ff), jnp.bfloat16),
            pltpu.VMEM((kinds, half, ff), jnp.bfloat16),
            sem(2), sem(2), sem(kinds), sem(kinds),
        ] + RowSum.scratch(plan, rows, width, parts.dtype, pieces),
        compiler_params=pltpu.CompilerParams(
            collective_id=collective_id, has_side_effects=True, vmem_limit_bytes=VMEM_MOST),
        name="scatter_experts",
    )(parts, *lefts, *rights)


def visible_bias(shape, first_key, start, first_query):
    key_pos = first_key + lax.broadcasted_iota(jnp.int32, shape, 0)
    query_pos = first_query + lax.broadcasted_iota(jnp.int32, shape, 1)
    seen = jnp.logical_and(key_pos >= start, key_pos <= query_pos)
    return jnp.where(seen, 0.0, masked_value)


def lanes(first):
    return pl.ds(pl.multiple_of(first, HEAD), HEAD)


def turned(values, cosine, sine):
    return values * cosine + pltpu.roll(values, HEAD // 2, 1) * sine


def whole_spec(*shape):
    return pl.BlockSpec(shape, lambda *s: (0,) * len(shape))


def project_kernel(x_ref, gain_ref, cos_ref, sin_ref, wq_ref, wk_ref, wv_ref, hid_ref, q_ref, kv_ref, hidden):
    @pl.when(pl.program_id(0) == 0)
    def _():
        hidden[...] = normed(x_ref[...].astype(jnp.float32), gain_ref[...]).astype(jnp.bfloat16)
        hid_ref[...] = hidden[...]

    cosine, sine = cos_ref[...], sin_ref[...]
    q = jnp.dot(hidden[...], wq_ref[...], preferred_element_type=jnp.float32)
    k = jnp.dot(hidden[...], wk_ref[...], preferred_element_type=jnp.float32)
    v = jnp.dot(hidden[...], wv_ref[...], preferred_element_type=jnp.float32)
    for h in range(q.shape[1] // HEAD):
        at = slice(h * HEAD, (h + 1) * HEAD)
        q_ref[:, at] = (turned(q[:, at], cosine, sine) * HEAD ** (-0.5)).astype(jnp.bfloat16)
        kv_ref[:, 2 * h * HEAD : (2 * h + 1) * HEAD] = turned(k[:, at], cosine, sine).astype(jnp.bfloat16)
        kv_ref[:, (2 * h + 1) * HEAD : (2 * h + 2) * HEAD] = v[:, at].astype(jnp.bfloat16)


def project(tokens, gain, cosine, sine, wq, wk, wv):
    rows, width = tokens.shape
    tile = 2 * HEAD
    column = pl.BlockSpec((width, tile), lambda i: (0, i))
    return pl.pallas_call(
        project_kernel,
        out_shape=(
            jax.ShapeDtypeStruct((rows, width), jnp.bfloat16),
            jax.ShapeDtypeStruct((rows, width), jnp.bfloat16),
            jax.ShapeDtypeStruct((rows, 2 * width), jnp.bfloat16),
        ),
        grid=(width // tile,),
        in_specs=[whole_spec(rows, width), whole_spec(1, width), whole_spec(rows, HEAD), whole_spec(rows, HEAD),
                  column, column, column],
        out_specs=(whole_spec(rows, width), pl.BlockSpec((rows, tile), lambda i: (0, i)),
                   pl.BlockSpec((rows, 2 * tile), lambda i: (0, i))),
        scratch_shapes=[pltpu.VMEM((rows, width), jnp.bfloat16)],
        cost_estimate=pl.CostEstimate(flops=6 * rows * width * width, bytes_accessed=6 * width * width, transcendentals=0),
        name="project",
    )(tokens, gain[None, :], cosine, sine, wq, wk, wv)


def attend_kernel(info, q_ref, start_ref, kv_ref, mixed_ref, low_ref, total_ref, bias, top, norm):
    step = pl.program_id(0)
    me, first_block = info[0], info[1]
    rows = q_ref.shape[0]
    block = me - step

    @pl.when(step == 0)
    def _():
        top[...] = jnp.full_like(top, masked_value)
        norm[...] = jnp.zeros_like(norm)
        mixed_ref[...] = jnp.zeros_like(mixed_ref)

    @pl.when(block >= first_block)
    def _():
        bias[...] = visible_bias((rows, rows), block * rows, start_ref[...], me * rows)

        @pl.loop(0, HEADS, unroll=2)
        def _(h):
            keys, values = kv_ref[0, :, lanes(2 * h * HEAD)], kv_ref[0, :, lanes((2 * h + 1) * HEAD)]
            scores = inner_right(keys, q_ref[:, lanes(h * HEAD)]) + bias[...]
            old = top[h]
            new = jnp.maximum(old, jnp.max(scores, axis=0, keepdims=True))
            weights = jnp.exp(scores - new)
            shrink = jnp.exp(old - new)
            top[h] = new
            norm[h] = norm[h] * shrink + jnp.sum(weights, axis=0, keepdims=True)
            mixed_ref[h] = mixed_ref[h] * shrink + inner_left(values, weights.astype(jnp.bfloat16))

    @pl.when(step == pl.num_programs(0) - 1)
    def _():
        for h in range(HEADS):
            mixed = mixed_ref[h] / norm[h]
            mixed_ref[h] = mixed
            low_ref[:, h * HEAD : (h + 1) * HEAD] = mixed.T.astype(jnp.bfloat16)
            total_ref[h] = top[h] + jnp.log(norm[h])


def attend(info, queries, start, pairs):
    rows, width = queries.shape
    steps = pairs.shape[0] // 2 + 1
    return pl.pallas_call(
        attend_kernel,
        out_shape=(
            jax.ShapeDtypeStruct((HEADS, HEAD, rows), jnp.float32),
            jax.ShapeDtypeStruct((rows, width), jnp.bfloat16),
            jax.ShapeDtypeStruct((HEADS, 1, rows), jnp.float32),
        ),
        grid_spec=pltpu.PrefetchScalarGridSpec(
            num_scalar_prefetch=1,
            grid=(steps,),
            in_specs=[
                whole_spec(rows, width),
                whole_spec(1, rows),
                pl.BlockSpec((1, rows, 2 * width), lambda s, info: (jnp.maximum(info[0] - s, info[1]), 0, 0)),
            ],
            out_specs=(whole_spec(HEADS, HEAD, rows), whole_spec(rows, width), whole_spec(HEADS, 1, rows)),
            scratch_shapes=[
                pltpu.VMEM((rows, rows), jnp.float32),
                pltpu.VMEM((HEADS, 1, rows), jnp.float32),
                pltpu.VMEM((HEADS, 1, rows), jnp.float32),
            ],
        ),
        cost_estimate=pl.CostEstimate(
            flops=4 * rows * rows * width * steps, bytes_accessed=4 * rows * width * steps, transcendentals=0
        ),
        name="attend",
    )(info, queries, start, pairs)


def attend_back_kernel(
    info, q_ref, g_ref, mixed_ref, start_ref, total_ref, cos_ref, sin_ref, kv_ref, dkv_ref, dq_ref, bias, acc, term
):
    step = pl.program_id(0)
    me, first_block = info[0], info[1]
    rows = q_ref.shape[0]
    block = me - step

    @pl.when(step == 0)
    def _():
        acc[...] = jnp.zeros_like(acc)
        for h in range(HEADS):
            grads = g_ref[:, h * HEAD : (h + 1) * HEAD].astype(jnp.float32).T
            term[h] = jnp.sum(grads * mixed_ref[h], axis=0, keepdims=True)

    @pl.when(block >= first_block)
    def _():
        bias[...] = visible_bias((rows, rows), block * rows, start_ref[...], me * rows)

        @pl.loop(0, HEADS, unroll=2)
        def _(h):
            early, late, at = lanes(2 * h * HEAD), lanes((2 * h + 1) * HEAD), lanes(h * HEAD)
            keys, values = kv_ref[0, :, early], kv_ref[0, :, late]
            queries, grads = q_ref[:, at], g_ref[:, at]
            probs = jnp.exp(inner_right(keys, queries) + bias[...] - total_ref[h])
            prob_grad = inner_right(values, grads)
            score_grad = (probs * (prob_grad - term[h])).astype(jnp.bfloat16)
            dkv_ref[0, :, late] = jnp.dot(
                probs.astype(jnp.bfloat16), grads, preferred_element_type=jnp.float32
            ).astype(jnp.bfloat16)
            dkv_ref[0, :, early] = jnp.dot(
                score_grad, queries, preferred_element_type=jnp.float32
            ).astype(jnp.bfloat16)
            acc[h] += inner_left(keys, score_grad)

    @pl.when(jnp.logical_and(block >= 0, block < first_block))
    def _():
        dkv_ref[...] = jnp.zeros_like(dkv_ref)

    @pl.when(step == pl.num_programs(0) - 1)
    def _():
        for h in range(HEADS):
            back = turned(acc[h].T * HEAD ** (-0.5), cos_ref[...], -sin_ref[...])
            dq_ref[:, h * HEAD : (h + 1) * HEAD] = back.astype(jnp.bfloat16)


def attend_back(info, queries, grads, mixed, start, total, cosine, sine, pairs):
    rows, width = queries.shape
    count = pairs.shape[0]
    steps = count // 2 + 1
    return pl.pallas_call(
        attend_back_kernel,
        out_shape=(
            jax.ShapeDtypeStruct(pairs.shape, jnp.bfloat16),
            jax.ShapeDtypeStruct((rows, width), jnp.bfloat16),
        ),
        grid_spec=pltpu.PrefetchScalarGridSpec(
            num_scalar_prefetch=1,
            grid=(steps,),
            in_specs=[
                whole_spec(rows, width),
                whole_spec(rows, width),
                whole_spec(HEADS, HEAD, rows),
                whole_spec(1, rows),
                whole_spec(HEADS, 1, rows),
                whole_spec(rows, HEAD),
                whole_spec(rows, HEAD),
                pl.BlockSpec((1, rows, 2 * width), lambda s, info: (jnp.maximum(info[0] - s, info[1]), 0, 0)),
            ],
            out_specs=(
                pl.BlockSpec((1, rows, 2 * width), lambda s, info: (jnp.maximum(info[0] - s, 0), 0, 0)),
                whole_spec(rows, width),
            ),
            scratch_shapes=[
                pltpu.VMEM((rows, rows), jnp.float32),
                pltpu.VMEM((HEADS, HEAD, rows), jnp.float32),
                pltpu.VMEM((HEADS, 1, rows), jnp.float32),
            ],
        ),
        cost_estimate=pl.CostEstimate(
            flops=10 * rows * rows * width * steps, bytes_accessed=8 * rows * width * steps, transcendentals=0
        ),
        name="attend_back",
    )(info, queries, grads, mixed, start, total, cosine, sine, pairs)


def finish_kernel(
    x_ref, gain_ref, res_ref, hid_ref, q_ref, kv_ref, cos_ref, sin_ref, wq_ref, wk_ref, wv_ref,
    dq_ref, dk_ref, dv_ref, out_ref, gain_out, acc,
):
    step = pl.program_id(0)

    @pl.when(step == 0)
    def _():
        acc[...] = jnp.zeros_like(acc)

    cosine, sine = cos_ref[...], sin_ref[...]
    count = q_ref.shape[1] // HEAD
    keys = jnp.concatenate(
        [turned(kv_ref[:, 2 * h * HEAD : (2 * h + 1) * HEAD].astype(jnp.float32), cosine, -sine).astype(jnp.bfloat16)
         for h in range(count)], axis=1)
    values = jnp.concatenate([kv_ref[:, (2 * h + 1) * HEAD : (2 * h + 2) * HEAD] for h in range(count)], axis=1)
    grads = (q_ref[...], keys, values)
    acc[...] += (
        inner_right(grads[0], wq_ref[...]) + inner_right(grads[1], wk_ref[...]) + inner_right(grads[2], wv_ref[...])
    )
    hidden = hid_ref[...]
    for ref, grad in zip((dq_ref, dk_ref, dv_ref), grads):
        ref[...] = inner_left(hidden, grad).astype(jnp.bfloat16)

    @pl.when(step == pl.num_programs(0) - 1)
    def _():
        values, gain, grad = x_ref[...].astype(jnp.float32), gain_ref[...], acc[...]
        scale = lax.rsqrt(jnp.mean(values * values, axis=1, keepdims=True) + epsilon)
        inner = jnp.mean(gain * grad * values, axis=1, keepdims=True)
        part = scale * gain * grad - values * (scale * scale * scale) * inner
        out_ref[...] = (res_ref[...] + part).astype(jnp.bfloat16)
        gain_out[...] = jnp.sum(grad * values * scale, axis=0, keepdims=True)


def finish(tokens, gain, residual_grad, hidden, query_grad, pair_grads, cosine, sine, wq, wk, wv):
    rows, width = tokens.shape
    tile = 2 * HEAD
    column = pl.BlockSpec((width, tile), lambda i: (0, i))
    return pl.pallas_call(
        finish_kernel,
        out_shape=(
            jax.ShapeDtypeStruct((width, width), jnp.bfloat16),
            jax.ShapeDtypeStruct((width, width), jnp.bfloat16),
            jax.ShapeDtypeStruct((width, width), jnp.bfloat16),
            jax.ShapeDtypeStruct((rows, width), jnp.bfloat16),
            jax.ShapeDtypeStruct((1, width), jnp.float32),
        ),
        grid=(width // tile,),
        in_specs=[whole_spec(rows, width), whole_spec(1, width), whole_spec(rows, width), whole_spec(rows, width),
                  pl.BlockSpec((rows, tile), lambda i: (0, i)), pl.BlockSpec((rows, 2 * tile), lambda i: (0, i)),
                  whole_spec(rows, HEAD), whole_spec(rows, HEAD), column, column, column],
        out_specs=(column, column, column, whole_spec(rows, width), whole_spec(1, width)),
        scratch_shapes=[pltpu.VMEM((rows, width), jnp.float32)],
        cost_estimate=pl.CostEstimate(flops=12 * rows * width * width, bytes_accessed=12 * width * width, transcendentals=0),
        name="finish",
    )(tokens, gain[None, :], residual_grad, hidden, query_grad, pair_grads, cosine, sine, wq, wk, wv)


def experts_kernel(
    where_ref, x_ref, g_ref, rank_row, rank_col, share_row, wg_ref, wu_ref, wd_ref,
    back_ref, routed_ref, in_ref, pre_ref, lift_ref, mid_ref, og_ref, grads,
):
    blocks, rows, side = x_ref.shape
    capacity = in_ref.shape[0] // blocks
    width = og_ref.shape[1]
    dot = lambda left, right: jnp.dot(left, right, preferred_element_type=jnp.float32)
    shares = []
    for i in range(blocks):
        at = slice(i * capacity, (i + 1) * capacity)
        hit = rank_row[i] == lax.broadcasted_iota(jnp.int32, (capacity, rows), 0)
        pick = jnp.where(hit, 1.0, 0.0)
        shares.append(jnp.sum(pick * share_row[i], axis=1, keepdims=True))
        pick = pick.astype(jnp.bfloat16)
        in_ref[at, :] = dot(pick, x_ref[i, :, :width]).astype(jnp.bfloat16)
        grads[at, :] = dot(pick, g_ref[i]).astype(jnp.bfloat16)
    share = jnp.concatenate(shares, axis=0)
    pre = dot(in_ref[...], wg_ref[0])
    lift = dot(in_ref[...], wu_ref[0])
    silu, slope = silu_parts(pre)
    mid_ref[...] = (silu * lift).astype(jnp.bfloat16)
    lift_slope = lift * slope
    result = dot(mid_ref[...], wd_ref[0]).astype(jnp.bfloat16).astype(jnp.float32)
    grad = grads[...].astype(jnp.float32)
    gate_grad = jnp.sum(result * grad, axis=1, keepdims=True)
    og_ref[...] = (share * grad).astype(jnp.bfloat16)
    given = (share * result).astype(jnp.bfloat16)
    mid_grad = inner_right(og_ref[...], wd_ref[0])
    pre_ref[...] = (mid_grad * lift_slope).astype(jnp.bfloat16)
    lift_ref[...] = (mid_grad * silu).astype(jnp.bfloat16)
    in_grad = (inner_right(pre_ref[...], wg_ref[0]) + inner_right(lift_ref[...], wu_ref[0])).astype(jnp.bfloat16)
    lane = lax.broadcasted_iota(jnp.int32, (blocks * capacity, side - width), 1)
    high = gate_grad.astype(jnp.bfloat16).astype(jnp.float32)
    extra = jnp.where(lane == where_ref[0], high, jnp.where(lane == where_ref[1], gate_grad - high, 0.0))
    extra = extra.astype(jnp.bfloat16)
    for i in range(blocks):
        at = slice(i * capacity, (i + 1) * capacity)
        hit = rank_col[i] == lax.broadcasted_iota(jnp.int32, (rows, capacity), 1)
        put = jnp.where(hit, 1.0, 0.0).astype(jnp.bfloat16)
        back_ref[i, :, :width] = dot(put, in_grad[at, :]).astype(jnp.bfloat16)
        back_ref[i, :, width:] = dot(put, extra[at, :]).astype(jnp.bfloat16)
        routed_ref[i] = dot(put, given[at, :]).astype(jnp.bfloat16)


def run_experts(places, arrived, grads, rank, share, gate, up, down, capacity):
    count, rows, side = arrived.shape
    width, ff = gate.shape[1], gate.shape[2]
    blocks = 384 // capacity
    flat = count * capacity
    once = lambda *shape: pl.BlockSpec(shape, lambda i, p: (0,) * len(shape), pipeline_mode=pl.Buffered(1))
    lead = lambda *shape: pl.BlockSpec((blocks,) + shape, lambda i, p: (i, 0, 0))
    tall = lambda wide: pl.BlockSpec((blocks * capacity, wide), lambda i, p: (i, 0))
    shape = lambda *dims: jax.ShapeDtypeStruct(dims, jnp.bfloat16)
    return pl.pallas_call(
        experts_kernel,
        out_shape=(shape(count, rows, side), shape(count, rows, width), shape(flat, width), shape(flat, ff),
                   shape(flat, ff), shape(flat, ff), shape(flat, width)),
        grid_spec=pltpu.PrefetchScalarGridSpec(
            num_scalar_prefetch=1,
            grid=(count // blocks,),
            in_specs=[lead(rows, side), lead(rows, width), lead(1, rows), lead(rows, 1), lead(1, rows),
                      once(1, width, ff), once(1, width, ff), once(1, ff, width)],
            out_specs=(lead(rows, side), lead(rows, width), tall(width), tall(ff), tall(ff), tall(ff), tall(width)),
            scratch_shapes=[pltpu.VMEM((blocks * capacity, width), jnp.bfloat16)],
        ),
        compiler_params=pltpu.CompilerParams(vmem_limit_bytes=VMEM_MOST),
        cost_estimate=pl.CostEstimate(flops=16 * flat * width * ff, bytes_accessed=16 * flat * width, transcendentals=0),
        name="run_experts",
    )(places, arrived, grads, rank[:, None, :], rank[:, :, None], share[:, None, :], gate, up, down)


def attend_back_sum(queries, grads, mixed, start, total, cosine, sine, pairs, parts, collective_id):
    rows, width = queries.shape
    ep_count = pairs.shape[0]
    part_rows, part_width = parts[0].shape[1], sum(part.shape[2] for part in parts)
    plan, pieces = Plan(ep_count, True), 4
    place = Place(lax.axis_size("grp"), ep_count)
    n, wide = plan.planes(), plan.wide
    cuts = [0, part_width // HEAD * 3 // 4 * HEAD, part_width]
    orders = ("xba", "bxa")

    def kernel(q_ref, g_ref, mixed_ref, start_ref, total_ref, cos_ref, sin_ref, pair_ref, *refs):
        sources, refs = refs[: len(parts)], refs[len(parts) :]
        out_ref, pair_out, dq_ref, bias, acc, term, kv, staged, kv_sem = refs[:9]
        refs = refs[9:]
        place.locate()
        sums = []
        for i in range(2):
            sums.append(WholeSum(place, orders[i], pieces_of(sources, cuts[i], cuts[i + 1]), refs[:14]))
            refs = refs[14:]
        sum_rows = RowSum(plan, pieces, staged, refs)
        a, b, c = sum_rows.a, sum_rows.b, sum_rows.c
        me = plan.slot(a, b, c)
        order, ks = sum_rows.order, from_far(wide)
        turns = [(k, d) for d in order for k in ks]

        def block(turn, other):
            k, d = turns[turn]
            b0, c0 = sum_rows.source(k), jnp.where(other, 1 - c, c)
            there = both(plan.inside(a - d), plan.need(d, b, c, b0, c0))
            return there, plan.slot(a - d, b0, c0)

        def fetch(turn, other):
            there, slot = block(turn, other)
            held = jnp.where(other, 0, 1)
            return there, lambda: pltpu.make_async_copy(pair_ref.at[slot], kv.at[held], kv_sem.at[held])

        def begin(turn, other):
            there, go = fetch(turn, other)
            run_if(there, lambda: go().start())

        def compute(turn, other, target):
            there, slot = block(turn, other)
            held = 0 if other else 1

            def work():
                fetch(turn, other)[1]().wait()
                bias[...] = visible_bias((rows, rows), slot * rows, start_ref[...], me * rows)

                @pl.loop(0, HEADS, unroll=2)
                def _(h):
                    early, late, at = lanes(2 * h * HEAD), lanes((2 * h + 1) * HEAD), lanes(h * HEAD)
                    keys, values = kv[held, :, early], kv[held, :, late]
                    own, grad = q_ref[:, at], g_ref[:, at]
                    probs = jnp.exp(inner_right(keys, own) + bias[...] - total_ref[h])
                    score_grad = (probs * (inner_right(values, grad) - term[h])).astype(jnp.bfloat16)
                    target[:, late] = jnp.dot(
                        probs.astype(jnp.bfloat16), grad, preferred_element_type=jnp.float32
                    ).astype(jnp.bfloat16)
                    target[:, early] = jnp.dot(
                        score_grad, own, preferred_element_type=jnp.float32
                    ).astype(jnp.bfloat16)
                    acc[h] += inner_left(keys, score_grad)

            run_if(there, work)

        def turn_of(turn):
            k, d = turns[turn]
            i = plan.plane(a, d)
            compute(turn, True, staged.at[i, k])
            if turn + 1 < len(turns):
                begin(turn + 1, True)
            cond = sum_rows.cross(d, k, 0)[0]
            for q in range(pieces):
                run_if(cond, lambda q=q: sum_rows.cross(d, k, q)[1]().start())
            compute(turn, False, sum_rows.held.at[i, k])
            if turn + 1 < len(turns):
                begin(turn + 1, False)

        def pass_on(turn):
            k, d = turns[turn]

            @pl.loop(0, pieces)
            def _(q):
                sum_rows.first(d, k, q)
                cond, go = sum_rows.over(d, k, q)
                run_if(cond, lambda: go().start())

        begin(0, True)
        begin(0, False)
        place.greet()
        first, second = sums
        for one in sums:
            for i in range(one.n1 - 1):
                one.start(i)
        acc[...] = jnp.zeros_like(acc)
        for h in range(HEADS):
            grad = g_ref[:, h * HEAD : (h + 1) * HEAD].astype(jnp.float32).T
            term[h] = jnp.sum(grad * mixed_ref[h], axis=0, keepdims=True)
        for one in sums:
            for i in range(one.n1 - 1):
                one.stage_core(i)
        last = len(turns) - 1
        for turn in range(len(turns)):
            turn_of(turn)
            if turns[turn][0]:
                pass_on(turn)
            if turn == 0:
                for one in sums:
                    one.start(one.n1 - 1)
            if turn == last - 3:
                for one in sums:
                    one.stage_core(one.n1 - 1)
                for k2 in from_far(second.n2)[:-1]:
                    second.stage_one(k2)
            if turn == last - 2:
                sum_rows.stage_dest(order[0], 0, 2)
            if turn == last - 1:
                for k2 in from_far(first.n2)[:-1]:
                    first.stage_one(k2)
                second.stage_one(0)
                sum_rows.stage_dest(order[0], 2, 3)
        sum_rows.stage_dest(order[0], 3, pieces)
        first.stage_one(0)
        for h in range(HEADS):
            back = turned(acc[h].T * HEAD ** (-0.5), cos_ref[...], -sin_ref[...])
            dq_ref[:, h * HEAD : (h + 1) * HEAD] = back.astype(jnp.bfloat16)
        second.stage_two()
        for d in order[1:]:
            sum_rows.stage_dest(d, 0, pieces)
        pair_out[...] = sum_rows.result()
        first.stage_two()
        for i, one in enumerate(sums):
            one.stage_three(out_ref.at[:, pl.ds(cuts[i], cuts[i + 1] - cuts[i])])
        sum_rows.drain()
        for one in sums:
            one.drain()

    anywhere, near = pl.BlockSpec(memory_space=pl.ANY), pl.BlockSpec(memory_space=pltpu.VMEM)
    scratch = [
        pltpu.VMEM((rows, rows), jnp.float32),
        pltpu.VMEM((HEADS, HEAD, rows), jnp.float32),
        pltpu.VMEM((HEADS, 1, rows), jnp.float32),
        pltpu.VMEM((2, rows, 2 * width), jnp.bfloat16),
        pltpu.VMEM((n, wide, rows, 2 * width), jnp.bfloat16),
        pltpu.SemaphoreType.DMA((2,)),
    ]
    for i in range(2):
        scratch += WholeSum.scratch(place.sizes, orders[i], part_rows, cuts[i + 1] - cuts[i], parts[0].dtype, len(parts))
    scratch += RowSum.scratch(plan, rows, 2 * width, pairs.dtype, pieces)
    return pl.pallas_call(
        kernel,
        out_shape=(jax.ShapeDtypeStruct((part_rows, part_width), jnp.float32),
                   jax.ShapeDtypeStruct((rows, 2 * width), pairs.dtype),
                   jax.ShapeDtypeStruct((rows, width), jnp.bfloat16)),
        in_specs=[near] * 7 + [anywhere] * (1 + len(parts)),
        out_specs=(near, near, near),
        scratch_shapes=scratch,
        compiler_params=pltpu.CompilerParams(
            collective_id=collective_id, has_side_effects=True, vmem_limit_bytes=VMEM_MOST),
        name="attend_back_sum",
    )(queries, grads, mixed, start, total, cosine, sine, pairs, *parts)


def local(
    tokens,
    doc_lengths,
    expert_ids,
    out_grad,
    mixer_gain,
    query_weight,
    key_weight,
    value_weight,
    output_weight,
    ffn_gain,
    router_weight,
    shared_gate,
    shared_up,
    shared_down,
    expert_gate,
    expert_up,
    expert_down,
):
    rows, width = tokens.shape[1], tokens.shape[2]
    ep_count = lax.axis_size("ep")
    device_count = ep_count * lax.axis_size("grp")
    ep_index = lax.axis_index("ep")
    expert_count = router_weight.shape[1]
    capacity = min(rows, 12 * rows * TOP // (7 * expert_count))
    low = lambda v: v.astype(jnp.bfloat16)
    wide = lambda v: v.astype(jnp.float32)
    dot = lambda left, right: jnp.dot(left, right, preferred_element_type=jnp.float32)

    grad_low = out_grad[0]

    doc_ends = jnp.cumsum(doc_lengths[0])
    query_pos = ep_index * rows + jnp.arange(rows, dtype=jnp.int32)
    before = query_pos[:, None] >= doc_ends[None, :]
    start = jnp.max(jnp.where(before, doc_ends[None, :], 0), axis=1)
    info = jnp.stack([ep_index, start[0] // rows]).astype(jnp.int32)
    half_dim = HEAD // 2
    frequency = rope_base ** (-jnp.arange(half_dim, dtype=jnp.float32) / half_dim)
    angles = wide(query_pos)[:, None] * frequency[None, :]
    cosine, sine = jnp.cos(angles), jnp.sin(angles)
    cosine = jnp.concatenate([cosine, cosine], axis=1)
    sine = jnp.concatenate([-sine, sine], axis=1)

    stream = wide(tokens[0])
    hidden_low, queries, own_pairs = project(
        tokens[0], mixer_gain, cosine, sine, query_weight, key_weight, value_weight
    )
    pairs = gather_rows(own_pairs, True, 1, 8)
    grad_later, pairs = lax.optimization_barrier((grad_low, pairs))
    grads_all = lax.all_gather(grad_later, "ep", axis=0, tiled=False)
    mixed, mixed_low, log_total = attend(info, queries, start[None, :], pairs)
    mixer_out = dot(mixed_low, output_weight)
    residual = stream + mixer_out
    ffn_low = low(normed(residual, ffn_gain))

    logits = dot(ffn_low, router_weight)
    experts = jnp.arange(expert_count, dtype=jnp.int32)
    assigned = jnp.any(expert_ids[0][:, :, None] == experts[None, None, :], axis=1)
    shown = jnp.where(assigned, logits, masked_value)
    powers = jnp.where(assigned, jnp.exp(shown - jnp.max(shown, axis=1, keepdims=True)), 0.0)
    gate_probs = powers / jnp.sum(powers, axis=1, keepdims=True)
    probs_high = low(gate_probs)
    probs_rest = low(gate_probs - wide(probs_high))
    side = width + 2 * HEAD if 2 * expert_count > HEAD else width + HEAD
    pad = jnp.zeros((rows, side - width - 2 * expert_count), jnp.bfloat16)
    sent = jnp.concatenate([ffn_low, probs_high, probs_rest, pad], axis=1)
    arrived, shared_out, ffn_grad, shared_gate_part, shared_up_part, shared_down_part = gather_shared(
        sent, grad_low, shared_gate, shared_up, shared_down, 2
    )

    own = experts[None, None, :] == ep_index
    high = arrived[:, :, width : width + expert_count]
    rest = arrived[:, :, width + expert_count : width + 2 * expert_count]
    share = jnp.sum(jnp.where(own, wide(high) + wide(rest), 0.0), axis=2)
    chosen = share > 0.0
    earlier = (jnp.arange(rows)[:, None] < jnp.arange(rows)[None, :]).astype(jnp.bfloat16)
    rank = dot(low(chosen), earlier).astype(jnp.int32)
    rank = jnp.where(chosen, rank, -1)
    places = jnp.stack([ep_index, expert_count + ep_index]).astype(jnp.int32)
    back, given, flat_in, pre_grad, lift_grad, middle, result_grad = run_experts(
        places, arrived, grads_all, rank, share, expert_gate, expert_up, expert_down, capacity
    )
    routed = lax.psum_scatter(given, "ep", scatter_dimension=0)
    group_count = lax.axis_size("grp")
    if group_count == 2:
        back_sum, gate_sum, up_sum, down_sum = scatter_experts(
            back, (flat_in, result_grad), (pre_grad, lift_grad, middle), 3
        )
        gate_sum, up_sum, down_sum = gate_sum[None], up_sum[None], down_sum.T[None]
    else:
        back_sum = scatter_rows(back, False, 3)
        split = width // group_count
        own_down_grad = jnp.concatenate(
            [low(inner_left(middle, result_grad[:, i * split : (i + 1) * split])) for i in range(group_count)], axis=0
        )
        over_groups = lambda v: wide(lax.psum_scatter(v, "grp", scatter_dimension=0, tiled=True))[None]
        gate_sum = over_groups(low(inner_left(flat_in, pre_grad)))
        up_sum = over_groups(low(inner_left(flat_in, lift_grad)))
        down_sum = over_groups(own_down_grad)

    grad_out = wide(grad_low)
    gate_back = wide(back_sum[:, width : width + expert_count]) + wide(
        back_sum[:, width + expert_count : width + 2 * expert_count]
    )
    chosen_grad = gate_probs * (gate_back - jnp.sum(gate_probs * gate_back, axis=1, keepdims=True))
    logit_grad = low(chosen_grad)
    ffn_grad = ffn_grad + wide(back_sum[:, :width]) + inner_right(logit_grad, router_weight)
    _, ffn_pull = jax.vjp(normed, residual, ffn_gain)
    residual_part, ffn_gain_grad = ffn_pull(ffn_grad)
    residual_grad = grad_out + residual_part
    mixer_grad_low = low(residual_grad)
    mixed_grad = low(inner_right(mixer_grad_low, output_weight))
    by_device = lambda v: low(v).reshape(device_count, width // device_count, -1)
    early = [
        by_device(part)
        for part in (shared_gate_part, shared_up_part, shared_down_part, inner_left(mixed_low, mixer_grad_low))
    ]
    if ep_count > 16:
        pair_parts, query_lin_grad = attend_back(
            info, queries, mixed_grad, mixed, start[None, :], log_total, cosine, sine, pairs
        )
        pair_grads = scatter_rows(pair_parts, True, 4)
        early_sum = scatter_whole(early, 5)
    else:
        early_sum, pair_grads, query_lin_grad = attend_back_sum(
            queries, mixed_grad, mixed, start[None, :], log_total, cosine, sine, pairs, early, 5
        )

    routed, pair_grads = lax.optimization_barrier((routed, pair_grads))
    layer_out = residual + shared_out + wide(routed)
    query_part, key_part, value_part, tokens_grad, mixer_gain_grad = finish(
        tokens[0], mixer_gain, residual_grad, hidden_low, query_lin_grad, pair_grads, cosine, sine,
        query_weight, key_weight, value_weight,
    )
    squares = jnp.stack(
        [jnp.sum(residual * residual), jnp.sum(mixer_out * mixer_out), jnp.sum(layer_out * layer_out)]
    )
    extras = jnp.concatenate(
        [inner_left(ffn_low, logit_grad), mixer_gain_grad.T, ffn_gain_grad[:, None],
         jnp.broadcast_to(squares[None, :], (width, 3))], axis=1
    )
    extras = jnp.pad(extras, ((0, 0), (0, HEAD - extras.shape[1])))
    late_sum = scatter_whole([by_device(v) for v in (query_part, key_part, value_part, extras)], 6)
    extra_sum = late_sum[:, 3 * width :]
    entry_count = rows * device_count * width
    stream_rms = jnp.sqrt(extra_sum[0, expert_count + 2 : expert_count + 5] / entry_count)
    ff = shared_gate.shape[1]
    return (
        low(layer_out)[None],
        tokens_grad[None],
        extra_sum[:, expert_count],
        late_sum[:, :width],
        late_sum[:, width : 2 * width],
        late_sum[:, 2 * width : 3 * width],
        early_sum[:, 3 * ff :],
        extra_sum[:, expert_count + 1],
        extra_sum[:, :expert_count],
        early_sum[:, :ff],
        early_sum[:, ff : 2 * ff],
        early_sum[:, 2 * ff : 3 * ff].T,
        gate_sum,
        up_sum,
        down_sum,
        stream_rms,
    )


def solution(mesh):
    return jax.shard_map(
        local,
        mesh=mesh,
        in_specs=(
            P("grp", "ep", None),
            P("grp", None),
            P("grp", "ep", None),
            P("grp", "ep", None),
            P(),
            P(),
            P(),
            P(),
            P(),
            P(),
            P(),
            P(),
            P(),
            P(),
            P("ep", None, None),
            P("ep", None, None),
            P("ep", None, None),
        ),
        out_specs=(
            P("grp", "ep", None),
            P("grp", "ep", None),
            P(("grp", "ep")),
            P(("grp", "ep"), None),
            P(("grp", "ep"), None),
            P(("grp", "ep"), None),
            P(("grp", "ep"), None),
            P(("grp", "ep")),
            P(("grp", "ep"), None),
            P(("grp", "ep"), None),
            P(("grp", "ep"), None),
            P(None, ("grp", "ep")),
            P("ep", "grp", None),
            P("ep", "grp", None),
            P("ep", None, "grp"),
            P(),
        ),
        check_vma=False,
    )
```

```python
import functools

import jax
import jax.numpy as jnp
from jax import lax
from jax.experimental import pallas as pl
from jax.experimental.pallas import tpu as pltpu
from jax.sharding import PartitionSpec as P

HEADS = 10
HEAD = 128
TOP = 7

epsilon = 1e-06
rope_base = 10000.0
masked_value = -1e30


def normed(values, gain_vec):
    return (
        values * lax.rsqrt(jnp.mean(values * values, axis=-1, keepdims=True) + epsilon) * gain_vec
    )


def inner_left(left_op, right_op):
    return lax.dot_general(
        left_op, right_op, (((0,), (0,)), ((), ())), preferred_element_type=jnp.float32
    )


def inner_right(left_op, right_op):
    return lax.dot_general(
        left_op, right_op, (((1,), (1,)), ((), ())), preferred_element_type=jnp.float32
    )


def silu_parts(pre_act):
    sigmoid_val = jax.nn.sigmoid(pre_act)
    return (pre_act * sigmoid_val, sigmoid_val * (1.0 + pre_act * (1.0 - sigmoid_val)))


MESH = pl.DeviceIdType.MESH
COUPLES = 2
VMEM_MOST = 64 * 1024 * 1024 - 65536


def when(cond):
    if cond is True:
        return lambda f: f()
    if cond is False:
        return lambda f: None
    return pl.when(cond)


def both(*conds):
    out = True
    for cond in conds:
        if cond is False:
            return False
        if cond is True:
            continue
        out = cond if out is True else jnp.logical_and(out, cond)
    return out


class Plan:
    def __init__(self, ep_count, window):
        self.long = 4
        self.wide = ep_count // 8
        self.window = window
        self.steps = (
            list(range(self.long // 2 + 1))
            if window
            else list(range(-(self.long - 1), self.long))
        )

    def place(self):
        me = lax.axis_index("ep")
        return me // (2 * self.wide), (me // 2) % self.wide, me % 2

    def slot(self, a, b, c):
        return (a * self.wide + b) * 2 + c

    def plane(self, a, d):
        return d if self.window else jnp.clip(a - d, 0, self.long - 1)

    def planes(self):
        return len(self.steps) if self.window else self.long

    def inside(self, a):
        return jnp.logical_and(a >= 0, a < self.long)

    def need(self, d, b, c, b0, c0):
        if not self.window or 0 < d < self.long // 2:
            return True
        if d == 0:
            return jnp.logical_or(b0 < b, jnp.logical_and(b0 == b, c0 <= c))
        return jnp.logical_or(b0 > b, jnp.logical_and(b0 == b, c0 >= c))

    def need_pair(self, d, b, b0):
        if not self.window or 0 < d < self.long // 2:
            return True
        return b0 < b if d == 0 else b0 > b

    def greet(self, a, b, c):
        barrier = pltpu.get_barrier_semaphore()

        def signal(cond, dev):
            @when(cond)
            def _():
                pl.semaphore_signal(barrier, inc=1, device_id={"ep": dev}, device_id_type=MESH)

        signal(a + 1 < self.long, self.slot(a + 1, b, c))
        signal(a > 0, self.slot(a - 1, b, c))
        for k in range(1, self.wide):
            signal(True, self.slot(a, (b + k) % self.wide, c))
        signal(True, self.slot(a, b, 1 - c))
        ends = (a == 0).astype(jnp.int32) + (a == self.long - 1).astype(jnp.int32)
        pl.semaphore_wait(barrier, self.wide + 2 - ends)


def gather_kernel(plan, pieces, beside, x_ref, out_ref, ra, sa_up, sa_dn, rb, sb, rc, sc, own):
    a, b, c = plan.place()
    steps, wide = plan.steps, plan.wide
    at = {d: i for i, d in enumerate(steps)}
    rows = x_ref.shape[0] // pieces

    def part(q):
        return pl.ds(pl.multiple_of(q * rows, rows), rows)

    def copy(q, src, slot, ssem, rsem, dev):
        return pltpu.make_async_remote_copy(
            src_ref=src, dst_ref=out_ref.at[slot, part(q)], send_sem=ssem, recv_sem=rsem,
            device_id={"ep": dev}, device_id_type=MESH,
        )

    def hops(d, q):
        i = at[d]
        slot = plan.slot(a - d, b, c)
        src = x_ref.at[part(q)] if d == 0 else out_ref.at[slot, part(q)]
        real = plan.inside(a - d)
        out = []
        if d >= 0 and d + 1 in at:
            out.append((both(real, a + 1 < plan.long), lambda: copy(
                q, src, slot, sa_up.at[i, q], ra.at[at[d + 1], q], plan.slot(a + 1, b, c))))
        if d <= 0 and d - 1 in at:
            out.append((both(real, a > 0), lambda: copy(
                q, src, slot, sa_dn.at[i, q], ra.at[at[d - 1], q], plan.slot(a - 1, b, c))))
        for k in range(1, wide):
            to = (b + k) % wide
            out.append((both(real, plan.need_pair(d, to, b)), lambda k=k, to=to: copy(
                q, src, slot, sb.at[i, k, q], rb.at[i, k, q], plan.slot(a, to, c))))
        out.append((both(real, plan.need(d, b, 1 - c, b, c)), lambda: copy(
            q, src, slot, sc.at[i, 0, q], rc.at[i, 0, q], plan.slot(a, b, 1 - c))))
        return out

    def cross(d, k, q):
        i = at[d]
        b0 = (b + wide - k) % wide
        slot = plan.slot(a - d, b0, c)
        real = plan.inside(a - d)
        come = lambda: copy(q, x_ref.at[part(q)], slot, sb.at[i, k, q], rb.at[i, k, q], plan.slot(a, b, c))
        go = lambda: copy(q, out_ref.at[slot, part(q)], slot, sc.at[i, k, q], rc.at[i, k, q],
                          plan.slot(a, b, 1 - c))
        return (both(real, plan.need_pair(d, b, b0)), come,
                both(real, plan.need(d, b, 1 - c, b0, c)), go)

    plan.greet(a, b, c)
    keep = pltpu.make_async_copy(x_ref, out_ref.at[plan.slot(a, b, c)], own)

    @pl.loop(0, pieces)
    def _(q):
        for cond, go in hops(0, q):
            @when(cond)
            def _(go=go):
                go().start()

    keep.start()
    far = max(abs(d) for d in steps)
    for step in range(1, far + 3):
        beside(step - 1)

        @pl.loop(0, pieces)
        def _(q, step=step):
            for d in (step, -step):
                if d in at:
                    @when(plan.inside(a - d))
                    def _(d=d):
                        slot = plan.slot(a - d, b, c)
                        copy(q, x_ref.at[part(q)], slot, sa_up.at[0, q], ra.at[at[d], q],
                             plan.slot(a, b, c)).wait_recv()
                        for cond, go in hops(d, q):
                            @when(cond)
                            def _(go=go):
                                go().start()
            for d in sorted({step - 2, 2 - step}) if step > 1 else ():
                if d in at:
                    for k in range(1, wide):
                        came, come, goes, go = cross(d, k, q)
                        @when(came)
                        def _(come=come):
                            come().wait_recv()
                        @when(goes)
                        def _(go=go):
                            go().start()
    keep.wait()

    @pl.loop(0, pieces)
    def _(q):
        for d in steps:
            i = at[d]
            real = plan.inside(a - d)
            for k in range(wide):
                b0 = (b + wide - k) % wide
                slot = plan.slot(a - d, b0, 1 - c)
                @when(both(real, plan.need(d, b, c, b0, 1 - c)))
                def _(slot=slot, i=i, k=k):
                    copy(q, x_ref.at[part(q)], slot, sc.at[i, k, q], rc.at[i, k, q],
                         plan.slot(a, b, c)).wait_recv()
            for cond, go in hops(d, q):
                @when(cond)
                def _(go=go):
                    go().wait_send()
            for k in range(1, wide):
                came, come, goes, go = cross(d, k, q)
                @when(goes)
                def _(go=go):
                    go().wait_send()


def gather_rows(block, window, collective_id, pieces=4):
    ep_count = lax.axis_size("ep")
    plan = Plan(ep_count, window)
    n, wide = len(plan.steps), plan.wide
    sem = pltpu.SemaphoreType.DMA
    return pl.pallas_call(
        functools.partial(gather_kernel, plan, pieces, lambda n: None),
        out_shape=jax.ShapeDtypeStruct((ep_count,) + block.shape, block.dtype),
        in_specs=[pl.BlockSpec(memory_space=pltpu.VMEM)],
        out_specs=pl.BlockSpec(memory_space=pl.ANY),
        scratch_shapes=[sem((n, pieces)), sem((n, pieces)), sem((n, pieces)), sem((n, wide, pieces)),
                        sem((n, wide, pieces)), sem((n, wide, pieces)), sem((n, wide, pieces)), sem],
        compiler_params=pltpu.CompilerParams(collective_id=collective_id, has_side_effects=True),
        name="gather_rows",
    )(block)


def gather_shared(block, grads, gate, up, down, collective_id, pieces=4):
    ep_count = lax.axis_size("ep")
    plan = Plan(ep_count, False)
    n, wide = len(plan.steps), plan.wide
    rows, width = grads.shape
    ff = gate.shape[1]
    sem = pltpu.SemaphoreType.DMA
    stages = max(plan.steps) + 2
    tiles = ff // HEAD

    def kernel(x_ref, g_ref, wg_ref, wu_ref, wd_ref, out_ref, shared_ref, back_ref, dg_ref, du_ref, dd_ref, *sems):
        dot = lambda left, right: jnp.dot(left, right, preferred_element_type=jnp.float32)

        def tile(i):
            at = pl.ds(pl.multiple_of(i * HEAD, HEAD), HEAD)
            x, g = x_ref[:, :width], g_ref[...]
            w_gate, w_up, w_down = wg_ref[:, at], wu_ref[:, at], wd_ref[at, :]
            silu, slope = silu_parts(dot(x, w_gate))
            lift = dot(x, w_up)
            mid = (silu * lift).astype(jnp.bfloat16)
            mid_grad = inner_right(g, w_down)
            pre_grad = (mid_grad * lift * slope).astype(jnp.bfloat16)
            lift_grad = (mid_grad * silu).astype(jnp.bfloat16)
            out = dot(mid, w_down)
            back = inner_right(pre_grad, w_gate) + inner_right(lift_grad, w_up)

            @pl.when(i == 0)
            def _():
                shared_ref[...] = out
                back_ref[...] = back

            @pl.when(i > 0)
            def _():
                shared_ref[...] += out
                back_ref[...] += back

            dg_ref[:, at] = inner_left(x, pre_grad).astype(jnp.bfloat16)
            du_ref[:, at] = inner_left(x, lift_grad).astype(jnp.bfloat16)
            dd_ref[:, at] = inner_left(g, mid).astype(jnp.bfloat16)

        def beside(stage):
            pl.loop(tiles * stage // stages, tiles * (stage + 1) // stages)(tile)

        gather_kernel(plan, pieces, beside, x_ref, out_ref, *sems)

    near = pl.BlockSpec(memory_space=pltpu.VMEM)
    return pl.pallas_call(
        kernel,
        out_shape=(
            jax.ShapeDtypeStruct((ep_count,) + block.shape, block.dtype),
            jax.ShapeDtypeStruct((rows, width), jnp.float32),
            jax.ShapeDtypeStruct((rows, width), jnp.float32),
        ) + (jax.ShapeDtypeStruct((width, ff), jnp.bfloat16),) * 3,
        in_specs=[near] * 5,
        out_specs=(pl.BlockSpec(memory_space=pl.ANY),) + (near,) * 5,
        scratch_shapes=[sem((n, pieces)), sem((n, pieces)), sem((n, pieces)), sem((n, wide, pieces)),
                        sem((n, wide, pieces)), sem((n, wide, pieces)), sem((n, wide, pieces)), sem],
        compiler_params=pltpu.CompilerParams(
            collective_id=collective_id, has_side_effects=True, vmem_limit_bytes=VMEM_MOST),
        name="gather_shared",
    )(block, grads, gate, up, down)


def add_rows(dst, others, out=None):
    rows, width = dst.shape
    out = dst if out is None else out
    small = rows <= 64
    piece = 32 if rows % 32 == 0 else rows
    lanes = width if rows % 32 == 0 else 4 * HEAD
    whole = width // lanes * lanes

    def add(at):
        if len(others) == 1 and out.dtype == jnp.bfloat16:
            out[at] = dst[at] + others[0][at]
        else:
            total = dst[at].astype(jnp.float32)
            for other in others:
                total = total + other[at].astype(jnp.float32)
            out[at] = total.astype(out.dtype)

    if piece == rows:
        @pl.loop(0, whole // lanes)
        def _(i):
            add((slice(None), pl.ds(pl.multiple_of(i * lanes, lanes), lanes)))

        if whole < width:
            add((slice(None), pl.ds(whole, width - whole)))
    else:
        @pl.loop(0, rows // piece)
        def _(i):
            add((pl.ds(pl.multiple_of(i * piece, piece), piece), slice(None)))


def send(src, dst, ssem, rsem, to):
    return pltpu.make_async_remote_copy(
        src_ref=src, dst_ref=dst, send_sem=ssem, recv_sem=rsem, device_id=to, device_id_type=MESH
    )


def run_if(cond, go):
    @when(cond)
    def _():
        go()


class RowSum:
    @staticmethod
    def scratch(plan, rows, width, dtype, pieces):
        n, wide = plan.planes(), plan.wide
        blocks = lambda *lead: pltpu.VMEM(lead + (rows, width), dtype)
        sem = lambda *lead: pltpu.SemaphoreType.DMA(lead + (pieces,))
        return [blocks(n, wide), blocks(n, wide), blocks(n, wide - 1), blocks(n), blocks(1 if plan.window else n),
                sem(n, wide), sem(n, wide), sem(n, wide), sem(n, wide), sem(n), sem(n), sem(n), sem(n, wide)]

    def __init__(self, plan, pieces, p_ref, scratch):
        self.plan, self.pieces, self.p_ref = plan, pieces, p_ref
        (self.held, self.rcb, self.rbb, self.r_hi, self.r_lo,
         self.sc, self.rc, self.sb, self.rb, self.sa, self.rhi, self.rlo, self.ld) = scratch
        self.a, self.b, self.c = plan.place()
        self.ready = len(p_ref.shape) == 4
        self.rows = p_ref.shape[-2] // pieces
        self.order = sorted(plan.steps, key=lambda d: -abs(d))

    def part(self, q):
        return pl.ds(pl.multiple_of(q * self.rows, self.rows), self.rows)

    def dev(self, a, b, c):
        return {"ep": self.plan.slot(a, b, c)}

    def source(self, k):
        return (self.b + self.plan.wide - k) % self.plan.wide

    def load(self, d, k, q):
        p, i, b0 = self.plan, self.plan.plane(self.a, d), self.source(k)
        return both(p.inside(self.a - d), p.need(d, self.b, self.c, b0, self.c)), lambda: pltpu.make_async_copy(
            self.p_ref.at[p.slot(self.a - d, b0, self.c), self.part(q)], self.held.at[i, k, self.part(q)],
            self.ld.at[i, k, q])

    def cross(self, d, k, q):
        p, i, b0, c = self.plan, self.plan.plane(self.a, d), self.source(k), self.c
        real = p.inside(self.a - d)
        at = (i, k) if self.ready else (p.slot(self.a - d, b0, 1 - c),)
        return (both(real, p.need(d, self.b, c, b0, 1 - c)), lambda: send(
            self.p_ref.at[at + (self.part(q),)], self.rcb.at[i, k, self.part(q)],
            self.sc.at[i, k, q], self.rc.at[i, k, q], self.dev(self.a, self.b, 1 - c)),
            both(real, p.need(d, self.b, 1 - c, b0, c)))

    def over(self, d, k, q):
        p, i, b0 = self.plan, self.plan.plane(self.a, d), self.source(k)
        return both(p.inside(self.a - d), p.need_pair(d, self.b, b0)), lambda: send(
            self.held.at[i, k, self.part(q)], self.rbb.at[i, k - 1, self.part(q)], self.sb.at[i, k, q],
            self.rb.at[i, k, q], self.dev(self.a, b0, self.c))

    def along(self, d, q):
        p, i, up = self.plan, self.plan.plane(self.a, d), d < 0
        j = d - 1 if p.window else i
        return p.inside(self.a - d), lambda: send(
            self.held.at[i, 0, self.part(q)], (self.r_lo if up else self.r_hi).at[j, self.part(q)],
            self.sa.at[i, q], (self.rlo if up else self.rhi).at[j, q],
            self.dev(self.a + (1 if up else -1), self.b, self.c))

    def start(self, ks):
        for k in ks:
            @pl.loop(0, self.pieces)
            def _(q, k=k):
                for d in self.order:
                    for cond, go in (self.cross(d, k, q)[:2], self.load(d, k, q)):
                        run_if(cond, lambda go=go: go().start())

    def first(self, d, k, q):
        i = self.plan.plane(self.a, d)
        if not self.ready:
            cond, go = self.load(d, k, q)
            run_if(cond, lambda: go().wait())
        _, come_go, come = self.cross(d, k, q)

        def take():
            come_go().wait_recv()
            add_rows(self.held.at[i, k, self.part(q)], [self.rcb.at[i, k, self.part(q)]])

        run_if(come, take)

    def stage_over(self, k):
        @pl.loop(0, self.pieces)
        def _(q):
            for d in self.order:
                self.first(d, k, q)
                cond, go = self.over(d, k, q)
                run_if(cond, lambda go=go: go().start())

    def stage_dests(self, low, high):
        @pl.loop(low, high)
        def _(q):
            for d in self.order:
                self.dest(d, q)

    def stage_dest(self, d, low, high):
        @pl.loop(low, high)
        def _(q):
            self.dest(d, q)

    def dest(self, d, q):
        p, a, b, steps = self.plan, self.a, self.b, self.plan.steps
        i = p.plane(a, d)
        real = p.inside(a - d)
        mine = self.held.at[i, 0, self.part(q)]
        self.first(d, 0, q)
        for k in range(1, p.wide):
            def take(k=k):
                self.over(d, k, q)[1]().wait_recv()
                add_rows(mine, [self.rbb.at[i, k - 1, self.part(q)]])

            run_if(both(real, p.need_pair(d, (b + k) % p.wide, b)), take)
        for inner, cond, buf, sem in ((d >= 0 and d + 1 in steps, a + 1 < p.long, self.r_hi, self.rhi),
                                      (d <= 0 and d - 1 in steps, a > 0, self.r_lo, self.rlo)):
            if inner:
                def take(buf=buf, sem=sem):
                    send(mine, buf.at[i, self.part(q)], self.sa.at[i, q], sem.at[i, q],
                         self.dev(a, b, self.c)).wait_recv()
                    add_rows(mine, [buf.at[i, self.part(q)]])

                run_if(both(real, cond), take)
        if d:
            cond, go = self.along(d, q)
            run_if(cond, lambda: go().start())

    def result(self):
        return self.held[self.plan.plane(self.a, 0), 0]

    def drain(self):
        @pl.loop(0, self.pieces)
        def _(q):
            for d in self.plan.steps:
                sends = [self.cross(d, k, q)[:2] for k in range(self.plan.wide)]
                sends += [self.over(d, k, q) for k in range(1, self.plan.wide)]
                if d:
                    sends.append(self.along(d, q))
                for cond, go in sends:
                    run_if(cond, lambda go=go: go().wait_send())


def scatter_rows(parts, window, collective_id, pieces=4):
    ep_count, rows, width = parts.shape
    plan = Plan(ep_count, window)

    def kernel(p_ref, out_ref, *scratch):
        total = RowSum(plan, pieces, p_ref, scratch)
        plan.greet(total.a, total.b, total.c)
        ks = list(range(1, plan.wide)) + [0]
        total.start(ks)
        for k in ks[:-1]:
            total.stage_over(k)
        total.stage_dests(0, pieces)
        out_ref[...] = total.result()
        total.drain()

    return pl.pallas_call(
        kernel,
        out_shape=jax.ShapeDtypeStruct((rows, width), parts.dtype),
        in_specs=[pl.BlockSpec(memory_space=pl.ANY)],
        out_specs=pl.BlockSpec(memory_space=pltpu.VMEM),
        scratch_shapes=RowSum.scratch(plan, rows, width, parts.dtype, pieces),
        compiler_params=pltpu.CompilerParams(
            collective_id=collective_id, has_side_effects=True, vmem_limit_bytes=VMEM_MOST),
        name="scatter_rows",
    )(parts)


class Place:
    def __init__(self, groups, ep_count):
        self.sizes = {"x": groups, "a": 4, "b": ep_count // 8}

    def locate(self):
        me, wide = lax.axis_index("ep"), self.sizes["b"]
        self.at = {"x": lax.axis_index("grp"), "a": me // (2 * wide), "b": (me // 2) % wide, "c": me % 2}

    def dev(self, **moved):
        at = {**self.at, **moved}
        return {"grp": at["x"], "ep": (at["a"] * self.sizes["b"] + at["b"]) * 2 + at["c"]}

    def slot(self, **moved):
        at = {**self.at, **moved}
        return ((at["x"] * self.sizes["a"] + at["a"]) * self.sizes["b"] + at["b"]) * 2 + at["c"]

    def back(self, axis, k):
        return (self.at[axis] + self.sizes[axis] - k) % self.sizes[axis]

    def greet(self):
        peers = [self.dev(c=1 - self.at["c"])] + [
            self.dev(**{axis: self.back(axis, k)}) for axis in "xba" for k in range(1, self.sizes[axis])]
        barrier = pltpu.get_barrier_semaphore()
        for to in peers:
            pl.semaphore_signal(barrier, inc=1, device_id=to, device_id_type=MESH)
        pl.semaphore_wait(barrier, len(peers))


def from_far(size):
    return list(range(1, size)) + [0]


class WholeSum:
    @staticmethod
    def scratch(sizes, axes, rows, width, dtype, sources):
        n1, n2, n3 = (sizes[axis] for axis in axes)
        blocks = lambda *lead: pltpu.VMEM(lead + (rows, width), dtype)
        sem = lambda *lead: pltpu.SemaphoreType.DMA(lead)
        full = (n1, n2, n3)
        one, two, three = (n1 - 1, n2, n3), (n2 - 1, n3), (n3 - 1,)
        return [blocks(*full), blocks(*full), blocks(*one), blocks(*two), blocks(*three),
                sem(*full, sources), sem(*full, sources), sem(*full, sources), sem(*one), sem(*one), sem(*two), sem(*two), sem(*three), sem(*three)]

    def __init__(self, place, axes, pieces, scratch):
        self.place, self.axes, self.pieces = place, axes, pieces
        (self.held, self.rcb, self.r1, self.r2, self.r3,
         self.ld, self.sc, self.rc, self.s1, self.q1, self.s2, self.q2, self.s3, self.q3) = scratch
        self.n1, self.n2, self.n3 = (place.sizes[axis] for axis in axes)
        self.groups = [[(k1, k2, k3) for k2 in from_far(self.n2) for k3 in from_far(self.n3)]
                       for k1 in from_far(self.n1)]

    def slot(self, key, c):
        return self.place.slot(c=c, **{axis: self.place.back(axis, k) for axis, k in zip(self.axes, key)})

    def loads(self, key):
        c = self.place.at["c"]
        for n, (ref, first, at, count) in enumerate(self.pieces):
            frm, to = pl.ds(first, count), pl.ds(at, count)
            yield pltpu.make_async_copy(
                ref.at[self.slot(key, c), :, frm], self.held.at[key + (slice(None), to)],
                self.ld.at[key + (n,)])

    def crossings(self, key):
        c = self.place.at["c"]
        for n, (ref, first, at, count) in enumerate(self.pieces):
            frm, to = pl.ds(first, count), pl.ds(at, count)
            yield send(ref.at[self.slot(key, 1 - c), :, frm], self.rcb.at[key + (slice(None), to)],
                       self.sc.at[key + (n,)], self.rc.at[key + (n,)], self.place.dev(c=1 - c))

    def hop(self, level, key):
        buf, ssem, rsem = ((self.r1, self.s1, self.q1), (self.r2, self.s2, self.q2), (self.r3, self.s3, self.q3))[level]
        axis, k = self.axes[level], key[level]
        far = (k - 1,) + key[level + 1 :]
        return send(self.held.at[key], buf.at[far], ssem.at[far], rsem.at[far],
                    self.place.dev(**{axis: self.place.back(axis, k)}))

    def start(self, i):
        for key in self.groups[i]:
            for go in self.crossings(key):
                go.start()
            for go in self.loads(key):
                go.start()

    def stage_core(self, i):
        for key in self.groups[i]:
            for go in self.loads(key):
                go.wait()
            for go in self.crossings(key):
                go.wait_recv()
            add_rows(self.held.at[key], [self.rcb.at[key]])
            if key[0]:
                self.hop(0, key).start()

    def stage_one(self, k2):
        for k3 in from_far(self.n3):
            for k1 in range(1, self.n1):
                self.hop(0, (k1, k2, k3)).wait_recv()
            add_rows(self.held.at[0, k2, k3], [self.r1.at[k1 - 1, k2, k3] for k1 in range(1, self.n1)])
            if k2:
                self.hop(1, (0, k2, k3)).start()

    def stage_two(self):
        for k3 in from_far(self.n3):
            for k2 in range(1, self.n2):
                self.hop(1, (0, k2, k3)).wait_recv()
            add_rows(self.held.at[0, 0, k3], [self.r2.at[k2 - 1, k3] for k2 in range(1, self.n2)])
            if k3:
                self.hop(2, (0, 0, k3)).start()

    def stage_three(self, out):
        for k3 in range(1, self.n3):
            self.hop(2, (0, 0, k3)).wait_recv()
        add_rows(self.held.at[0, 0, 0], [self.r3.at[k3 - 1] for k3 in range(1, self.n3)], out)

    def drain(self):
        for group in self.groups:
            for key in group:
                for go in self.crossings(key):
                    go.wait_send()
                if key[0]:
                    self.hop(0, key).wait_send()
                elif key[1]:
                    self.hop(1, key).wait_send()
                elif key[2]:
                    self.hop(2, key).wait_send()


def pieces_of(sources, low, high):
    pieces, first = [], 0
    for ref in sources:
        begin, end = max(low, first), min(high, first + ref.shape[2])
        if begin < end:
            pieces.append((ref, begin - first, begin - low, end - begin))
        first += ref.shape[2]
    return pieces


def scatter_whole(parts, collective_id):
    rows = parts[0].shape[1]
    width = sum(part.shape[2] for part in parts)
    groups, ep_count = lax.axis_size("grp"), lax.axis_size("ep")
    place = Place(groups, ep_count)
    tiles = width // HEAD
    count = 2 * COUPLES
    cuts = [tiles * n // count * HEAD for n in range(count + 1)]
    orders = ["xba", "bxa"] * COUPLES

    def kernel(*refs):
        sources, refs = refs[: len(parts)], refs[len(parts) :]
        out_ref, refs = refs[0], refs[1:]
        place.locate()
        sums = []
        for n, axes in enumerate(orders):
            pieces = pieces_of(sources, cuts[n], cuts[n + 1])
            sums.append(WholeSum(place, axes, pieces, refs[:14]))
            refs = refs[14:]
        outs = [out_ref.at[:, pl.ds(cuts[n], cuts[n + 1] - cuts[n])] for n in range(len(orders))]
        place.greet()
        couples = [sums[n : n + 2] for n in range(0, len(sums), 2)]
        for couple in couples:
            for i in range(max(s.n1 for s in couple)):
                for s in couple:
                    if i < s.n1:
                        s.start(i)

        def core(couple):
            for i in range(max(s.n1 for s in couple)):
                for s in couple:
                    if i < s.n1:
                        s.stage_core(i)

        def one(couple):
            for i in range(max(s.n2 for s in couple)):
                for s in couple:
                    if i < s.n2:
                        s.stage_one(from_far(s.n2)[i])

        def two(couple):
            for s in couple:
                s.stage_two()

        core(couples[0])
        for n, couple in enumerate(couples):
            one(couple)
            if n + 1 < len(couples):
                core(couples[n + 1])
            two(couple)
        for s, out in zip(sums, outs):
            s.stage_three(out)
        for s in sums:
            s.drain()

    operands, anywhere = list(parts), pl.BlockSpec(memory_space=pl.ANY)
    out_shape = [jax.ShapeDtypeStruct((rows, width), jnp.float32)]
    scratch = []
    for n, axes in enumerate(orders):
        scratch += WholeSum.scratch(place.sizes, axes, rows, cuts[n + 1] - cuts[n], parts[0].dtype, len(parts))
    got = pl.pallas_call(
        kernel,
        out_shape=tuple(out_shape),
        in_specs=[anywhere] * len(operands),
        out_specs=tuple(pl.BlockSpec(memory_space=pltpu.VMEM) for _ in out_shape),
        scratch_shapes=scratch,
        compiler_params=pltpu.CompilerParams(
            collective_id=collective_id, has_side_effects=True, vmem_limit_bytes=VMEM_MOST),
        name="scatter_whole",
    )(*operands)
    return got[0]


def scatter_experts(parts, lefts, rights, collective_id):
    ep_count, rows, width = parts.shape
    flat, tall = lefts[0].shape
    ff = rights[0].shape[1]
    half, depth = tall // 2, flat // 3
    plan, pieces = Plan(ep_count, False), 4
    place = Place(lax.axis_size("grp"), ep_count)
    left_of = [0, 0, 1]
    hooks = (4, 5, 6, 7, 10, 11, 12, 13, 16, 17)
    kinds, units = len(rights), 2 * len(rights)
    steps = units * 3

    def kernel(p_ref, in_ref, og_ref, pre_ref, lift_ref, mid_ref, out_ref, w0, w1, w2, acc, left, right, gone, came,
               ls, rs, gs, cs, *scratch):
        left_refs, right_refs, outs = (in_ref, og_ref), (pre_ref, lift_ref, mid_ref), (w0, w1, w2)
        place.locate()
        total = RowSum(plan, pieces, p_ref, scratch)
        g = place.at["x"]
        place.greet()

        def fetch(kind, step):
            chunk, slot = step % 3, step % 2
            mine = (step >= 3 * kinds).astype(jnp.int32)
            first = pl.multiple_of(jnp.where(mine == 1, g, 1 - g) * half, HEAD)
            at = pl.ds(pl.multiple_of(chunk * depth, depth), depth)
            return (pltpu.make_async_copy(left_refs[left_of[kind]].at[at, pl.ds(first, half)], left.at[slot], ls.at[slot]),
                    pltpu.make_async_copy(right_refs[kind].at[at, :], right.at[slot], rs.at[slot]))

        def per_kind(step, go):
            for kind in range(kinds):
                run_if((step // 3) % kinds == kind, lambda kind=kind: go(kind))

        def begin(step):
            def go(kind):
                for copy in fetch(kind, step):
                    copy.start()
            per_kind(step, go)

        def away(kind):
            return send(gone.at[kind], came.at[kind], gs.at[kind], cs.at[kind], place.dev(x=place.back("x", 1)))

        def meet(n):
            q, distance = n // plan.long, plan.long - 1 - n % plan.long
            for d in sorted({-distance, distance}):
                total.dest(d, q)

        ks = from_far(plan.wide)
        total.start(ks)
        begin(jnp.int32(0))
        for k in ks[:-1]:
            total.stage_over(k)

        @pl.loop(0, steps)
        def _(step):
            run_if(step + 1 < steps, lambda: begin(step + 1))

            def ready(kind):
                for copy in fetch(kind, step):
                    copy.wait()
            per_kind(step, ready)
            slot = step % 2
            product = inner_left(left[slot], right[slot])
            fresh = step % 3 == 0

            @pl.when(fresh)
            def _():
                acc[...] = product

            @pl.when(jnp.logical_not(fresh))
            def _():
                acc[...] += product

            def done(kind):
                @pl.when(step < 3 * kinds)
                def _():
                    gone[kind] = acc[...].astype(jnp.bfloat16)
                    away(kind).start()

                @pl.when(step >= 3 * kinds)
                def _():
                    outs[kind][...] = acc[...]

            run_if(step % 3 == 2, lambda: per_kind(step, done))
            for n, at in enumerate(hooks):
                run_if(step == at, lambda n=n: meet(n))

        for n in range(len(hooks), pieces * plan.long):
            meet(n)
        out_ref[...] = total.result()
        for kind in range(kinds):
            away(kind).wait_recv()
            piece = 32

            @pl.loop(0, half // piece)
            def _(i, kind=kind):
                at = pl.ds(pl.multiple_of(i * piece, piece), piece)
                outs[kind][at, :] = outs[kind][at, :] + came[kind, at, :].astype(jnp.float32)

        for kind in range(kinds):
            away(kind).wait_send()
        total.drain()

    anywhere = pl.BlockSpec(memory_space=pl.ANY)
    sem = lambda n: pltpu.SemaphoreType.DMA((n,))
    outs = [jax.ShapeDtypeStruct((rows, width), parts.dtype)] + [jax.ShapeDtypeStruct((half, ff), jnp.float32)] * kinds
    return pl.pallas_call(
        kernel,
        out_shape=tuple(outs),
        in_specs=[anywhere] * 6,
        out_specs=tuple(pl.BlockSpec(memory_space=pltpu.VMEM) for _ in outs),
        scratch_shapes=[
            pltpu.VMEM((half, ff), jnp.float32),
            pltpu.VMEM((2, depth, half), jnp.bfloat16),
            pltpu.VMEM((2, depth, ff), jnp.bfloat16),
            pltpu.VMEM((kinds, half, ff), jnp.bfloat16),
            pltpu.VMEM((kinds, half, ff), jnp.bfloat16),
            sem(2), sem(2), sem(kinds), sem(kinds),
        ] + RowSum.scratch(plan, rows, width, parts.dtype, pieces),
        compiler_params=pltpu.CompilerParams(
            collective_id=collective_id, has_side_effects=True, vmem_limit_bytes=VMEM_MOST),
        name="scatter_experts",
    )(parts, *lefts, *rights)


def visible_bias(shape, first_key, start, first_query):
    key_pos = first_key + lax.broadcasted_iota(jnp.int32, shape, 0)
    query_pos = first_query + lax.broadcasted_iota(jnp.int32, shape, 1)
    seen = jnp.logical_and(key_pos >= start, key_pos <= query_pos)
    return jnp.where(seen, 0.0, masked_value)


def lanes(first):
    return pl.ds(pl.multiple_of(first, HEAD), HEAD)


def turned(values, cosine, sine):
    return values * cosine + pltpu.roll(values, HEAD // 2, 1) * sine


def whole_spec(*shape):
    return pl.BlockSpec(shape, lambda *s: (0,) * len(shape))


def project_kernel(x_ref, gain_ref, cos_ref, sin_ref, wq_ref, wk_ref, wv_ref, hid_ref, q_ref, kv_ref, hidden):
    @pl.when(pl.program_id(0) == 0)
    def _():
        hidden[...] = normed(x_ref[...].astype(jnp.float32), gain_ref[...]).astype(jnp.bfloat16)
        hid_ref[...] = hidden[...]

    cosine, sine = cos_ref[...], sin_ref[...]
    q = jnp.dot(hidden[...], wq_ref[...], preferred_element_type=jnp.float32)
    k = jnp.dot(hidden[...], wk_ref[...], preferred_element_type=jnp.float32)
    v = jnp.dot(hidden[...], wv_ref[...], preferred_element_type=jnp.float32)
    for h in range(q.shape[1] // HEAD):
        at = slice(h * HEAD, (h + 1) * HEAD)
        q_ref[:, at] = (turned(q[:, at], cosine, sine) * HEAD ** (-0.5)).astype(jnp.bfloat16)
        kv_ref[:, 2 * h * HEAD : (2 * h + 1) * HEAD] = turned(k[:, at], cosine, sine).astype(jnp.bfloat16)
        kv_ref[:, (2 * h + 1) * HEAD : (2 * h + 2) * HEAD] = v[:, at].astype(jnp.bfloat16)


def project(tokens, gain, cosine, sine, wq, wk, wv):
    rows, width = tokens.shape
    tile = 2 * HEAD
    column = pl.BlockSpec((width, tile), lambda i: (0, i))
    return pl.pallas_call(
        project_kernel,
        out_shape=(
            jax.ShapeDtypeStruct((rows, width), jnp.bfloat16),
            jax.ShapeDtypeStruct((rows, width), jnp.bfloat16),
            jax.ShapeDtypeStruct((rows, 2 * width), jnp.bfloat16),
        ),
        grid=(width // tile,),
        in_specs=[whole_spec(rows, width), whole_spec(1, width), whole_spec(rows, HEAD), whole_spec(rows, HEAD),
                  column, column, column],
        out_specs=(whole_spec(rows, width), pl.BlockSpec((rows, tile), lambda i: (0, i)),
                   pl.BlockSpec((rows, 2 * tile), lambda i: (0, i))),
        scratch_shapes=[pltpu.VMEM((rows, width), jnp.bfloat16)],
        cost_estimate=pl.CostEstimate(flops=6 * rows * width * width, bytes_accessed=6 * width * width, transcendentals=0),
        name="project",
    )(tokens, gain[None, :], cosine, sine, wq, wk, wv)


def attend_kernel(info, q_ref, start_ref, kv_ref, mixed_ref, low_ref, total_ref, bias, top, norm):
    step = pl.program_id(0)
    me, first_block = info[0], info[1]
    rows = q_ref.shape[0]
    block = me - step

    @pl.when(step == 0)
    def _():
        top[...] = jnp.full_like(top, masked_value)
        norm[...] = jnp.zeros_like(norm)
        mixed_ref[...] = jnp.zeros_like(mixed_ref)

    @pl.when(block >= first_block)
    def _():
        bias[...] = visible_bias((rows, rows), block * rows, start_ref[...], me * rows)

        @pl.loop(0, HEADS, unroll=2)
        def _(h):
            keys, values = kv_ref[0, :, lanes(2 * h * HEAD)], kv_ref[0, :, lanes((2 * h + 1) * HEAD)]
            scores = inner_right(keys, q_ref[:, lanes(h * HEAD)]) + bias[...]
            old = top[h]
            new = jnp.maximum(old, jnp.max(scores, axis=0, keepdims=True))
            weights = jnp.exp(scores - new)
            shrink = jnp.exp(old - new)
            top[h] = new
            norm[h] = norm[h] * shrink + jnp.sum(weights, axis=0, keepdims=True)
            mixed_ref[h] = mixed_ref[h] * shrink + inner_left(values, weights.astype(jnp.bfloat16))

    @pl.when(step == pl.num_programs(0) - 1)
    def _():
        for h in range(HEADS):
            mixed = mixed_ref[h] / norm[h]
            mixed_ref[h] = mixed
            low_ref[:, h * HEAD : (h + 1) * HEAD] = mixed.T.astype(jnp.bfloat16)
            total_ref[h] = top[h] + jnp.log(norm[h])


def attend(info, queries, start, pairs):
    rows, width = queries.shape
    steps = pairs.shape[0] // 2 + 1
    return pl.pallas_call(
        attend_kernel,
        out_shape=(
            jax.ShapeDtypeStruct((HEADS, HEAD, rows), jnp.float32),
            jax.ShapeDtypeStruct((rows, width), jnp.bfloat16),
            jax.ShapeDtypeStruct((HEADS, 1, rows), jnp.float32),
        ),
        grid_spec=pltpu.PrefetchScalarGridSpec(
            num_scalar_prefetch=1,
            grid=(steps,),
            in_specs=[
                whole_spec(rows, width),
                whole_spec(1, rows),
                pl.BlockSpec((1, rows, 2 * width), lambda s, info: (jnp.maximum(info[0] - s, info[1]), 0, 0)),
            ],
            out_specs=(whole_spec(HEADS, HEAD, rows), whole_spec(rows, width), whole_spec(HEADS, 1, rows)),
            scratch_shapes=[
                pltpu.VMEM((rows, rows), jnp.float32),
                pltpu.VMEM((HEADS, 1, rows), jnp.float32),
                pltpu.VMEM((HEADS, 1, rows), jnp.float32),
            ],
        ),
        cost_estimate=pl.CostEstimate(
            flops=4 * rows * rows * width * steps, bytes_accessed=4 * rows * width * steps, transcendentals=0
        ),
        name="attend",
    )(info, queries, start, pairs)


def attend_back_kernel(
    info, q_ref, g_ref, mixed_ref, start_ref, total_ref, cos_ref, sin_ref, kv_ref, dkv_ref, dq_ref, bias, acc, term
):
    step = pl.program_id(0)
    me, first_block = info[0], info[1]
    rows = q_ref.shape[0]
    block = me - step

    @pl.when(step == 0)
    def _():
        acc[...] = jnp.zeros_like(acc)
        for h in range(HEADS):
            grads = g_ref[:, h * HEAD : (h + 1) * HEAD].astype(jnp.float32).T
            term[h] = jnp.sum(grads * mixed_ref[h], axis=0, keepdims=True)

    @pl.when(block >= first_block)
    def _():
        bias[...] = visible_bias((rows, rows), block * rows, start_ref[...], me * rows)

        @pl.loop(0, HEADS, unroll=2)
        def _(h):
            early, late, at = lanes(2 * h * HEAD), lanes((2 * h + 1) * HEAD), lanes(h * HEAD)
            keys, values = kv_ref[0, :, early], kv_ref[0, :, late]
            queries, grads = q_ref[:, at], g_ref[:, at]
            probs = jnp.exp(inner_right(keys, queries) + bias[...] - total_ref[h])
            prob_grad = inner_right(values, grads)
            score_grad = (probs * (prob_grad - term[h])).astype(jnp.bfloat16)
            dkv_ref[0, :, late] = jnp.dot(
                probs.astype(jnp.bfloat16), grads, preferred_element_type=jnp.float32
            ).astype(jnp.bfloat16)
            dkv_ref[0, :, early] = jnp.dot(
                score_grad, queries, preferred_element_type=jnp.float32
            ).astype(jnp.bfloat16)
            acc[h] += inner_left(keys, score_grad)

    @pl.when(jnp.logical_and(block >= 0, block < first_block))
    def _():
        dkv_ref[...] = jnp.zeros_like(dkv_ref)

    @pl.when(step == pl.num_programs(0) - 1)
    def _():
        for h in range(HEADS):
            back = turned(acc[h].T * HEAD ** (-0.5), cos_ref[...], -sin_ref[...])
            dq_ref[:, h * HEAD : (h + 1) * HEAD] = back.astype(jnp.bfloat16)


def attend_back(info, queries, grads, mixed, start, total, cosine, sine, pairs):
    rows, width = queries.shape
    count = pairs.shape[0]
    steps = count // 2 + 1
    return pl.pallas_call(
        attend_back_kernel,
        out_shape=(
            jax.ShapeDtypeStruct(pairs.shape, jnp.bfloat16),
            jax.ShapeDtypeStruct((rows, width), jnp.bfloat16),
        ),
        grid_spec=pltpu.PrefetchScalarGridSpec(
            num_scalar_prefetch=1,
            grid=(steps,),
            in_specs=[
                whole_spec(rows, width),
                whole_spec(rows, width),
                whole_spec(HEADS, HEAD, rows),
                whole_spec(1, rows),
                whole_spec(HEADS, 1, rows),
                whole_spec(rows, HEAD),
                whole_spec(rows, HEAD),
                pl.BlockSpec((1, rows, 2 * width), lambda s, info: (jnp.maximum(info[0] - s, info[1]), 0, 0)),
            ],
            out_specs=(
                pl.BlockSpec((1, rows, 2 * width), lambda s, info: (jnp.maximum(info[0] - s, 0), 0, 0)),
                whole_spec(rows, width),
            ),
            scratch_shapes=[
                pltpu.VMEM((rows, rows), jnp.float32),
                pltpu.VMEM((HEADS, HEAD, rows), jnp.float32),
                pltpu.VMEM((HEADS, 1, rows), jnp.float32),
            ],
        ),
        cost_estimate=pl.CostEstimate(
            flops=10 * rows * rows * width * steps, bytes_accessed=8 * rows * width * steps, transcendentals=0
        ),
        name="attend_back",
    )(info, queries, grads, mixed, start, total, cosine, sine, pairs)


def finish_kernel(
    x_ref, gain_ref, res_ref, hid_ref, q_ref, kv_ref, cos_ref, sin_ref, wq_ref, wk_ref, wv_ref,
    dq_ref, dk_ref, dv_ref, out_ref, gain_out, acc,
):
    step = pl.program_id(0)

    @pl.when(step == 0)
    def _():
        acc[...] = jnp.zeros_like(acc)

    cosine, sine = cos_ref[...], sin_ref[...]
    count = q_ref.shape[1] // HEAD
    keys = jnp.concatenate(
        [turned(kv_ref[:, 2 * h * HEAD : (2 * h + 1) * HEAD].astype(jnp.float32), cosine, -sine).astype(jnp.bfloat16)
         for h in range(count)], axis=1)
    values = jnp.concatenate([kv_ref[:, (2 * h + 1) * HEAD : (2 * h + 2) * HEAD] for h in range(count)], axis=1)
    grads = (q_ref[...], keys, values)
    acc[...] += (
        inner_right(grads[0], wq_ref[...]) + inner_right(grads[1], wk_ref[...]) + inner_right(grads[2], wv_ref[...])
    )
    hidden = hid_ref[...]
    for ref, grad in zip((dq_ref, dk_ref, dv_ref), grads):
        ref[...] = inner_left(hidden, grad).astype(jnp.bfloat16)

    @pl.when(step == pl.num_programs(0) - 1)
    def _():
        values, gain, grad = x_ref[...].astype(jnp.float32), gain_ref[...], acc[...]
        scale = lax.rsqrt(jnp.mean(values * values, axis=1, keepdims=True) + epsilon)
        inner = jnp.mean(gain * grad * values, axis=1, keepdims=True)
        part = scale * gain * grad - values * (scale * scale * scale) * inner
        out_ref[...] = (res_ref[...] + part).astype(jnp.bfloat16)
        gain_out[...] = jnp.sum(grad * values * scale, axis=0, keepdims=True)


def finish(tokens, gain, residual_grad, hidden, query_grad, pair_grads, cosine, sine, wq, wk, wv):
    rows, width = tokens.shape
    tile = 2 * HEAD
    column = pl.BlockSpec((width, tile), lambda i: (0, i))
    return pl.pallas_call(
        finish_kernel,
        out_shape=(
            jax.ShapeDtypeStruct((width, width), jnp.bfloat16),
            jax.ShapeDtypeStruct((width, width), jnp.bfloat16),
            jax.ShapeDtypeStruct((width, width), jnp.bfloat16),
            jax.ShapeDtypeStruct((rows, width), jnp.bfloat16),
            jax.ShapeDtypeStruct((1, width), jnp.float32),
        ),
        grid=(width // tile,),
        in_specs=[whole_spec(rows, width), whole_spec(1, width), whole_spec(rows, width), whole_spec(rows, width),
                  pl.BlockSpec((rows, tile), lambda i: (0, i)), pl.BlockSpec((rows, 2 * tile), lambda i: (0, i)),
                  whole_spec(rows, HEAD), whole_spec(rows, HEAD), column, column, column],
        out_specs=(column, column, column, whole_spec(rows, width), whole_spec(1, width)),
        scratch_shapes=[pltpu.VMEM((rows, width), jnp.float32)],
        cost_estimate=pl.CostEstimate(flops=12 * rows * width * width, bytes_accessed=12 * width * width, transcendentals=0),
        name="finish",
    )(tokens, gain[None, :], residual_grad, hidden, query_grad, pair_grads, cosine, sine, wq, wk, wv)


def experts_kernel(
    where_ref, x_ref, g_ref, rank_row, rank_col, share_row, wg_ref, wu_ref, wd_ref,
    back_ref, routed_ref, in_ref, pre_ref, lift_ref, mid_ref, og_ref, grads,
):
    blocks, rows, side = x_ref.shape
    capacity = in_ref.shape[0] // blocks
    width = og_ref.shape[1]
    dot = lambda left, right: jnp.dot(left, right, preferred_element_type=jnp.float32)
    shares = []
    for i in range(blocks):
        at = slice(i * capacity, (i + 1) * capacity)
        hit = rank_row[i] == lax.broadcasted_iota(jnp.int32, (capacity, rows), 0)
        pick = jnp.where(hit, 1.0, 0.0)
        shares.append(jnp.sum(pick * share_row[i], axis=1, keepdims=True))
        pick = pick.astype(jnp.bfloat16)
        in_ref[at, :] = dot(pick, x_ref[i, :, :width]).astype(jnp.bfloat16)
        grads[at, :] = dot(pick, g_ref[i]).astype(jnp.bfloat16)
    share = jnp.concatenate(shares, axis=0)
    pre = dot(in_ref[...], wg_ref[0])
    lift = dot(in_ref[...], wu_ref[0])
    silu, slope = silu_parts(pre)
    mid_ref[...] = (silu * lift).astype(jnp.bfloat16)
    lift_slope = lift * slope
    result = dot(mid_ref[...], wd_ref[0]).astype(jnp.bfloat16).astype(jnp.float32)
    grad = grads[...].astype(jnp.float32)
    gate_grad = jnp.sum(result * grad, axis=1, keepdims=True)
    og_ref[...] = (share * grad).astype(jnp.bfloat16)
    given = (share * result).astype(jnp.bfloat16)
    mid_grad = inner_right(og_ref[...], wd_ref[0])
    pre_ref[...] = (mid_grad * lift_slope).astype(jnp.bfloat16)
    lift_ref[...] = (mid_grad * silu).astype(jnp.bfloat16)
    in_grad = (inner_right(pre_ref[...], wg_ref[0]) + inner_right(lift_ref[...], wu_ref[0])).astype(jnp.bfloat16)
    lane = lax.broadcasted_iota(jnp.int32, (blocks * capacity, side - width), 1)
    high = gate_grad.astype(jnp.bfloat16).astype(jnp.float32)
    extra = jnp.where(lane == where_ref[0], high, jnp.where(lane == where_ref[1], gate_grad - high, 0.0))
    extra = extra.astype(jnp.bfloat16)
    for i in range(blocks):
        at = slice(i * capacity, (i + 1) * capacity)
        hit = rank_col[i] == lax.broadcasted_iota(jnp.int32, (rows, capacity), 1)
        put = jnp.where(hit, 1.0, 0.0).astype(jnp.bfloat16)
        back_ref[i, :, :width] = dot(put, in_grad[at, :]).astype(jnp.bfloat16)
        back_ref[i, :, width:] = dot(put, extra[at, :]).astype(jnp.bfloat16)
        routed_ref[i] = dot(put, given[at, :]).astype(jnp.bfloat16)


def run_experts(places, arrived, grads, rank, share, gate, up, down, capacity):
    count, rows, side = arrived.shape
    width, ff = gate.shape[1], gate.shape[2]
    blocks = 384 // capacity
    flat = count * capacity
    once = lambda *shape: pl.BlockSpec(shape, lambda i, p: (0,) * len(shape), pipeline_mode=pl.Buffered(1))
    lead = lambda *shape: pl.BlockSpec((blocks,) + shape, lambda i, p: (i, 0, 0))
    tall = lambda wide: pl.BlockSpec((blocks * capacity, wide), lambda i, p: (i, 0))
    shape = lambda *dims: jax.ShapeDtypeStruct(dims, jnp.bfloat16)
    return pl.pallas_call(
        experts_kernel,
        out_shape=(shape(count, rows, side), shape(count, rows, width), shape(flat, width), shape(flat, ff),
                   shape(flat, ff), shape(flat, ff), shape(flat, width)),
        grid_spec=pltpu.PrefetchScalarGridSpec(
            num_scalar_prefetch=1,
            grid=(count // blocks,),
            in_specs=[lead(rows, side), lead(rows, width), lead(1, rows), lead(rows, 1), lead(1, rows),
                      once(1, width, ff), once(1, width, ff), once(1, ff, width)],
            out_specs=(lead(rows, side), lead(rows, width), tall(width), tall(ff), tall(ff), tall(ff), tall(width)),
            scratch_shapes=[pltpu.VMEM((blocks * capacity, width), jnp.bfloat16)],
        ),
        compiler_params=pltpu.CompilerParams(vmem_limit_bytes=VMEM_MOST),
        cost_estimate=pl.CostEstimate(flops=16 * flat * width * ff, bytes_accessed=16 * flat * width, transcendentals=0),
        name="run_experts",
    )(places, arrived, grads, rank[:, None, :], rank[:, :, None], share[:, None, :], gate, up, down)


def gather_attend_kernel(plan, pieces, attention, x_ref, out_ref, ra, sa_up, sa_dn, rb, sb, rc, sc, own):
    a, b, c = plan.place()
    steps, wide = plan.steps, plan.wide
    at = {d: i for i, d in enumerate(steps)}
    rows = x_ref.shape[0] // pieces

    def part(q):
        return pl.ds(pl.multiple_of(q * rows, rows), rows)

    def copy(q, src, slot, ssem, rsem, dev):
        return pltpu.make_async_remote_copy(
            src_ref=src, dst_ref=out_ref.at[slot, part(q)], send_sem=ssem, recv_sem=rsem,
            device_id={"ep": dev}, device_id_type=MESH,
        )

    def hops(d, q):
        i = at[d]
        slot = plan.slot(a - d, b, c)
        src = x_ref.at[part(q)] if d == 0 else out_ref.at[slot, part(q)]
        real = plan.inside(a - d)
        out = []
        if d >= 0 and d + 1 in at:
            out.append((both(real, a + 1 < plan.long), lambda: copy(
                q, src, slot, sa_up.at[i, q], ra.at[at[d + 1], q], plan.slot(a + 1, b, c))))
        if d <= 0 and d - 1 in at:
            out.append((both(real, a > 0), lambda: copy(
                q, src, slot, sa_dn.at[i, q], ra.at[at[d - 1], q], plan.slot(a - 1, b, c))))
        for k in range(1, wide):
            to = (b + k) % wide
            out.append((both(real, plan.need_pair(d, to, b)), lambda k=k, to=to: copy(
                q, src, slot, sb.at[i, k, q], rb.at[i, k, q], plan.slot(a, to, c))))
        out.append((both(real, plan.need(d, b, 1 - c, b, c)), lambda: copy(
            q, src, slot, sc.at[i, 0, q], rc.at[i, 0, q], plan.slot(a, b, 1 - c))))
        return out

    def cross(d, k, q):
        i = at[d]
        b0 = (b + wide - k) % wide
        slot = plan.slot(a - d, b0, c)
        real = plan.inside(a - d)
        come = lambda: copy(q, x_ref.at[part(q)], slot, sb.at[i, k, q], rb.at[i, k, q], plan.slot(a, b, c))
        go = lambda: copy(q, out_ref.at[slot, part(q)], slot, sc.at[i, k, q], rc.at[i, k, q],
                          plan.slot(a, b, 1 - c))
        return (both(real, plan.need_pair(d, b, b0)), come,
                both(real, plan.need(d, b, 1 - c, b0, c)), go)

    plan.greet(a, b, c)
    keep = pltpu.make_async_copy(x_ref, out_ref.at[plan.slot(a, b, c)], own)

    @pl.loop(0, pieces)
    def _(q):
        for cond, go in hops(0, q):
            @when(cond)
            def _(go=go):
                go().start()

    keep.start()
    far = max(abs(d) for d in steps)

    def arrive(d, k):
        b0 = (b + wide - k) % wide
        slot = plan.slot(a - d, b0, 1 - c)

        @pl.loop(0, pieces)
        def _(q):
            copy(q, x_ref.at[part(q)], slot, sc.at[at[d], k, q], rc.at[at[d], k, q], plan.slot(a, b, c)).wait_recv()

    work = attention(a, b, c, arrive)
    work.own()
    for step in range(1, far + 2):
        @pl.loop(0, pieces)
        def _(q, step=step):
            for d in (step, -step):
                if d in at:
                    @when(plan.inside(a - d))
                    def _(d=d):
                        slot = plan.slot(a - d, b, c)
                        copy(q, x_ref.at[part(q)], slot, sa_up.at[0, q], ra.at[at[d], q],
                             plan.slot(a, b, c)).wait_recv()
                        for cond, go in hops(d, q):
                            @when(cond)
                            def _(go=go):
                                go().start()
            for d in (step - 1,):
                if d in at:
                    for k in range(1, wide):
                        came, come, goes, go = cross(d, k, q)
                        @when(came)
                        def _(come=come):
                            come().wait_recv()
                        @when(goes)
                        def _(go=go):
                            go().start()
            work.beside(step, q)

    work.rest()
    keep.wait()

    @pl.loop(0, pieces)
    def _(q):
        for d in steps:
            i = at[d]
            real = plan.inside(a - d)
            for cond, go in hops(d, q):
                @when(cond)
                def _(go=go):
                    go().wait_send()
            for k in range(1, wide):
                came, come, goes, go = cross(d, k, q)
                @when(goes)
                def _(go=go):
                    go().wait_send()


class Attention:
    def __init__(self, plan, a, b, c, arrive, x_ref, pair_ref, q_ref, start_ref, mixed_ref, low_ref, total_ref,
                 bias, top, norm, kv, kv_sem):
        self.plan, self.a, self.b, self.c, self.arrive = plan, a, b, c, arrive
        self.x_ref, self.pair_ref, self.q_ref, self.start_ref = x_ref, pair_ref, q_ref, start_ref
        self.mixed_ref, self.low_ref, self.total_ref = mixed_ref, low_ref, total_ref
        self.bias, self.top, self.norm, self.kv, self.kv_sem = bias, top, norm, kv, kv_sem
        self.turns = [(0, 0, True), (1, 0, False), (1, 0, True), (0, 1, False), (0, 1, True), (2, 0, False), (2, 0, True),
                      (1, 1, False), (1, 1, True), (2, 1, False), (2, 1, True)]

    def block(self, n):
        d, k, other = self.turns[n]
        b0, c0 = (self.b + self.plan.wide - k) % self.plan.wide, 1 - self.c if other else self.c
        there = both(self.plan.inside(self.a - d), self.plan.need(d, self.b, self.c, b0, c0))
        return there, self.plan.slot(self.a - d, b0, c0)

    def copy(self, n):
        return pltpu.make_async_copy(self.pair_ref.at[self.block(n)[1]], self.kv.at[n % 2], self.kv_sem.at[n % 2])

    def fetch(self, n):
        if n < len(self.turns):
            d, k, other = self.turns[n]

            def go():
                if other:
                    self.arrive(d, k)
                self.copy(n).start()

            run_if(self.block(n)[0], go)

    def use(self, n):
        def go():
            self.copy(n).wait()
            self.step(self.kv.at[n % 2], self.block(n)[1])

        run_if(self.block(n)[0], go)

    def step(self, pair, slot):
        rows = self.q_ref.shape[0]
        me = self.plan.slot(self.a, self.b, self.c)
        self.bias[...] = visible_bias((rows, rows), slot * rows, self.start_ref[...], me * rows)

        @pl.loop(0, HEADS)
        def _(h):
            keys, values = pair[:, lanes(2 * h * HEAD)], pair[:, lanes((2 * h + 1) * HEAD)]
            scores = inner_right(keys, self.q_ref[:, lanes(h * HEAD)]) + self.bias[...]
            old = self.top[h]
            new = jnp.maximum(old, jnp.max(scores, axis=0, keepdims=True))
            weights = jnp.exp(scores - new)
            shrink = jnp.exp(old - new)
            self.top[h] = new
            self.norm[h] = self.norm[h] * shrink + jnp.sum(weights, axis=0, keepdims=True)
            self.mixed_ref[h] = self.mixed_ref[h] * shrink + inner_left(values, weights.astype(jnp.bfloat16))

    def own(self):
        self.top[...] = jnp.full_like(self.top, masked_value)
        self.norm[...] = jnp.zeros_like(self.norm)
        self.mixed_ref[...] = jnp.zeros_like(self.mixed_ref)
        self.step(self.x_ref, self.plan.slot(self.a, self.b, self.c))
        self.fetch(0)
        self.use(0)

    def beside(self, step, q):
        if step == 1:
            return
        if step == 2:
            run_if(q == 0, lambda: self.fetch(1))
        first = 4 * step - 7
        for i in range(4):
            def go(n=first + i):
                self.fetch(n + 1)
                self.use(n)

            run_if(q == 2 * i + 1, go)

    def rest(self):
        self.fetch(10)
        self.use(9)
        self.use(10)
        for h in range(HEADS):
            mixed = self.mixed_ref[h] / self.norm[h]
            self.mixed_ref[h] = mixed
            self.low_ref[:, h * HEAD : (h + 1) * HEAD] = mixed.T.astype(jnp.bfloat16)
            self.total_ref[h] = self.top[h] + jnp.log(self.norm[h])


def gather_attend(block, queries, start, collective_id):
    ep_count, pieces = lax.axis_size("ep"), 8
    plan = Plan(ep_count, True)
    n, wide = len(plan.steps), plan.wide
    rows, width = queries.shape
    sem = pltpu.SemaphoreType.DMA

    def kernel(x_ref, q_ref, start_ref, out_ref, mixed_ref, low_ref, total_ref, bias, top, norm, kv, kv_sem, *sems):
        def attention(a, b, c, arrive):
            return Attention(plan, a, b, c, arrive, x_ref, out_ref, q_ref, start_ref, mixed_ref, low_ref, total_ref,
                             bias, top, norm, kv, kv_sem)

        gather_attend_kernel(plan, pieces, attention, x_ref, out_ref, *sems)

    near = pl.BlockSpec(memory_space=pltpu.VMEM)
    return pl.pallas_call(
        kernel,
        out_shape=(
            jax.ShapeDtypeStruct((ep_count,) + block.shape, block.dtype),
            jax.ShapeDtypeStruct((HEADS, HEAD, rows), jnp.float32),
            jax.ShapeDtypeStruct((rows, width), jnp.bfloat16),
            jax.ShapeDtypeStruct((HEADS, 1, rows), jnp.float32),
        ),
        in_specs=[near] * 3,
        out_specs=(pl.BlockSpec(memory_space=pl.ANY), near, near, near),
        scratch_shapes=[
            pltpu.VMEM((rows, rows), jnp.float32),
            pltpu.VMEM((HEADS, 1, rows), jnp.float32),
            pltpu.VMEM((HEADS, 1, rows), jnp.float32),
            pltpu.VMEM((2,) + block.shape, block.dtype),
            sem((2,)),
            sem((n, pieces)), sem((n, pieces)), sem((n, pieces)), sem((n, wide, pieces)),
            sem((n, wide, pieces)), sem((n, wide, pieces)), sem((n, wide, pieces)), sem,
        ],
        compiler_params=pltpu.CompilerParams(
            collective_id=collective_id, has_side_effects=True, vmem_limit_bytes=VMEM_MOST),
        name="gather_attend",
    )(block, queries, start)


def attend_back_sum(queries, grads, mixed, start, total, cosine, sine, pairs, parts, collective_id):
    rows, width = queries.shape
    ep_count = pairs.shape[0]
    part_rows, part_width = parts[0].shape[1], sum(part.shape[2] for part in parts)
    plan, pieces = Plan(ep_count, True), 4
    place = Place(lax.axis_size("grp"), ep_count)
    n, wide = plan.planes(), plan.wide
    cuts = [0, part_width // HEAD * 3 // 4 * HEAD, part_width]
    orders = ("xba", "bxa")

    def kernel(q_ref, g_ref, mixed_ref, start_ref, total_ref, cos_ref, sin_ref, pair_ref, *refs):
        sources, refs = refs[: len(parts)], refs[len(parts) :]
        out_ref, pair_out, dq_ref, bias, acc, term, kv, staged, kv_sem = refs[:9]
        refs = refs[9:]
        place.locate()
        sums = []
        for i in range(2):
            sums.append(WholeSum(place, orders[i], pieces_of(sources, cuts[i], cuts[i + 1]), refs[:14]))
            refs = refs[14:]
        sum_rows = RowSum(plan, pieces, staged, refs)
        a, b, c = sum_rows.a, sum_rows.b, sum_rows.c
        me = plan.slot(a, b, c)
        order, ks = sum_rows.order, from_far(wide)
        turns = [(k, d) for d in order for k in ks]

        def block(turn, other):
            k, d = turns[turn]
            b0, c0 = sum_rows.source(k), jnp.where(other, 1 - c, c)
            there = both(plan.inside(a - d), plan.need(d, b, c, b0, c0))
            return there, plan.slot(a - d, b0, c0)

        def fetch(turn, other):
            there, slot = block(turn, other)
            held = jnp.where(other, 0, 1)
            return there, lambda: pltpu.make_async_copy(pair_ref.at[slot], kv.at[held], kv_sem.at[held])

        def begin(turn, other):
            there, go = fetch(turn, other)
            run_if(there, lambda: go().start())

        def compute(turn, other, target):
            there, slot = block(turn, other)
            held = 0 if other else 1

            def work():
                fetch(turn, other)[1]().wait()
                bias[...] = visible_bias((rows, rows), slot * rows, start_ref[...], me * rows)

                @pl.loop(0, HEADS)
                def _(h):
                    early, late, at = lanes(2 * h * HEAD), lanes((2 * h + 1) * HEAD), lanes(h * HEAD)
                    keys, values = kv[held, :, early], kv[held, :, late]
                    own, grad = q_ref[:, at], g_ref[:, at]
                    probs = jnp.exp(inner_right(keys, own) + bias[...] - total_ref[h])
                    score_grad = (probs * (inner_right(values, grad) - term[h])).astype(jnp.bfloat16)
                    target[:, late] = jnp.dot(
                        probs.astype(jnp.bfloat16), grad, preferred_element_type=jnp.float32
                    ).astype(jnp.bfloat16)
                    target[:, early] = jnp.dot(
                        score_grad, own, preferred_element_type=jnp.float32
                    ).astype(jnp.bfloat16)
                    acc[h] += inner_left(keys, score_grad)

            run_if(there, work)

        def turn_of(turn):
            k, d = turns[turn]
            i = plan.plane(a, d)
            compute(turn, True, staged.at[i, k])
            if turn + 1 < len(turns):
                begin(turn + 1, True)
            cond = sum_rows.cross(d, k, 0)[0]
            for q in range(pieces):
                run_if(cond, lambda q=q: sum_rows.cross(d, k, q)[1]().start())
            compute(turn, False, sum_rows.held.at[i, k])
            if turn + 1 < len(turns):
                begin(turn + 1, False)

        def pass_on(turn):
            k, d = turns[turn]

            @pl.loop(0, pieces)
            def _(q):
                sum_rows.first(d, k, q)
                cond, go = sum_rows.over(d, k, q)
                run_if(cond, lambda: go().start())

        begin(0, True)
        begin(0, False)
        place.greet()
        first, second = sums
        for one in sums:
            for i in range(one.n1 - 1):
                one.start(i)
        acc[...] = jnp.zeros_like(acc)
        for h in range(HEADS):
            grad = g_ref[:, h * HEAD : (h + 1) * HEAD].astype(jnp.float32).T
            term[h] = jnp.sum(grad * mixed_ref[h], axis=0, keepdims=True)
        for one in sums:
            for i in range(one.n1 - 1):
                one.stage_core(i)
        last = len(turns) - 1
        for turn in range(len(turns)):
            turn_of(turn)
            if turns[turn][0]:
                pass_on(turn)
            if turn == 0:
                for one in sums:
                    one.start(one.n1 - 1)
            if turn == last - 3:
                for one in sums:
                    one.stage_core(one.n1 - 1)
                for k2 in from_far(second.n2)[:-1]:
                    second.stage_one(k2)
            if turn == last - 2:
                sum_rows.stage_dest(order[0], 0, 2)
            if turn == last - 1:
                for k2 in from_far(first.n2)[:-1]:
                    first.stage_one(k2)
                second.stage_one(0)
                sum_rows.stage_dest(order[0], 2, 3)
        sum_rows.stage_dest(order[0], 3, pieces)
        first.stage_one(0)
        for h in range(HEADS):
            back = turned(acc[h].T * HEAD ** (-0.5), cos_ref[...], -sin_ref[...])
            dq_ref[:, h * HEAD : (h + 1) * HEAD] = back.astype(jnp.bfloat16)
        second.stage_two()
        for d in order[1:]:
            sum_rows.stage_dest(d, 0, pieces)
        pair_out[...] = sum_rows.result()
        first.stage_two()
        for i, one in enumerate(sums):
            one.stage_three(out_ref.at[:, pl.ds(cuts[i], cuts[i + 1] - cuts[i])])
        sum_rows.drain()
        for one in sums:
            one.drain()

    anywhere, near = pl.BlockSpec(memory_space=pl.ANY), pl.BlockSpec(memory_space=pltpu.VMEM)
    scratch = [
        pltpu.VMEM((rows, rows), jnp.float32),
        pltpu.VMEM((HEADS, HEAD, rows), jnp.float32),
        pltpu.VMEM((HEADS, 1, rows), jnp.float32),
        pltpu.VMEM((2, rows, 2 * width), jnp.bfloat16),
        pltpu.VMEM((n, wide, rows, 2 * width), jnp.bfloat16),
        pltpu.SemaphoreType.DMA((2,)),
    ]
    for i in range(2):
        scratch += WholeSum.scratch(place.sizes, orders[i], part_rows, cuts[i + 1] - cuts[i], parts[0].dtype, len(parts))
    scratch += RowSum.scratch(plan, rows, 2 * width, pairs.dtype, pieces)
    return pl.pallas_call(
        kernel,
        out_shape=(jax.ShapeDtypeStruct((part_rows, part_width), jnp.float32),
                   jax.ShapeDtypeStruct((rows, 2 * width), pairs.dtype),
                   jax.ShapeDtypeStruct((rows, width), jnp.bfloat16)),
        in_specs=[near] * 7 + [anywhere] * (1 + len(parts)),
        out_specs=(near, near, near),
        scratch_shapes=scratch,
        compiler_params=pltpu.CompilerParams(
            collective_id=collective_id, has_side_effects=True, vmem_limit_bytes=VMEM_MOST),
        name="attend_back_sum",
    )(queries, grads, mixed, start, total, cosine, sine, pairs, *parts)


def local(
    tokens,
    doc_lengths,
    expert_ids,
    out_grad,
    mixer_gain,
    query_weight,
    key_weight,
    value_weight,
    output_weight,
    ffn_gain,
    router_weight,
    shared_gate,
    shared_up,
    shared_down,
    expert_gate,
    expert_up,
    expert_down,
):
    rows, width = tokens.shape[1], tokens.shape[2]
    ep_count = lax.axis_size("ep")
    device_count = ep_count * lax.axis_size("grp")
    ep_index = lax.axis_index("ep")
    expert_count = router_weight.shape[1]
    capacity = min(rows, 12 * rows * TOP // (7 * expert_count))
    low = lambda v: v.astype(jnp.bfloat16)
    wide = lambda v: v.astype(jnp.float32)
    dot = lambda left, right: jnp.dot(left, right, preferred_element_type=jnp.float32)

    grad_low = out_grad[0]

    doc_ends = jnp.cumsum(doc_lengths[0])
    query_pos = ep_index * rows + jnp.arange(rows, dtype=jnp.int32)
    before = query_pos[:, None] >= doc_ends[None, :]
    start = jnp.max(jnp.where(before, doc_ends[None, :], 0), axis=1)
    info = jnp.stack([ep_index, start[0] // rows]).astype(jnp.int32)
    half_dim = HEAD // 2
    frequency = rope_base ** (-jnp.arange(half_dim, dtype=jnp.float32) / half_dim)
    angles = wide(query_pos)[:, None] * frequency[None, :]
    cosine, sine = jnp.cos(angles), jnp.sin(angles)
    cosine = jnp.concatenate([cosine, cosine], axis=1)
    sine = jnp.concatenate([-sine, sine], axis=1)

    stream = wide(tokens[0])
    hidden_low, queries, own_pairs = project(
        tokens[0], mixer_gain, cosine, sine, query_weight, key_weight, value_weight
    )
    if ep_count > 16:
        pairs = gather_rows(own_pairs, True, 1, 8)
        mixed, mixed_low, log_total = attend(info, queries, start[None, :], pairs)
    else:
        pairs, mixed, mixed_low, log_total = gather_attend(own_pairs, queries, start[None, :], 1)
    grad_later, pairs = lax.optimization_barrier((grad_low, pairs))
    grads_all = lax.all_gather(grad_later, "ep", axis=0, tiled=False)
    mixer_out = dot(mixed_low, output_weight)
    residual = stream + mixer_out
    ffn_low = low(normed(residual, ffn_gain))

    logits = dot(ffn_low, router_weight)
    experts = jnp.arange(expert_count, dtype=jnp.int32)
    assigned = jnp.any(expert_ids[0][:, :, None] == experts[None, None, :], axis=1)
    shown = jnp.where(assigned, logits, masked_value)
    powers = jnp.where(assigned, jnp.exp(shown - jnp.max(shown, axis=1, keepdims=True)), 0.0)
    gate_probs = powers / jnp.sum(powers, axis=1, keepdims=True)
    probs_high = low(gate_probs)
    probs_rest = low(gate_probs - wide(probs_high))
    side = width + 2 * HEAD if 2 * expert_count > HEAD else width + HEAD
    pad = jnp.zeros((rows, side - width - 2 * expert_count), jnp.bfloat16)
    sent = jnp.concatenate([ffn_low, probs_high, probs_rest, pad], axis=1)
    arrived, shared_out, ffn_grad, shared_gate_part, shared_up_part, shared_down_part = gather_shared(
        sent, grad_low, shared_gate, shared_up, shared_down, 2
    )

    own = experts[None, None, :] == ep_index
    high = arrived[:, :, width : width + expert_count]
    rest = arrived[:, :, width + expert_count : width + 2 * expert_count]
    share = jnp.sum(jnp.where(own, wide(high) + wide(rest), 0.0), axis=2)
    chosen = share > 0.0
    earlier = (jnp.arange(rows)[:, None] < jnp.arange(rows)[None, :]).astype(jnp.bfloat16)
    rank = dot(low(chosen), earlier).astype(jnp.int32)
    rank = jnp.where(chosen, rank, -1)
    places = jnp.stack([ep_index, expert_count + ep_index]).astype(jnp.int32)
    back, given, flat_in, pre_grad, lift_grad, middle, result_grad = run_experts(
        places, arrived, grads_all, rank, share, expert_gate, expert_up, expert_down, capacity
    )
    routed = lax.psum_scatter(given, "ep", scatter_dimension=0)
    group_count = lax.axis_size("grp")
    if group_count == 2:
        back_sum, gate_sum, up_sum, down_sum = scatter_experts(
            back, (flat_in, result_grad), (pre_grad, lift_grad, middle), 3
        )
        gate_sum, up_sum, down_sum = gate_sum[None], up_sum[None], down_sum.T[None]
    else:
        back_sum = scatter_rows(back, False, 3)
        split = width // group_count
        own_down_grad = jnp.concatenate(
            [low(inner_left(middle, result_grad[:, i * split : (i + 1) * split])) for i in range(group_count)], axis=0
        )
        over_groups = lambda v: wide(lax.psum_scatter(v, "grp", scatter_dimension=0, tiled=True))[None]
        gate_sum = over_groups(low(inner_left(flat_in, pre_grad)))
        up_sum = over_groups(low(inner_left(flat_in, lift_grad)))
        down_sum = over_groups(own_down_grad)

    grad_out = wide(grad_low)
    gate_back = wide(back_sum[:, width : width + expert_count]) + wide(
        back_sum[:, width + expert_count : width + 2 * expert_count]
    )
    chosen_grad = gate_probs * (gate_back - jnp.sum(gate_probs * gate_back, axis=1, keepdims=True))
    logit_grad = low(chosen_grad)
    ffn_grad = ffn_grad + wide(back_sum[:, :width]) + inner_right(logit_grad, router_weight)
    _, ffn_pull = jax.vjp(normed, residual, ffn_gain)
    residual_part, ffn_gain_grad = ffn_pull(ffn_grad)
    residual_grad = grad_out + residual_part
    mixer_grad_low = low(residual_grad)
    mixed_grad = low(inner_right(mixer_grad_low, output_weight))
    by_device = lambda v: low(v).reshape(device_count, width // device_count, -1)
    early = [
        by_device(part)
        for part in (shared_gate_part, shared_up_part, shared_down_part, inner_left(mixed_low, mixer_grad_low))
    ]
    if ep_count > 16:
        pair_parts, query_lin_grad = attend_back(
            info, queries, mixed_grad, mixed, start[None, :], log_total, cosine, sine, pairs
        )
        pair_grads = scatter_rows(pair_parts, True, 4)
        early_sum = scatter_whole(early, 5)
    else:
        early_sum, pair_grads, query_lin_grad = attend_back_sum(
            queries, mixed_grad, mixed, start[None, :], log_total, cosine, sine, pairs, early, 5
        )

    routed, pair_grads = lax.optimization_barrier((routed, pair_grads))
    layer_out = residual + shared_out + wide(routed)
    query_part, key_part, value_part, tokens_grad, mixer_gain_grad = finish(
        tokens[0], mixer_gain, residual_grad, hidden_low, query_lin_grad, pair_grads, cosine, sine,
        query_weight, key_weight, value_weight,
    )
    squares = jnp.stack(
        [jnp.sum(residual * residual), jnp.sum(mixer_out * mixer_out), jnp.sum(layer_out * layer_out)]
    )
    extras = jnp.concatenate(
        [inner_left(ffn_low, logit_grad), mixer_gain_grad.T, ffn_gain_grad[:, None],
         jnp.broadcast_to(squares[None, :], (width, 3))], axis=1
    )
    extras = jnp.pad(extras, ((0, 0), (0, HEAD - extras.shape[1])))
    late_sum = scatter_whole([by_device(v) for v in (query_part, key_part, value_part, extras)], 6)
    extra_sum = late_sum[:, 3 * width :]
    entry_count = rows * device_count * width
    stream_rms = jnp.sqrt(extra_sum[0, expert_count + 2 : expert_count + 5] / entry_count)
    ff = shared_gate.shape[1]
    return (
        low(layer_out)[None],
        tokens_grad[None],
        extra_sum[:, expert_count],
        late_sum[:, :width],
        late_sum[:, width : 2 * width],
        late_sum[:, 2 * width : 3 * width],
        early_sum[:, 3 * ff :],
        extra_sum[:, expert_count + 1],
        extra_sum[:, :expert_count],
        early_sum[:, :ff],
        early_sum[:, ff : 2 * ff],
        early_sum[:, 2 * ff : 3 * ff].T,
        gate_sum,
        up_sum,
        down_sum,
        stream_rms,
    )


def solution(mesh):
    return jax.shard_map(
        local,
        mesh=mesh,
        in_specs=(
            P("grp", "ep", None),
            P("grp", None),
            P("grp", "ep", None),
            P("grp", "ep", None),
            P(),
            P(),
            P(),
            P(),
            P(),
            P(),
            P(),
            P(),
            P(),
            P(),
            P("ep", None, None),
            P("ep", None, None),
            P("ep", None, None),
        ),
        out_specs=(
            P("grp", "ep", None),
            P("grp", "ep", None),
            P(("grp", "ep")),
            P(("grp", "ep"), None),
            P(("grp", "ep"), None),
            P(("grp", "ep"), None),
            P(("grp", "ep"), None),
            P(("grp", "ep")),
            P(("grp", "ep"), None),
            P(("grp", "ep"), None),
            P(("grp", "ep"), None),
            P(None, ("grp", "ep")),
            P("ep", "grp", None),
            P("ep", "grp", None),
            P("ep", None, "grp"),
            P(),
        ),
        check_vma=False,
    )
```

```python
import functools

import jax
import jax.numpy as jnp
from jax import lax
from jax.experimental import pallas as pl
from jax.experimental.pallas import tpu as pltpu
from jax.sharding import PartitionSpec as P

HEADS = 10
HEAD = 128
TOP = 7

epsilon = 1e-06
rope_base = 10000.0
masked_value = -1e30


def normed(values, gain_vec):
    return (
        values * lax.rsqrt(jnp.mean(values * values, axis=-1, keepdims=True) + epsilon) * gain_vec
    )


def inner_left(left_op, right_op):
    return lax.dot_general(
        left_op, right_op, (((0,), (0,)), ((), ())), preferred_element_type=jnp.float32
    )


def inner_right(left_op, right_op):
    return lax.dot_general(
        left_op, right_op, (((1,), (1,)), ((), ())), preferred_element_type=jnp.float32
    )


def silu_parts(pre_act):
    sigmoid_val = jax.nn.sigmoid(pre_act)
    return (pre_act * sigmoid_val, sigmoid_val * (1.0 + pre_act * (1.0 - sigmoid_val)))


MESH = pl.DeviceIdType.MESH
COUPLES = 2
VMEM_MOST = 64 * 1024 * 1024 - 65536


def when(cond):
    if cond is True:
        return lambda f: f()
    if cond is False:
        return lambda f: None
    return pl.when(cond)


def both(*conds):
    out = True
    for cond in conds:
        if cond is False:
            return False
        if cond is True:
            continue
        out = cond if out is True else jnp.logical_and(out, cond)
    return out


class Plan:
    def __init__(self, ep_count, window):
        self.long = 4
        self.wide = ep_count // 8
        self.window = window
        self.steps = (
            list(range(self.long // 2 + 1))
            if window
            else list(range(-(self.long - 1), self.long))
        )

    def place(self):
        me = lax.axis_index("ep")
        return me // (2 * self.wide), (me // 2) % self.wide, me % 2

    def slot(self, a, b, c):
        return (a * self.wide + b) * 2 + c

    def plane(self, a, d):
        return d if self.window else jnp.clip(a - d, 0, self.long - 1)

    def planes(self):
        return len(self.steps) if self.window else self.long

    def inside(self, a):
        return jnp.logical_and(a >= 0, a < self.long)

    def need(self, d, b, c, b0, c0):
        if not self.window or 0 < d < self.long // 2:
            return True
        if d == 0:
            return jnp.logical_or(b0 < b, jnp.logical_and(b0 == b, c0 <= c))
        return jnp.logical_or(b0 > b, jnp.logical_and(b0 == b, c0 >= c))

    def need_pair(self, d, b, b0):
        if not self.window or 0 < d < self.long // 2:
            return True
        return b0 < b if d == 0 else b0 > b

    def greet(self, a, b, c):
        barrier = pltpu.get_barrier_semaphore()

        def signal(cond, dev):
            @when(cond)
            def _():
                pl.semaphore_signal(barrier, inc=1, device_id={"ep": dev}, device_id_type=MESH)

        signal(a + 1 < self.long, self.slot(a + 1, b, c))
        signal(a > 0, self.slot(a - 1, b, c))
        for k in range(1, self.wide):
            signal(True, self.slot(a, (b + k) % self.wide, c))
        signal(True, self.slot(a, b, 1 - c))
        ends = (a == 0).astype(jnp.int32) + (a == self.long - 1).astype(jnp.int32)
        pl.semaphore_wait(barrier, self.wide + 2 - ends)


def gather_steps(plan, pieces, beside, greet, x_ref, out_ref, ra, sa_up, sa_dn, rb, sb, rc, sc, own):
    a, b, c = plan.place()
    steps, wide = plan.steps, plan.wide
    at = {d: i for i, d in enumerate(steps)}
    rows = x_ref.shape[0] // pieces

    def part(q):
        return pl.ds(pl.multiple_of(q * rows, rows), rows)

    def copy(q, src, slot, ssem, rsem, dev):
        return pltpu.make_async_remote_copy(
            src_ref=src, dst_ref=out_ref.at[slot, part(q)], send_sem=ssem, recv_sem=rsem,
            device_id={"ep": dev}, device_id_type=MESH,
        )

    def hops(d, q):
        i = at[d]
        slot = plan.slot(a - d, b, c)
        src = x_ref.at[part(q)] if d == 0 else out_ref.at[slot, part(q)]
        real = plan.inside(a - d)
        out = []
        if d >= 0 and d + 1 in at:
            out.append((both(real, a + 1 < plan.long), lambda: copy(
                q, src, slot, sa_up.at[i, q], ra.at[at[d + 1], q], plan.slot(a + 1, b, c))))
        if d <= 0 and d - 1 in at:
            out.append((both(real, a > 0), lambda: copy(
                q, src, slot, sa_dn.at[i, q], ra.at[at[d - 1], q], plan.slot(a - 1, b, c))))
        for k in range(1, wide):
            to = (b + k) % wide
            out.append((both(real, plan.need_pair(d, to, b)), lambda k=k, to=to: copy(
                q, src, slot, sb.at[i, k, q], rb.at[i, k, q], plan.slot(a, to, c))))
        out.append((both(real, plan.need(d, b, 1 - c, b, c)), lambda: copy(
            q, src, slot, sc.at[i, 0, q], rc.at[i, 0, q], plan.slot(a, b, 1 - c))))
        return out

    def cross(d, k, q):
        i = at[d]
        b0 = (b + wide - k) % wide
        slot = plan.slot(a - d, b0, c)
        real = plan.inside(a - d)
        come = lambda: copy(q, x_ref.at[part(q)], slot, sb.at[i, k, q], rb.at[i, k, q], plan.slot(a, b, c))
        go = lambda: copy(q, out_ref.at[slot, part(q)], slot, sc.at[i, k, q], rc.at[i, k, q],
                          plan.slot(a, b, 1 - c))
        return (both(real, plan.need_pair(d, b, b0)), come,
                both(real, plan.need(d, b, 1 - c, b0, c)), go)

    if greet:
        plan.greet(a, b, c)
    keep = pltpu.make_async_copy(x_ref, out_ref.at[plan.slot(a, b, c)], own)

    @pl.loop(0, pieces)
    def _(q):
        for cond, go in hops(0, q):
            @when(cond)
            def _(go=go):
                go().start()

    keep.start()
    yield
    far = max(abs(d) for d in steps)
    for step in range(1, far + 3):
        beside(step - 1)

        @pl.loop(0, pieces)
        def _(q, step=step):
            for d in (step, -step):
                if d in at:
                    @when(plan.inside(a - d))
                    def _(d=d):
                        slot = plan.slot(a - d, b, c)
                        copy(q, x_ref.at[part(q)], slot, sa_up.at[0, q], ra.at[at[d], q],
                             plan.slot(a, b, c)).wait_recv()
                        for cond, go in hops(d, q):
                            @when(cond)
                            def _(go=go):
                                go().start()
            for d in sorted({step - 2, 2 - step}) if step > 1 else ():
                if d in at:
                    for k in range(1, wide):
                        came, come, goes, go = cross(d, k, q)
                        @when(came)
                        def _(come=come):
                            come().wait_recv()
                        @when(goes)
                        def _(go=go):
                            go().start()
    keep.wait()

    @pl.loop(0, pieces)
    def _(q):
        for d in steps:
            i = at[d]
            real = plan.inside(a - d)
            for k in range(wide):
                b0 = (b + wide - k) % wide
                slot = plan.slot(a - d, b0, 1 - c)
                @when(both(real, plan.need(d, b, c, b0, 1 - c)))
                def _(slot=slot, i=i, k=k):
                    copy(q, x_ref.at[part(q)], slot, sc.at[i, k, q], rc.at[i, k, q],
                         plan.slot(a, b, c)).wait_recv()
            for cond, go in hops(d, q):
                @when(cond)
                def _(go=go):
                    go().wait_send()
            for k in range(1, wide):
                came, come, goes, go = cross(d, k, q)
                @when(goes)
                def _(go=go):
                    go().wait_send()


def gather_kernel(plan, pieces, beside, *refs):
    for _ in gather_steps(plan, pieces, beside, True, *refs):
        pass


def gather_rows(block, window, collective_id, pieces=4):
    ep_count = lax.axis_size("ep")
    plan = Plan(ep_count, window)
    n, wide = len(plan.steps), plan.wide
    sem = pltpu.SemaphoreType.DMA
    return pl.pallas_call(
        functools.partial(gather_kernel, plan, pieces, lambda n: None),
        out_shape=jax.ShapeDtypeStruct((ep_count,) + block.shape, block.dtype),
        in_specs=[pl.BlockSpec(memory_space=pltpu.VMEM)],
        out_specs=pl.BlockSpec(memory_space=pl.ANY),
        scratch_shapes=[sem((n, pieces)), sem((n, pieces)), sem((n, pieces)), sem((n, wide, pieces)),
                        sem((n, wide, pieces)), sem((n, wide, pieces)), sem((n, wide, pieces)), sem],
        compiler_params=pltpu.CompilerParams(collective_id=collective_id, has_side_effects=True),
        name="gather_rows",
    )(block)


def gather_shared(block, grads, gate, up, down, collective_id, pieces=4):
    ep_count = lax.axis_size("ep")
    plan = Plan(ep_count, False)
    n, wide = len(plan.steps), plan.wide
    rows, width = grads.shape
    ff = gate.shape[1]
    sem = pltpu.SemaphoreType.DMA
    stages = max(plan.steps) + 2
    tiles = ff // HEAD

    def kernel(x_ref, g_ref, wg_ref, wu_ref, wd_ref, out_ref, shared_ref, back_ref, dg_ref, du_ref, dd_ref, *sems):
        dot = lambda left, right: jnp.dot(left, right, preferred_element_type=jnp.float32)

        def tile(i):
            at = pl.ds(pl.multiple_of(i * HEAD, HEAD), HEAD)
            x, g = x_ref[:, :width], g_ref[...]
            w_gate, w_up, w_down = wg_ref[:, at], wu_ref[:, at], wd_ref[at, :]
            silu, slope = silu_parts(dot(x, w_gate))
            lift = dot(x, w_up)
            mid = (silu * lift).astype(jnp.bfloat16)
            mid_grad = inner_right(g, w_down)
            pre_grad = (mid_grad * lift * slope).astype(jnp.bfloat16)
            lift_grad = (mid_grad * silu).astype(jnp.bfloat16)
            out = dot(mid, w_down)
            back = inner_right(pre_grad, w_gate) + inner_right(lift_grad, w_up)

            @pl.when(i == 0)
            def _():
                shared_ref[...] = out
                back_ref[...] = back

            @pl.when(i > 0)
            def _():
                shared_ref[...] += out
                back_ref[...] += back

            dg_ref[:, at] = inner_left(x, pre_grad).astype(jnp.bfloat16)
            du_ref[:, at] = inner_left(x, lift_grad).astype(jnp.bfloat16)
            dd_ref[:, at] = inner_left(g, mid).astype(jnp.bfloat16)

        def beside(stage):
            pl.loop(tiles * stage // stages, tiles * (stage + 1) // stages)(tile)

        gather_kernel(plan, pieces, beside, x_ref, out_ref, *sems)

    near = pl.BlockSpec(memory_space=pltpu.VMEM)
    return pl.pallas_call(
        kernel,
        out_shape=(
            jax.ShapeDtypeStruct((ep_count,) + block.shape, block.dtype),
            jax.ShapeDtypeStruct((rows, width), jnp.float32),
            jax.ShapeDtypeStruct((rows, width), jnp.float32),
        ) + (jax.ShapeDtypeStruct((width, ff), jnp.bfloat16),) * 3,
        in_specs=[near] * 5,
        out_specs=(pl.BlockSpec(memory_space=pl.ANY),) + (near,) * 5,
        scratch_shapes=[sem((n, pieces)), sem((n, pieces)), sem((n, pieces)), sem((n, wide, pieces)),
                        sem((n, wide, pieces)), sem((n, wide, pieces)), sem((n, wide, pieces)), sem],
        compiler_params=pltpu.CompilerParams(
            collective_id=collective_id, has_side_effects=True, vmem_limit_bytes=VMEM_MOST),
        name="gather_shared",
    )(block, grads, gate, up, down)


def add_rows(dst, others, out=None):
    rows, width = dst.shape
    out = dst if out is None else out
    small = rows <= 64
    piece = 32 if rows % 32 == 0 else rows
    lanes = width if rows % 32 == 0 else 4 * HEAD
    whole = width // lanes * lanes

    def add(at):
        if len(others) == 1 and out.dtype == jnp.bfloat16:
            out[at] = dst[at] + others[0][at]
        else:
            total = dst[at].astype(jnp.float32)
            for other in others:
                total = total + other[at].astype(jnp.float32)
            out[at] = total.astype(out.dtype)

    if piece == rows:
        @pl.loop(0, whole // lanes)
        def _(i):
            add((slice(None), pl.ds(pl.multiple_of(i * lanes, lanes), lanes)))

        if whole < width:
            add((slice(None), pl.ds(whole, width - whole)))
    else:
        @pl.loop(0, rows // piece)
        def _(i):
            add((pl.ds(pl.multiple_of(i * piece, piece), piece), slice(None)))


def send(src, dst, ssem, rsem, to):
    return pltpu.make_async_remote_copy(
        src_ref=src, dst_ref=dst, send_sem=ssem, recv_sem=rsem, device_id=to, device_id_type=MESH
    )


def run_if(cond, go):
    @when(cond)
    def _():
        go()


class RowSum:
    @staticmethod
    def scratch(plan, rows, width, dtype, pieces):
        n, wide = plan.planes(), plan.wide
        blocks = lambda *lead: pltpu.VMEM(lead + (rows, width), dtype)
        sem = lambda *lead: pltpu.SemaphoreType.DMA(lead + (pieces,))
        return [blocks(n, wide), blocks(n, wide), blocks(n, wide - 1), blocks(n), blocks(1 if plan.window else n),
                sem(n, wide), sem(n, wide), sem(n, wide), sem(n, wide), sem(n), sem(n), sem(n), sem(n, wide)]

    def __init__(self, plan, pieces, p_ref, scratch):
        self.plan, self.pieces, self.p_ref = plan, pieces, p_ref
        (self.held, self.rcb, self.rbb, self.r_hi, self.r_lo,
         self.sc, self.rc, self.sb, self.rb, self.sa, self.rhi, self.rlo, self.ld) = scratch
        self.a, self.b, self.c = plan.place()
        self.ready = len(p_ref.shape) == 4
        self.rows = p_ref.shape[-2] // pieces
        self.order = sorted(plan.steps, key=lambda d: -abs(d))

    def part(self, q):
        return pl.ds(pl.multiple_of(q * self.rows, self.rows), self.rows)

    def dev(self, a, b, c):
        return {"ep": self.plan.slot(a, b, c)}

    def source(self, k):
        return (self.b + self.plan.wide - k) % self.plan.wide

    def load(self, d, k, q):
        p, i, b0 = self.plan, self.plan.plane(self.a, d), self.source(k)
        return both(p.inside(self.a - d), p.need(d, self.b, self.c, b0, self.c)), lambda: pltpu.make_async_copy(
            self.p_ref.at[p.slot(self.a - d, b0, self.c), self.part(q)], self.held.at[i, k, self.part(q)],
            self.ld.at[i, k, q])

    def cross(self, d, k, q):
        p, i, b0, c = self.plan, self.plan.plane(self.a, d), self.source(k), self.c
        real = p.inside(self.a - d)
        at = (i, k) if self.ready else (p.slot(self.a - d, b0, 1 - c),)
        return (both(real, p.need(d, self.b, c, b0, 1 - c)), lambda: send(
            self.p_ref.at[at + (self.part(q),)], self.rcb.at[i, k, self.part(q)],
            self.sc.at[i, k, q], self.rc.at[i, k, q], self.dev(self.a, self.b, 1 - c)),
            both(real, p.need(d, self.b, 1 - c, b0, c)))

    def over(self, d, k, q):
        p, i, b0 = self.plan, self.plan.plane(self.a, d), self.source(k)
        return both(p.inside(self.a - d), p.need_pair(d, self.b, b0)), lambda: send(
            self.held.at[i, k, self.part(q)], self.rbb.at[i, k - 1, self.part(q)], self.sb.at[i, k, q],
            self.rb.at[i, k, q], self.dev(self.a, b0, self.c))

    def along(self, d, q):
        p, i, up = self.plan, self.plan.plane(self.a, d), d < 0
        j = d - 1 if p.window else i
        return p.inside(self.a - d), lambda: send(
            self.held.at[i, 0, self.part(q)], (self.r_lo if up else self.r_hi).at[j, self.part(q)],
            self.sa.at[i, q], (self.rlo if up else self.rhi).at[j, q],
            self.dev(self.a + (1 if up else -1), self.b, self.c))

    def start(self, ks):
        for k in ks:
            @pl.loop(0, self.pieces)
            def _(q, k=k):
                for d in self.order:
                    for cond, go in (self.cross(d, k, q)[:2], self.load(d, k, q)):
                        run_if(cond, lambda go=go: go().start())

    def first(self, d, k, q):
        i = self.plan.plane(self.a, d)
        if not self.ready:
            cond, go = self.load(d, k, q)
            run_if(cond, lambda: go().wait())
        _, come_go, come = self.cross(d, k, q)

        def take():
            come_go().wait_recv()
            add_rows(self.held.at[i, k, self.part(q)], [self.rcb.at[i, k, self.part(q)]])

        run_if(come, take)

    def stage_over(self, k):
        @pl.loop(0, self.pieces)
        def _(q):
            for d in self.order:
                self.first(d, k, q)
                cond, go = self.over(d, k, q)
                run_if(cond, lambda go=go: go().start())

    def stage_dests(self, low, high):
        @pl.loop(low, high)
        def _(q):
            for d in self.order:
                self.dest(d, q)

    def stage_dest(self, d, low, high):
        @pl.loop(low, high)
        def _(q):
            self.dest(d, q)

    def dest(self, d, q):
        p, a, b, steps = self.plan, self.a, self.b, self.plan.steps
        i = p.plane(a, d)
        real = p.inside(a - d)
        mine = self.held.at[i, 0, self.part(q)]
        self.first(d, 0, q)
        for k in range(1, p.wide):
            def take(k=k):
                self.over(d, k, q)[1]().wait_recv()
                add_rows(mine, [self.rbb.at[i, k - 1, self.part(q)]])

            run_if(both(real, p.need_pair(d, (b + k) % p.wide, b)), take)
        for inner, cond, buf, sem in ((d >= 0 and d + 1 in steps, a + 1 < p.long, self.r_hi, self.rhi),
                                      (d <= 0 and d - 1 in steps, a > 0, self.r_lo, self.rlo)):
            if inner:
                def take(buf=buf, sem=sem):
                    send(mine, buf.at[i, self.part(q)], self.sa.at[i, q], sem.at[i, q],
                         self.dev(a, b, self.c)).wait_recv()
                    add_rows(mine, [buf.at[i, self.part(q)]])

                run_if(both(real, cond), take)
        if d:
            cond, go = self.along(d, q)
            run_if(cond, lambda: go().start())

    def result(self):
        return self.held[self.plan.plane(self.a, 0), 0]

    def drain(self):
        @pl.loop(0, self.pieces)
        def _(q):
            for d in self.plan.steps:
                sends = [self.cross(d, k, q)[:2] for k in range(self.plan.wide)]
                sends += [self.over(d, k, q) for k in range(1, self.plan.wide)]
                if d:
                    sends.append(self.along(d, q))
                for cond, go in sends:
                    run_if(cond, lambda go=go: go().wait_send())


def scatter_rows(parts, window, collective_id, pieces=4):
    ep_count, rows, width = parts.shape
    plan = Plan(ep_count, window)

    def kernel(p_ref, out_ref, *scratch):
        total = RowSum(plan, pieces, p_ref, scratch)
        plan.greet(total.a, total.b, total.c)
        ks = list(range(1, plan.wide)) + [0]
        total.start(ks)
        for k in ks[:-1]:
            total.stage_over(k)
        total.stage_dests(0, pieces)
        out_ref[...] = total.result()
        total.drain()

    return pl.pallas_call(
        kernel,
        out_shape=jax.ShapeDtypeStruct((rows, width), parts.dtype),
        in_specs=[pl.BlockSpec(memory_space=pl.ANY)],
        out_specs=pl.BlockSpec(memory_space=pltpu.VMEM),
        scratch_shapes=RowSum.scratch(plan, rows, width, parts.dtype, pieces),
        compiler_params=pltpu.CompilerParams(
            collective_id=collective_id, has_side_effects=True, vmem_limit_bytes=VMEM_MOST),
        name="scatter_rows",
    )(parts)


class Place:
    def __init__(self, groups, ep_count):
        self.sizes = {"x": groups, "a": 4, "b": ep_count // 8}

    def locate(self):
        me, wide = lax.axis_index("ep"), self.sizes["b"]
        self.at = {"x": lax.axis_index("grp"), "a": me // (2 * wide), "b": (me // 2) % wide, "c": me % 2}

    def dev(self, **moved):
        at = {**self.at, **moved}
        return {"grp": at["x"], "ep": (at["a"] * self.sizes["b"] + at["b"]) * 2 + at["c"]}

    def slot(self, **moved):
        at = {**self.at, **moved}
        return ((at["x"] * self.sizes["a"] + at["a"]) * self.sizes["b"] + at["b"]) * 2 + at["c"]

    def back(self, axis, k):
        return (self.at[axis] + self.sizes[axis] - k) % self.sizes[axis]

    def greet(self):
        peers = [self.dev(c=1 - self.at["c"])] + [
            self.dev(**{axis: self.back(axis, k)}) for axis in "xba" for k in range(1, self.sizes[axis])]
        barrier = pltpu.get_barrier_semaphore()
        for to in peers:
            pl.semaphore_signal(barrier, inc=1, device_id=to, device_id_type=MESH)
        pl.semaphore_wait(barrier, len(peers))


def from_far(size):
    return list(range(1, size)) + [0]


class WholeSum:
    @staticmethod
    def scratch(sizes, axes, rows, width, dtype, sources):
        n1, n2, n3 = (sizes[axis] for axis in axes)
        blocks = lambda *lead: pltpu.VMEM(lead + (rows, width), dtype)
        sem = lambda *lead: pltpu.SemaphoreType.DMA(lead)
        full = (n1, n2, n3)
        one, two, three = (n1 - 1, n2, n3), (n2 - 1, n3), (n3 - 1,)
        return [blocks(*full), blocks(*full), blocks(*one), blocks(*two), blocks(*three),
                sem(*full, sources), sem(*full, sources), sem(*full, sources), sem(*one), sem(*one), sem(*two), sem(*two), sem(*three), sem(*three)]

    def __init__(self, place, axes, pieces, scratch):
        self.place, self.axes, self.pieces = place, axes, pieces
        (self.held, self.rcb, self.r1, self.r2, self.r3,
         self.ld, self.sc, self.rc, self.s1, self.q1, self.s2, self.q2, self.s3, self.q3) = scratch
        self.n1, self.n2, self.n3 = (place.sizes[axis] for axis in axes)
        self.groups = [[(k1, k2, k3) for k2 in from_far(self.n2) for k3 in from_far(self.n3)]
                       for k1 in from_far(self.n1)]

    def slot(self, key, c):
        return self.place.slot(c=c, **{axis: self.place.back(axis, k) for axis, k in zip(self.axes, key)})

    def loads(self, key):
        c = self.place.at["c"]
        for n, (ref, first, at, count) in enumerate(self.pieces):
            frm, to = pl.ds(first, count), pl.ds(at, count)
            yield pltpu.make_async_copy(
                ref.at[self.slot(key, c), :, frm], self.held.at[key + (slice(None), to)],
                self.ld.at[key + (n,)])

    def crossings(self, key):
        c = self.place.at["c"]
        for n, (ref, first, at, count) in enumerate(self.pieces):
            frm, to = pl.ds(first, count), pl.ds(at, count)
            yield send(ref.at[self.slot(key, 1 - c), :, frm], self.rcb.at[key + (slice(None), to)],
                       self.sc.at[key + (n,)], self.rc.at[key + (n,)], self.place.dev(c=1 - c))

    def hop(self, level, key):
        buf, ssem, rsem = ((self.r1, self.s1, self.q1), (self.r2, self.s2, self.q2), (self.r3, self.s3, self.q3))[level]
        axis, k = self.axes[level], key[level]
        far = (k - 1,) + key[level + 1 :]
        return send(self.held.at[key], buf.at[far], ssem.at[far], rsem.at[far],
                    self.place.dev(**{axis: self.place.back(axis, k)}))

    def start(self, i):
        for key in self.groups[i]:
            for go in self.crossings(key):
                go.start()
            for go in self.loads(key):
                go.start()

    def stage_core(self, i):
        for key in self.groups[i]:
            for go in self.loads(key):
                go.wait()
            for go in self.crossings(key):
                go.wait_recv()
            add_rows(self.held.at[key], [self.rcb.at[key]])
            if key[0]:
                self.hop(0, key).start()

    def stage_one(self, k2):
        for k3 in from_far(self.n3):
            for k1 in range(1, self.n1):
                self.hop(0, (k1, k2, k3)).wait_recv()
            add_rows(self.held.at[0, k2, k3], [self.r1.at[k1 - 1, k2, k3] for k1 in range(1, self.n1)])
            if k2:
                self.hop(1, (0, k2, k3)).start()

    def stage_two(self):
        for k3 in from_far(self.n3):
            for k2 in range(1, self.n2):
                self.hop(1, (0, k2, k3)).wait_recv()
            add_rows(self.held.at[0, 0, k3], [self.r2.at[k2 - 1, k3] for k2 in range(1, self.n2)])
            if k3:
                self.hop(2, (0, 0, k3)).start()

    def stage_three(self, out):
        for k3 in range(1, self.n3):
            self.hop(2, (0, 0, k3)).wait_recv()
        add_rows(self.held.at[0, 0, 0], [self.r3.at[k3 - 1] for k3 in range(1, self.n3)], out)

    def drain(self):
        for group in self.groups:
            for key in group:
                for go in self.crossings(key):
                    go.wait_send()
                if key[0]:
                    self.hop(0, key).wait_send()
                elif key[1]:
                    self.hop(1, key).wait_send()
                elif key[2]:
                    self.hop(2, key).wait_send()


def pieces_of(sources, low, high):
    pieces, first = [], 0
    for ref in sources:
        begin, end = max(low, first), min(high, first + ref.shape[2])
        if begin < end:
            pieces.append((ref, begin - first, begin - low, end - begin))
        first += ref.shape[2]
    return pieces


def scatter_whole(parts, collective_id):
    rows = parts[0].shape[1]
    width = sum(part.shape[2] for part in parts)
    groups, ep_count = lax.axis_size("grp"), lax.axis_size("ep")
    place = Place(groups, ep_count)
    tiles = width // HEAD
    count = 2 * COUPLES
    cuts = [tiles * n // count * HEAD for n in range(count + 1)]
    orders = ["xba", "bxa"] * COUPLES

    def kernel(*refs):
        sources, refs = refs[: len(parts)], refs[len(parts) :]
        out_ref, refs = refs[0], refs[1:]
        place.locate()
        sums = []
        for n, axes in enumerate(orders):
            pieces = pieces_of(sources, cuts[n], cuts[n + 1])
            sums.append(WholeSum(place, axes, pieces, refs[:14]))
            refs = refs[14:]
        outs = [out_ref.at[:, pl.ds(cuts[n], cuts[n + 1] - cuts[n])] for n in range(len(orders))]
        place.greet()
        couples = [sums[n : n + 2] for n in range(0, len(sums), 2)]
        for couple in couples:
            for i in range(max(s.n1 for s in couple)):
                for s in couple:
                    if i < s.n1:
                        s.start(i)

        def core(couple):
            for i in range(max(s.n1 for s in couple)):
                for s in couple:
                    if i < s.n1:
                        s.stage_core(i)

        def one(couple):
            for i in range(max(s.n2 for s in couple)):
                for s in couple:
                    if i < s.n2:
                        s.stage_one(from_far(s.n2)[i])

        def two(couple):
            for s in couple:
                s.stage_two()

        core(couples[0])
        for n, couple in enumerate(couples):
            one(couple)
            if n + 1 < len(couples):
                core(couples[n + 1])
            two(couple)
        for s, out in zip(sums, outs):
            s.stage_three(out)
        for s in sums:
            s.drain()

    operands, anywhere = list(parts), pl.BlockSpec(memory_space=pl.ANY)
    out_shape = [jax.ShapeDtypeStruct((rows, width), jnp.float32)]
    scratch = []
    for n, axes in enumerate(orders):
        scratch += WholeSum.scratch(place.sizes, axes, rows, cuts[n + 1] - cuts[n], parts[0].dtype, len(parts))
    got = pl.pallas_call(
        kernel,
        out_shape=tuple(out_shape),
        in_specs=[anywhere] * len(operands),
        out_specs=tuple(pl.BlockSpec(memory_space=pltpu.VMEM) for _ in out_shape),
        scratch_shapes=scratch,
        compiler_params=pltpu.CompilerParams(
            collective_id=collective_id, has_side_effects=True, vmem_limit_bytes=VMEM_MOST),
        name="scatter_whole",
    )(*operands)
    return got[0]


def scatter_experts(parts, lefts, rights, collective_id):
    ep_count, rows, width = parts.shape
    flat, tall = lefts[0].shape
    ff = rights[0].shape[1]
    half, depth = tall // 2, flat // 3
    plan, pieces = Plan(ep_count, False), 4
    place = Place(lax.axis_size("grp"), ep_count)
    left_of = [0, 0, 1]
    hooks = (12, 13, 14, 15)
    kinds, units = len(rights), 2 * len(rights)
    steps = units * 3

    def kernel(p_ref, in_ref, og_ref, pre_ref, lift_ref, mid_ref, out_ref, w0, w1, w2, acc, left, right, gone, came,
               ls, rs, gs, cs, *scratch):
        left_refs, right_refs, outs = (in_ref, og_ref), (pre_ref, lift_ref, mid_ref), (w0, w1, w2)
        place.locate()
        total = RowSum(plan, pieces, p_ref, scratch)
        g = place.at["x"]
        place.greet()

        def fetch(kind, step):
            chunk, slot = step % 3, step % 2
            mine = (step >= 3 * kinds).astype(jnp.int32)
            first = pl.multiple_of(jnp.where(mine == 1, g, 1 - g) * half, HEAD)
            at = pl.ds(pl.multiple_of(chunk * depth, depth), depth)
            return (pltpu.make_async_copy(left_refs[left_of[kind]].at[at, pl.ds(first, half)], left.at[slot], ls.at[slot]),
                    pltpu.make_async_copy(right_refs[kind].at[at, :], right.at[slot], rs.at[slot]))

        def per_kind(step, go):
            for kind in range(kinds):
                run_if((step // 3) % kinds == kind, lambda kind=kind: go(kind))

        def begin(step):
            def go(kind):
                for copy in fetch(kind, step):
                    copy.start()
            per_kind(step, go)

        def away(kind):
            return send(gone.at[kind], came.at[kind], gs.at[kind], cs.at[kind], place.dev(x=place.back("x", 1)))

        def meet(n):
            q, distance = n // plan.long, plan.long - 1 - n % plan.long
            for d in sorted({-distance, distance}):
                total.dest(d, q)

        ks = from_far(plan.wide)
        total.start(ks)
        begin(jnp.int32(0))
        for k in ks[:-1]:
            total.stage_over(k)

        @pl.loop(0, steps)
        def _(step):
            run_if(step + 1 < steps, lambda: begin(step + 1))

            def ready(kind):
                for copy in fetch(kind, step):
                    copy.wait()
            per_kind(step, ready)
            slot = step % 2
            product = inner_left(left[slot], right[slot])
            fresh = step % 3 == 0

            @pl.when(fresh)
            def _():
                acc[...] = product

            @pl.when(jnp.logical_not(fresh))
            def _():
                acc[...] += product

            def done(kind):
                @pl.when(step < 3 * kinds)
                def _():
                    gone[kind] = acc[...].astype(jnp.bfloat16)
                    away(kind).start()

                @pl.when(step >= 3 * kinds)
                def _():
                    outs[kind][...] = acc[...]

            run_if(step % 3 == 2, lambda: per_kind(step, done))
            for n, at in enumerate(hooks):
                run_if(step == at, lambda n=n: meet(n))

        for n in range(len(hooks), pieces * plan.long):
            meet(n)
        out_ref[...] = total.result()
        for kind in range(kinds):
            away(kind).wait_recv()
            piece = 32

            @pl.loop(0, half // piece)
            def _(i, kind=kind):
                at = pl.ds(pl.multiple_of(i * piece, piece), piece)
                outs[kind][at, :] = outs[kind][at, :] + came[kind, at, :].astype(jnp.float32)

        for kind in range(kinds):
            away(kind).wait_send()
        total.drain()

    anywhere = pl.BlockSpec(memory_space=pl.ANY)
    sem = lambda n: pltpu.SemaphoreType.DMA((n,))
    outs = [jax.ShapeDtypeStruct((rows, width), parts.dtype)] + [jax.ShapeDtypeStruct((half, ff), jnp.float32)] * kinds
    return pl.pallas_call(
        kernel,
        out_shape=tuple(outs),
        in_specs=[anywhere] * 6,
        out_specs=tuple(pl.BlockSpec(memory_space=pltpu.VMEM) for _ in outs),
        scratch_shapes=[
            pltpu.VMEM((half, ff), jnp.float32),
            pltpu.VMEM((2, depth, half), jnp.bfloat16),
            pltpu.VMEM((2, depth, ff), jnp.bfloat16),
            pltpu.VMEM((kinds, half, ff), jnp.bfloat16),
            pltpu.VMEM((kinds, half, ff), jnp.bfloat16),
            sem(2), sem(2), sem(kinds), sem(kinds),
        ] + RowSum.scratch(plan, rows, width, parts.dtype, pieces),
        compiler_params=pltpu.CompilerParams(
            collective_id=collective_id, has_side_effects=True, vmem_limit_bytes=VMEM_MOST),
        name="scatter_experts",
    )(parts, *lefts, *rights)


def visible_bias(shape, first_key, start, first_query):
    key_pos = first_key + lax.broadcasted_iota(jnp.int32, shape, 0)
    query_pos = first_query + lax.broadcasted_iota(jnp.int32, shape, 1)
    seen = jnp.logical_and(key_pos >= start, key_pos <= query_pos)
    return jnp.where(seen, 0.0, masked_value)


def lanes(first):
    return pl.ds(pl.multiple_of(first, HEAD), HEAD)


def turned(values, cosine, sine):
    return values * cosine + pltpu.roll(values, HEAD // 2, 1) * sine


def whole_spec(*shape):
    return pl.BlockSpec(shape, lambda *s: (0,) * len(shape))


def project_kernel(x_ref, gain_ref, cos_ref, sin_ref, wq_ref, wk_ref, wv_ref, hid_ref, q_ref, kv_ref, hidden):
    @pl.when(pl.program_id(0) == 0)
    def _():
        hidden[...] = normed(x_ref[...].astype(jnp.float32), gain_ref[...]).astype(jnp.bfloat16)
        hid_ref[...] = hidden[...]

    cosine, sine = cos_ref[...], sin_ref[...]
    q = jnp.dot(hidden[...], wq_ref[...], preferred_element_type=jnp.float32)
    k = jnp.dot(hidden[...], wk_ref[...], preferred_element_type=jnp.float32)
    v = jnp.dot(hidden[...], wv_ref[...], preferred_element_type=jnp.float32)
    for h in range(q.shape[1] // HEAD):
        at = slice(h * HEAD, (h + 1) * HEAD)
        q_ref[:, at] = (turned(q[:, at], cosine, sine) * HEAD ** (-0.5)).astype(jnp.bfloat16)
        kv_ref[:, 2 * h * HEAD : (2 * h + 1) * HEAD] = turned(k[:, at], cosine, sine).astype(jnp.bfloat16)
        kv_ref[:, (2 * h + 1) * HEAD : (2 * h + 2) * HEAD] = v[:, at].astype(jnp.bfloat16)


def project(tokens, gain, cosine, sine, wq, wk, wv):
    rows, width = tokens.shape
    tile = 2 * HEAD
    column = pl.BlockSpec((width, tile), lambda i: (0, i))
    return pl.pallas_call(
        project_kernel,
        out_shape=(
            jax.ShapeDtypeStruct((rows, width), jnp.bfloat16),
            jax.ShapeDtypeStruct((rows, width), jnp.bfloat16),
            jax.ShapeDtypeStruct((rows, 2 * width), jnp.bfloat16),
        ),
        grid=(width // tile,),
        in_specs=[whole_spec(rows, width), whole_spec(1, width), whole_spec(rows, HEAD), whole_spec(rows, HEAD),
                  column, column, column],
        out_specs=(whole_spec(rows, width), pl.BlockSpec((rows, tile), lambda i: (0, i)),
                   pl.BlockSpec((rows, 2 * tile), lambda i: (0, i))),
        scratch_shapes=[pltpu.VMEM((rows, width), jnp.bfloat16)],
        cost_estimate=pl.CostEstimate(flops=6 * rows * width * width, bytes_accessed=6 * width * width, transcendentals=0),
        name="project",
    )(tokens, gain[None, :], cosine, sine, wq, wk, wv)


def attend_kernel(info, q_ref, start_ref, kv_ref, mixed_ref, low_ref, total_ref, bias, top, norm):
    step = pl.program_id(0)
    me, first_block = info[0], info[1]
    rows = q_ref.shape[0]
    block = me - step

    @pl.when(step == 0)
    def _():
        top[...] = jnp.full_like(top, masked_value)
        norm[...] = jnp.zeros_like(norm)
        mixed_ref[...] = jnp.zeros_like(mixed_ref)

    @pl.when(block >= first_block)
    def _():
        bias[...] = visible_bias((rows, rows), block * rows, start_ref[...], me * rows)

        @pl.loop(0, HEADS, unroll=2)
        def _(h):
            keys, values = kv_ref[0, :, lanes(2 * h * HEAD)], kv_ref[0, :, lanes((2 * h + 1) * HEAD)]
            scores = inner_right(keys, q_ref[:, lanes(h * HEAD)]) + bias[...]
            old = top[h]
            new = jnp.maximum(old, jnp.max(scores, axis=0, keepdims=True))
            weights = jnp.exp(scores - new)
            shrink = jnp.exp(old - new)
            top[h] = new
            norm[h] = norm[h] * shrink + jnp.sum(weights, axis=0, keepdims=True)
            mixed_ref[h] = mixed_ref[h] * shrink + inner_left(values, weights.astype(jnp.bfloat16))

    @pl.when(step == pl.num_programs(0) - 1)
    def _():
        for h in range(HEADS):
            mixed = mixed_ref[h] / norm[h]
            mixed_ref[h] = mixed
            low_ref[:, h * HEAD : (h + 1) * HEAD] = mixed.T.astype(jnp.bfloat16)
            total_ref[h] = top[h] + jnp.log(norm[h])


def attend(info, queries, start, pairs):
    rows, width = queries.shape
    steps = pairs.shape[0] // 2 + 1
    return pl.pallas_call(
        attend_kernel,
        out_shape=(
            jax.ShapeDtypeStruct((HEADS, HEAD, rows), jnp.float32),
            jax.ShapeDtypeStruct((rows, width), jnp.bfloat16),
            jax.ShapeDtypeStruct((HEADS, 1, rows), jnp.float32),
        ),
        grid_spec=pltpu.PrefetchScalarGridSpec(
            num_scalar_prefetch=1,
            grid=(steps,),
            in_specs=[
                whole_spec(rows, width),
                whole_spec(1, rows),
                pl.BlockSpec((1, rows, 2 * width), lambda s, info: (jnp.maximum(info[0] - s, info[1]), 0, 0)),
            ],
            out_specs=(whole_spec(HEADS, HEAD, rows), whole_spec(rows, width), whole_spec(HEADS, 1, rows)),
            scratch_shapes=[
                pltpu.VMEM((rows, rows), jnp.float32),
                pltpu.VMEM((HEADS, 1, rows), jnp.float32),
                pltpu.VMEM((HEADS, 1, rows), jnp.float32),
            ],
        ),
        cost_estimate=pl.CostEstimate(
            flops=4 * rows * rows * width * steps, bytes_accessed=4 * rows * width * steps, transcendentals=0
        ),
        name="attend",
    )(info, queries, start, pairs)


def attend_back_kernel(
    info, q_ref, g_ref, mixed_ref, start_ref, total_ref, cos_ref, sin_ref, kv_ref, dkv_ref, dq_ref, bias, acc, term
):
    step = pl.program_id(0)
    me, first_block = info[0], info[1]
    rows = q_ref.shape[0]
    block = me - step

    @pl.when(step == 0)
    def _():
        acc[...] = jnp.zeros_like(acc)
        for h in range(HEADS):
            grads = g_ref[:, h * HEAD : (h + 1) * HEAD].astype(jnp.float32).T
            term[h] = jnp.sum(grads * mixed_ref[h], axis=0, keepdims=True)

    @pl.when(block >= first_block)
    def _():
        bias[...] = visible_bias((rows, rows), block * rows, start_ref[...], me * rows)

        @pl.loop(0, HEADS, unroll=2)
        def _(h):
            early, late, at = lanes(2 * h * HEAD), lanes((2 * h + 1) * HEAD), lanes(h * HEAD)
            keys, values = kv_ref[0, :, early], kv_ref[0, :, late]
            queries, grads = q_ref[:, at], g_ref[:, at]
            probs = jnp.exp(inner_right(keys, queries) + bias[...] - total_ref[h])
            prob_grad = inner_right(values, grads)
            score_grad = (probs * (prob_grad - term[h])).astype(jnp.bfloat16)
            dkv_ref[0, :, late] = jnp.dot(
                probs.astype(jnp.bfloat16), grads, preferred_element_type=jnp.float32
            ).astype(jnp.bfloat16)
            dkv_ref[0, :, early] = jnp.dot(
                score_grad, queries, preferred_element_type=jnp.float32
            ).astype(jnp.bfloat16)
            acc[h] += inner_left(keys, score_grad)

    @pl.when(jnp.logical_and(block >= 0, block < first_block))
    def _():
        dkv_ref[...] = jnp.zeros_like(dkv_ref)

    @pl.when(step == pl.num_programs(0) - 1)
    def _():
        for h in range(HEADS):
            back = turned(acc[h].T * HEAD ** (-0.5), cos_ref[...], -sin_ref[...])
            dq_ref[:, h * HEAD : (h + 1) * HEAD] = back.astype(jnp.bfloat16)


def attend_back(info, queries, grads, mixed, start, total, cosine, sine, pairs):
    rows, width = queries.shape
    count = pairs.shape[0]
    steps = count // 2 + 1
    return pl.pallas_call(
        attend_back_kernel,
        out_shape=(
            jax.ShapeDtypeStruct(pairs.shape, jnp.bfloat16),
            jax.ShapeDtypeStruct((rows, width), jnp.bfloat16),
        ),
        grid_spec=pltpu.PrefetchScalarGridSpec(
            num_scalar_prefetch=1,
            grid=(steps,),
            in_specs=[
                whole_spec(rows, width),
                whole_spec(rows, width),
                whole_spec(HEADS, HEAD, rows),
                whole_spec(1, rows),
                whole_spec(HEADS, 1, rows),
                whole_spec(rows, HEAD),
                whole_spec(rows, HEAD),
                pl.BlockSpec((1, rows, 2 * width), lambda s, info: (jnp.maximum(info[0] - s, info[1]), 0, 0)),
            ],
            out_specs=(
                pl.BlockSpec((1, rows, 2 * width), lambda s, info: (jnp.maximum(info[0] - s, 0), 0, 0)),
                whole_spec(rows, width),
            ),
            scratch_shapes=[
                pltpu.VMEM((rows, rows), jnp.float32),
                pltpu.VMEM((HEADS, HEAD, rows), jnp.float32),
                pltpu.VMEM((HEADS, 1, rows), jnp.float32),
            ],
        ),
        cost_estimate=pl.CostEstimate(
            flops=10 * rows * rows * width * steps, bytes_accessed=8 * rows * width * steps, transcendentals=0
        ),
        name="attend_back",
    )(info, queries, grads, mixed, start, total, cosine, sine, pairs)


def finish_kernel(
    x_ref, gain_ref, res_ref, hid_ref, q_ref, kv_ref, cos_ref, sin_ref, wq_ref, wk_ref, wv_ref,
    dq_ref, dk_ref, dv_ref, out_ref, gain_out, acc,
):
    step = pl.program_id(0)

    @pl.when(step == 0)
    def _():
        acc[...] = jnp.zeros_like(acc)

    cosine, sine = cos_ref[...], sin_ref[...]
    count = q_ref.shape[1] // HEAD
    keys = jnp.concatenate(
        [turned(kv_ref[:, 2 * h * HEAD : (2 * h + 1) * HEAD].astype(jnp.float32), cosine, -sine).astype(jnp.bfloat16)
         for h in range(count)], axis=1)
    values = jnp.concatenate([kv_ref[:, (2 * h + 1) * HEAD : (2 * h + 2) * HEAD] for h in range(count)], axis=1)
    grads = (q_ref[...], keys, values)
    acc[...] += (
        inner_right(grads[0], wq_ref[...]) + inner_right(grads[1], wk_ref[...]) + inner_right(grads[2], wv_ref[...])
    )
    hidden = hid_ref[...]
    for ref, grad in zip((dq_ref, dk_ref, dv_ref), grads):
        ref[...] = inner_left(hidden, grad).astype(jnp.bfloat16)

    @pl.when(step == pl.num_programs(0) - 1)
    def _():
        values, gain, grad = x_ref[...].astype(jnp.float32), gain_ref[...], acc[...]
        scale = lax.rsqrt(jnp.mean(values * values, axis=1, keepdims=True) + epsilon)
        inner = jnp.mean(gain * grad * values, axis=1, keepdims=True)
        part = scale * gain * grad - values * (scale * scale * scale) * inner
        out_ref[...] = (res_ref[...] + part).astype(jnp.bfloat16)
        gain_out[...] = jnp.sum(grad * values * scale, axis=0, keepdims=True)


def finish(tokens, gain, residual_grad, hidden, query_grad, pair_grads, cosine, sine, wq, wk, wv):
    rows, width = tokens.shape
    tile = 2 * HEAD
    column = pl.BlockSpec((width, tile), lambda i: (0, i))
    return pl.pallas_call(
        finish_kernel,
        out_shape=(
            jax.ShapeDtypeStruct((width, width), jnp.bfloat16),
            jax.ShapeDtypeStruct((width, width), jnp.bfloat16),
            jax.ShapeDtypeStruct((width, width), jnp.bfloat16),
            jax.ShapeDtypeStruct((rows, width), jnp.bfloat16),
            jax.ShapeDtypeStruct((1, width), jnp.float32),
        ),
        grid=(width // tile,),
        in_specs=[whole_spec(rows, width), whole_spec(1, width), whole_spec(rows, width), whole_spec(rows, width),
                  pl.BlockSpec((rows, tile), lambda i: (0, i)), pl.BlockSpec((rows, 2 * tile), lambda i: (0, i)),
                  whole_spec(rows, HEAD), whole_spec(rows, HEAD), column, column, column],
        out_specs=(column, column, column, whole_spec(rows, width), whole_spec(1, width)),
        scratch_shapes=[pltpu.VMEM((rows, width), jnp.float32)],
        cost_estimate=pl.CostEstimate(flops=12 * rows * width * width, bytes_accessed=12 * width * width, transcendentals=0),
        name="finish",
    )(tokens, gain[None, :], residual_grad, hidden, query_grad, pair_grads, cosine, sine, wq, wk, wv)


def experts_kernel(
    where_ref, x_ref, g_ref, rank_row, rank_col, share_row, wg_ref, wu_ref, wd_ref,
    back_ref, in_ref, pre_ref, lift_ref, mid_ref, og_ref, grads,
):
    blocks, rows, side = x_ref.shape
    capacity = in_ref.shape[0] // blocks
    width = og_ref.shape[1]
    dot = lambda left, right: jnp.dot(left, right, preferred_element_type=jnp.float32)
    shares = []
    for i in range(blocks):
        at = slice(i * capacity, (i + 1) * capacity)
        hit = rank_row[i] == lax.broadcasted_iota(jnp.int32, (capacity, rows), 0)
        pick = jnp.where(hit, 1.0, 0.0)
        shares.append(jnp.sum(pick * share_row[i], axis=1, keepdims=True))
        pick = pick.astype(jnp.bfloat16)
        in_ref[at, :] = dot(pick, x_ref[i, :, :width]).astype(jnp.bfloat16)
        grads[at, :] = dot(pick, g_ref[i]).astype(jnp.bfloat16)
    share = jnp.concatenate(shares, axis=0)
    pre = dot(in_ref[...], wg_ref[0])
    lift = dot(in_ref[...], wu_ref[0])
    silu, slope = silu_parts(pre)
    mid_ref[...] = (silu * lift).astype(jnp.bfloat16)
    lift_slope = lift * slope
    result = dot(mid_ref[...], wd_ref[0]).astype(jnp.bfloat16).astype(jnp.float32)
    grad = grads[...].astype(jnp.float32)
    gate_grad = jnp.sum(result * grad, axis=1, keepdims=True)
    og_ref[...] = (share * grad).astype(jnp.bfloat16)
    given = (share * result).astype(jnp.bfloat16)
    mid_grad = inner_right(og_ref[...], wd_ref[0])
    pre_ref[...] = (mid_grad * lift_slope).astype(jnp.bfloat16)
    lift_ref[...] = (mid_grad * silu).astype(jnp.bfloat16)
    in_grad = (inner_right(pre_ref[...], wg_ref[0]) + inner_right(lift_ref[...], wu_ref[0])).astype(jnp.bfloat16)
    lane = lax.broadcasted_iota(jnp.int32, (blocks * capacity, side - width), 1)
    high = gate_grad.astype(jnp.bfloat16).astype(jnp.float32)
    extra = jnp.where(lane == where_ref[0], high, jnp.where(lane == where_ref[1], gate_grad - high, 0.0))
    extra = extra.astype(jnp.bfloat16)
    for i in range(blocks):
        at = slice(i * capacity, (i + 1) * capacity)
        hit = rank_col[i] == lax.broadcasted_iota(jnp.int32, (rows, capacity), 1)
        put = jnp.where(hit, 1.0, 0.0).astype(jnp.bfloat16)
        back_ref[i, :, :width] = dot(put, in_grad[at, :]).astype(jnp.bfloat16)
        back_ref[i, :, width:side] = dot(put, extra[at, :]).astype(jnp.bfloat16)
        back_ref[i, :, side:] = dot(put, given[at, :]).astype(jnp.bfloat16)


def run_experts(places, arrived, grads, rank, share, gate, up, down, capacity):
    count, rows, side = arrived.shape
    width, ff = gate.shape[1], gate.shape[2]
    blocks = 384 // capacity
    flat = count * capacity
    once = lambda *shape: pl.BlockSpec(shape, lambda i, p: (0,) * len(shape), pipeline_mode=pl.Buffered(1))
    lead = lambda *shape: pl.BlockSpec((blocks,) + shape, lambda i, p: (i, 0, 0))
    tall = lambda wide: pl.BlockSpec((blocks * capacity, wide), lambda i, p: (i, 0))
    shape = lambda *dims: jax.ShapeDtypeStruct(dims, jnp.bfloat16)
    return pl.pallas_call(
        experts_kernel,
        out_shape=(shape(count, rows, side + width), shape(flat, width), shape(flat, ff),
                   shape(flat, ff), shape(flat, ff), shape(flat, width)),
        grid_spec=pltpu.PrefetchScalarGridSpec(
            num_scalar_prefetch=1,
            grid=(count // blocks,),
            in_specs=[lead(rows, side), lead(rows, width), lead(1, rows), lead(rows, 1), lead(1, rows),
                      once(1, width, ff), once(1, width, ff), once(1, ff, width)],
            out_specs=(lead(rows, side + width), tall(width), tall(ff), tall(ff), tall(ff), tall(width)),
            scratch_shapes=[pltpu.VMEM((blocks * capacity, width), jnp.bfloat16)],
        ),
        compiler_params=pltpu.CompilerParams(vmem_limit_bytes=VMEM_MOST),
        cost_estimate=pl.CostEstimate(flops=16 * flat * width * ff, bytes_accessed=16 * flat * width, transcendentals=0),
        name="run_experts",
    )(places, arrived, grads, rank[:, None, :], rank[:, :, None], share[:, None, :], gate, up, down)


def gather_attend_steps(plan, pieces, attention, x_ref, out_ref, ra, sa_up, sa_dn, rb, sb, rc, sc, own):
    a, b, c = plan.place()
    steps, wide = plan.steps, plan.wide
    at = {d: i for i, d in enumerate(steps)}
    rows = x_ref.shape[0] // pieces

    def part(q):
        return pl.ds(pl.multiple_of(q * rows, rows), rows)

    def copy(q, src, slot, ssem, rsem, dev):
        return pltpu.make_async_remote_copy(
            src_ref=src, dst_ref=out_ref.at[slot, part(q)], send_sem=ssem, recv_sem=rsem,
            device_id={"ep": dev}, device_id_type=MESH,
        )

    def hops(d, q):
        i = at[d]
        slot = plan.slot(a - d, b, c)
        src = x_ref.at[part(q)] if d == 0 else out_ref.at[slot, part(q)]
        real = plan.inside(a - d)
        out = []
        if d >= 0 and d + 1 in at:
            out.append((both(real, a + 1 < plan.long), lambda: copy(
                q, src, slot, sa_up.at[i, q], ra.at[at[d + 1], q], plan.slot(a + 1, b, c))))
        if d <= 0 and d - 1 in at:
            out.append((both(real, a > 0), lambda: copy(
                q, src, slot, sa_dn.at[i, q], ra.at[at[d - 1], q], plan.slot(a - 1, b, c))))
        for k in range(1, wide):
            to = (b + k) % wide
            out.append((both(real, plan.need_pair(d, to, b)), lambda k=k, to=to: copy(
                q, src, slot, sb.at[i, k, q], rb.at[i, k, q], plan.slot(a, to, c))))
        out.append((both(real, plan.need(d, b, 1 - c, b, c)), lambda: copy(
            q, src, slot, sc.at[i, 0, q], rc.at[i, 0, q], plan.slot(a, b, 1 - c))))
        return out

    def cross(d, k, q):
        i = at[d]
        b0 = (b + wide - k) % wide
        slot = plan.slot(a - d, b0, c)
        real = plan.inside(a - d)
        come = lambda: copy(q, x_ref.at[part(q)], slot, sb.at[i, k, q], rb.at[i, k, q], plan.slot(a, b, c))
        go = lambda: copy(q, out_ref.at[slot, part(q)], slot, sc.at[i, k, q], rc.at[i, k, q],
                          plan.slot(a, b, 1 - c))
        return (both(real, plan.need_pair(d, b, b0)), come,
                both(real, plan.need(d, b, 1 - c, b0, c)), go)

    plan.greet(a, b, c)
    keep = pltpu.make_async_copy(x_ref, out_ref.at[plan.slot(a, b, c)], own)

    @pl.loop(0, pieces)
    def _(q):
        for cond, go in hops(0, q):
            @when(cond)
            def _(go=go):
                go().start()

    keep.start()
    yield
    far = max(abs(d) for d in steps)

    def arrive(d, k):
        b0 = (b + wide - k) % wide
        slot = plan.slot(a - d, b0, 1 - c)

        @pl.loop(0, pieces)
        def _(q):
            copy(q, x_ref.at[part(q)], slot, sc.at[at[d], k, q], rc.at[at[d], k, q], plan.slot(a, b, c)).wait_recv()

    work = attention(a, b, c, arrive)
    work.own()
    for step in range(1, far + 2):
        @pl.loop(0, pieces)
        def _(q, step=step):
            for d in (step, -step):
                if d in at:
                    @when(plan.inside(a - d))
                    def _(d=d):
                        slot = plan.slot(a - d, b, c)
                        copy(q, x_ref.at[part(q)], slot, sa_up.at[0, q], ra.at[at[d], q],
                             plan.slot(a, b, c)).wait_recv()
                        for cond, go in hops(d, q):
                            @when(cond)
                            def _(go=go):
                                go().start()
            for d in (step - 1,):
                if d in at:
                    for k in range(1, wide):
                        came, come, goes, go = cross(d, k, q)
                        @when(came)
                        def _(come=come):
                            come().wait_recv()
                        @when(goes)
                        def _(go=go):
                            go().start()
            work.beside(step, q)

    work.rest()
    keep.wait()

    @pl.loop(0, pieces)
    def _(q):
        for d in steps:
            i = at[d]
            real = plan.inside(a - d)
            for cond, go in hops(d, q):
                @when(cond)
                def _(go=go):
                    go().wait_send()
            for k in range(1, wide):
                came, come, goes, go = cross(d, k, q)
                @when(goes)
                def _(go=go):
                    go().wait_send()


class Attention:
    def __init__(self, plan, a, b, c, arrive, x_ref, pair_ref, q_ref, start_ref, mixed_ref, low_ref, total_ref,
                 bias, top, norm, kv, kv_sem):
        self.plan, self.a, self.b, self.c, self.arrive = plan, a, b, c, arrive
        self.x_ref, self.pair_ref, self.q_ref, self.start_ref = x_ref, pair_ref, q_ref, start_ref
        self.mixed_ref, self.low_ref, self.total_ref = mixed_ref, low_ref, total_ref
        self.bias, self.top, self.norm, self.kv, self.kv_sem = bias, top, norm, kv, kv_sem
        self.turns = [(0, 0, True), (1, 0, False), (1, 0, True), (0, 1, False), (0, 1, True), (2, 0, False), (2, 0, True),
                      (1, 1, False), (1, 1, True), (2, 1, False), (2, 1, True)]

    def block(self, n):
        d, k, other = self.turns[n]
        b0, c0 = (self.b + self.plan.wide - k) % self.plan.wide, 1 - self.c if other else self.c
        there = both(self.plan.inside(self.a - d), self.plan.need(d, self.b, self.c, b0, c0))
        return there, self.plan.slot(self.a - d, b0, c0)

    def copy(self, n):
        return pltpu.make_async_copy(self.pair_ref.at[self.block(n)[1]], self.kv.at[n % 2], self.kv_sem.at[n % 2])

    def fetch(self, n):
        if n < len(self.turns):
            d, k, other = self.turns[n]

            def go():
                if other:
                    self.arrive(d, k)
                self.copy(n).start()

            run_if(self.block(n)[0], go)

    def use(self, n):
        def go():
            self.copy(n).wait()
            self.step(self.kv.at[n % 2], self.block(n)[1])

        run_if(self.block(n)[0], go)

    def step(self, pair, slot):
        rows = self.q_ref.shape[0]
        me = self.plan.slot(self.a, self.b, self.c)
        self.bias[...] = visible_bias((rows, rows), slot * rows, self.start_ref[...], me * rows)

        @pl.loop(0, HEADS)
        def _(h):
            keys, values = pair[:, lanes(2 * h * HEAD)], pair[:, lanes((2 * h + 1) * HEAD)]
            scores = inner_right(keys, self.q_ref[:, lanes(h * HEAD)]) + self.bias[...]
            old = self.top[h]
            new = jnp.maximum(old, jnp.max(scores, axis=0, keepdims=True))
            weights = jnp.exp(scores - new)
            shrink = jnp.exp(old - new)
            self.top[h] = new
            self.norm[h] = self.norm[h] * shrink + jnp.sum(weights, axis=0, keepdims=True)
            self.mixed_ref[h] = self.mixed_ref[h] * shrink + inner_left(values, weights.astype(jnp.bfloat16))

    def own(self):
        self.top[...] = jnp.full_like(self.top, masked_value)
        self.norm[...] = jnp.zeros_like(self.norm)
        self.mixed_ref[...] = jnp.zeros_like(self.mixed_ref)
        self.step(self.x_ref, self.plan.slot(self.a, self.b, self.c))
        self.fetch(0)
        self.use(0)

    def beside(self, step, q):
        if step == 1:
            return
        if step == 2:
            run_if(q == 0, lambda: self.fetch(1))
        first = 4 * step - 7
        for i in range(4):
            def go(n=first + i):
                self.fetch(n + 1)
                self.use(n)

            run_if(q == 2 * i + 1, go)

    def rest(self):
        self.fetch(10)
        self.use(9)
        self.use(10)
        for h in range(HEADS):
            mixed = self.mixed_ref[h] / self.norm[h]
            self.mixed_ref[h] = mixed
            self.low_ref[:, h * HEAD : (h + 1) * HEAD] = mixed.T.astype(jnp.bfloat16)
            self.total_ref[h] = self.top[h] + jnp.log(self.norm[h])


def gather_attend(block, grads, queries, start, collective_id):
    ep_count, pieces = lax.axis_size("ep"), 8
    plan, other = Plan(ep_count, True), Plan(ep_count, False)
    n, wide, more = len(plan.steps), plan.wide, len(other.steps)
    rows, width = queries.shape
    sem = pltpu.SemaphoreType.DMA
    sems_of = lambda n, pieces: [sem((n, pieces))] * 3 + [sem((n, wide, pieces))] * 4 + [sem]

    def kernel(x_ref, g_ref, q_ref, start_ref, out_ref, all_ref, mixed_ref, low_ref, total_ref, bias, top, norm, kv,
               kv_sem, *sems):
        def attention(a, b, c, arrive):
            return Attention(plan, a, b, c, arrive, x_ref, out_ref, q_ref, start_ref, mixed_ref, low_ref, total_ref,
                             bias, top, norm, kv, kv_sem)

        keys = gather_attend_steps(plan, pieces, attention, x_ref, out_ref, *sems[:8])
        rest = gather_steps(other, 4, lambda n: None, False, g_ref, all_ref, *sems[8:])
        next(keys)
        next(rest)
        for part in (keys, rest):
            for _ in part:
                pass

    near = pl.BlockSpec(memory_space=pltpu.VMEM)
    return pl.pallas_call(
        kernel,
        out_shape=(
            jax.ShapeDtypeStruct((ep_count,) + block.shape, block.dtype),
            jax.ShapeDtypeStruct((ep_count,) + grads.shape, grads.dtype),
            jax.ShapeDtypeStruct((HEADS, HEAD, rows), jnp.float32),
            jax.ShapeDtypeStruct((rows, width), jnp.bfloat16),
            jax.ShapeDtypeStruct((HEADS, 1, rows), jnp.float32),
        ),
        in_specs=[near] * 4,
        out_specs=(pl.BlockSpec(memory_space=pl.ANY), pl.BlockSpec(memory_space=pl.ANY), near, near, near),
        scratch_shapes=[
            pltpu.VMEM((rows, rows), jnp.float32),
            pltpu.VMEM((HEADS, 1, rows), jnp.float32),
            pltpu.VMEM((HEADS, 1, rows), jnp.float32),
            pltpu.VMEM((2,) + block.shape, block.dtype),
            sem((2,)),
        ] + sems_of(n, pieces) + sems_of(more, 4),
        compiler_params=pltpu.CompilerParams(
            collective_id=collective_id, has_side_effects=True, vmem_limit_bytes=VMEM_MOST),
        name="gather_attend",
    )(block, grads, queries, start)


def attend_back_sum(queries, grads, mixed, start, total, cosine, sine, pairs, parts, collective_id):
    rows, width = queries.shape
    ep_count = pairs.shape[0]
    part_rows, part_width = parts[0].shape[1], sum(part.shape[2] for part in parts)
    plan, pieces = Plan(ep_count, True), 4
    place = Place(lax.axis_size("grp"), ep_count)
    n, wide = plan.planes(), plan.wide
    cuts = [0, part_width // HEAD * 3 // 4 * HEAD, part_width]
    orders = ("xba", "bxa")

    def kernel(q_ref, g_ref, mixed_ref, start_ref, total_ref, cos_ref, sin_ref, pair_ref, *refs):
        sources, refs = refs[: len(parts)], refs[len(parts) :]
        out_ref, pair_out, dq_ref, bias, acc, term, kv, staged, kv_sem = refs[:9]
        refs = refs[9:]
        place.locate()
        sums = []
        for i in range(2):
            sums.append(WholeSum(place, orders[i], pieces_of(sources, cuts[i], cuts[i + 1]), refs[:14]))
            refs = refs[14:]
        sum_rows = RowSum(plan, pieces, staged, refs)
        a, b, c = sum_rows.a, sum_rows.b, sum_rows.c
        me = plan.slot(a, b, c)
        order, ks = sum_rows.order, from_far(wide)
        turns = [(k, d) for d in order for k in ks]

        def block(turn, other):
            k, d = turns[turn]
            b0, c0 = sum_rows.source(k), jnp.where(other, 1 - c, c)
            there = both(plan.inside(a - d), plan.need(d, b, c, b0, c0))
            return there, plan.slot(a - d, b0, c0)

        def fetch(turn, other):
            there, slot = block(turn, other)
            held = jnp.where(other, 0, 1)
            return there, lambda: pltpu.make_async_copy(pair_ref.at[slot], kv.at[held], kv_sem.at[held])

        def begin(turn, other):
            there, go = fetch(turn, other)
            run_if(there, lambda: go().start())

        def compute(turn, other, target):
            there, slot = block(turn, other)
            held = 0 if other else 1

            def work():
                fetch(turn, other)[1]().wait()
                bias[...] = visible_bias((rows, rows), slot * rows, start_ref[...], me * rows)

                @pl.loop(0, HEADS)
                def _(h):
                    early, late, at = lanes(2 * h * HEAD), lanes((2 * h + 1) * HEAD), lanes(h * HEAD)
                    keys, values = kv[held, :, early], kv[held, :, late]
                    own, grad = q_ref[:, at], g_ref[:, at]
                    probs = jnp.exp(inner_right(keys, own) + bias[...] - total_ref[h])
                    score_grad = (probs * (inner_right(values, grad) - term[h])).astype(jnp.bfloat16)
                    target[:, late] = jnp.dot(
                        probs.astype(jnp.bfloat16), grad, preferred_element_type=jnp.float32
                    ).astype(jnp.bfloat16)
                    target[:, early] = jnp.dot(
                        score_grad, own, preferred_element_type=jnp.float32
                    ).astype(jnp.bfloat16)
                    acc[h] += inner_left(keys, score_grad)

            run_if(there, work)

        def turn_of(turn):
            k, d = turns[turn]
            i = plan.plane(a, d)
            compute(turn, True, staged.at[i, k])
            if turn + 1 < len(turns):
                begin(turn + 1, True)
            cond = sum_rows.cross(d, k, 0)[0]
            for q in range(pieces):
                run_if(cond, lambda q=q: sum_rows.cross(d, k, q)[1]().start())
            compute(turn, False, sum_rows.held.at[i, k])
            if turn + 1 < len(turns):
                begin(turn + 1, False)

        def pass_on(turn):
            k, d = turns[turn]

            @pl.loop(0, pieces)
            def _(q):
                sum_rows.first(d, k, q)
                cond, go = sum_rows.over(d, k, q)
                run_if(cond, lambda: go().start())

        begin(0, True)
        begin(0, False)
        place.greet()
        first, second = sums
        for one in sums:
            for i in range(one.n1 - 1):
                one.start(i)
        acc[...] = jnp.zeros_like(acc)
        for h in range(HEADS):
            grad = g_ref[:, h * HEAD : (h + 1) * HEAD].astype(jnp.float32).T
            term[h] = jnp.sum(grad * mixed_ref[h], axis=0, keepdims=True)
        for one in sums:
            for i in range(one.n1 - 1):
                one.stage_core(i)
        last = len(turns) - 1
        for turn in range(len(turns)):
            turn_of(turn)
            if turns[turn][0]:
                pass_on(turn)
            if turn == 0:
                for one in sums:
                    one.start(one.n1 - 1)
            if turn == last - 3:
                for one in sums:
                    one.stage_core(one.n1 - 1)
                for k2 in from_far(second.n2)[:-1]:
                    second.stage_one(k2)
            if turn == last - 2:
                sum_rows.stage_dest(order[0], 0, 2)
            if turn == last - 1:
                for k2 in from_far(first.n2)[:-1]:
                    first.stage_one(k2)
                second.stage_one(0)
                sum_rows.stage_dest(order[0], 2, 3)
        sum_rows.stage_dest(order[0], 3, pieces)
        first.stage_one(0)
        for h in range(HEADS):
            back = turned(acc[h].T * HEAD ** (-0.5), cos_ref[...], -sin_ref[...])
            dq_ref[:, h * HEAD : (h + 1) * HEAD] = back.astype(jnp.bfloat16)
        second.stage_two()
        for d in order[1:]:
            sum_rows.stage_dest(d, 0, pieces)
        pair_out[...] = sum_rows.result()
        first.stage_two()
        for i, one in enumerate(sums):
            one.stage_three(out_ref.at[:, pl.ds(cuts[i], cuts[i + 1] - cuts[i])])
        sum_rows.drain()
        for one in sums:
            one.drain()

    anywhere, near = pl.BlockSpec(memory_space=pl.ANY), pl.BlockSpec(memory_space=pltpu.VMEM)
    scratch = [
        pltpu.VMEM((rows, rows), jnp.float32),
        pltpu.VMEM((HEADS, HEAD, rows), jnp.float32),
        pltpu.VMEM((HEADS, 1, rows), jnp.float32),
        pltpu.VMEM((2, rows, 2 * width), jnp.bfloat16),
        pltpu.VMEM((n, wide, rows, 2 * width), jnp.bfloat16),
        pltpu.SemaphoreType.DMA((2,)),
    ]
    for i in range(2):
        scratch += WholeSum.scratch(place.sizes, orders[i], part_rows, cuts[i + 1] - cuts[i], parts[0].dtype, len(parts))
    scratch += RowSum.scratch(plan, rows, 2 * width, pairs.dtype, pieces)
    return pl.pallas_call(
        kernel,
        out_shape=(jax.ShapeDtypeStruct((part_rows, part_width), jnp.float32),
                   jax.ShapeDtypeStruct((rows, 2 * width), pairs.dtype),
                   jax.ShapeDtypeStruct((rows, width), jnp.bfloat16)),
        in_specs=[near] * 7 + [anywhere] * (1 + len(parts)),
        out_specs=(near, near, near),
        scratch_shapes=scratch,
        compiler_params=pltpu.CompilerParams(
            collective_id=collective_id, has_side_effects=True, vmem_limit_bytes=VMEM_MOST),
        name="attend_back_sum",
    )(queries, grads, mixed, start, total, cosine, sine, pairs, *parts)


def local(
    tokens,
    doc_lengths,
    expert_ids,
    out_grad,
    mixer_gain,
    query_weight,
    key_weight,
    value_weight,
    output_weight,
    ffn_gain,
    router_weight,
    shared_gate,
    shared_up,
    shared_down,
    expert_gate,
    expert_up,
    expert_down,
):
    rows, width = tokens.shape[1], tokens.shape[2]
    ep_count = lax.axis_size("ep")
    device_count = ep_count * lax.axis_size("grp")
    ep_index = lax.axis_index("ep")
    expert_count = router_weight.shape[1]
    capacity = min(rows, 12 * rows * TOP // (7 * expert_count))
    low = lambda v: v.astype(jnp.bfloat16)
    wide = lambda v: v.astype(jnp.float32)
    dot = lambda left, right: jnp.dot(left, right, preferred_element_type=jnp.float32)

    grad_low = out_grad[0]

    doc_ends = jnp.cumsum(doc_lengths[0])
    query_pos = ep_index * rows + jnp.arange(rows, dtype=jnp.int32)
    before = query_pos[:, None] >= doc_ends[None, :]
    start = jnp.max(jnp.where(before, doc_ends[None, :], 0), axis=1)
    info = jnp.stack([ep_index, start[0] // rows]).astype(jnp.int32)
    half_dim = HEAD // 2
    frequency = rope_base ** (-jnp.arange(half_dim, dtype=jnp.float32) / half_dim)
    angles = wide(query_pos)[:, None] * frequency[None, :]
    cosine, sine = jnp.cos(angles), jnp.sin(angles)
    cosine = jnp.concatenate([cosine, cosine], axis=1)
    sine = jnp.concatenate([-sine, sine], axis=1)

    stream = wide(tokens[0])
    hidden_low, queries, own_pairs = project(
        tokens[0], mixer_gain, cosine, sine, query_weight, key_weight, value_weight
    )
    if ep_count > 16:
        pairs = gather_rows(own_pairs, True, 1, 8)
        mixed, mixed_low, log_total = attend(info, queries, start[None, :], pairs)
        grad_later, pairs = lax.optimization_barrier((grad_low, pairs))
        grads_all = lax.all_gather(grad_later, "ep", axis=0, tiled=False)
    else:
        pairs, grads_all, mixed, mixed_low, log_total = gather_attend(own_pairs, grad_low, queries, start[None, :], 1)
    mixer_out = dot(mixed_low, output_weight)
    residual = stream + mixer_out
    ffn_low = low(normed(residual, ffn_gain))

    logits = dot(ffn_low, router_weight)
    experts = jnp.arange(expert_count, dtype=jnp.int32)
    assigned = jnp.any(expert_ids[0][:, :, None] == experts[None, None, :], axis=1)
    shown = jnp.where(assigned, logits, masked_value)
    powers = jnp.where(assigned, jnp.exp(shown - jnp.max(shown, axis=1, keepdims=True)), 0.0)
    gate_probs = powers / jnp.sum(powers, axis=1, keepdims=True)
    probs_high = low(gate_probs)
    probs_rest = low(gate_probs - wide(probs_high))
    side = width + 2 * HEAD if 2 * expert_count > HEAD else width + HEAD
    pad = jnp.zeros((rows, side - width - 2 * expert_count), jnp.bfloat16)
    sent = jnp.concatenate([ffn_low, probs_high, probs_rest, pad], axis=1)
    arrived, shared_out, ffn_grad, shared_gate_part, shared_up_part, shared_down_part = gather_shared(
        sent, grad_low, shared_gate, shared_up, shared_down, 2
    )

    own = experts[None, None, :] == ep_index
    high = arrived[:, :, width : width + expert_count]
    rest = arrived[:, :, width + expert_count : width + 2 * expert_count]
    share = jnp.sum(jnp.where(own, wide(high) + wide(rest), 0.0), axis=2)
    chosen = share > 0.0
    earlier = (jnp.arange(rows)[:, None] < jnp.arange(rows)[None, :]).astype(jnp.bfloat16)
    rank = dot(low(chosen), earlier).astype(jnp.int32)
    rank = jnp.where(chosen, rank, -1)
    places = jnp.stack([ep_index, expert_count + ep_index]).astype(jnp.int32)
    back, flat_in, pre_grad, lift_grad, middle, result_grad = run_experts(
        places, arrived, grads_all, rank, share, expert_gate, expert_up, expert_down, capacity
    )
    group_count = lax.axis_size("grp")
    if group_count == 2:
        back_sum, gate_sum, up_sum, down_sum = scatter_experts(
            back, (flat_in, result_grad), (pre_grad, lift_grad, middle), 3
        )
        gate_sum, up_sum, down_sum = gate_sum[None], up_sum[None], down_sum.T[None]
        routed = back_sum[:, side:]
    else:
        back_sum = scatter_rows(back[:, :, :side], False, 3)
        routed = lax.psum_scatter(back[:, :, side:], "ep", scatter_dimension=0)
        split = width // group_count
        own_down_grad = jnp.concatenate(
            [low(inner_left(middle, result_grad[:, i * split : (i + 1) * split])) for i in range(group_count)], axis=0
        )
        over_groups = lambda v: wide(lax.psum_scatter(v, "grp", scatter_dimension=0, tiled=True))[None]
        gate_sum = over_groups(low(inner_left(flat_in, pre_grad)))
        up_sum = over_groups(low(inner_left(flat_in, lift_grad)))
        down_sum = over_groups(own_down_grad)

    grad_out = wide(grad_low)
    gate_back = wide(back_sum[:, width : width + expert_count]) + wide(
        back_sum[:, width + expert_count : width + 2 * expert_count]
    )
    chosen_grad = gate_probs * (gate_back - jnp.sum(gate_probs * gate_back, axis=1, keepdims=True))
    logit_grad = low(chosen_grad)
    ffn_grad = ffn_grad + wide(back_sum[:, :width]) + inner_right(logit_grad, router_weight)
    _, ffn_pull = jax.vjp(normed, residual, ffn_gain)
    residual_part, ffn_gain_grad = ffn_pull(ffn_grad)
    residual_grad = grad_out + residual_part
    mixer_grad_low = low(residual_grad)
    mixed_grad = low(inner_right(mixer_grad_low, output_weight))
    by_device = lambda v: low(v).reshape(device_count, width // device_count, -1)
    early = [
        by_device(part)
        for part in (shared_gate_part, shared_up_part, shared_down_part, inner_left(mixed_low, mixer_grad_low))
    ]
    if ep_count > 16:
        pair_parts, query_lin_grad = attend_back(
            info, queries, mixed_grad, mixed, start[None, :], log_total, cosine, sine, pairs
        )
        pair_grads = scatter_rows(pair_parts, True, 4)
        early_sum = scatter_whole(early, 5)
    else:
        early_sum, pair_grads, query_lin_grad = attend_back_sum(
            queries, mixed_grad, mixed, start[None, :], log_total, cosine, sine, pairs, early, 5
        )

    routed, pair_grads = lax.optimization_barrier((routed, pair_grads))
    layer_out = residual + shared_out + wide(routed)
    query_part, key_part, value_part, tokens_grad, mixer_gain_grad = finish(
        tokens[0], mixer_gain, residual_grad, hidden_low, query_lin_grad, pair_grads, cosine, sine,
        query_weight, key_weight, value_weight,
    )
    squares = jnp.stack(
        [jnp.sum(residual * residual), jnp.sum(mixer_out * mixer_out), jnp.sum(layer_out * layer_out)]
    )
    extras = jnp.concatenate(
        [inner_left(ffn_low, logit_grad), mixer_gain_grad.T, ffn_gain_grad[:, None],
         jnp.broadcast_to(squares[None, :], (width, 3))], axis=1
    )
    extras = jnp.pad(extras, ((0, 0), (0, HEAD - extras.shape[1])))
    late_sum = scatter_whole([by_device(v) for v in (query_part, key_part, value_part, extras)], 6)
    extra_sum = late_sum[:, 3 * width :]
    entry_count = rows * device_count * width
    stream_rms = jnp.sqrt(extra_sum[0, expert_count + 2 : expert_count + 5] / entry_count)
    ff = shared_gate.shape[1]
    return (
        low(layer_out)[None],
        tokens_grad[None],
        extra_sum[:, expert_count],
        late_sum[:, :width],
        late_sum[:, width : 2 * width],
        late_sum[:, 2 * width : 3 * width],
        early_sum[:, 3 * ff :],
        extra_sum[:, expert_count + 1],
        extra_sum[:, :expert_count],
        early_sum[:, :ff],
        early_sum[:, ff : 2 * ff],
        early_sum[:, 2 * ff : 3 * ff].T,
        gate_sum,
        up_sum,
        down_sum,
        stream_rms,
    )


def solution(mesh):
    return jax.shard_map(
        local,
        mesh=mesh,
        in_specs=(
            P("grp", "ep", None),
            P("grp", None),
            P("grp", "ep", None),
            P("grp", "ep", None),
            P(),
            P(),
            P(),
            P(),
            P(),
            P(),
            P(),
            P(),
            P(),
            P(),
            P("ep", None, None),
            P("ep", None, None),
            P("ep", None, None),
        ),
        out_specs=(
            P("grp", "ep", None),
            P("grp", "ep", None),
            P(("grp", "ep")),
            P(("grp", "ep"), None),
            P(("grp", "ep"), None),
            P(("grp", "ep"), None),
            P(("grp", "ep"), None),
            P(("grp", "ep")),
            P(("grp", "ep"), None),
            P(("grp", "ep"), None),
            P(("grp", "ep"), None),
            P(None, ("grp", "ep")),
            P("ep", "grp", None),
            P("ep", "grp", None),
            P("ep", None, "grp"),
            P(),
        ),
        check_vma=False,
    )
```

```python
import functools

import jax
import jax.numpy as jnp
from jax import lax
from jax.experimental import pallas as pl
from jax.experimental.pallas import tpu as pltpu
from jax.sharding import PartitionSpec as P

HEADS = 10
HEAD = 128
TOP = 7

epsilon = 1e-06
rope_base = 10000.0
masked_value = -1e30


def normed(values, gain_vec):
    return (
        values * lax.rsqrt(jnp.mean(values * values, axis=-1, keepdims=True) + epsilon) * gain_vec
    )


def inner_left(left_op, right_op):
    return lax.dot_general(
        left_op, right_op, (((0,), (0,)), ((), ())), preferred_element_type=jnp.float32
    )


def inner_right(left_op, right_op):
    return lax.dot_general(
        left_op, right_op, (((1,), (1,)), ((), ())), preferred_element_type=jnp.float32
    )


def silu_parts(pre_act):
    sigmoid_val = jax.nn.sigmoid(pre_act)
    return (pre_act * sigmoid_val, sigmoid_val * (1.0 + pre_act * (1.0 - sigmoid_val)))


MESH = pl.DeviceIdType.MESH
COUPLES = 2
VMEM_MOST = 64 * 1024 * 1024 - 65536


def when(cond):
    if cond is True:
        return lambda f: f()
    if cond is False:
        return lambda f: None
    return pl.when(cond)


def both(*conds):
    out = True
    for cond in conds:
        if cond is False:
            return False
        if cond is True:
            continue
        out = cond if out is True else jnp.logical_and(out, cond)
    return out


class Plan:
    def __init__(self, ep_count, window):
        self.long = 4
        self.wide = ep_count // 8
        self.window = window
        self.steps = (
            list(range(self.long // 2 + 1))
            if window
            else list(range(-(self.long - 1), self.long))
        )

    def place(self):
        me = lax.axis_index("ep")
        return me // (2 * self.wide), (me // 2) % self.wide, me % 2

    def slot(self, a, b, c):
        return (a * self.wide + b) * 2 + c

    def plane(self, a, d):
        return d if self.window else jnp.clip(a - d, 0, self.long - 1)

    def planes(self):
        return len(self.steps) if self.window else self.long

    def inside(self, a):
        return jnp.logical_and(a >= 0, a < self.long)

    def need(self, d, b, c, b0, c0):
        if not self.window or 0 < d < self.long // 2:
            return True
        if d == 0:
            return jnp.logical_or(b0 < b, jnp.logical_and(b0 == b, c0 <= c))
        return jnp.logical_or(b0 > b, jnp.logical_and(b0 == b, c0 >= c))

    def need_pair(self, d, b, b0):
        if not self.window or 0 < d < self.long // 2:
            return True
        return b0 < b if d == 0 else b0 > b

    def greet(self, a, b, c):
        barrier = pltpu.get_barrier_semaphore()

        def signal(cond, dev):
            @when(cond)
            def _():
                pl.semaphore_signal(barrier, inc=1, device_id={"ep": dev}, device_id_type=MESH)

        signal(a + 1 < self.long, self.slot(a + 1, b, c))
        signal(a > 0, self.slot(a - 1, b, c))
        for k in range(1, self.wide):
            signal(True, self.slot(a, (b + k) % self.wide, c))
        signal(True, self.slot(a, b, 1 - c))
        ends = (a == 0).astype(jnp.int32) + (a == self.long - 1).astype(jnp.int32)
        pl.semaphore_wait(barrier, self.wide + 2 - ends)


def gather_kernel(plan, pieces, beside, x_ref, out_ref, ra, sa_up, sa_dn, rb, sb, rc, sc, own):
    a, b, c = plan.place()
    steps, wide = plan.steps, plan.wide
    at = {d: i for i, d in enumerate(steps)}
    rows = x_ref.shape[0] // pieces

    def part(q):
        return pl.ds(pl.multiple_of(q * rows, rows), rows)

    def copy(q, src, slot, ssem, rsem, dev):
        return pltpu.make_async_remote_copy(
            src_ref=src, dst_ref=out_ref.at[slot, part(q)], send_sem=ssem, recv_sem=rsem,
            device_id={"ep": dev}, device_id_type=MESH,
        )

    def hops(d, q):
        i = at[d]
        slot = plan.slot(a - d, b, c)
        src = x_ref.at[part(q)] if d == 0 else out_ref.at[slot, part(q)]
        real = plan.inside(a - d)
        out = []
        if d >= 0 and d + 1 in at:
            out.append((both(real, a + 1 < plan.long), lambda: copy(
                q, src, slot, sa_up.at[i, q], ra.at[at[d + 1], q], plan.slot(a + 1, b, c))))
        if d <= 0 and d - 1 in at:
            out.append((both(real, a > 0), lambda: copy(
                q, src, slot, sa_dn.at[i, q], ra.at[at[d - 1], q], plan.slot(a - 1, b, c))))
        for k in range(1, wide):
            to = (b + k) % wide
            out.append((both(real, plan.need_pair(d, to, b)), lambda k=k, to=to: copy(
                q, src, slot, sb.at[i, k, q], rb.at[i, k, q], plan.slot(a, to, c))))
        out.append((both(real, plan.need(d, b, 1 - c, b, c)), lambda: copy(
            q, src, slot, sc.at[i, 0, q], rc.at[i, 0, q], plan.slot(a, b, 1 - c))))
        return out

    def cross(d, k, q):
        i = at[d]
        b0 = (b + wide - k) % wide
        slot = plan.slot(a - d, b0, c)
        real = plan.inside(a - d)
        come = lambda: copy(q, x_ref.at[part(q)], slot, sb.at[i, k, q], rb.at[i, k, q], plan.slot(a, b, c))
        go = lambda: copy(q, out_ref.at[slot, part(q)], slot, sc.at[i, k, q], rc.at[i, k, q],
                          plan.slot(a, b, 1 - c))
        return (both(real, plan.need_pair(d, b, b0)), come,
                both(real, plan.need(d, b, 1 - c, b0, c)), go)

    plan.greet(a, b, c)
    keep = pltpu.make_async_copy(x_ref, out_ref.at[plan.slot(a, b, c)], own)

    @pl.loop(0, pieces)
    def _(q):
        for cond, go in hops(0, q):
            @when(cond)
            def _(go=go):
                go().start()

    keep.start()
    far = max(abs(d) for d in steps)
    for step in range(1, far + 3):
        beside(step - 1)

        @pl.loop(0, pieces)
        def _(q, step=step):
            for d in (step, -step):
                if d in at:
                    @when(plan.inside(a - d))
                    def _(d=d):
                        slot = plan.slot(a - d, b, c)
                        copy(q, x_ref.at[part(q)], slot, sa_up.at[0, q], ra.at[at[d], q],
                             plan.slot(a, b, c)).wait_recv()
                        for cond, go in hops(d, q):
                            @when(cond)
                            def _(go=go):
                                go().start()
            for d in sorted({step - 2, 2 - step}) if step > 1 else ():
                if d in at:
                    for k in range(1, wide):
                        came, come, goes, go = cross(d, k, q)
                        @when(came)
                        def _(come=come):
                            come().wait_recv()
                        @when(goes)
                        def _(go=go):
                            go().start()
    keep.wait()

    @pl.loop(0, pieces)
    def _(q):
        for d in steps:
            i = at[d]
            real = plan.inside(a - d)
            for k in range(wide):
                b0 = (b + wide - k) % wide
                slot = plan.slot(a - d, b0, 1 - c)
                @when(both(real, plan.need(d, b, c, b0, 1 - c)))
                def _(slot=slot, i=i, k=k):
                    copy(q, x_ref.at[part(q)], slot, sc.at[i, k, q], rc.at[i, k, q],
                         plan.slot(a, b, c)).wait_recv()
            for cond, go in hops(d, q):
                @when(cond)
                def _(go=go):
                    go().wait_send()
            for k in range(1, wide):
                came, come, goes, go = cross(d, k, q)
                @when(goes)
                def _(go=go):
                    go().wait_send()


def gather_rows(block, window, collective_id, pieces=4):
    ep_count = lax.axis_size("ep")
    plan = Plan(ep_count, window)
    n, wide = len(plan.steps), plan.wide
    sem = pltpu.SemaphoreType.DMA
    return pl.pallas_call(
        functools.partial(gather_kernel, plan, pieces, lambda n: None),
        out_shape=jax.ShapeDtypeStruct((ep_count,) + block.shape, block.dtype),
        in_specs=[pl.BlockSpec(memory_space=pltpu.VMEM)],
        out_specs=pl.BlockSpec(memory_space=pl.ANY),
        scratch_shapes=[sem((n, pieces)), sem((n, pieces)), sem((n, pieces)), sem((n, wide, pieces)),
                        sem((n, wide, pieces)), sem((n, wide, pieces)), sem((n, wide, pieces)), sem],
        compiler_params=pltpu.CompilerParams(collective_id=collective_id, has_side_effects=True),
        name="gather_rows",
    )(block)


def gather_shared(block, grads, gate, up, down, collective_id, pieces=4):
    ep_count = lax.axis_size("ep")
    plan = Plan(ep_count, False)
    n, wide = len(plan.steps), plan.wide
    rows, width = grads.shape
    ff = gate.shape[1]
    sem = pltpu.SemaphoreType.DMA
    stages = max(plan.steps) + 2
    tiles = ff // HEAD

    def kernel(x_ref, g_ref, wg_ref, wu_ref, wd_ref, out_ref, shared_ref, back_ref, dg_ref, du_ref, dd_ref, *sems):
        dot = lambda left, right: jnp.dot(left, right, preferred_element_type=jnp.float32)

        def tile(i):
            at = pl.ds(pl.multiple_of(i * HEAD, HEAD), HEAD)
            x, g = x_ref[:, :width], g_ref[...]
            w_gate, w_up, w_down = wg_ref[:, at], wu_ref[:, at], wd_ref[at, :]
            silu, slope = silu_parts(dot(x, w_gate))
            lift = dot(x, w_up)
            mid = (silu * lift).astype(jnp.bfloat16)
            mid_grad = inner_right(g, w_down)
            pre_grad = (mid_grad * lift * slope).astype(jnp.bfloat16)
            lift_grad = (mid_grad * silu).astype(jnp.bfloat16)
            out = dot(mid, w_down)
            back = inner_right(pre_grad, w_gate) + inner_right(lift_grad, w_up)

            @pl.when(i == 0)
            def _():
                shared_ref[...] = out
                back_ref[...] = back

            @pl.when(i > 0)
            def _():
                shared_ref[...] += out
                back_ref[...] += back

            dg_ref[:, at] = inner_left(x, pre_grad).astype(jnp.bfloat16)
            du_ref[:, at] = inner_left(x, lift_grad).astype(jnp.bfloat16)
            dd_ref[:, at] = inner_left(g, mid).astype(jnp.bfloat16)

        def beside(stage):
            pl.loop(tiles * stage // stages, tiles * (stage + 1) // stages)(tile)

        gather_kernel(plan, pieces, beside, x_ref, out_ref, *sems)

    near = pl.BlockSpec(memory_space=pltpu.VMEM)
    return pl.pallas_call(
        kernel,
        out_shape=(
            jax.ShapeDtypeStruct((ep_count,) + block.shape, block.dtype),
            jax.ShapeDtypeStruct((rows, width), jnp.float32),
            jax.ShapeDtypeStruct((rows, width), jnp.float32),
        ) + (jax.ShapeDtypeStruct((width, ff), jnp.bfloat16),) * 3,
        in_specs=[near] * 5,
        out_specs=(pl.BlockSpec(memory_space=pl.ANY),) + (near,) * 5,
        scratch_shapes=[sem((n, pieces)), sem((n, pieces)), sem((n, pieces)), sem((n, wide, pieces)),
                        sem((n, wide, pieces)), sem((n, wide, pieces)), sem((n, wide, pieces)), sem],
        compiler_params=pltpu.CompilerParams(
            collective_id=collective_id, has_side_effects=True, vmem_limit_bytes=VMEM_MOST),
        name="gather_shared",
    )(block, grads, gate, up, down)


def add_rows(dst, others, out=None):
    rows, width = dst.shape
    out = dst if out is None else out
    small = rows <= 64
    piece = 32 if rows % 32 == 0 else rows
    lanes = width if rows % 32 == 0 else 4 * HEAD
    whole = width // lanes * lanes

    def add(at):
        if len(others) == 1 and out.dtype == jnp.bfloat16:
            out[at] = dst[at] + others[0][at]
        else:
            total = dst[at].astype(jnp.float32)
            for other in others:
                total = total + other[at].astype(jnp.float32)
            out[at] = total.astype(out.dtype)

    if piece == rows:
        @pl.loop(0, whole // lanes)
        def _(i):
            add((slice(None), pl.ds(pl.multiple_of(i * lanes, lanes), lanes)))

        if whole < width:
            add((slice(None), pl.ds(whole, width - whole)))
    else:
        @pl.loop(0, rows // piece)
        def _(i):
            add((pl.ds(pl.multiple_of(i * piece, piece), piece), slice(None)))


def send(src, dst, ssem, rsem, to):
    return pltpu.make_async_remote_copy(
        src_ref=src, dst_ref=dst, send_sem=ssem, recv_sem=rsem, device_id=to, device_id_type=MESH
    )


def run_if(cond, go):
    @when(cond)
    def _():
        go()


class RowSum:
    @staticmethod
    def scratch(plan, rows, width, dtype, pieces):
        n, wide = plan.planes(), plan.wide
        blocks = lambda *lead: pltpu.VMEM(lead + (rows, width), dtype)
        sem = lambda *lead: pltpu.SemaphoreType.DMA(lead + (pieces,))
        return [blocks(n, wide), blocks(n, wide), blocks(n, wide - 1), blocks(n), blocks(1 if plan.window else n),
                sem(n, wide), sem(n, wide), sem(n, wide), sem(n, wide), sem(n), sem(n), sem(n), sem(n, wide)]

    def __init__(self, plan, pieces, p_ref, scratch):
        self.plan, self.pieces, self.p_ref = plan, pieces, p_ref
        (self.held, self.rcb, self.rbb, self.r_hi, self.r_lo,
         self.sc, self.rc, self.sb, self.rb, self.sa, self.rhi, self.rlo, self.ld) = scratch
        self.a, self.b, self.c = plan.place()
        self.ready = len(p_ref.shape) == 4
        self.rows = p_ref.shape[-2] // pieces
        self.order = sorted(plan.steps, key=lambda d: -abs(d))

    def part(self, q):
        return pl.ds(pl.multiple_of(q * self.rows, self.rows), self.rows)

    def dev(self, a, b, c):
        return {"ep": self.plan.slot(a, b, c)}

    def source(self, k):
        return (self.b + self.plan.wide - k) % self.plan.wide

    def load(self, d, k, q):
        p, i, b0 = self.plan, self.plan.plane(self.a, d), self.source(k)
        return both(p.inside(self.a - d), p.need(d, self.b, self.c, b0, self.c)), lambda: pltpu.make_async_copy(
            self.p_ref.at[p.slot(self.a - d, b0, self.c), self.part(q)], self.held.at[i, k, self.part(q)],
            self.ld.at[i, k, q])

    def cross(self, d, k, q):
        p, i, b0, c = self.plan, self.plan.plane(self.a, d), self.source(k), self.c
        real = p.inside(self.a - d)
        at = (i, k) if self.ready else (p.slot(self.a - d, b0, 1 - c),)
        return (both(real, p.need(d, self.b, c, b0, 1 - c)), lambda: send(
            self.p_ref.at[at + (self.part(q),)], self.rcb.at[i, k, self.part(q)],
            self.sc.at[i, k, q], self.rc.at[i, k, q], self.dev(self.a, self.b, 1 - c)),
            both(real, p.need(d, self.b, 1 - c, b0, c)))

    def over(self, d, k, q):
        p, i, b0 = self.plan, self.plan.plane(self.a, d), self.source(k)
        return both(p.inside(self.a - d), p.need_pair(d, self.b, b0)), lambda: send(
            self.held.at[i, k, self.part(q)], self.rbb.at[i, k - 1, self.part(q)], self.sb.at[i, k, q],
            self.rb.at[i, k, q], self.dev(self.a, b0, self.c))

    def along(self, d, q):
        p, i, up = self.plan, self.plan.plane(self.a, d), d < 0
        j = d - 1 if p.window else i
        return p.inside(self.a - d), lambda: send(
            self.held.at[i, 0, self.part(q)], (self.r_lo if up else self.r_hi).at[j, self.part(q)],
            self.sa.at[i, q], (self.rlo if up else self.rhi).at[j, q],
            self.dev(self.a + (1 if up else -1), self.b, self.c))

    def start(self, ks):
        for k in ks:
            @pl.loop(0, self.pieces)
            def _(q, k=k):
                for d in self.order:
                    for cond, go in (self.cross(d, k, q)[:2], self.load(d, k, q)):
                        run_if(cond, lambda go=go: go().start())

    def first(self, d, k, q):
        i = self.plan.plane(self.a, d)
        if not self.ready:
            cond, go = self.load(d, k, q)
            run_if(cond, lambda: go().wait())
        _, come_go, come = self.cross(d, k, q)

        def take():
            come_go().wait_recv()
            add_rows(self.held.at[i, k, self.part(q)], [self.rcb.at[i, k, self.part(q)]])

        run_if(come, take)

    def stage_over(self, k):
        @pl.loop(0, self.pieces)
        def _(q):
            for d in self.order:
                self.first(d, k, q)
                cond, go = self.over(d, k, q)
                run_if(cond, lambda go=go: go().start())

    def stage_dests(self, low, high):
        @pl.loop(low, high)
        def _(q):
            for d in self.order:
                self.dest(d, q)

    def stage_dest(self, d, low, high):
        @pl.loop(low, high)
        def _(q):
            self.dest(d, q)

    def dest(self, d, q):
        p, a, b, steps = self.plan, self.a, self.b, self.plan.steps
        i = p.plane(a, d)
        real = p.inside(a - d)
        mine = self.held.at[i, 0, self.part(q)]
        self.first(d, 0, q)
        for k in range(1, p.wide):
            def take(k=k):
                self.over(d, k, q)[1]().wait_recv()
                add_rows(mine, [self.rbb.at[i, k - 1, self.part(q)]])

            run_if(both(real, p.need_pair(d, (b + k) % p.wide, b)), take)
        for inner, cond, buf, sem in ((d >= 0 and d + 1 in steps, a + 1 < p.long, self.r_hi, self.rhi),
                                      (d <= 0 and d - 1 in steps, a > 0, self.r_lo, self.rlo)):
            if inner:
                def take(buf=buf, sem=sem):
                    send(mine, buf.at[i, self.part(q)], self.sa.at[i, q], sem.at[i, q],
                         self.dev(a, b, self.c)).wait_recv()
                    add_rows(mine, [buf.at[i, self.part(q)]])

                run_if(both(real, cond), take)
        if d:
            cond, go = self.along(d, q)
            run_if(cond, lambda: go().start())

    def result(self):
        return self.held[self.plan.plane(self.a, 0), 0]

    def drain(self):
        @pl.loop(0, self.pieces)
        def _(q):
            for d in self.plan.steps:
                sends = [self.cross(d, k, q)[:2] for k in range(self.plan.wide)]
                sends += [self.over(d, k, q) for k in range(1, self.plan.wide)]
                if d:
                    sends.append(self.along(d, q))
                for cond, go in sends:
                    run_if(cond, lambda go=go: go().wait_send())


def scatter_rows(parts, window, collective_id, pieces=4):
    ep_count, rows, width = parts.shape
    plan = Plan(ep_count, window)

    def kernel(p_ref, out_ref, *scratch):
        total = RowSum(plan, pieces, p_ref, scratch)
        plan.greet(total.a, total.b, total.c)
        ks = list(range(1, plan.wide)) + [0]
        total.start(ks)
        for k in ks[:-1]:
            total.stage_over(k)
        total.stage_dests(0, pieces)
        out_ref[...] = total.result()
        total.drain()

    return pl.pallas_call(
        kernel,
        out_shape=jax.ShapeDtypeStruct((rows, width), parts.dtype),
        in_specs=[pl.BlockSpec(memory_space=pl.ANY)],
        out_specs=pl.BlockSpec(memory_space=pltpu.VMEM),
        scratch_shapes=RowSum.scratch(plan, rows, width, parts.dtype, pieces),
        compiler_params=pltpu.CompilerParams(
            collective_id=collective_id, has_side_effects=True, vmem_limit_bytes=VMEM_MOST),
        name="scatter_rows",
    )(parts)


class Place:
    def __init__(self, groups, ep_count):
        self.sizes = {"x": groups, "a": 4, "b": ep_count // 8}

    def locate(self):
        me, wide = lax.axis_index("ep"), self.sizes["b"]
        self.at = {"x": lax.axis_index("grp"), "a": me // (2 * wide), "b": (me // 2) % wide, "c": me % 2}

    def dev(self, **moved):
        at = {**self.at, **moved}
        return {"grp": at["x"], "ep": (at["a"] * self.sizes["b"] + at["b"]) * 2 + at["c"]}

    def slot(self, **moved):
        at = {**self.at, **moved}
        return ((at["x"] * self.sizes["a"] + at["a"]) * self.sizes["b"] + at["b"]) * 2 + at["c"]

    def back(self, axis, k):
        return (self.at[axis] + self.sizes[axis] - k) % self.sizes[axis]

    def greet(self):
        peers = [self.dev(c=1 - self.at["c"])] + [
            self.dev(**{axis: self.back(axis, k)}) for axis in "xba" for k in range(1, self.sizes[axis])]
        barrier = pltpu.get_barrier_semaphore()
        for to in peers:
            pl.semaphore_signal(barrier, inc=1, device_id=to, device_id_type=MESH)
        pl.semaphore_wait(barrier, len(peers))


def from_far(size):
    return list(range(1, size)) + [0]


class WholeSum:
    @staticmethod
    def scratch(sizes, axes, rows, width, dtype, sources):
        n1, n2, n3 = (sizes[axis] for axis in axes)
        blocks = lambda *lead: pltpu.VMEM(lead + (rows, width), dtype)
        sem = lambda *lead: pltpu.SemaphoreType.DMA(lead)
        full = (n1, n2, n3)
        one, two, three = (n1 - 1, n2, n3), (n2 - 1, n3), (n3 - 1,)
        return [blocks(*full), blocks(*full), blocks(*one), blocks(*two), blocks(*three),
                sem(*full, sources), sem(*full, sources), sem(*full, sources), sem(*one), sem(*one), sem(*two), sem(*two), sem(*three), sem(*three)]

    def __init__(self, place, axes, pieces, scratch):
        self.place, self.axes, self.pieces = place, axes, pieces
        (self.held, self.rcb, self.r1, self.r2, self.r3,
         self.ld, self.sc, self.rc, self.s1, self.q1, self.s2, self.q2, self.s3, self.q3) = scratch
        self.n1, self.n2, self.n3 = (place.sizes[axis] for axis in axes)
        self.groups = [[(k1, k2, k3) for k2 in from_far(self.n2) for k3 in from_far(self.n3)]
                       for k1 in from_far(self.n1)]

    def slot(self, key, c):
        return self.place.slot(c=c, **{axis: self.place.back(axis, k) for axis, k in zip(self.axes, key)})

    def loads(self, key):
        c = self.place.at["c"]
        for n, (ref, first, at, count) in enumerate(self.pieces):
            frm, to = pl.ds(first, count), pl.ds(at, count)
            yield pltpu.make_async_copy(
                ref.at[self.slot(key, c), :, frm], self.held.at[key + (slice(None), to)],
                self.ld.at[key + (n,)])

    def crossings(self, key):
        c = self.place.at["c"]
        for n, (ref, first, at, count) in enumerate(self.pieces):
            frm, to = pl.ds(first, count), pl.ds(at, count)
            yield send(ref.at[self.slot(key, 1 - c), :, frm], self.rcb.at[key + (slice(None), to)],
                       self.sc.at[key + (n,)], self.rc.at[key + (n,)], self.place.dev(c=1 - c))

    def hop(self, level, key):
        buf, ssem, rsem = ((self.r1, self.s1, self.q1), (self.r2, self.s2, self.q2), (self.r3, self.s3, self.q3))[level]
        axis, k = self.axes[level], key[level]
        far = (k - 1,) + key[level + 1 :]
        return send(self.held.at[key], buf.at[far], ssem.at[far], rsem.at[far],
                    self.place.dev(**{axis: self.place.back(axis, k)}))

    def start(self, i):
        for key in self.groups[i]:
            for go in self.crossings(key):
                go.start()
            for go in self.loads(key):
                go.start()

    def stage_core(self, i):
        for key in self.groups[i]:
            for go in self.loads(key):
                go.wait()
            for go in self.crossings(key):
                go.wait_recv()
            add_rows(self.held.at[key], [self.rcb.at[key]])
            if key[0]:
                self.hop(0, key).start()

    def stage_one(self, k2):
        for k3 in from_far(self.n3):
            for k1 in range(1, self.n1):
                self.hop(0, (k1, k2, k3)).wait_recv()
            add_rows(self.held.at[0, k2, k3], [self.r1.at[k1 - 1, k2, k3] for k1 in range(1, self.n1)])
            if k2:
                self.hop(1, (0, k2, k3)).start()

    def stage_two(self):
        for k3 in from_far(self.n3):
            for k2 in range(1, self.n2):
                self.hop(1, (0, k2, k3)).wait_recv()
            add_rows(self.held.at[0, 0, k3], [self.r2.at[k2 - 1, k3] for k2 in range(1, self.n2)])
            if k3:
                self.hop(2, (0, 0, k3)).start()

    def stage_three(self, out):
        for k3 in range(1, self.n3):
            self.hop(2, (0, 0, k3)).wait_recv()
        add_rows(self.held.at[0, 0, 0], [self.r3.at[k3 - 1] for k3 in range(1, self.n3)], out)

    def drain(self):
        for group in self.groups:
            for key in group:
                for go in self.crossings(key):
                    go.wait_send()
                if key[0]:
                    self.hop(0, key).wait_send()
                elif key[1]:
                    self.hop(1, key).wait_send()
                elif key[2]:
                    self.hop(2, key).wait_send()


def pieces_of(sources, low, high):
    pieces, first = [], 0
    for ref in sources:
        begin, end = max(low, first), min(high, first + ref.shape[2])
        if begin < end:
            pieces.append((ref, begin - first, begin - low, end - begin))
        first += ref.shape[2]
    return pieces


def scatter_whole(parts, collective_id):
    rows = parts[0].shape[1]
    width = sum(part.shape[2] for part in parts)
    groups, ep_count = lax.axis_size("grp"), lax.axis_size("ep")
    place = Place(groups, ep_count)
    tiles = width // HEAD
    count = 2 * COUPLES
    cuts = [tiles * n // count * HEAD for n in range(count + 1)]
    orders = ["xba", "bxa"] * COUPLES

    def kernel(*refs):
        sources, refs = refs[: len(parts)], refs[len(parts) :]
        out_ref, refs = refs[0], refs[1:]
        place.locate()
        sums = []
        for n, axes in enumerate(orders):
            pieces = pieces_of(sources, cuts[n], cuts[n + 1])
            sums.append(WholeSum(place, axes, pieces, refs[:14]))
            refs = refs[14:]
        outs = [out_ref.at[:, pl.ds(cuts[n], cuts[n + 1] - cuts[n])] for n in range(len(orders))]
        place.greet()
        couples = [sums[n : n + 2] for n in range(0, len(sums), 2)]
        for couple in couples:
            for i in range(max(s.n1 for s in couple)):
                for s in couple:
                    if i < s.n1:
                        s.start(i)

        def core(couple):
            for i in range(max(s.n1 for s in couple)):
                for s in couple:
                    if i < s.n1:
                        s.stage_core(i)

        def one(couple):
            for i in range(max(s.n2 for s in couple)):
                for s in couple:
                    if i < s.n2:
                        s.stage_one(from_far(s.n2)[i])

        def two(couple):
            for s in couple:
                s.stage_two()

        core(couples[0])
        for n, couple in enumerate(couples):
            one(couple)
            if n + 1 < len(couples):
                core(couples[n + 1])
            two(couple)
        for s, out in zip(sums, outs):
            s.stage_three(out)
        for s in sums:
            s.drain()

    operands, anywhere = list(parts), pl.BlockSpec(memory_space=pl.ANY)
    out_shape = [jax.ShapeDtypeStruct((rows, width), jnp.float32)]
    scratch = []
    for n, axes in enumerate(orders):
        scratch += WholeSum.scratch(place.sizes, axes, rows, cuts[n + 1] - cuts[n], parts[0].dtype, len(parts))
    got = pl.pallas_call(
        kernel,
        out_shape=tuple(out_shape),
        in_specs=[anywhere] * len(operands),
        out_specs=tuple(pl.BlockSpec(memory_space=pltpu.VMEM) for _ in out_shape),
        scratch_shapes=scratch,
        compiler_params=pltpu.CompilerParams(
            collective_id=collective_id, has_side_effects=True, vmem_limit_bytes=VMEM_MOST),
        name="scatter_whole",
    )(*operands)
    return got[0]


def scatter_experts(parts, lefts, rights, collective_id):
    ep_count, rows, width = parts.shape
    flat, tall = lefts[0].shape
    ff = rights[0].shape[1]
    half, depth = tall // 2, flat // 3
    plan, pieces = Plan(ep_count, False), 4
    place = Place(lax.axis_size("grp"), ep_count)
    left_of = [0, 0, 1]
    hooks = (4, 5, 6, 7, 10, 11, 12, 13, 16, 17)
    kinds, units = len(rights), 2 * len(rights)
    steps = units * 3

    def kernel(p_ref, in_ref, og_ref, pre_ref, lift_ref, mid_ref, out_ref, w0, w1, w2, acc, left, right, gone, came,
               ls, rs, gs, cs, *scratch):
        left_refs, right_refs, outs = (in_ref, og_ref), (pre_ref, lift_ref, mid_ref), (w0, w1, w2)
        place.locate()
        total = RowSum(plan, pieces, p_ref, scratch)
        g = place.at["x"]
        place.greet()

        def fetch(kind, step):
            chunk, slot = step % 3, step % 2
            mine = (step >= 3 * kinds).astype(jnp.int32)
            first = pl.multiple_of(jnp.where(mine == 1, g, 1 - g) * half, HEAD)
            at = pl.ds(pl.multiple_of(chunk * depth, depth), depth)
            return (pltpu.make_async_copy(left_refs[left_of[kind]].at[at, pl.ds(first, half)], left.at[slot], ls.at[slot]),
                    pltpu.make_async_copy(right_refs[kind].at[at, :], right.at[slot], rs.at[slot]))

        def per_kind(step, go):
            for kind in range(kinds):
                run_if((step // 3) % kinds == kind, lambda kind=kind: go(kind))

        def begin(step):
            def go(kind):
                for copy in fetch(kind, step):
                    copy.start()
            per_kind(step, go)

        def away(kind):
            return send(gone.at[kind], came.at[kind], gs.at[kind], cs.at[kind], place.dev(x=place.back("x", 1)))

        def meet(n):
            q, distance = n // plan.long, plan.long - 1 - n % plan.long
            for d in sorted({-distance, distance}):
                total.dest(d, q)

        ks = from_far(plan.wide)
        total.start(ks)
        begin(jnp.int32(0))
        for k in ks[:-1]:
            total.stage_over(k)

        @pl.loop(0, steps)
        def _(step):
            run_if(step + 1 < steps, lambda: begin(step + 1))

            def ready(kind):
                for copy in fetch(kind, step):
                    copy.wait()
            per_kind(step, ready)
            slot = step % 2
            product = inner_left(left[slot], right[slot])
            fresh = step % 3 == 0

            @pl.when(fresh)
            def _():
                acc[...] = product

            @pl.when(jnp.logical_not(fresh))
            def _():
                acc[...] += product

            def done(kind):
                @pl.when(step < 3 * kinds)
                def _():
                    gone[kind] = acc[...].astype(jnp.bfloat16)
                    away(kind).start()

                @pl.when(step >= 3 * kinds)
                def _():
                    outs[kind][...] = acc[...]

            run_if(step % 3 == 2, lambda: per_kind(step, done))
            for n, at in enumerate(hooks):
                run_if(step == at, lambda n=n: meet(n))

        for n in range(len(hooks), pieces * plan.long):
            meet(n)
        out_ref[...] = total.result()
        for kind in range(kinds):
            away(kind).wait_recv()
            piece = 32

            @pl.loop(0, half // piece)
            def _(i, kind=kind):
                at = pl.ds(pl.multiple_of(i * piece, piece), piece)
                outs[kind][at, :] = outs[kind][at, :] + came[kind, at, :].astype(jnp.float32)

        for kind in range(kinds):
            away(kind).wait_send()
        total.drain()

    anywhere = pl.BlockSpec(memory_space=pl.ANY)
    sem = lambda n: pltpu.SemaphoreType.DMA((n,))
    outs = [jax.ShapeDtypeStruct((rows, width), parts.dtype)] + [jax.ShapeDtypeStruct((half, ff), jnp.float32)] * kinds
    return pl.pallas_call(
        kernel,
        out_shape=tuple(outs),
        in_specs=[anywhere] * 6,
        out_specs=tuple(pl.BlockSpec(memory_space=pltpu.VMEM) for _ in outs),
        scratch_shapes=[
            pltpu.VMEM((half, ff), jnp.float32),
            pltpu.VMEM((2, depth, half), jnp.bfloat16),
            pltpu.VMEM((2, depth, ff), jnp.bfloat16),
            pltpu.VMEM((kinds, half, ff), jnp.bfloat16),
            pltpu.VMEM((kinds, half, ff), jnp.bfloat16),
            sem(2), sem(2), sem(kinds), sem(kinds),
        ] + RowSum.scratch(plan, rows, width, parts.dtype, pieces),
        compiler_params=pltpu.CompilerParams(
            collective_id=collective_id, has_side_effects=True, vmem_limit_bytes=VMEM_MOST),
        name="scatter_experts",
    )(parts, *lefts, *rights)


def visible_bias(shape, first_key, start, first_query):
    key_pos = first_key + lax.broadcasted_iota(jnp.int32, shape, 0)
    query_pos = first_query + lax.broadcasted_iota(jnp.int32, shape, 1)
    seen = jnp.logical_and(key_pos >= start, key_pos <= query_pos)
    return jnp.where(seen, 0.0, masked_value)


def lanes(first):
    return pl.ds(pl.multiple_of(first, HEAD), HEAD)


def turned(values, cosine, sine):
    return values * cosine + pltpu.roll(values, HEAD // 2, 1) * sine


def whole_spec(*shape):
    return pl.BlockSpec(shape, lambda *s: (0,) * len(shape))


def project_kernel(x_ref, gain_ref, cos_ref, sin_ref, wq_ref, wk_ref, wv_ref, hid_ref, q_ref, kv_ref, hidden):
    @pl.when(pl.program_id(0) == 0)
    def _():
        hidden[...] = normed(x_ref[...].astype(jnp.float32), gain_ref[...]).astype(jnp.bfloat16)
        hid_ref[...] = hidden[...]

    cosine, sine = cos_ref[...], sin_ref[...]
    q = jnp.dot(hidden[...], wq_ref[...], preferred_element_type=jnp.float32)
    k = jnp.dot(hidden[...], wk_ref[...], preferred_element_type=jnp.float32)
    v = jnp.dot(hidden[...], wv_ref[...], preferred_element_type=jnp.float32)
    for h in range(q.shape[1] // HEAD):
        at = slice(h * HEAD, (h + 1) * HEAD)
        q_ref[:, at] = (turned(q[:, at], cosine, sine) * HEAD ** (-0.5)).astype(jnp.bfloat16)
        kv_ref[:, 2 * h * HEAD : (2 * h + 1) * HEAD] = turned(k[:, at], cosine, sine).astype(jnp.bfloat16)
        kv_ref[:, (2 * h + 1) * HEAD : (2 * h + 2) * HEAD] = v[:, at].astype(jnp.bfloat16)


def project(tokens, gain, cosine, sine, wq, wk, wv):
    rows, width = tokens.shape
    tile = 2 * HEAD
    column = pl.BlockSpec((width, tile), lambda i: (0, i))
    return pl.pallas_call(
        project_kernel,
        out_shape=(
            jax.ShapeDtypeStruct((rows, width), jnp.bfloat16),
            jax.ShapeDtypeStruct((rows, width), jnp.bfloat16),
            jax.ShapeDtypeStruct((rows, 2 * width), jnp.bfloat16),
        ),
        grid=(width // tile,),
        in_specs=[whole_spec(rows, width), whole_spec(1, width), whole_spec(rows, HEAD), whole_spec(rows, HEAD),
                  column, column, column],
        out_specs=(whole_spec(rows, width), pl.BlockSpec((rows, tile), lambda i: (0, i)),
                   pl.BlockSpec((rows, 2 * tile), lambda i: (0, i))),
        scratch_shapes=[pltpu.VMEM((rows, width), jnp.bfloat16)],
        cost_estimate=pl.CostEstimate(flops=6 * rows * width * width, bytes_accessed=6 * width * width, transcendentals=0),
        name="project",
    )(tokens, gain[None, :], cosine, sine, wq, wk, wv)


def attend_kernel(info, q_ref, start_ref, kv_ref, mixed_ref, low_ref, total_ref, bias, top, norm):
    step = pl.program_id(0)
    me, first_block = info[0], info[1]
    rows = q_ref.shape[0]
    block = me - step

    @pl.when(step == 0)
    def _():
        top[...] = jnp.full_like(top, masked_value)
        norm[...] = jnp.zeros_like(norm)
        mixed_ref[...] = jnp.zeros_like(mixed_ref)

    @pl.when(block >= first_block)
    def _():
        bias[...] = visible_bias((rows, rows), block * rows, start_ref[...], me * rows)

        @pl.loop(0, HEADS, unroll=5)
        def _(h):
            keys, values = kv_ref[0, :, lanes(2 * h * HEAD)], kv_ref[0, :, lanes((2 * h + 1) * HEAD)]
            scores = inner_right(keys, q_ref[:, lanes(h * HEAD)]) + bias[...]
            old = top[h]
            new = jnp.maximum(old, jnp.max(scores, axis=0, keepdims=True))
            weights = jnp.exp(scores - new)
            shrink = jnp.exp(old - new)
            top[h] = new
            norm[h] = norm[h] * shrink + jnp.sum(weights, axis=0, keepdims=True)
            mixed_ref[h] = mixed_ref[h] * shrink + inner_left(values, weights.astype(jnp.bfloat16))

    @pl.when(step == pl.num_programs(0) - 1)
    def _():
        for h in range(HEADS):
            mixed = mixed_ref[h] / norm[h]
            mixed_ref[h] = mixed
            low_ref[:, h * HEAD : (h + 1) * HEAD] = mixed.T.astype(jnp.bfloat16)
            total_ref[h] = top[h] + jnp.log(norm[h])


def attend(info, queries, start, pairs):
    rows, width = queries.shape
    steps = pairs.shape[0] // 2 + 1
    return pl.pallas_call(
        attend_kernel,
        out_shape=(
            jax.ShapeDtypeStruct((HEADS, HEAD, rows), jnp.float32),
            jax.ShapeDtypeStruct((rows, width), jnp.bfloat16),
            jax.ShapeDtypeStruct((HEADS, 1, rows), jnp.float32),
        ),
        grid_spec=pltpu.PrefetchScalarGridSpec(
            num_scalar_prefetch=1,
            grid=(steps,),
            in_specs=[
                whole_spec(rows, width),
                whole_spec(1, rows),
                pl.BlockSpec((1, rows, 2 * width), lambda s, info: (jnp.maximum(info[0] - s, info[1]), 0, 0)),
            ],
            out_specs=(whole_spec(HEADS, HEAD, rows), whole_spec(rows, width), whole_spec(HEADS, 1, rows)),
            scratch_shapes=[
                pltpu.VMEM((rows, rows), jnp.float32),
                pltpu.VMEM((HEADS, 1, rows), jnp.float32),
                pltpu.VMEM((HEADS, 1, rows), jnp.float32),
            ],
        ),
        cost_estimate=pl.CostEstimate(
            flops=4 * rows * rows * width * steps, bytes_accessed=4 * rows * width * steps, transcendentals=0
        ),
        name="attend",
    )(info, queries, start, pairs)


def attend_back_kernel(
    info, q_ref, g_ref, mixed_ref, start_ref, total_ref, cos_ref, sin_ref, kv_ref, dkv_ref, dq_ref, bias, acc, term
):
    step = pl.program_id(0)
    me, first_block = info[0], info[1]
    rows = q_ref.shape[0]
    block = me - step

    @pl.when(step == 0)
    def _():
        acc[...] = jnp.zeros_like(acc)
        for h in range(HEADS):
            grads = g_ref[:, h * HEAD : (h + 1) * HEAD].astype(jnp.float32).T
            term[h] = jnp.sum(grads * mixed_ref[h], axis=0, keepdims=True)

    @pl.when(block >= first_block)
    def _():
        bias[...] = visible_bias((rows, rows), block * rows, start_ref[...], me * rows)

        @pl.loop(0, HEADS, unroll=2)
        def _(h):
            early, late, at = lanes(2 * h * HEAD), lanes((2 * h + 1) * HEAD), lanes(h * HEAD)
            keys, values = kv_ref[0, :, early], kv_ref[0, :, late]
            queries, grads = q_ref[:, at], g_ref[:, at]
            probs = jnp.exp(inner_right(keys, queries) + bias[...] - total_ref[h])
            prob_grad = inner_right(values, grads)
            score_grad = (probs * (prob_grad - term[h])).astype(jnp.bfloat16)
            dkv_ref[0, :, late] = jnp.dot(
                probs.astype(jnp.bfloat16), grads, preferred_element_type=jnp.float32
            ).astype(jnp.bfloat16)
            dkv_ref[0, :, early] = jnp.dot(
                score_grad, queries, preferred_element_type=jnp.float32
            ).astype(jnp.bfloat16)
            acc[h] += inner_left(keys, score_grad)

    @pl.when(jnp.logical_and(block >= 0, block < first_block))
    def _():
        dkv_ref[...] = jnp.zeros_like(dkv_ref)

    @pl.when(step == pl.num_programs(0) - 1)
    def _():
        for h in range(HEADS):
            back = turned(acc[h].T * HEAD ** (-0.5), cos_ref[...], -sin_ref[...])
            dq_ref[:, h * HEAD : (h + 1) * HEAD] = back.astype(jnp.bfloat16)


def attend_back(info, queries, grads, mixed, start, total, cosine, sine, pairs):
    rows, width = queries.shape
    count = pairs.shape[0]
    steps = count // 2 + 1
    return pl.pallas_call(
        attend_back_kernel,
        out_shape=(
            jax.ShapeDtypeStruct(pairs.shape, jnp.bfloat16),
            jax.ShapeDtypeStruct((rows, width), jnp.bfloat16),
        ),
        grid_spec=pltpu.PrefetchScalarGridSpec(
            num_scalar_prefetch=1,
            grid=(steps,),
            in_specs=[
                whole_spec(rows, width),
                whole_spec(rows, width),
                whole_spec(HEADS, HEAD, rows),
                whole_spec(1, rows),
                whole_spec(HEADS, 1, rows),
                whole_spec(rows, HEAD),
                whole_spec(rows, HEAD),
                pl.BlockSpec((1, rows, 2 * width), lambda s, info: (jnp.maximum(info[0] - s, info[1]), 0, 0)),
            ],
            out_specs=(
                pl.BlockSpec((1, rows, 2 * width), lambda s, info: (jnp.maximum(info[0] - s, 0), 0, 0)),
                whole_spec(rows, width),
            ),
            scratch_shapes=[
                pltpu.VMEM((rows, rows), jnp.float32),
                pltpu.VMEM((HEADS, HEAD, rows), jnp.float32),
                pltpu.VMEM((HEADS, 1, rows), jnp.float32),
            ],
        ),
        cost_estimate=pl.CostEstimate(
            flops=10 * rows * rows * width * steps, bytes_accessed=8 * rows * width * steps, transcendentals=0
        ),
        name="attend_back",
    )(info, queries, grads, mixed, start, total, cosine, sine, pairs)


def finish_kernel(
    x_ref, gain_ref, res_ref, hid_ref, q_ref, kv_ref, cos_ref, sin_ref, wq_ref, wk_ref, wv_ref, *refs
):
    carried = (len(refs) - 6) // 2
    sums, (dq_ref, dk_ref, dv_ref, out_ref, gain_out), acc = refs[:carried], refs[carried : carried + 5], refs[-1]
    step = pl.program_id(0)
    for n, (own, out) in enumerate(zip(sums, refs[carried + 5 : -1])):
        out[...] = own[...].T if n == 2 else own[...]

    @pl.when(step == 0)
    def _():
        acc[...] = jnp.zeros_like(acc)

    cosine, sine = cos_ref[...], sin_ref[...]
    count = q_ref.shape[1] // HEAD
    keys = jnp.concatenate(
        [turned(kv_ref[:, 2 * h * HEAD : (2 * h + 1) * HEAD].astype(jnp.float32), cosine, -sine).astype(jnp.bfloat16)
         for h in range(count)], axis=1)
    values = jnp.concatenate([kv_ref[:, (2 * h + 1) * HEAD : (2 * h + 2) * HEAD] for h in range(count)], axis=1)
    grads = (q_ref[...], keys, values)
    acc[...] += (
        inner_right(grads[0], wq_ref[...]) + inner_right(grads[1], wk_ref[...]) + inner_right(grads[2], wv_ref[...])
    )
    hidden = hid_ref[...]
    for ref, grad in zip((dq_ref, dk_ref, dv_ref), grads):
        ref[...] = inner_left(hidden, grad).astype(jnp.bfloat16)

    @pl.when(step == pl.num_programs(0) - 1)
    def _():
        values, gain, grad = x_ref[...].astype(jnp.float32), gain_ref[...], acc[...]
        scale = lax.rsqrt(jnp.mean(values * values, axis=1, keepdims=True) + epsilon)
        inner = jnp.mean(gain * grad * values, axis=1, keepdims=True)
        part = scale * gain * grad - values * (scale * scale * scale) * inner
        out_ref[...] = (res_ref[...] + part).astype(jnp.bfloat16)
        gain_out[...] = jnp.sum(grad * values * scale, axis=0, keepdims=True)


def finish(tokens, gain, residual_grad, hidden, query_grad, pair_grads, cosine, sine, wq, wk, wv, sums):
    rows, width = tokens.shape
    tile = 2 * HEAD
    column = pl.BlockSpec((width, tile), lambda i: (0, i))
    part = sums[0].shape[0] * tile // width if sums else 0
    return pl.pallas_call(
        finish_kernel,
        out_shape=(
            jax.ShapeDtypeStruct((width, width), jnp.bfloat16),
            jax.ShapeDtypeStruct((width, width), jnp.bfloat16),
            jax.ShapeDtypeStruct((width, width), jnp.bfloat16),
            jax.ShapeDtypeStruct((rows, width), jnp.bfloat16),
            jax.ShapeDtypeStruct((1, width), jnp.float32),
        ) + tuple(jax.ShapeDtypeStruct(v.shape[::-1] if n == 2 else v.shape, v.dtype) for n, v in enumerate(sums)),
        grid=(width // tile,),
        in_specs=[whole_spec(rows, width), whole_spec(1, width), whole_spec(rows, width), whole_spec(rows, width),
                  pl.BlockSpec((rows, tile), lambda i: (0, i)), pl.BlockSpec((rows, 2 * tile), lambda i: (0, i)),
                  whole_spec(rows, HEAD), whole_spec(rows, HEAD), column, column, column]
        + [pl.BlockSpec((part, v.shape[1]), lambda i: (i, 0)) for v in sums],
        out_specs=(column, column, column, whole_spec(rows, width), whole_spec(1, width)) + tuple(
            pl.BlockSpec((v.shape[1], part), lambda i: (0, i)) if n == 2
            else pl.BlockSpec((part, v.shape[1]), lambda i: (i, 0)) for n, v in enumerate(sums)),
        scratch_shapes=[pltpu.VMEM((rows, width), jnp.float32)],
        cost_estimate=pl.CostEstimate(flops=12 * rows * width * width, bytes_accessed=12 * width * width, transcendentals=0),
        name="finish",
    )(tokens, gain[None, :], residual_grad, hidden, query_grad, pair_grads, cosine, sine, wq, wk, wv, *sums)


def experts_kernel(
    where_ref, x_ref, g_ref, rank_row, rank_col, share_row, wg_ref, wu_ref, wd_ref,
    back_ref, routed_ref, in_ref, pre_ref, lift_ref, mid_ref, og_ref, grads,
):
    blocks, rows, side = x_ref.shape
    capacity = in_ref.shape[0] // blocks
    width = og_ref.shape[1]
    dot = lambda left, right: jnp.dot(left, right, preferred_element_type=jnp.float32)
    shares = []
    for i in range(blocks):
        at = slice(i * capacity, (i + 1) * capacity)
        hit = rank_row[i] == lax.broadcasted_iota(jnp.int32, (capacity, rows), 0)
        pick = jnp.where(hit, 1.0, 0.0)
        shares.append(jnp.sum(pick * share_row[i], axis=1, keepdims=True))
        pick = pick.astype(jnp.bfloat16)
        in_ref[at, :] = dot(pick, x_ref[i, :, :width]).astype(jnp.bfloat16)
        grads[at, :] = dot(pick, g_ref[i]).astype(jnp.bfloat16)
    share = jnp.concatenate(shares, axis=0)
    pre = dot(in_ref[...], wg_ref[0])
    lift = dot(in_ref[...], wu_ref[0])
    silu, slope = silu_parts(pre)
    mid_ref[...] = (silu * lift).astype(jnp.bfloat16)
    lift_slope = lift * slope
    result = dot(mid_ref[...], wd_ref[0]).astype(jnp.bfloat16).astype(jnp.float32)
    grad = grads[...].astype(jnp.float32)
    gate_grad = jnp.sum(result * grad, axis=1, keepdims=True)
    og_ref[...] = (share * grad).astype(jnp.bfloat16)
    given = (share * result).astype(jnp.bfloat16)
    mid_grad = inner_right(og_ref[...], wd_ref[0])
    pre_ref[...] = (mid_grad * lift_slope).astype(jnp.bfloat16)
    lift_ref[...] = (mid_grad * silu).astype(jnp.bfloat16)
    in_grad = (inner_right(pre_ref[...], wg_ref[0]) + inner_right(lift_ref[...], wu_ref[0])).astype(jnp.bfloat16)
    lane = lax.broadcasted_iota(jnp.int32, (blocks * capacity, side - width), 1)
    high = gate_grad.astype(jnp.bfloat16).astype(jnp.float32)
    extra = jnp.where(lane == where_ref[0], high, jnp.where(lane == where_ref[1], gate_grad - high, 0.0))
    extra = extra.astype(jnp.bfloat16)
    for i in range(blocks):
        at = slice(i * capacity, (i + 1) * capacity)
        hit = rank_col[i] == lax.broadcasted_iota(jnp.int32, (rows, capacity), 1)
        put = jnp.where(hit, 1.0, 0.0).astype(jnp.bfloat16)
        back_ref[i, :, :width] = dot(put, in_grad[at, :]).astype(jnp.bfloat16)
        back_ref[i, :, width:] = dot(put, extra[at, :]).astype(jnp.bfloat16)
        routed_ref[i] = dot(put, given[at, :]).astype(jnp.bfloat16)


def run_experts(places, arrived, grads, rank, share, gate, up, down, capacity):
    count, rows, side = arrived.shape
    width, ff = gate.shape[1], gate.shape[2]
    blocks = 384 // capacity
    flat = count * capacity
    once = lambda *shape: pl.BlockSpec(shape, lambda i, p: (0,) * len(shape), pipeline_mode=pl.Buffered(1))
    lead = lambda *shape: pl.BlockSpec((blocks,) + shape, lambda i, p: (i, 0, 0))
    tall = lambda wide: pl.BlockSpec((blocks * capacity, wide), lambda i, p: (i, 0))
    shape = lambda *dims: jax.ShapeDtypeStruct(dims, jnp.bfloat16)
    return pl.pallas_call(
        experts_kernel,
        out_shape=(shape(count, rows, side), shape(count, rows, width), shape(flat, width), shape(flat, ff),
                   shape(flat, ff), shape(flat, ff), shape(flat, width)),
        grid_spec=pltpu.PrefetchScalarGridSpec(
            num_scalar_prefetch=1,
            grid=(count // blocks,),
            in_specs=[lead(rows, side), lead(rows, width), lead(1, rows), lead(rows, 1), lead(1, rows),
                      once(1, width, ff), once(1, width, ff), once(1, ff, width)],
            out_specs=(lead(rows, side), lead(rows, width), tall(width), tall(ff), tall(ff), tall(ff), tall(width)),
            scratch_shapes=[pltpu.VMEM((blocks * capacity, width), jnp.bfloat16)],
        ),
        compiler_params=pltpu.CompilerParams(vmem_limit_bytes=VMEM_MOST),
        cost_estimate=pl.CostEstimate(flops=16 * flat * width * ff, bytes_accessed=16 * flat * width, transcendentals=0),
        name="run_experts",
    )(places, arrived, grads, rank[:, None, :], rank[:, :, None], share[:, None, :], gate, up, down)


def attend_back_sum(queries, grads, mixed, start, total, cosine, sine, pairs, parts, collective_id):
    rows, width = queries.shape
    ep_count = pairs.shape[0]
    part_rows, part_width = parts[0].shape[1], sum(part.shape[2] for part in parts)
    plan, pieces = Plan(ep_count, True), 4
    place = Place(lax.axis_size("grp"), ep_count)
    n, wide = plan.planes(), plan.wide
    cuts = [0, part_width // HEAD * 3 // 4 * HEAD, part_width]
    orders = ("xba", "bxa")

    def kernel(q_ref, g_ref, mixed_ref, start_ref, total_ref, cos_ref, sin_ref, pair_ref, *refs):
        sources, refs = refs[: len(parts)], refs[len(parts) :]
        out_ref, pair_out, dq_ref, bias, acc, term, kv, staged, kv_sem = refs[:9]
        refs = refs[9:]
        place.locate()
        sums = []
        for i in range(2):
            sums.append(WholeSum(place, orders[i], pieces_of(sources, cuts[i], cuts[i + 1]), refs[:14]))
            refs = refs[14:]
        sum_rows = RowSum(plan, pieces, staged, refs)
        a, b, c = sum_rows.a, sum_rows.b, sum_rows.c
        me = plan.slot(a, b, c)
        order, ks = sum_rows.order, from_far(wide)
        turns = [(k, d) for d in order for k in ks]

        def block(turn, other):
            k, d = turns[turn]
            b0, c0 = sum_rows.source(k), jnp.where(other, 1 - c, c)
            there = both(plan.inside(a - d), plan.need(d, b, c, b0, c0))
            return there, plan.slot(a - d, b0, c0)

        def fetch(turn, other):
            there, slot = block(turn, other)
            held = jnp.where(other, 0, 1)
            return there, lambda: pltpu.make_async_copy(pair_ref.at[slot], kv.at[held], kv_sem.at[held])

        def begin(turn, other):
            there, go = fetch(turn, other)
            run_if(there, lambda: go().start())

        def compute(turn, other, target):
            there, slot = block(turn, other)
            held = 0 if other else 1

            def work():
                fetch(turn, other)[1]().wait()
                bias[...] = visible_bias((rows, rows), slot * rows, start_ref[...], me * rows)

                @pl.loop(0, HEADS, unroll=2)
                def _(h):
                    early, late, at = lanes(2 * h * HEAD), lanes((2 * h + 1) * HEAD), lanes(h * HEAD)
                    keys, values = kv[held, :, early], kv[held, :, late]
                    own, grad = q_ref[:, at], g_ref[:, at]
                    probs = jnp.exp(inner_right(keys, own) + bias[...] - total_ref[h])
                    score_grad = (probs * (inner_right(values, grad) - term[h])).astype(jnp.bfloat16)
                    target[:, late] = jnp.dot(
                        probs.astype(jnp.bfloat16), grad, preferred_element_type=jnp.float32
                    ).astype(jnp.bfloat16)
                    target[:, early] = jnp.dot(
                        score_grad, own, preferred_element_type=jnp.float32
                    ).astype(jnp.bfloat16)
                    acc[h] += inner_left(keys, score_grad)

            run_if(there, work)

        def turn_of(turn):
            k, d = turns[turn]
            i = plan.plane(a, d)
            compute(turn, True, staged.at[i, k])
            if turn + 1 < len(turns):
                begin(turn + 1, True)
            cond = sum_rows.cross(d, k, 0)[0]
            for q in range(pieces):
                run_if(cond, lambda q=q: sum_rows.cross(d, k, q)[1]().start())
            compute(turn, False, sum_rows.held.at[i, k])
            if turn + 1 < len(turns):
                begin(turn + 1, False)

        def pass_on(turn):
            k, d = turns[turn]

            @pl.loop(0, pieces)
            def _(q):
                sum_rows.first(d, k, q)
                cond, go = sum_rows.over(d, k, q)
                run_if(cond, lambda: go().start())

        begin(0, True)
        begin(0, False)
        place.greet()
        first, second = sums
        for one in sums:
            for i in range(one.n1 - 1):
                one.start(i)
        acc[...] = jnp.zeros_like(acc)
        for h in range(HEADS):
            grad = g_ref[:, h * HEAD : (h + 1) * HEAD].astype(jnp.float32).T
            term[h] = jnp.sum(grad * mixed_ref[h], axis=0, keepdims=True)
        for one in sums:
            for i in range(one.n1 - 1):
                one.stage_core(i)
        last = len(turns) - 1
        for turn in range(len(turns)):
            turn_of(turn)
            if turns[turn][0]:
                pass_on(turn)
            if turn == 0:
                for one in sums:
                    one.start(one.n1 - 1)
            if turn == last - 3:
                for one in sums:
                    one.stage_core(one.n1 - 1)
                for k2 in from_far(second.n2)[:-1]:
                    second.stage_one(k2)
            if turn == last - 2:
                sum_rows.stage_dest(order[0], 0, 2)
            if turn == last - 1:
                for k2 in from_far(first.n2)[:-1]:
                    first.stage_one(k2)
                second.stage_one(0)
                sum_rows.stage_dest(order[0], 2, 3)
        sum_rows.stage_dest(order[0], 3, pieces)
        first.stage_one(0)
        for h in range(HEADS):
            back = turned(acc[h].T * HEAD ** (-0.5), cos_ref[...], -sin_ref[...])
            dq_ref[:, h * HEAD : (h + 1) * HEAD] = back.astype(jnp.bfloat16)
        second.stage_two()
        for d in order[1:]:
            sum_rows.stage_dest(d, 0, pieces)
        pair_out[...] = sum_rows.result()
        first.stage_two()
        for i, one in enumerate(sums):
            one.stage_three(out_ref.at[:, pl.ds(cuts[i], cuts[i + 1] - cuts[i])])
        sum_rows.drain()
        for one in sums:
            one.drain()

    anywhere, near = pl.BlockSpec(memory_space=pl.ANY), pl.BlockSpec(memory_space=pltpu.VMEM)
    scratch = [
        pltpu.VMEM((rows, rows), jnp.float32),
        pltpu.VMEM((HEADS, HEAD, rows), jnp.float32),
        pltpu.VMEM((HEADS, 1, rows), jnp.float32),
        pltpu.VMEM((2, rows, 2 * width), jnp.bfloat16),
        pltpu.VMEM((n, wide, rows, 2 * width), jnp.bfloat16),
        pltpu.SemaphoreType.DMA((2,)),
    ]
    for i in range(2):
        scratch += WholeSum.scratch(place.sizes, orders[i], part_rows, cuts[i + 1] - cuts[i], parts[0].dtype, len(parts))
    scratch += RowSum.scratch(plan, rows, 2 * width, pairs.dtype, pieces)
    return pl.pallas_call(
        kernel,
        out_shape=(jax.ShapeDtypeStruct((part_rows, part_width), jnp.float32),
                   jax.ShapeDtypeStruct((rows, 2 * width), pairs.dtype),
                   jax.ShapeDtypeStruct((rows, width), jnp.bfloat16)),
        in_specs=[near] * 7 + [anywhere] * (1 + len(parts)),
        out_specs=(near, near, near),
        scratch_shapes=scratch,
        compiler_params=pltpu.CompilerParams(
            collective_id=collective_id, has_side_effects=True, vmem_limit_bytes=VMEM_MOST),
        name="attend_back_sum",
    )(queries, grads, mixed, start, total, cosine, sine, pairs, *parts)


def local(
    tokens,
    doc_lengths,
    expert_ids,
    out_grad,
    mixer_gain,
    query_weight,
    key_weight,
    value_weight,
    output_weight,
    ffn_gain,
    router_weight,
    shared_gate,
    shared_up,
    shared_down,
    expert_gate,
    expert_up,
    expert_down,
):
    rows, width = tokens.shape[1], tokens.shape[2]
    ep_count = lax.axis_size("ep")
    device_count = ep_count * lax.axis_size("grp")
    ep_index = lax.axis_index("ep")
    expert_count = router_weight.shape[1]
    capacity = min(rows, 12 * rows * TOP // (7 * expert_count))
    low = lambda v: v.astype(jnp.bfloat16)
    wide = lambda v: v.astype(jnp.float32)
    dot = lambda left, right: jnp.dot(left, right, preferred_element_type=jnp.float32)

    grad_low = out_grad[0]

    doc_ends = jnp.cumsum(doc_lengths[0])
    query_pos = ep_index * rows + jnp.arange(rows, dtype=jnp.int32)
    before = query_pos[:, None] >= doc_ends[None, :]
    start = jnp.max(jnp.where(before, doc_ends[None, :], 0), axis=1)
    info = jnp.stack([ep_index, start[0] // rows]).astype(jnp.int32)
    half_dim = HEAD // 2
    frequency = rope_base ** (-jnp.arange(half_dim, dtype=jnp.float32) / half_dim)
    angles = wide(query_pos)[:, None] * frequency[None, :]
    cosine, sine = jnp.cos(angles), jnp.sin(angles)
    cosine = jnp.concatenate([cosine, cosine], axis=1)
    sine = jnp.concatenate([-sine, sine], axis=1)

    stream = wide(tokens[0])
    hidden_low, queries, own_pairs = project(
        tokens[0], mixer_gain, cosine, sine, query_weight, key_weight, value_weight
    )
    pairs = gather_rows(own_pairs, True, 1, 8)
    grad_later, pairs = lax.optimization_barrier((grad_low, pairs))
    grads_all = lax.all_gather(grad_later, "ep", axis=0, tiled=False)
    mixed, mixed_low, log_total = attend(info, queries, start[None, :], pairs)
    mixer_out = dot(mixed_low, output_weight)
    residual = stream + mixer_out
    ffn_low = low(normed(residual, ffn_gain))

    logits = dot(ffn_low, router_weight)
    experts = jnp.arange(expert_count, dtype=jnp.int32)
    assigned = jnp.any(expert_ids[0][:, :, None] == experts[None, None, :], axis=1)
    shown = jnp.where(assigned, logits, masked_value)
    powers = jnp.where(assigned, jnp.exp(shown - jnp.max(shown, axis=1, keepdims=True)), 0.0)
    gate_probs = powers / jnp.sum(powers, axis=1, keepdims=True)
    probs_high = low(gate_probs)
    probs_rest = low(gate_probs - wide(probs_high))
    side = width + 2 * HEAD if 2 * expert_count > HEAD else width + HEAD
    pad = jnp.zeros((rows, side - width - 2 * expert_count), jnp.bfloat16)
    sent = jnp.concatenate([ffn_low, probs_high, probs_rest, pad], axis=1)
    arrived, shared_out, ffn_grad, shared_gate_part, shared_up_part, shared_down_part = gather_shared(
        sent, grad_low, shared_gate, shared_up, shared_down, 2
    )

    own = experts[None, None, :] == ep_index
    high = arrived[:, :, width : width + expert_count]
    rest = arrived[:, :, width + expert_count : width + 2 * expert_count]
    share = jnp.sum(jnp.where(own, wide(high) + wide(rest), 0.0), axis=2)
    chosen = share > 0.0
    earlier = (jnp.arange(rows)[:, None] < jnp.arange(rows)[None, :]).astype(jnp.bfloat16)
    rank = dot(low(chosen), earlier).astype(jnp.int32)
    rank = jnp.where(chosen, rank, -1)
    places = jnp.stack([ep_index, expert_count + ep_index]).astype(jnp.int32)
    back, given, flat_in, pre_grad, lift_grad, middle, result_grad = run_experts(
        places, arrived, grads_all, rank, share, expert_gate, expert_up, expert_down, capacity
    )
    routed = lax.psum_scatter(given, "ep", scatter_dimension=0)
    group_count = lax.axis_size("grp")
    if group_count == 2:
        back_sum, gate_sum, up_sum, down_sum = scatter_experts(
            back, (flat_in, result_grad), (pre_grad, lift_grad, middle), 3
        )
    else:
        back_sum = scatter_rows(back, False, 3)
        split = width // group_count
        own_down_grad = jnp.concatenate(
            [low(inner_left(middle, result_grad[:, i * split : (i + 1) * split])) for i in range(group_count)], axis=0
        )
        over_groups = lambda v: wide(lax.psum_scatter(v, "grp", scatter_dimension=0, tiled=True))[None]
        gate_sum = over_groups(low(inner_left(flat_in, pre_grad)))
        up_sum = over_groups(low(inner_left(flat_in, lift_grad)))
        down_sum = over_groups(own_down_grad)

    grad_out = wide(grad_low)
    gate_back = wide(back_sum[:, width : width + expert_count]) + wide(
        back_sum[:, width + expert_count : width + 2 * expert_count]
    )
    chosen_grad = gate_probs * (gate_back - jnp.sum(gate_probs * gate_back, axis=1, keepdims=True))
    logit_grad = low(chosen_grad)
    ffn_grad = ffn_grad + wide(back_sum[:, :width]) + inner_right(logit_grad, router_weight)
    _, ffn_pull = jax.vjp(normed, residual, ffn_gain)
    residual_part, ffn_gain_grad = ffn_pull(ffn_grad)
    residual_grad = grad_out + residual_part
    mixer_grad_low = low(residual_grad)
    mixed_grad = low(inner_right(mixer_grad_low, output_weight))
    by_device = lambda v: low(v).reshape(device_count, width // device_count, -1)
    early = [
        by_device(part)
        for part in (shared_gate_part, shared_up_part, shared_down_part, inner_left(mixed_low, mixer_grad_low))
    ]
    if ep_count > 16:
        pair_parts, query_lin_grad = attend_back(
            info, queries, mixed_grad, mixed, start[None, :], log_total, cosine, sine, pairs
        )
        pair_grads = scatter_rows(pair_parts, True, 4)
        early_sum = scatter_whole(early, 5)
    else:
        early_sum, pair_grads, query_lin_grad = attend_back_sum(
            queries, mixed_grad, mixed, start[None, :], log_total, cosine, sine, pairs, early, 5
        )

    routed, pair_grads = lax.optimization_barrier((routed, pair_grads))
    layer_out = residual + shared_out + wide(routed)
    query_part, key_part, value_part, tokens_grad, mixer_gain_grad, *carried = finish(
        tokens[0], mixer_gain, residual_grad, hidden_low, query_lin_grad, pair_grads, cosine, sine,
        query_weight, key_weight, value_weight, (gate_sum, up_sum, down_sum) if group_count == 2 else (),
    )
    if carried:
        gate_sum, up_sum, down_sum = (v[None] for v in carried)
    squares = jnp.stack(
        [jnp.sum(residual * residual), jnp.sum(mixer_out * mixer_out), jnp.sum(layer_out * layer_out)]
    )
    extras = jnp.concatenate(
        [inner_left(ffn_low, logit_grad), mixer_gain_grad.T, ffn_gain_grad[:, None],
         jnp.broadcast_to(squares[None, :], (width, 3))], axis=1
    )
    extras = jnp.pad(extras, ((0, 0), (0, HEAD - extras.shape[1])))
    late_sum = scatter_whole([by_device(v) for v in (query_part, key_part, value_part, extras)], 6)
    extra_sum = late_sum[:, 3 * width :]
    entry_count = rows * device_count * width
    stream_rms = jnp.sqrt(extra_sum[0, expert_count + 2 : expert_count + 5] / entry_count)
    ff = shared_gate.shape[1]
    return (
        low(layer_out)[None],
        tokens_grad[None],
        extra_sum[:, expert_count],
        late_sum[:, :width],
        late_sum[:, width : 2 * width],
        late_sum[:, 2 * width : 3 * width],
        early_sum[:, 3 * ff :],
        extra_sum[:, expert_count + 1],
        extra_sum[:, :expert_count],
        early_sum[:, :ff],
        early_sum[:, ff : 2 * ff],
        early_sum[:, 2 * ff : 3 * ff].T,
        gate_sum,
        up_sum,
        down_sum,
        stream_rms,
    )


def solution(mesh):
    return jax.shard_map(
        local,
        mesh=mesh,
        in_specs=(
            P("grp", "ep", None),
            P("grp", None),
            P("grp", "ep", None),
            P("grp", "ep", None),
            P(),
            P(),
            P(),
            P(),
            P(),
            P(),
            P(),
            P(),
            P(),
            P(),
            P("ep", None, None),
            P("ep", None, None),
            P("ep", None, None),
        ),
        out_specs=(
            P("grp", "ep", None),
            P("grp", "ep", None),
            P(("grp", "ep")),
            P(("grp", "ep"), None),
            P(("grp", "ep"), None),
            P(("grp", "ep"), None),
            P(("grp", "ep"), None),
            P(("grp", "ep")),
            P(("grp", "ep"), None),
            P(("grp", "ep"), None),
            P(("grp", "ep"), None),
            P(None, ("grp", "ep")),
            P("ep", "grp", None),
            P("ep", "grp", None),
            P("ep", None, "grp"),
            P(),
        ),
        check_vma=False,
    )
```

```python
import functools

import jax
import jax.numpy as jnp
from jax import lax
from jax.experimental import pallas as pl
from jax.experimental.pallas import tpu as pltpu
from jax.sharding import PartitionSpec as P

HEADS = 10
HEAD = 128
TOP = 7

epsilon = 1e-06
rope_base = 10000.0
masked_value = -1e30


def normed(values, gain_vec):
    return (
        values * lax.rsqrt(jnp.mean(values * values, axis=-1, keepdims=True) + epsilon) * gain_vec
    )


def inner_left(left_op, right_op):
    return lax.dot_general(
        left_op, right_op, (((0,), (0,)), ((), ())), preferred_element_type=jnp.float32
    )


def inner_right(left_op, right_op):
    return lax.dot_general(
        left_op, right_op, (((1,), (1,)), ((), ())), preferred_element_type=jnp.float32
    )


def silu_parts(pre_act):
    sigmoid_val = jax.nn.sigmoid(pre_act)
    return (pre_act * sigmoid_val, sigmoid_val * (1.0 + pre_act * (1.0 - sigmoid_val)))


MESH = pl.DeviceIdType.MESH
COUPLES = 2
VMEM_MOST = 64 * 1024 * 1024 - 65536


def when(cond):
    if cond is True:
        return lambda f: f()
    if cond is False:
        return lambda f: None
    return pl.when(cond)


def both(*conds):
    out = True
    for cond in conds:
        if cond is False:
            return False
        if cond is True:
            continue
        out = cond if out is True else jnp.logical_and(out, cond)
    return out


class Plan:
    def __init__(self, ep_count, window):
        self.long = 4
        self.wide = ep_count // 8
        self.window = window
        self.steps = (
            list(range(self.long // 2 + 1))
            if window
            else list(range(-(self.long - 1), self.long))
        )

    def place(self):
        me = lax.axis_index("ep")
        return me // (2 * self.wide), (me // 2) % self.wide, me % 2

    def slot(self, a, b, c):
        return (a * self.wide + b) * 2 + c

    def plane(self, a, d):
        return d if self.window else jnp.clip(a - d, 0, self.long - 1)

    def planes(self):
        return len(self.steps) if self.window else self.long

    def inside(self, a):
        return jnp.logical_and(a >= 0, a < self.long)

    def need(self, d, b, c, b0, c0):
        if not self.window or 0 < d < self.long // 2:
            return True
        if d == 0:
            return jnp.logical_or(b0 < b, jnp.logical_and(b0 == b, c0 <= c))
        return jnp.logical_or(b0 > b, jnp.logical_and(b0 == b, c0 >= c))

    def need_pair(self, d, b, b0):
        if not self.window or 0 < d < self.long // 2:
            return True
        return b0 < b if d == 0 else b0 > b

    def greet(self, a, b, c):
        barrier = pltpu.get_barrier_semaphore()

        def signal(cond, dev):
            @when(cond)
            def _():
                pl.semaphore_signal(barrier, inc=1, device_id={"ep": dev}, device_id_type=MESH)

        signal(a + 1 < self.long, self.slot(a + 1, b, c))
        signal(a > 0, self.slot(a - 1, b, c))
        for k in range(1, self.wide):
            signal(True, self.slot(a, (b + k) % self.wide, c))
        signal(True, self.slot(a, b, 1 - c))
        ends = (a == 0).astype(jnp.int32) + (a == self.long - 1).astype(jnp.int32)
        pl.semaphore_wait(barrier, self.wide + 2 - ends)


def gather_kernel(plan, pieces, beside, x_ref, out_ref, ra, sa_up, sa_dn, rb, sb, rc, sc, own):
    a, b, c = plan.place()
    steps, wide = plan.steps, plan.wide
    at = {d: i for i, d in enumerate(steps)}
    rows = x_ref.shape[0] // pieces

    def part(q):
        return pl.ds(pl.multiple_of(q * rows, rows), rows)

    def copy(q, src, slot, ssem, rsem, dev):
        return pltpu.make_async_remote_copy(
            src_ref=src, dst_ref=out_ref.at[slot, part(q)], send_sem=ssem, recv_sem=rsem,
            device_id={"ep": dev}, device_id_type=MESH,
        )

    def hops(d, q):
        i = at[d]
        slot = plan.slot(a - d, b, c)
        src = x_ref.at[part(q)] if d == 0 else out_ref.at[slot, part(q)]
        real = plan.inside(a - d)
        out = []
        if d >= 0 and d + 1 in at:
            out.append((both(real, a + 1 < plan.long), lambda: copy(
                q, src, slot, sa_up.at[i, q], ra.at[at[d + 1], q], plan.slot(a + 1, b, c))))
        if d <= 0 and d - 1 in at:
            out.append((both(real, a > 0), lambda: copy(
                q, src, slot, sa_dn.at[i, q], ra.at[at[d - 1], q], plan.slot(a - 1, b, c))))
        for k in range(1, wide):
            to = (b + k) % wide
            out.append((both(real, plan.need_pair(d, to, b)), lambda k=k, to=to: copy(
                q, src, slot, sb.at[i, k, q], rb.at[i, k, q], plan.slot(a, to, c))))
        out.append((both(real, plan.need(d, b, 1 - c, b, c)), lambda: copy(
            q, src, slot, sc.at[i, 0, q], rc.at[i, 0, q], plan.slot(a, b, 1 - c))))
        return out

    def cross(d, k, q):
        i = at[d]
        b0 = (b + wide - k) % wide
        slot = plan.slot(a - d, b0, c)
        real = plan.inside(a - d)
        come = lambda: copy(q, x_ref.at[part(q)], slot, sb.at[i, k, q], rb.at[i, k, q], plan.slot(a, b, c))
        go = lambda: copy(q, out_ref.at[slot, part(q)], slot, sc.at[i, k, q], rc.at[i, k, q],
                          plan.slot(a, b, 1 - c))
        return (both(real, plan.need_pair(d, b, b0)), come,
                both(real, plan.need(d, b, 1 - c, b0, c)), go)

    plan.greet(a, b, c)
    keep = pltpu.make_async_copy(x_ref, out_ref.at[plan.slot(a, b, c)], own)

    @pl.loop(0, pieces)
    def _(q):
        for cond, go in hops(0, q):
            @when(cond)
            def _(go=go):
                go().start()

    keep.start()
    far = max(abs(d) for d in steps)
    for step in range(1, far + 3):
        beside(step - 1)

        @pl.loop(0, pieces)
        def _(q, step=step):
            for d in (step, -step):
                if d in at:
                    @when(plan.inside(a - d))
                    def _(d=d):
                        slot = plan.slot(a - d, b, c)
                        copy(q, x_ref.at[part(q)], slot, sa_up.at[0, q], ra.at[at[d], q],
                             plan.slot(a, b, c)).wait_recv()
                        for cond, go in hops(d, q):
                            @when(cond)
                            def _(go=go):
                                go().start()
            for d in sorted({step - 2, 2 - step}) if step > 1 else ():
                if d in at:
                    for k in range(1, wide):
                        came, come, goes, go = cross(d, k, q)
                        @when(came)
                        def _(come=come):
                            come().wait_recv()
                        @when(goes)
                        def _(go=go):
                            go().start()
    keep.wait()

    @pl.loop(0, pieces)
    def _(q):
        for d in steps:
            i = at[d]
            real = plan.inside(a - d)
            for k in range(wide):
                b0 = (b + wide - k) % wide
                slot = plan.slot(a - d, b0, 1 - c)
                @when(both(real, plan.need(d, b, c, b0, 1 - c)))
                def _(slot=slot, i=i, k=k):
                    copy(q, x_ref.at[part(q)], slot, sc.at[i, k, q], rc.at[i, k, q],
                         plan.slot(a, b, c)).wait_recv()
            for cond, go in hops(d, q):
                @when(cond)
                def _(go=go):
                    go().wait_send()
            for k in range(1, wide):
                came, come, goes, go = cross(d, k, q)
                @when(goes)
                def _(go=go):
                    go().wait_send()


def gather_rows(block, window, collective_id, pieces=4):
    ep_count = lax.axis_size("ep")
    plan = Plan(ep_count, window)
    n, wide = len(plan.steps), plan.wide
    sem = pltpu.SemaphoreType.DMA
    return pl.pallas_call(
        functools.partial(gather_kernel, plan, pieces, lambda n: None),
        out_shape=jax.ShapeDtypeStruct((ep_count,) + block.shape, block.dtype),
        in_specs=[pl.BlockSpec(memory_space=pltpu.VMEM)],
        out_specs=pl.BlockSpec(memory_space=pl.ANY),
        scratch_shapes=[sem((n, pieces)), sem((n, pieces)), sem((n, pieces)), sem((n, wide, pieces)),
                        sem((n, wide, pieces)), sem((n, wide, pieces)), sem((n, wide, pieces)), sem],
        compiler_params=pltpu.CompilerParams(collective_id=collective_id, has_side_effects=True),
        name="gather_rows",
    )(block)


def gather_shared(block, grads, gate, up, down, collective_id, pieces=4):
    ep_count = lax.axis_size("ep")
    plan = Plan(ep_count, False)
    n, wide = len(plan.steps), plan.wide
    rows, width = grads.shape
    ff = gate.shape[1]
    sem = pltpu.SemaphoreType.DMA
    stages = max(plan.steps) + 2
    tiles = ff // HEAD

    def kernel(x_ref, g_ref, wg_ref, wu_ref, wd_ref, out_ref, shared_ref, back_ref, dg_ref, du_ref, dd_ref, *sems):
        dot = lambda left, right: jnp.dot(left, right, preferred_element_type=jnp.float32)

        def tile(i):
            at = pl.ds(pl.multiple_of(i * HEAD, HEAD), HEAD)
            x, g = x_ref[:, :width], g_ref[...]
            w_gate, w_up, w_down = wg_ref[:, at], wu_ref[:, at], wd_ref[at, :]
            silu, slope = silu_parts(dot(x, w_gate))
            lift = dot(x, w_up)
            mid = (silu * lift).astype(jnp.bfloat16)
            mid_grad = inner_right(g, w_down)
            pre_grad = (mid_grad * lift * slope).astype(jnp.bfloat16)
            lift_grad = (mid_grad * silu).astype(jnp.bfloat16)
            out = dot(mid, w_down)
            back = inner_right(pre_grad, w_gate) + inner_right(lift_grad, w_up)

            @pl.when(i == 0)
            def _():
                shared_ref[...] = out
                back_ref[...] = back

            @pl.when(i > 0)
            def _():
                shared_ref[...] += out
                back_ref[...] += back

            dg_ref[:, at] = inner_left(x, pre_grad).astype(jnp.bfloat16)
            du_ref[:, at] = inner_left(x, lift_grad).astype(jnp.bfloat16)
            dd_ref[:, at] = inner_left(g, mid).astype(jnp.bfloat16)

        def beside(stage):
            pl.loop(tiles * stage // stages, tiles * (stage + 1) // stages)(tile)

        gather_kernel(plan, pieces, beside, x_ref, out_ref, *sems)

    near = pl.BlockSpec(memory_space=pltpu.VMEM)
    return pl.pallas_call(
        kernel,
        out_shape=(
            jax.ShapeDtypeStruct((ep_count,) + block.shape, block.dtype),
            jax.ShapeDtypeStruct((rows, width), jnp.float32),
            jax.ShapeDtypeStruct((rows, width), jnp.float32),
        ) + (jax.ShapeDtypeStruct((width, ff), jnp.bfloat16),) * 3,
        in_specs=[near] * 5,
        out_specs=(pl.BlockSpec(memory_space=pl.ANY),) + (near,) * 5,
        scratch_shapes=[sem((n, pieces)), sem((n, pieces)), sem((n, pieces)), sem((n, wide, pieces)),
                        sem((n, wide, pieces)), sem((n, wide, pieces)), sem((n, wide, pieces)), sem],
        compiler_params=pltpu.CompilerParams(
            collective_id=collective_id, has_side_effects=True, vmem_limit_bytes=VMEM_MOST),
        name="gather_shared",
    )(block, grads, gate, up, down)


def add_rows(dst, others, out=None):
    rows, width = dst.shape
    out = dst if out is None else out
    small = rows <= 64
    piece = 32 if rows % 32 == 0 else rows
    lanes = width if rows % 32 == 0 else 4 * HEAD
    whole = width // lanes * lanes

    def add(at):
        if len(others) == 1 and out.dtype == jnp.bfloat16:
            out[at] = dst[at] + others[0][at]
        else:
            total = dst[at].astype(jnp.float32)
            for other in others:
                total = total + other[at].astype(jnp.float32)
            out[at] = total.astype(out.dtype)

    if piece == rows:
        @pl.loop(0, whole // lanes)
        def _(i):
            add((slice(None), pl.ds(pl.multiple_of(i * lanes, lanes), lanes)))

        if whole < width:
            add((slice(None), pl.ds(whole, width - whole)))
    else:
        @pl.loop(0, rows // piece)
        def _(i):
            add((pl.ds(pl.multiple_of(i * piece, piece), piece), slice(None)))


def send(src, dst, ssem, rsem, to):
    return pltpu.make_async_remote_copy(
        src_ref=src, dst_ref=dst, send_sem=ssem, recv_sem=rsem, device_id=to, device_id_type=MESH
    )


def run_if(cond, go):
    @when(cond)
    def _():
        go()


class RowSum:
    @staticmethod
    def scratch(plan, rows, width, dtype, pieces):
        n, wide = plan.planes(), plan.wide
        blocks = lambda *lead: pltpu.VMEM(lead + (rows, width), dtype)
        sem = lambda *lead: pltpu.SemaphoreType.DMA(lead + (pieces,))
        return [blocks(n, wide), blocks(n, wide), blocks(n, wide - 1), blocks(n), blocks(1 if plan.window else n),
                sem(n, wide), sem(n, wide), sem(n, wide), sem(n, wide), sem(n), sem(n), sem(n), sem(n, wide)]

    def __init__(self, plan, pieces, p_ref, scratch):
        self.plan, self.pieces, self.p_ref = plan, pieces, p_ref
        (self.held, self.rcb, self.rbb, self.r_hi, self.r_lo,
         self.sc, self.rc, self.sb, self.rb, self.sa, self.rhi, self.rlo, self.ld) = scratch
        self.a, self.b, self.c = plan.place()
        self.ready = len(p_ref.shape) == 4
        self.rows = p_ref.shape[-2] // pieces
        self.order = sorted(plan.steps, key=lambda d: -abs(d))

    def part(self, q):
        return pl.ds(pl.multiple_of(q * self.rows, self.rows), self.rows)

    def dev(self, a, b, c):
        return {"ep": self.plan.slot(a, b, c)}

    def source(self, k):
        return (self.b + self.plan.wide - k) % self.plan.wide

    def load(self, d, k, q):
        p, i, b0 = self.plan, self.plan.plane(self.a, d), self.source(k)
        return both(p.inside(self.a - d), p.need(d, self.b, self.c, b0, self.c)), lambda: pltpu.make_async_copy(
            self.p_ref.at[p.slot(self.a - d, b0, self.c), self.part(q)], self.held.at[i, k, self.part(q)],
            self.ld.at[i, k, q])

    def cross(self, d, k, q):
        p, i, b0, c = self.plan, self.plan.plane(self.a, d), self.source(k), self.c
        real = p.inside(self.a - d)
        at = (i, k) if self.ready else (p.slot(self.a - d, b0, 1 - c),)
        return (both(real, p.need(d, self.b, c, b0, 1 - c)), lambda: send(
            self.p_ref.at[at + (self.part(q),)], self.rcb.at[i, k, self.part(q)],
            self.sc.at[i, k, q], self.rc.at[i, k, q], self.dev(self.a, self.b, 1 - c)),
            both(real, p.need(d, self.b, 1 - c, b0, c)))

    def over(self, d, k, q):
        p, i, b0 = self.plan, self.plan.plane(self.a, d), self.source(k)
        return both(p.inside(self.a - d), p.need_pair(d, self.b, b0)), lambda: send(
            self.held.at[i, k, self.part(q)], self.rbb.at[i, k - 1, self.part(q)], self.sb.at[i, k, q],
            self.rb.at[i, k, q], self.dev(self.a, b0, self.c))

    def along(self, d, q):
        p, i, up = self.plan, self.plan.plane(self.a, d), d < 0
        j = d - 1 if p.window else i
        return p.inside(self.a - d), lambda: send(
            self.held.at[i, 0, self.part(q)], (self.r_lo if up else self.r_hi).at[j, self.part(q)],
            self.sa.at[i, q], (self.rlo if up else self.rhi).at[j, q],
            self.dev(self.a + (1 if up else -1), self.b, self.c))

    def start(self, ks):
        for k in ks:
            @pl.loop(0, self.pieces)
            def _(q, k=k):
                for d in self.order:
                    for cond, go in (self.cross(d, k, q)[:2], self.load(d, k, q)):
                        run_if(cond, lambda go=go: go().start())

    def first(self, d, k, q):
        i = self.plan.plane(self.a, d)
        if not self.ready:
            cond, go = self.load(d, k, q)
            run_if(cond, lambda: go().wait())
        _, come_go, come = self.cross(d, k, q)

        def take():
            come_go().wait_recv()
            add_rows(self.held.at[i, k, self.part(q)], [self.rcb.at[i, k, self.part(q)]])

        run_if(come, take)

    def stage_over(self, k):
        @pl.loop(0, self.pieces)
        def _(q):
            for d in self.order:
                self.first(d, k, q)
                cond, go = self.over(d, k, q)
                run_if(cond, lambda go=go: go().start())

    def stage_dests(self, low, high):
        @pl.loop(low, high)
        def _(q):
            for d in self.order:
                self.dest(d, q)

    def stage_dest(self, d, low, high):
        @pl.loop(low, high)
        def _(q):
            self.dest(d, q)

    def dest(self, d, q):
        p, a, b, steps = self.plan, self.a, self.b, self.plan.steps
        i = p.plane(a, d)
        real = p.inside(a - d)
        mine = self.held.at[i, 0, self.part(q)]
        self.first(d, 0, q)
        for k in range(1, p.wide):
            def take(k=k):
                self.over(d, k, q)[1]().wait_recv()
                add_rows(mine, [self.rbb.at[i, k - 1, self.part(q)]])

            run_if(both(real, p.need_pair(d, (b + k) % p.wide, b)), take)
        for inner, cond, buf, sem in ((d >= 0 and d + 1 in steps, a + 1 < p.long, self.r_hi, self.rhi),
                                      (d <= 0 and d - 1 in steps, a > 0, self.r_lo, self.rlo)):
            if inner:
                def take(buf=buf, sem=sem):
                    send(mine, buf.at[i, self.part(q)], self.sa.at[i, q], sem.at[i, q],
                         self.dev(a, b, self.c)).wait_recv()
                    add_rows(mine, [buf.at[i, self.part(q)]])

                run_if(both(real, cond), take)
        if d:
            cond, go = self.along(d, q)
            run_if(cond, lambda: go().start())

    def result(self):
        return self.held[self.plan.plane(self.a, 0), 0]

    def drain(self):
        @pl.loop(0, self.pieces)
        def _(q):
            for d in self.plan.steps:
                sends = [self.cross(d, k, q)[:2] for k in range(self.plan.wide)]
                sends += [self.over(d, k, q) for k in range(1, self.plan.wide)]
                if d:
                    sends.append(self.along(d, q))
                for cond, go in sends:
                    run_if(cond, lambda go=go: go().wait_send())


def scatter_rows(parts, window, collective_id, pieces=4):
    ep_count, rows, width = parts.shape
    plan = Plan(ep_count, window)

    def kernel(p_ref, out_ref, *scratch):
        total = RowSum(plan, pieces, p_ref, scratch)
        plan.greet(total.a, total.b, total.c)
        ks = list(range(1, plan.wide)) + [0]
        total.start(ks)
        for k in ks[:-1]:
            total.stage_over(k)
        total.stage_dests(0, pieces)
        out_ref[...] = total.result()
        total.drain()

    return pl.pallas_call(
        kernel,
        out_shape=jax.ShapeDtypeStruct((rows, width), parts.dtype),
        in_specs=[pl.BlockSpec(memory_space=pl.ANY)],
        out_specs=pl.BlockSpec(memory_space=pltpu.VMEM),
        scratch_shapes=RowSum.scratch(plan, rows, width, parts.dtype, pieces),
        compiler_params=pltpu.CompilerParams(
            collective_id=collective_id, has_side_effects=True, vmem_limit_bytes=VMEM_MOST),
        name="scatter_rows",
    )(parts)


class Place:
    def __init__(self, groups, ep_count):
        self.sizes = {"x": groups, "a": 4, "b": ep_count // 8}

    def locate(self):
        me, wide = lax.axis_index("ep"), self.sizes["b"]
        self.at = {"x": lax.axis_index("grp"), "a": me // (2 * wide), "b": (me // 2) % wide, "c": me % 2}

    def dev(self, **moved):
        at = {**self.at, **moved}
        return {"grp": at["x"], "ep": (at["a"] * self.sizes["b"] + at["b"]) * 2 + at["c"]}

    def slot(self, **moved):
        at = {**self.at, **moved}
        return ((at["x"] * self.sizes["a"] + at["a"]) * self.sizes["b"] + at["b"]) * 2 + at["c"]

    def back(self, axis, k):
        return (self.at[axis] + self.sizes[axis] - k) % self.sizes[axis]

    def greet(self):
        peers = [self.dev(c=1 - self.at["c"])] + [
            self.dev(**{axis: self.back(axis, k)}) for axis in "xba" for k in range(1, self.sizes[axis])]
        barrier = pltpu.get_barrier_semaphore()
        for to in peers:
            pl.semaphore_signal(barrier, inc=1, device_id=to, device_id_type=MESH)
        pl.semaphore_wait(barrier, len(peers))


def from_far(size):
    return list(range(1, size)) + [0]


class WholeSum:
    @staticmethod
    def scratch(sizes, axes, rows, width, dtype, sources):
        n1, n2, n3 = (sizes[axis] for axis in axes)
        blocks = lambda *lead: pltpu.VMEM(lead + (rows, width), dtype)
        sem = lambda *lead: pltpu.SemaphoreType.DMA(lead)
        full = (n1, n2, n3)
        one, two, three = (n1 - 1, n2, n3), (n2 - 1, n3), (n3 - 1,)
        return [blocks(*full), blocks(*full), blocks(*one), blocks(*two), blocks(*three),
                sem(*full, sources), sem(*full, sources), sem(*full, sources), sem(*one), sem(*one), sem(*two), sem(*two), sem(*three), sem(*three)]

    def __init__(self, place, axes, pieces, scratch):
        self.place, self.axes, self.pieces = place, axes, pieces
        (self.held, self.rcb, self.r1, self.r2, self.r3,
         self.ld, self.sc, self.rc, self.s1, self.q1, self.s2, self.q2, self.s3, self.q3) = scratch
        self.n1, self.n2, self.n3 = (place.sizes[axis] for axis in axes)
        self.groups = [[(k1, k2, k3) for k2 in from_far(self.n2) for k3 in from_far(self.n3)]
                       for k1 in from_far(self.n1)]

    def slot(self, key, c):
        return self.place.slot(c=c, **{axis: self.place.back(axis, k) for axis, k in zip(self.axes, key)})

    def loads(self, key):
        c = self.place.at["c"]
        for n, (ref, first, at, count) in enumerate(self.pieces):
            frm, to = pl.ds(first, count), pl.ds(at, count)
            yield pltpu.make_async_copy(
                ref.at[self.slot(key, c), :, frm], self.held.at[key + (slice(None), to)],
                self.ld.at[key + (n,)])

    def crossings(self, key):
        c = self.place.at["c"]
        for n, (ref, first, at, count) in enumerate(self.pieces):
            frm, to = pl.ds(first, count), pl.ds(at, count)
            yield send(ref.at[self.slot(key, 1 - c), :, frm], self.rcb.at[key + (slice(None), to)],
                       self.sc.at[key + (n,)], self.rc.at[key + (n,)], self.place.dev(c=1 - c))

    def hop(self, level, key):
        buf, ssem, rsem = ((self.r1, self.s1, self.q1), (self.r2, self.s2, self.q2), (self.r3, self.s3, self.q3))[level]
        axis, k = self.axes[level], key[level]
        far = (k - 1,) + key[level + 1 :]
        return send(self.held.at[key], buf.at[far], ssem.at[far], rsem.at[far],
                    self.place.dev(**{axis: self.place.back(axis, k)}))

    def start(self, i):
        for key in self.groups[i]:
            for go in self.crossings(key):
                go.start()
            for go in self.loads(key):
                go.start()

    def stage_core(self, i):
        for key in self.groups[i]:
            for go in self.loads(key):
                go.wait()
            for go in self.crossings(key):
                go.wait_recv()
            add_rows(self.held.at[key], [self.rcb.at[key]])
            if key[0]:
                self.hop(0, key).start()

    def stage_one(self, k2):
        for k3 in from_far(self.n3):
            for k1 in range(1, self.n1):
                self.hop(0, (k1, k2, k3)).wait_recv()
            add_rows(self.held.at[0, k2, k3], [self.r1.at[k1 - 1, k2, k3] for k1 in range(1, self.n1)])
            if k2:
                self.hop(1, (0, k2, k3)).start()

    def stage_two(self):
        for k3 in from_far(self.n3):
            for k2 in range(1, self.n2):
                self.hop(1, (0, k2, k3)).wait_recv()
            add_rows(self.held.at[0, 0, k3], [self.r2.at[k2 - 1, k3] for k2 in range(1, self.n2)])
            if k3:
                self.hop(2, (0, 0, k3)).start()

    def stage_three(self, out):
        for k3 in range(1, self.n3):
            self.hop(2, (0, 0, k3)).wait_recv()
        add_rows(self.held.at[0, 0, 0], [self.r3.at[k3 - 1] for k3 in range(1, self.n3)], out)

    def drain(self):
        for group in self.groups:
            for key in group:
                for go in self.crossings(key):
                    go.wait_send()
                if key[0]:
                    self.hop(0, key).wait_send()
                elif key[1]:
                    self.hop(1, key).wait_send()
                elif key[2]:
                    self.hop(2, key).wait_send()


def pieces_of(sources, low, high):
    pieces, first = [], 0
    for ref in sources:
        begin, end = max(low, first), min(high, first + ref.shape[2])
        if begin < end:
            pieces.append((ref, begin - first, begin - low, end - begin))
        first += ref.shape[2]
    return pieces


def scatter_whole(parts, collective_id):
    rows = parts[0].shape[1]
    width = sum(part.shape[2] for part in parts)
    groups, ep_count = lax.axis_size("grp"), lax.axis_size("ep")
    place = Place(groups, ep_count)
    tiles = width // HEAD
    count = 2 * COUPLES
    cuts = [tiles * n // count * HEAD for n in range(count + 1)]
    orders = ["xba", "bxa"] * COUPLES

    def kernel(*refs):
        sources, refs = refs[: len(parts)], refs[len(parts) :]
        out_ref, refs = refs[0], refs[1:]
        place.locate()
        sums = []
        for n, axes in enumerate(orders):
            pieces = pieces_of(sources, cuts[n], cuts[n + 1])
            sums.append(WholeSum(place, axes, pieces, refs[:14]))
            refs = refs[14:]
        outs = [out_ref.at[:, pl.ds(cuts[n], cuts[n + 1] - cuts[n])] for n in range(len(orders))]
        place.greet()
        couples = [sums[n : n + 2] for n in range(0, len(sums), 2)]
        for couple in couples:
            for i in range(max(s.n1 for s in couple)):
                for s in couple:
                    if i < s.n1:
                        s.start(i)

        def core(couple):
            for i in range(max(s.n1 for s in couple)):
                for s in couple:
                    if i < s.n1:
                        s.stage_core(i)

        def one(couple):
            for i in range(max(s.n2 for s in couple)):
                for s in couple:
                    if i < s.n2:
                        s.stage_one(from_far(s.n2)[i])

        def two(couple):
            for s in couple:
                s.stage_two()

        core(couples[0])
        for n, couple in enumerate(couples):
            one(couple)
            if n + 1 < len(couples):
                core(couples[n + 1])
            two(couple)
        for s, out in zip(sums, outs):
            s.stage_three(out)
        for s in sums:
            s.drain()

    operands, anywhere = list(parts), pl.BlockSpec(memory_space=pl.ANY)
    out_shape = [jax.ShapeDtypeStruct((rows, width), jnp.float32)]
    scratch = []
    for n, axes in enumerate(orders):
        scratch += WholeSum.scratch(place.sizes, axes, rows, cuts[n + 1] - cuts[n], parts[0].dtype, len(parts))
    got = pl.pallas_call(
        kernel,
        out_shape=tuple(out_shape),
        in_specs=[anywhere] * len(operands),
        out_specs=tuple(pl.BlockSpec(memory_space=pltpu.VMEM) for _ in out_shape),
        scratch_shapes=scratch,
        compiler_params=pltpu.CompilerParams(
            collective_id=collective_id, has_side_effects=True, vmem_limit_bytes=VMEM_MOST),
        name="scatter_whole",
    )(*operands)
    return got[0]


def scatter_experts(parts, lefts, rights, collective_id):
    ep_count, rows, width = parts.shape
    flat, tall = lefts[0].shape
    ff = rights[0].shape[1]
    half, depth = tall // 2, flat // 3
    plan, pieces = Plan(ep_count, False), 4
    place = Place(lax.axis_size("grp"), ep_count)
    left_of = [0, 0, 1]
    hooks = (8, 9, 10, 11, 13, 14, 15, 16)
    kinds, units = len(rights), 2 * len(rights)
    steps = units * 3

    def kernel(p_ref, in_ref, og_ref, pre_ref, lift_ref, mid_ref, out_ref, w0, w1, w2, acc, left, right, gone, came,
               ls, rs, gs, cs, *scratch):
        left_refs, right_refs, outs = (in_ref, og_ref), (pre_ref, lift_ref, mid_ref), (w0, w1, w2)
        place.locate()
        total = RowSum(plan, pieces, p_ref, scratch)
        g = place.at["x"]
        place.greet()

        def fetch(kind, step):
            chunk, slot = step % 3, step % 2
            mine = (step >= 3 * kinds).astype(jnp.int32)
            first = pl.multiple_of(jnp.where(mine == 1, g, 1 - g) * half, HEAD)
            at = pl.ds(pl.multiple_of(chunk * depth, depth), depth)
            return (pltpu.make_async_copy(left_refs[left_of[kind]].at[at, pl.ds(first, half)], left.at[slot], ls.at[slot]),
                    pltpu.make_async_copy(right_refs[kind].at[at, :], right.at[slot], rs.at[slot]))

        def per_kind(step, go):
            for kind in range(kinds):
                run_if((step // 3) % kinds == kind, lambda kind=kind: go(kind))

        def begin(step):
            def go(kind):
                for copy in fetch(kind, step):
                    copy.start()
            per_kind(step, go)

        def away(kind):
            return send(gone.at[kind], came.at[kind], gs.at[kind], cs.at[kind], place.dev(x=place.back("x", 1)))

        def meet(n):
            q, distance = n // plan.long, plan.long - 1 - n % plan.long
            for d in sorted({-distance, distance}):
                total.dest(d, q)

        ks = from_far(plan.wide)
        total.start(ks)
        begin(jnp.int32(0))
        for k in ks[:-1]:
            total.stage_over(k)

        @pl.loop(0, steps)
        def _(step):
            run_if(step + 1 < steps, lambda: begin(step + 1))

            def ready(kind):
                for copy in fetch(kind, step):
                    copy.wait()
            per_kind(step, ready)
            slot = step % 2
            product = inner_left(left[slot], right[slot])
            fresh = step % 3 == 0

            @pl.when(fresh)
            def _():
                acc[...] = product

            @pl.when(jnp.logical_not(fresh))
            def _():
                acc[...] += product

            def done(kind):
                @pl.when(step < 3 * kinds)
                def _():
                    gone[kind] = acc[...].astype(jnp.bfloat16)
                    away(kind).start()

                @pl.when(step >= 3 * kinds)
                def _():
                    outs[kind][...] = acc[...]

            run_if(step % 3 == 2, lambda: per_kind(step, done))
            for n, at in enumerate(hooks):
                run_if(step == at, lambda n=n: meet(n))

        for n in range(len(hooks), pieces * plan.long):
            meet(n)
        out_ref[...] = total.result()
        for kind in range(kinds):
            away(kind).wait_recv()
            piece = 32

            @pl.loop(0, half // piece)
            def _(i, kind=kind):
                at = pl.ds(pl.multiple_of(i * piece, piece), piece)
                outs[kind][at, :] = outs[kind][at, :] + came[kind, at, :].astype(jnp.float32)

        for kind in range(kinds):
            away(kind).wait_send()
        total.drain()

    anywhere = pl.BlockSpec(memory_space=pl.ANY)
    sem = lambda n: pltpu.SemaphoreType.DMA((n,))
    outs = [jax.ShapeDtypeStruct((rows, width), parts.dtype)] + [jax.ShapeDtypeStruct((half, ff), jnp.float32)] * kinds
    return pl.pallas_call(
        kernel,
        out_shape=tuple(outs),
        in_specs=[anywhere] * 6,
        out_specs=tuple(pl.BlockSpec(memory_space=pltpu.VMEM) for _ in outs),
        scratch_shapes=[
            pltpu.VMEM((half, ff), jnp.float32),
            pltpu.VMEM((2, depth, half), jnp.bfloat16),
            pltpu.VMEM((2, depth, ff), jnp.bfloat16),
            pltpu.VMEM((kinds, half, ff), jnp.bfloat16),
            pltpu.VMEM((kinds, half, ff), jnp.bfloat16),
            sem(2), sem(2), sem(kinds), sem(kinds),
        ] + RowSum.scratch(plan, rows, width, parts.dtype, pieces),
        compiler_params=pltpu.CompilerParams(
            collective_id=collective_id, has_side_effects=True, vmem_limit_bytes=VMEM_MOST),
        name="scatter_experts",
    )(parts, *lefts, *rights)


def visible_bias(shape, first_key, start, first_query):
    key_pos = first_key + lax.broadcasted_iota(jnp.int32, shape, 0)
    query_pos = first_query + lax.broadcasted_iota(jnp.int32, shape, 1)
    seen = jnp.logical_and(key_pos >= start, key_pos <= query_pos)
    return jnp.where(seen, 0.0, masked_value)


def lanes(first):
    return pl.ds(pl.multiple_of(first, HEAD), HEAD)


def turned(values, cosine, sine):
    return values * cosine + pltpu.roll(values, HEAD // 2, 1) * sine


def whole_spec(*shape):
    return pl.BlockSpec(shape, lambda *s: (0,) * len(shape))


def project_kernel(x_ref, gain_ref, cos_ref, sin_ref, wq_ref, wk_ref, wv_ref, hid_ref, q_ref, kv_ref, hidden):
    @pl.when(pl.program_id(0) == 0)
    def _():
        hidden[...] = normed(x_ref[...].astype(jnp.float32), gain_ref[...]).astype(jnp.bfloat16)
        hid_ref[...] = hidden[...]

    cosine, sine = cos_ref[...], sin_ref[...]
    q = jnp.dot(hidden[...], wq_ref[...], preferred_element_type=jnp.float32)
    k = jnp.dot(hidden[...], wk_ref[...], preferred_element_type=jnp.float32)
    v = jnp.dot(hidden[...], wv_ref[...], preferred_element_type=jnp.float32)
    for h in range(q.shape[1] // HEAD):
        at = slice(h * HEAD, (h + 1) * HEAD)
        q_ref[:, at] = (turned(q[:, at], cosine, sine) * HEAD ** (-0.5)).astype(jnp.bfloat16)
        kv_ref[:, 2 * h * HEAD : (2 * h + 1) * HEAD] = turned(k[:, at], cosine, sine).astype(jnp.bfloat16)
        kv_ref[:, (2 * h + 1) * HEAD : (2 * h + 2) * HEAD] = v[:, at].astype(jnp.bfloat16)


def project(tokens, gain, cosine, sine, wq, wk, wv):
    rows, width = tokens.shape
    tile = 2 * HEAD
    column = pl.BlockSpec((width, tile), lambda i: (0, i))
    return pl.pallas_call(
        project_kernel,
        out_shape=(
            jax.ShapeDtypeStruct((rows, width), jnp.bfloat16),
            jax.ShapeDtypeStruct((rows, width), jnp.bfloat16),
            jax.ShapeDtypeStruct((rows, 2 * width), jnp.bfloat16),
        ),
        grid=(width // tile,),
        in_specs=[whole_spec(rows, width), whole_spec(1, width), whole_spec(rows, HEAD), whole_spec(rows, HEAD),
                  column, column, column],
        out_specs=(whole_spec(rows, width), pl.BlockSpec((rows, tile), lambda i: (0, i)),
                   pl.BlockSpec((rows, 2 * tile), lambda i: (0, i))),
        scratch_shapes=[pltpu.VMEM((rows, width), jnp.bfloat16)],
        cost_estimate=pl.CostEstimate(flops=6 * rows * width * width, bytes_accessed=6 * width * width, transcendentals=0),
        name="project",
    )(tokens, gain[None, :], cosine, sine, wq, wk, wv)


def attend_kernel(info, q_ref, start_ref, kv_ref, mixed_ref, low_ref, total_ref, bias, top, norm):
    step = pl.program_id(0)
    me, first_block = info[0], info[1]
    rows = q_ref.shape[0]
    block = me - step

    @pl.when(step == 0)
    def _():
        top[...] = jnp.full_like(top, masked_value)
        norm[...] = jnp.zeros_like(norm)
        mixed_ref[...] = jnp.zeros_like(mixed_ref)

    @pl.when(block >= first_block)
    def _():
        bias[...] = visible_bias((rows, rows), block * rows, start_ref[...], me * rows)

        @pl.loop(0, HEADS, unroll=5)
        def _(h):
            keys, values = kv_ref[0, :, lanes(2 * h * HEAD)], kv_ref[0, :, lanes((2 * h + 1) * HEAD)]
            scores = inner_right(keys, q_ref[:, lanes(h * HEAD)]) + bias[...]
            old = top[h]
            new = jnp.maximum(old, jnp.max(scores, axis=0, keepdims=True))
            weights = jnp.exp(scores - new)
            shrink = jnp.exp(old - new)
            top[h] = new
            norm[h] = norm[h] * shrink + jnp.sum(weights, axis=0, keepdims=True)
            mixed_ref[h] = mixed_ref[h] * shrink + inner_left(values, weights.astype(jnp.bfloat16))

    @pl.when(step == pl.num_programs(0) - 1)
    def _():
        for h in range(HEADS):
            mixed = mixed_ref[h] / norm[h]
            mixed_ref[h] = mixed
            low_ref[:, h * HEAD : (h + 1) * HEAD] = mixed.T.astype(jnp.bfloat16)
            total_ref[h] = top[h] + jnp.log(norm[h])


def attend(info, queries, start, pairs):
    rows, width = queries.shape
    steps = pairs.shape[0] // 2 + 1
    return pl.pallas_call(
        attend_kernel,
        out_shape=(
            jax.ShapeDtypeStruct((HEADS, HEAD, rows), jnp.float32),
            jax.ShapeDtypeStruct((rows, width), jnp.bfloat16),
            jax.ShapeDtypeStruct((HEADS, 1, rows), jnp.float32),
        ),
        grid_spec=pltpu.PrefetchScalarGridSpec(
            num_scalar_prefetch=1,
            grid=(steps,),
            in_specs=[
                whole_spec(rows, width),
                whole_spec(1, rows),
                pl.BlockSpec((1, rows, 2 * width), lambda s, info: (jnp.maximum(info[0] - s, info[1]), 0, 0)),
            ],
            out_specs=(whole_spec(HEADS, HEAD, rows), whole_spec(rows, width), whole_spec(HEADS, 1, rows)),
            scratch_shapes=[
                pltpu.VMEM((rows, rows), jnp.float32),
                pltpu.VMEM((HEADS, 1, rows), jnp.float32),
                pltpu.VMEM((HEADS, 1, rows), jnp.float32),
            ],
        ),
        cost_estimate=pl.CostEstimate(
            flops=4 * rows * rows * width * steps, bytes_accessed=4 * rows * width * steps, transcendentals=0
        ),
        name="attend",
    )(info, queries, start, pairs)


def attend_back_kernel(
    info, q_ref, g_ref, mixed_ref, start_ref, total_ref, cos_ref, sin_ref, kv_ref, dkv_ref, dq_ref, bias, acc, term
):
    step = pl.program_id(0)
    me, first_block = info[0], info[1]
    rows = q_ref.shape[0]
    block = me - step

    @pl.when(step == 0)
    def _():
        acc[...] = jnp.zeros_like(acc)
        for h in range(HEADS):
            grads = g_ref[:, h * HEAD : (h + 1) * HEAD].astype(jnp.float32).T
            term[h] = jnp.sum(grads * mixed_ref[h], axis=0, keepdims=True)

    @pl.when(block >= first_block)
    def _():
        bias[...] = visible_bias((rows, rows), block * rows, start_ref[...], me * rows)

        @pl.loop(0, HEADS, unroll=2)
        def _(h):
            early, late, at = lanes(2 * h * HEAD), lanes((2 * h + 1) * HEAD), lanes(h * HEAD)
            keys, values = kv_ref[0, :, early], kv_ref[0, :, late]
            queries, grads = q_ref[:, at], g_ref[:, at]
            probs = jnp.exp(inner_right(keys, queries) + bias[...] - total_ref[h])
            prob_grad = inner_right(values, grads)
            score_grad = (probs * (prob_grad - term[h])).astype(jnp.bfloat16)
            dkv_ref[0, :, late] = jnp.dot(
                probs.astype(jnp.bfloat16), grads, preferred_element_type=jnp.float32
            ).astype(jnp.bfloat16)
            dkv_ref[0, :, early] = jnp.dot(
                score_grad, queries, preferred_element_type=jnp.float32
            ).astype(jnp.bfloat16)
            acc[h] += inner_left(keys, score_grad)

    @pl.when(jnp.logical_and(block >= 0, block < first_block))
    def _():
        dkv_ref[...] = jnp.zeros_like(dkv_ref)

    @pl.when(step == pl.num_programs(0) - 1)
    def _():
        for h in range(HEADS):
            back = turned(acc[h].T * HEAD ** (-0.5), cos_ref[...], -sin_ref[...])
            dq_ref[:, h * HEAD : (h + 1) * HEAD] = back.astype(jnp.bfloat16)


def attend_back(info, queries, grads, mixed, start, total, cosine, sine, pairs):
    rows, width = queries.shape
    count = pairs.shape[0]
    steps = count // 2 + 1
    return pl.pallas_call(
        attend_back_kernel,
        out_shape=(
            jax.ShapeDtypeStruct(pairs.shape, jnp.bfloat16),
            jax.ShapeDtypeStruct((rows, width), jnp.bfloat16),
        ),
        grid_spec=pltpu.PrefetchScalarGridSpec(
            num_scalar_prefetch=1,
            grid=(steps,),
            in_specs=[
                whole_spec(rows, width),
                whole_spec(rows, width),
                whole_spec(HEADS, HEAD, rows),
                whole_spec(1, rows),
                whole_spec(HEADS, 1, rows),
                whole_spec(rows, HEAD),
                whole_spec(rows, HEAD),
                pl.BlockSpec((1, rows, 2 * width), lambda s, info: (jnp.maximum(info[0] - s, info[1]), 0, 0)),
            ],
            out_specs=(
                pl.BlockSpec((1, rows, 2 * width), lambda s, info: (jnp.maximum(info[0] - s, 0), 0, 0)),
                whole_spec(rows, width),
            ),
            scratch_shapes=[
                pltpu.VMEM((rows, rows), jnp.float32),
                pltpu.VMEM((HEADS, HEAD, rows), jnp.float32),
                pltpu.VMEM((HEADS, 1, rows), jnp.float32),
            ],
        ),
        cost_estimate=pl.CostEstimate(
            flops=10 * rows * rows * width * steps, bytes_accessed=8 * rows * width * steps, transcendentals=0
        ),
        name="attend_back",
    )(info, queries, grads, mixed, start, total, cosine, sine, pairs)


def finish_kernel(
    x_ref, gain_ref, res_ref, hid_ref, q_ref, kv_ref, cos_ref, sin_ref, wq_ref, wk_ref, wv_ref, *refs
):
    carried = (len(refs) - 6) // 2
    sums, (dq_ref, dk_ref, dv_ref, out_ref, gain_out), acc = refs[:carried], refs[carried : carried + 5], refs[-1]
    step = pl.program_id(0)
    for n, (own, out) in enumerate(zip(sums, refs[carried + 5 : -1])):
        out[...] = own[...].T if n == 2 else own[...]

    @pl.when(step == 0)
    def _():
        acc[...] = jnp.zeros_like(acc)

    cosine, sine = cos_ref[...], sin_ref[...]
    count = q_ref.shape[1] // HEAD
    keys = jnp.concatenate(
        [turned(kv_ref[:, 2 * h * HEAD : (2 * h + 1) * HEAD].astype(jnp.float32), cosine, -sine).astype(jnp.bfloat16)
         for h in range(count)], axis=1)
    values = jnp.concatenate([kv_ref[:, (2 * h + 1) * HEAD : (2 * h + 2) * HEAD] for h in range(count)], axis=1)
    grads = (q_ref[...], keys, values)
    acc[...] += (
        inner_right(grads[0], wq_ref[...]) + inner_right(grads[1], wk_ref[...]) + inner_right(grads[2], wv_ref[...])
    )
    hidden = hid_ref[...]
    for ref, grad in zip((dq_ref, dk_ref, dv_ref), grads):
        ref[...] = inner_left(hidden, grad).astype(jnp.bfloat16)

    @pl.when(step == pl.num_programs(0) - 1)
    def _():
        values, gain, grad = x_ref[...].astype(jnp.float32), gain_ref[...], acc[...]
        scale = lax.rsqrt(jnp.mean(values * values, axis=1, keepdims=True) + epsilon)
        inner = jnp.mean(gain * grad * values, axis=1, keepdims=True)
        part = scale * gain * grad - values * (scale * scale * scale) * inner
        out_ref[...] = (res_ref[...] + part).astype(jnp.bfloat16)
        gain_out[...] = jnp.sum(grad * values * scale, axis=0, keepdims=True)


def finish(tokens, gain, residual_grad, hidden, query_grad, pair_grads, cosine, sine, wq, wk, wv, sums):
    rows, width = tokens.shape
    tile = 2 * HEAD
    column = pl.BlockSpec((width, tile), lambda i: (0, i))
    part = sums[0].shape[0] * tile // width if sums else 0
    return pl.pallas_call(
        finish_kernel,
        out_shape=(
            jax.ShapeDtypeStruct((width, width), jnp.bfloat16),
            jax.ShapeDtypeStruct((width, width), jnp.bfloat16),
            jax.ShapeDtypeStruct((width, width), jnp.bfloat16),
            jax.ShapeDtypeStruct((rows, width), jnp.bfloat16),
            jax.ShapeDtypeStruct((1, width), jnp.float32),
        ) + tuple(jax.ShapeDtypeStruct(v.shape[::-1] if n == 2 else v.shape, v.dtype) for n, v in enumerate(sums)),
        grid=(width // tile,),
        in_specs=[whole_spec(rows, width), whole_spec(1, width), whole_spec(rows, width), whole_spec(rows, width),
                  pl.BlockSpec((rows, tile), lambda i: (0, i)), pl.BlockSpec((rows, 2 * tile), lambda i: (0, i)),
                  whole_spec(rows, HEAD), whole_spec(rows, HEAD), column, column, column]
        + [pl.BlockSpec((part, v.shape[1]), lambda i: (i, 0)) for v in sums],
        out_specs=(column, column, column, whole_spec(rows, width), whole_spec(1, width)) + tuple(
            pl.BlockSpec((v.shape[1], part), lambda i: (0, i)) if n == 2
            else pl.BlockSpec((part, v.shape[1]), lambda i: (i, 0)) for n, v in enumerate(sums)),
        scratch_shapes=[pltpu.VMEM((rows, width), jnp.float32)],
        cost_estimate=pl.CostEstimate(flops=12 * rows * width * width, bytes_accessed=12 * width * width, transcendentals=0),
        name="finish",
    )(tokens, gain[None, :], residual_grad, hidden, query_grad, pair_grads, cosine, sine, wq, wk, wv, *sums)


def experts_kernel(
    where_ref, x_ref, g_ref, rank_row, rank_col, share_row, wg_ref, wu_ref, wd_ref,
    back_ref, routed_ref, in_ref, pre_ref, lift_ref, mid_ref, og_ref, grads,
):
    blocks, rows, side = x_ref.shape
    capacity = in_ref.shape[0] // blocks
    width = og_ref.shape[1]
    dot = lambda left, right: jnp.dot(left, right, preferred_element_type=jnp.float32)
    shares = []
    for i in range(blocks):
        at = slice(i * capacity, (i + 1) * capacity)
        hit = rank_row[i] == lax.broadcasted_iota(jnp.int32, (capacity, rows), 0)
        pick = jnp.where(hit, 1.0, 0.0)
        shares.append(jnp.sum(pick * share_row[i], axis=1, keepdims=True))
        pick = pick.astype(jnp.bfloat16)
        in_ref[at, :] = dot(pick, x_ref[i, :, :width]).astype(jnp.bfloat16)
        grads[at, :] = dot(pick, g_ref[i]).astype(jnp.bfloat16)
    share = jnp.concatenate(shares, axis=0)
    pre = dot(in_ref[...], wg_ref[0])
    lift = dot(in_ref[...], wu_ref[0])
    silu, slope = silu_parts(pre)
    mid_ref[...] = (silu * lift).astype(jnp.bfloat16)
    lift_slope = lift * slope
    result = dot(mid_ref[...], wd_ref[0]).astype(jnp.bfloat16).astype(jnp.float32)
    grad = grads[...].astype(jnp.float32)
    gate_grad = jnp.sum(result * grad, axis=1, keepdims=True)
    og_ref[...] = (share * grad).astype(jnp.bfloat16)
    given = (share * result).astype(jnp.bfloat16)
    mid_grad = inner_right(og_ref[...], wd_ref[0])
    pre_ref[...] = (mid_grad * lift_slope).astype(jnp.bfloat16)
    lift_ref[...] = (mid_grad * silu).astype(jnp.bfloat16)
    in_grad = (inner_right(pre_ref[...], wg_ref[0]) + inner_right(lift_ref[...], wu_ref[0])).astype(jnp.bfloat16)
    lane = lax.broadcasted_iota(jnp.int32, (blocks * capacity, side - width), 1)
    high = gate_grad.astype(jnp.bfloat16).astype(jnp.float32)
    extra = jnp.where(lane == where_ref[0], high, jnp.where(lane == where_ref[1], gate_grad - high, 0.0))
    extra = extra.astype(jnp.bfloat16)
    for i in range(blocks):
        at = slice(i * capacity, (i + 1) * capacity)
        hit = rank_col[i] == lax.broadcasted_iota(jnp.int32, (rows, capacity), 1)
        put = jnp.where(hit, 1.0, 0.0).astype(jnp.bfloat16)
        back_ref[i, :, :width] = dot(put, in_grad[at, :]).astype(jnp.bfloat16)
        back_ref[i, :, width:] = dot(put, extra[at, :]).astype(jnp.bfloat16)
        routed_ref[i] = dot(put, given[at, :]).astype(jnp.bfloat16)


def run_experts(places, arrived, grads, rank, share, gate, up, down, capacity):
    count, rows, side = arrived.shape
    width, ff = gate.shape[1], gate.shape[2]
    blocks = 384 // capacity
    flat = count * capacity
    once = lambda *shape: pl.BlockSpec(shape, lambda i, p: (0,) * len(shape), pipeline_mode=pl.Buffered(1))
    lead = lambda *shape: pl.BlockSpec((blocks,) + shape, lambda i, p: (i, 0, 0))
    tall = lambda wide: pl.BlockSpec((blocks * capacity, wide), lambda i, p: (i, 0))
    shape = lambda *dims: jax.ShapeDtypeStruct(dims, jnp.bfloat16)
    return pl.pallas_call(
        experts_kernel,
        out_shape=(shape(count, rows, side), shape(count, rows, width), shape(flat, width), shape(flat, ff),
                   shape(flat, ff), shape(flat, ff), shape(flat, width)),
        grid_spec=pltpu.PrefetchScalarGridSpec(
            num_scalar_prefetch=1,
            grid=(count // blocks,),
            in_specs=[lead(rows, side), lead(rows, width), lead(1, rows), lead(rows, 1), lead(1, rows),
                      once(1, width, ff), once(1, width, ff), once(1, ff, width)],
            out_specs=(lead(rows, side), lead(rows, width), tall(width), tall(ff), tall(ff), tall(ff), tall(width)),
            scratch_shapes=[pltpu.VMEM((blocks * capacity, width), jnp.bfloat16)],
        ),
        compiler_params=pltpu.CompilerParams(vmem_limit_bytes=VMEM_MOST),
        cost_estimate=pl.CostEstimate(flops=16 * flat * width * ff, bytes_accessed=16 * flat * width, transcendentals=0),
        name="run_experts",
    )(places, arrived, grads, rank[:, None, :], rank[:, :, None], share[:, None, :], gate, up, down)


def attend_back_sum(queries, grads, mixed, start, total, cosine, sine, pairs, parts, collective_id):
    rows, width = queries.shape
    ep_count = pairs.shape[0]
    part_rows, part_width = parts[0].shape[1], sum(part.shape[2] for part in parts)
    plan, pieces = Plan(ep_count, True), 4
    place = Place(lax.axis_size("grp"), ep_count)
    n, wide = plan.planes(), plan.wide
    cuts = [0, part_width // HEAD * 3 // 4 * HEAD, part_width]
    orders = ("xba", "bxa")

    def kernel(q_ref, g_ref, mixed_ref, start_ref, total_ref, cos_ref, sin_ref, pair_ref, *refs):
        sources, refs = refs[: len(parts)], refs[len(parts) :]
        out_ref, pair_out, dq_ref, bias, acc, term, kv, staged, kv_sem = refs[:9]
        refs = refs[9:]
        place.locate()
        sums = []
        for i in range(2):
            sums.append(WholeSum(place, orders[i], pieces_of(sources, cuts[i], cuts[i + 1]), refs[:14]))
            refs = refs[14:]
        sum_rows = RowSum(plan, pieces, staged, refs)
        a, b, c = sum_rows.a, sum_rows.b, sum_rows.c
        me = plan.slot(a, b, c)
        order, ks = sum_rows.order, from_far(wide)
        turns = [(k, d) for d in order for k in ks]

        def block(turn, other):
            k, d = turns[turn]
            b0, c0 = sum_rows.source(k), jnp.where(other, 1 - c, c)
            there = both(plan.inside(a - d), plan.need(d, b, c, b0, c0))
            return there, plan.slot(a - d, b0, c0)

        def fetch(turn, other):
            there, slot = block(turn, other)
            held = jnp.where(other, 0, 1)
            return there, lambda: pltpu.make_async_copy(pair_ref.at[slot], kv.at[held], kv_sem.at[held])

        def begin(turn, other):
            there, go = fetch(turn, other)
            run_if(there, lambda: go().start())

        def compute(turn, other, target):
            there, slot = block(turn, other)
            held = 0 if other else 1

            def work():
                fetch(turn, other)[1]().wait()
                bias[...] = visible_bias((rows, rows), slot * rows, start_ref[...], me * rows)

                @pl.loop(0, HEADS, unroll=2)
                def _(h):
                    early, late, at = lanes(2 * h * HEAD), lanes((2 * h + 1) * HEAD), lanes(h * HEAD)
                    keys, values = kv[held, :, early], kv[held, :, late]
                    own, grad = q_ref[:, at], g_ref[:, at]
                    probs = jnp.exp(inner_right(keys, own) + bias[...] - total_ref[h])
                    score_grad = (probs * (inner_right(values, grad) - term[h])).astype(jnp.bfloat16)
                    target[:, late] = jnp.dot(
                        probs.astype(jnp.bfloat16), grad, preferred_element_type=jnp.float32
                    ).astype(jnp.bfloat16)
                    target[:, early] = jnp.dot(
                        score_grad, own, preferred_element_type=jnp.float32
                    ).astype(jnp.bfloat16)
                    acc[h] += inner_left(keys, score_grad)

            run_if(there, work)

        def turn_of(turn):
            k, d = turns[turn]
            i = plan.plane(a, d)
            compute(turn, True, staged.at[i, k])
            if turn + 1 < len(turns):
                begin(turn + 1, True)
            cond = sum_rows.cross(d, k, 0)[0]
            for q in range(pieces):
                run_if(cond, lambda q=q: sum_rows.cross(d, k, q)[1]().start())
            compute(turn, False, sum_rows.held.at[i, k])
            if turn + 1 < len(turns):
                begin(turn + 1, False)

        def pass_on(turn):
            k, d = turns[turn]

            @pl.loop(0, pieces)
            def _(q):
                sum_rows.first(d, k, q)
                cond, go = sum_rows.over(d, k, q)
                run_if(cond, lambda: go().start())

        begin(0, True)
        begin(0, False)
        place.greet()
        first, second = sums
        for one in sums:
            for i in range(one.n1 - 1):
                one.start(i)
        acc[...] = jnp.zeros_like(acc)
        for h in range(HEADS):
            grad = g_ref[:, h * HEAD : (h + 1) * HEAD].astype(jnp.float32).T
            term[h] = jnp.sum(grad * mixed_ref[h], axis=0, keepdims=True)
        for one in sums:
            for i in range(one.n1 - 1):
                one.stage_core(i)
        last = len(turns) - 1
        for turn in range(len(turns)):
            turn_of(turn)
            if turns[turn][0]:
                pass_on(turn)
            if turn == 0:
                for one in sums:
                    one.start(one.n1 - 1)
            if turn == last - 3:
                for one in sums:
                    one.stage_core(one.n1 - 1)
                for k2 in from_far(second.n2)[:-1]:
                    second.stage_one(k2)
            if turn == last - 2:
                sum_rows.stage_dest(order[0], 0, 2)
            if turn == last - 1:
                for k2 in from_far(first.n2)[:-1]:
                    first.stage_one(k2)
                second.stage_one(0)
                sum_rows.stage_dest(order[0], 2, 3)
        sum_rows.stage_dest(order[0], 3, pieces)
        first.stage_one(0)
        for h in range(HEADS):
            back = turned(acc[h].T * HEAD ** (-0.5), cos_ref[...], -sin_ref[...])
            dq_ref[:, h * HEAD : (h + 1) * HEAD] = back.astype(jnp.bfloat16)
        second.stage_two()
        for d in order[1:]:
            sum_rows.stage_dest(d, 0, pieces)
        pair_out[...] = sum_rows.result()
        first.stage_two()
        for i, one in enumerate(sums):
            one.stage_three(out_ref.at[:, pl.ds(cuts[i], cuts[i + 1] - cuts[i])])
        sum_rows.drain()
        for one in sums:
            one.drain()

    anywhere, near = pl.BlockSpec(memory_space=pl.ANY), pl.BlockSpec(memory_space=pltpu.VMEM)
    scratch = [
        pltpu.VMEM((rows, rows), jnp.float32),
        pltpu.VMEM((HEADS, HEAD, rows), jnp.float32),
        pltpu.VMEM((HEADS, 1, rows), jnp.float32),
        pltpu.VMEM((2, rows, 2 * width), jnp.bfloat16),
        pltpu.VMEM((n, wide, rows, 2 * width), jnp.bfloat16),
        pltpu.SemaphoreType.DMA((2,)),
    ]
    for i in range(2):
        scratch += WholeSum.scratch(place.sizes, orders[i], part_rows, cuts[i + 1] - cuts[i], parts[0].dtype, len(parts))
    scratch += RowSum.scratch(plan, rows, 2 * width, pairs.dtype, pieces)
    return pl.pallas_call(
        kernel,
        out_shape=(jax.ShapeDtypeStruct((part_rows, part_width), jnp.float32),
                   jax.ShapeDtypeStruct((rows, 2 * width), pairs.dtype),
                   jax.ShapeDtypeStruct((rows, width), jnp.bfloat16)),
        in_specs=[near] * 7 + [anywhere] * (1 + len(parts)),
        out_specs=(near, near, near),
        scratch_shapes=scratch,
        compiler_params=pltpu.CompilerParams(
            collective_id=collective_id, has_side_effects=True, vmem_limit_bytes=VMEM_MOST),
        name="attend_back_sum",
    )(queries, grads, mixed, start, total, cosine, sine, pairs, *parts)


def local(
    tokens,
    doc_lengths,
    expert_ids,
    out_grad,
    mixer_gain,
    query_weight,
    key_weight,
    value_weight,
    output_weight,
    ffn_gain,
    router_weight,
    shared_gate,
    shared_up,
    shared_down,
    expert_gate,
    expert_up,
    expert_down,
):
    rows, width = tokens.shape[1], tokens.shape[2]
    ep_count = lax.axis_size("ep")
    device_count = ep_count * lax.axis_size("grp")
    ep_index = lax.axis_index("ep")
    expert_count = router_weight.shape[1]
    capacity = min(rows, 12 * rows * TOP // (7 * expert_count))
    low = lambda v: v.astype(jnp.bfloat16)
    wide = lambda v: v.astype(jnp.float32)
    dot = lambda left, right: jnp.dot(left, right, preferred_element_type=jnp.float32)

    grad_low = out_grad[0]

    doc_ends = jnp.cumsum(doc_lengths[0])
    query_pos = ep_index * rows + jnp.arange(rows, dtype=jnp.int32)
    before = query_pos[:, None] >= doc_ends[None, :]
    start = jnp.max(jnp.where(before, doc_ends[None, :], 0), axis=1)
    info = jnp.stack([ep_index, start[0] // rows]).astype(jnp.int32)
    half_dim = HEAD // 2
    frequency = rope_base ** (-jnp.arange(half_dim, dtype=jnp.float32) / half_dim)
    angles = wide(query_pos)[:, None] * frequency[None, :]
    cosine, sine = jnp.cos(angles), jnp.sin(angles)
    cosine = jnp.concatenate([cosine, cosine], axis=1)
    sine = jnp.concatenate([-sine, sine], axis=1)

    stream = wide(tokens[0])
    hidden_low, queries, own_pairs = project(
        tokens[0], mixer_gain, cosine, sine, query_weight, key_weight, value_weight
    )
    pairs = gather_rows(own_pairs, True, 1, 8)
    grad_later, pairs = lax.optimization_barrier((grad_low, pairs))
    grads_all = lax.all_gather(grad_later, "ep", axis=0, tiled=False)
    mixed, mixed_low, log_total = attend(info, queries, start[None, :], pairs)
    mixer_out = dot(mixed_low, output_weight)
    residual = stream + mixer_out
    ffn_low = low(normed(residual, ffn_gain))

    logits = dot(ffn_low, router_weight)
    experts = jnp.arange(expert_count, dtype=jnp.int32)
    assigned = jnp.any(expert_ids[0][:, :, None] == experts[None, None, :], axis=1)
    shown = jnp.where(assigned, logits, masked_value)
    powers = jnp.where(assigned, jnp.exp(shown - jnp.max(shown, axis=1, keepdims=True)), 0.0)
    gate_probs = powers / jnp.sum(powers, axis=1, keepdims=True)
    probs_high = low(gate_probs)
    probs_rest = low(gate_probs - wide(probs_high))
    side = width + 2 * HEAD if 2 * expert_count > HEAD else width + HEAD
    pad = jnp.zeros((rows, side - width - 2 * expert_count), jnp.bfloat16)
    sent = jnp.concatenate([ffn_low, probs_high, probs_rest, pad], axis=1)
    arrived, shared_out, ffn_grad, shared_gate_part, shared_up_part, shared_down_part = gather_shared(
        sent, grad_low, shared_gate, shared_up, shared_down, 2
    )

    own = experts[None, None, :] == ep_index
    high = arrived[:, :, width : width + expert_count]
    rest = arrived[:, :, width + expert_count : width + 2 * expert_count]
    share = jnp.sum(jnp.where(own, wide(high) + wide(rest), 0.0), axis=2)
    chosen = share > 0.0
    earlier = (jnp.arange(rows)[:, None] < jnp.arange(rows)[None, :]).astype(jnp.bfloat16)
    rank = dot(low(chosen), earlier).astype(jnp.int32)
    rank = jnp.where(chosen, rank, -1)
    places = jnp.stack([ep_index, expert_count + ep_index]).astype(jnp.int32)
    back, given, flat_in, pre_grad, lift_grad, middle, result_grad = run_experts(
        places, arrived, grads_all, rank, share, expert_gate, expert_up, expert_down, capacity
    )
    routed = lax.psum_scatter(given, "ep", scatter_dimension=0)
    group_count = lax.axis_size("grp")
    if group_count == 2:
        back_sum, gate_sum, up_sum, down_sum = scatter_experts(
            back, (flat_in, result_grad), (pre_grad, lift_grad, middle), 3
        )
    else:
        back_sum = scatter_rows(back, False, 3)
        split = width // group_count
        own_down_grad = jnp.concatenate(
            [low(inner_left(middle, result_grad[:, i * split : (i + 1) * split])) for i in range(group_count)], axis=0
        )
        over_groups = lambda v: wide(lax.psum_scatter(v, "grp", scatter_dimension=0, tiled=True))[None]
        gate_sum = over_groups(low(inner_left(flat_in, pre_grad)))
        up_sum = over_groups(low(inner_left(flat_in, lift_grad)))
        down_sum = over_groups(own_down_grad)

    grad_out = wide(grad_low)
    gate_back = wide(back_sum[:, width : width + expert_count]) + wide(
        back_sum[:, width + expert_count : width + 2 * expert_count]
    )
    chosen_grad = gate_probs * (gate_back - jnp.sum(gate_probs * gate_back, axis=1, keepdims=True))
    logit_grad = low(chosen_grad)
    ffn_grad = ffn_grad + wide(back_sum[:, :width]) + inner_right(logit_grad, router_weight)
    _, ffn_pull = jax.vjp(normed, residual, ffn_gain)
    residual_part, ffn_gain_grad = ffn_pull(ffn_grad)
    residual_grad = grad_out + residual_part
    mixer_grad_low = low(residual_grad)
    mixed_grad = low(inner_right(mixer_grad_low, output_weight))
    by_device = lambda v: low(v).reshape(device_count, width // device_count, -1)
    early = [
        by_device(part)
        for part in (shared_gate_part, shared_up_part, shared_down_part, inner_left(mixed_low, mixer_grad_low))
    ]
    if ep_count > 16:
        pair_parts, query_lin_grad = attend_back(
            info, queries, mixed_grad, mixed, start[None, :], log_total, cosine, sine, pairs
        )
        pair_grads = scatter_rows(pair_parts, True, 4)
        early_sum = scatter_whole(early, 5)
    else:
        early_sum, pair_grads, query_lin_grad = attend_back_sum(
            queries, mixed_grad, mixed, start[None, :], log_total, cosine, sine, pairs, early, 5
        )

    routed, pair_grads = lax.optimization_barrier((routed, pair_grads))
    layer_out = residual + shared_out + wide(routed)
    query_part, key_part, value_part, tokens_grad, mixer_gain_grad, *carried = finish(
        tokens[0], mixer_gain, residual_grad, hidden_low, query_lin_grad, pair_grads, cosine, sine,
        query_weight, key_weight, value_weight, (gate_sum, up_sum, down_sum) if group_count == 2 else (),
    )
    if carried:
        gate_sum, up_sum, down_sum = (v[None] for v in carried)
    squares = jnp.stack(
        [jnp.sum(residual * residual), jnp.sum(mixer_out * mixer_out), jnp.sum(layer_out * layer_out)]
    )
    extras = jnp.concatenate(
        [inner_left(ffn_low, logit_grad), mixer_gain_grad.T, ffn_gain_grad[:, None],
         jnp.broadcast_to(squares[None, :], (width, 3))], axis=1
    )
    extras = jnp.pad(extras, ((0, 0), (0, HEAD - extras.shape[1])))
    late_sum = scatter_whole([by_device(v) for v in (query_part, key_part, value_part, extras)], 6)
    extra_sum = late_sum[:, 3 * width :]
    entry_count = rows * device_count * width
    stream_rms = jnp.sqrt(extra_sum[0, expert_count + 2 : expert_count + 5] / entry_count)
    ff = shared_gate.shape[1]
    return (
        low(layer_out)[None],
        tokens_grad[None],
        extra_sum[:, expert_count],
        late_sum[:, :width],
        late_sum[:, width : 2 * width],
        late_sum[:, 2 * width : 3 * width],
        early_sum[:, 3 * ff :],
        extra_sum[:, expert_count + 1],
        extra_sum[:, :expert_count],
        early_sum[:, :ff],
        early_sum[:, ff : 2 * ff],
        early_sum[:, 2 * ff : 3 * ff].T,
        gate_sum,
        up_sum,
        down_sum,
        stream_rms,
    )


def solution(mesh):
    return jax.shard_map(
        local,
        mesh=mesh,
        in_specs=(
            P("grp", "ep", None),
            P("grp", None),
            P("grp", "ep", None),
            P("grp", "ep", None),
            P(),
            P(),
            P(),
            P(),
            P(),
            P(),
            P(),
            P(),
            P(),
            P(),
            P("ep", None, None),
            P("ep", None, None),
            P("ep", None, None),
        ),
        out_specs=(
            P("grp", "ep", None),
            P("grp", "ep", None),
            P(("grp", "ep")),
            P(("grp", "ep"), None),
            P(("grp", "ep"), None),
            P(("grp", "ep"), None),
            P(("grp", "ep"), None),
            P(("grp", "ep")),
            P(("grp", "ep"), None),
            P(("grp", "ep"), None),
            P(("grp", "ep"), None),
            P(None, ("grp", "ep")),
            P("ep", "grp", None),
            P("ep", "grp", None),
            P("ep", None, "grp"),
            P(),
        ),
        check_vma=False,
    )
```
